32 devices in a mesh: dom: 8 (over z, x), mode: 4 (over y, core).
Axes of the slice: x: 2, y: 2, z: 4, core: 2. Of those that a mesh axis runs over, the one named last changes fastest.
Arguments:
- shapes: bfloat16 [3, 2048, 4096], P(None, 'dom', 'mode'), may hold values from -6 to 6
- masses: float32 [2048], P('dom'), may hold values from 0.1 to 30, as said below
- spectral: float32 [3, 4096], replicated, may hold values from 2 to 16, as said below
- frequencies: float32 [4096], replicated, may hold values from 2 to 300, as said below
- damping: float32 [4096], replicated, may hold values from 0.015 to 0.03, as said below
- recovery: bfloat16 [512, 8, 4, 3], P('dom'), may hold values from -1.75 to 1.75
- connectivity: int32 [512, 4], P('dom'), may hold values from 0 to 383
- node_count: int32 [512], P('dom'), may hold values from 2 to 4
- shared: int32 [2, 512], P(None, 'dom'), may hold values from 0 to 255
Outputs:
- response: float32 [4096], P('dom')
The draws below stay inside these ranges and needn't reach their ends.
Inputs may be any that keep to these rules, and one draw needn't show every extreme that they name: Positive node masses. Positive spectral displacements. Positive circular frequencies. Positive damping ratios. `connectivity`: codes below 256 are own nodes; the next 64 codes name the lower neighbour's upper list, the last 64 the upper neighbour's lower list. `shared`: local node numbers; entries may repeat.
All inputs are finite; a program needn't handle non-finite values.
Results may differ from the reference program's by a relative error of at most 0.0025.
Values may be sent and summed in bfloat16 or wider, within the bound.
No kernel may reach another device: no remote copies, remote signals or barrier semaphores. Data moves between devices by JAX's collectives and lax.ppermute only.
A program may use at most 64 MiB of HBM per device.

```python
import math
import jax
import jax.numpy as jnp
from jax import lax

M = 4096
CPE = 8
SLOTS = 4
ELEM_DEV = 64
NODE_DEV = 256
SHARE = 64
ELEMS = 512
NODES = 2048
COMP = 4096
N_DOM = 8


close_count = 8


def close_modes(key):
    ranking = jax.random.permutation(jax.random.fold_in(key, 101), M)
    return ranking < close_count


def draw_masses(key, part):
    position = jnp.arange(NODES, dtype=jnp.float32) / NODES
    rising = jnp.exp(math.log(3.0) * (1.0 - position))
    spread = jnp.exp(jax.random.uniform(key, (NODES,), jnp.float32, math.log(0.5), math.log(2.0)))
    return (rising * spread).astype(jnp.float32)


def draw_frequencies(key, part):
    chosen = close_modes(key)
    low_key = jax.random.fold_in(key, 102)
    high_key = jax.random.fold_in(key, 103)
    close_band = jnp.exp(jax.random.uniform(low_key, (M,), jnp.float32, math.log(2.0), math.log(2.2)))
    broad_band = jnp.exp(jax.random.uniform(high_key, (M,), jnp.float32, math.log(2.4), math.log(300.0)))
    return jnp.where(chosen, close_band, broad_band).astype(jnp.float32)


def draw_spectral(key, part):
    chosen = close_modes(key)
    broad_key = jax.random.fold_in(key, 104)
    strong_key = jax.random.fold_in(key, 105)
    broad_band = jnp.exp(jax.random.uniform(broad_key, (3, M), jnp.float32, math.log(2.0), math.log(4.0)))
    strong = jax.random.uniform(strong_key, (3, M), jnp.float32, 14.0, 16.0)
    return jnp.where(chosen[None, :], strong, broad_band).astype(jnp.float32)


def draw_damping(key, part):
    rate_key = jax.random.fold_in(key, 106)
    rates = jnp.exp(jax.random.uniform(rate_key, (M,), jnp.float32, math.log(0.015), math.log(0.03)))
    return rates.astype(jnp.float32)


def place_ends(result, key, smallest, largest):
    longest = result.shape.index(max(result.shape))
    spots = []
    for shift in (0, 1):
        where = [jax.random.randint(jax.random.fold_in(key, axis), (), 0, length) for axis, length in enumerate(result.shape)]
        where[longest] = (where[longest] + shift) % result.shape[longest]
        spots.append(tuple(where))
    return result.at[spots[0]].set(smallest).at[spots[1]].set(largest)


def levels(rng, dims, cuts, smallest, largest):
    def one(dim, shards_of):
        draws = jax.random.uniform(jax.random.fold_in(jax.random.fold_in(rng, 6), dim), (shards_of,), jnp.float32, smallest / len(cuts), largest / len(cuts))
        return jnp.repeat(jnp.exp(draws), dims[dim] // shards_of).reshape((-1,) + (1,) * (len(dims) - dim - 1))

    level = one(*cuts[0])
    for cut in cuts[1:]:
        level = level * one(*cut)
    return level


def scatter_about(stream_key, dims, scale, limit, cuts=(), held_as=jnp.bfloat16):
    result = scale * jax.random.normal(stream_key, dims, jnp.float32)
    if cuts:
        result = result * levels(stream_key, dims, cuts, -0.22, 0.18)
    return jnp.clip(result, -limit, limit).astype(held_as)


def setup_inputs(seed: int = 0) -> dict:
    seeds = jax.random.split(jax.random.key(seed), 10)
    shapes = scatter_about(seeds[0], (3, NODES, M), 1.0, 6.0, ((1, 8), (2, 4)))
    masses = draw_masses(jax.random.fold_in(seeds[9], 71), 0)
    spectral = draw_spectral(jax.random.fold_in(seeds[9], 71), 0)
    frequencies = draw_frequencies(jax.random.fold_in(seeds[9], 71), 0)
    damping = draw_damping(jax.random.fold_in(seeds[9], 71), 0)
    recovery = scatter_about(seeds[5], (ELEMS, CPE, SLOTS, 3), 12 ** -0.5, 1.75, ((0, 8),))
    connectivity = place_ends(jax.random.randint(seeds[6], (ELEMS, SLOTS), 0, NODE_DEV + 2 * SHARE), jax.random.fold_in(seeds[6], 1), 0, (NODE_DEV + 2 * SHARE) - 1).astype(jnp.int32)
    node_count = place_ends(jax.random.randint(seeds[7], (ELEMS,), 2, SLOTS + 1), jax.random.fold_in(seeds[7], 1), 2, SLOTS).astype(jnp.int32)
    shared = place_ends(jax.random.randint(seeds[8], (2, SHARE * N_DOM), 0, NODE_DEV), jax.random.fold_in(seeds[8], 1), 0, NODE_DEV - 1).astype(jnp.int32)
    return {"shapes": shapes, "masses": masses, "spectral": spectral, "frequencies": frequencies, "damping": damping, "recovery": recovery, "connectivity": connectivity, "node_count": node_count, "shared": shared}


def correlation_weights(amp_rows, amp_cols, freq_rows, freq_cols, rate_rows, rate_cols):
    ratio = freq_cols[None, :] / freq_rows[:, None]
    ratio_sq = ratio * ratio
    rate_row = rate_rows[:, None]
    rate_col = rate_cols[None, :]
    top_part = 8.0 * jnp.sqrt(rate_row * rate_col) * (rate_row + ratio * rate_col) * ratio * jnp.sqrt(ratio)
    spread = 1.0 - ratio_sq
    bottom_part = spread * spread + 4.0 * rate_row * rate_col * ratio * (1.0 + ratio_sq) + 4.0 * (rate_row * rate_row + rate_col * rate_col) * ratio_sq
    correlation = top_part / bottom_part
    return (amp_rows[:, None] * correlation * amp_cols[None, :]).astype(jnp.bfloat16)

def reference(shapes, masses, spectral, frequencies, damping, recovery, connectivity, node_count, shared):
    shape_wide = shapes.astype(jnp.float32)
    weighted = masses[None, :, None] * shape_wide
    lever_arm = lax.optimization_barrier(jnp.sum(weighted, axis=1))
    general = lax.optimization_barrier(jnp.sum(weighted * shape_wide, axis=(0, 1)))
    amplitudes = lever_arm / general[None, :] * spectral
    partition = (jnp.arange(ELEMS) // ELEM_DEV).astype(jnp.int32)[:, None]
    node_code = connectivity.astype(jnp.int32)
    local_node = partition * NODE_DEV + node_code
    low_slot = jnp.clip(node_code - NODE_DEV, 0, SHARE - 1)
    high_slot = jnp.clip(node_code - NODE_DEV - SHARE, 0, SHARE - 1)
    low_part = jnp.clip(partition - 1, 0, N_DOM - 1)
    high_part = jnp.clip(partition + 1, 0, N_DOM - 1)
    low_node = low_part * NODE_DEV + shared[1][low_part * SHARE + low_slot]
    high_node = high_part * NODE_DEV + shared[0][high_part * SHARE + high_slot]
    is_local = node_code < NODE_DEV
    is_low = jnp.logical_and(node_code >= NODE_DEV, node_code < NODE_DEV + SHARE)
    is_high = jnp.logical_and(jnp.logical_not(is_local), jnp.logical_not(is_low))
    node_index = jnp.where(is_local, local_node, jnp.where(is_low, low_node, high_node)).astype(jnp.int32)
    present = is_local | is_low & (partition > 0) | is_high & (partition < N_DOM - 1)
    gathered = jnp.take(shapes, node_index.reshape(-1), axis=1).reshape(3, ELEMS, SLOTS, M)
    gathered = jnp.where(present[None, :, :, None], gathered, jnp.zeros_like(gathered))
    slot_live = (jnp.arange(SLOTS)[None, :] < node_count[:, None]).astype(jnp.bfloat16)
    masked = recovery * slot_live[:, None, :, None]
    forces = jnp.einsum('ekna,aenm->ekm', masked.astype(jnp.float32), gathered.astype(jnp.float32))
    forces = forces.astype(jnp.bfloat16).reshape(COMP, M)
    force_wide = forces.astype(jnp.float32)
    summed = jnp.zeros((COMP,), jnp.float32)
    for direction in range(3):
        weights = correlation_weights(amplitudes[direction], amplitudes[direction], frequencies, frequencies, damping, damping)
        projected = jnp.dot(force_wide, weights.astype(jnp.float32), precision=lax.Precision.HIGHEST, preferred_element_type=jnp.float32)
        summed = summed + lax.optimization_barrier(jnp.sum(projected * force_wide, axis=1))
    return summed
```

```python
import functools
import jax
import jax.numpy as jnp
from jax import lax
from jax.experimental import pallas as pl
from jax.experimental.pallas import tpu as pltpu
from jax.sharding import PartitionSpec as P

F32 = jnp.float32
BF16 = jnp.bfloat16
VMEM = pl.BlockSpec(memory_space=pltpu.VMEM)
SMEM = pl.BlockSpec(memory_space=pltpu.SMEM)
AMP_ROWS = 16


def call(kernel, out_shape, args, flops, nbytes, smem=(), scratch=(), vmem=None):
    specs = [SMEM if i in smem else VMEM for i in range(len(args))]
    many = isinstance(out_shape, (tuple, list))
    return pl.pallas_call(
        kernel,
        out_shape=out_shape,
        in_specs=specs,
        out_specs=[VMEM] * len(out_shape) if many else VMEM,
        scratch_shapes=list(scratch),
        cost_estimate=pl.CostEstimate(flops=flops, bytes_accessed=nbytes, transcendentals=0),
        compiler_params=pltpu.CompilerParams(vmem_limit_bytes=vmem),
    )(*args)


def gather_kernel(rows_ref, shapes_ref, up_ref, down_ref):
    dims, nodes, _ = shapes_ref.shape
    width = up_ref.shape[0] // dims
    count = rows_ref.shape[1]
    node = lax.broadcasted_iota(jnp.int32, (nodes, count), 0)
    pick = jnp.where(node == rows_ref[...], 1.0, 0.0).astype(F32).T.astype(BF16)
    for d in range(dims):
        got = jnp.dot(pick, shapes_ref[d], preferred_element_type=F32).astype(BF16)
        up_ref[d * width : (d + 1) * width, :] = got[:width]
        down_ref[d * width : (d + 1) * width, :] = got[width:]


def stats_kernel(mass_ref, shapes_ref, out_ref, mass_scr):
    dims, nodes, block = shapes_ref.shape
    column = jnp.broadcast_to(mass_ref[...], (8, nodes)).T
    mass_scr[...] = jnp.broadcast_to(column[:, 0:1], (nodes, 128))

    @pl.loop(0, block // 128)
    def _(t):
        lanes = pl.ds(pl.multiple_of(t * 128, 128), 128)
        general = jnp.zeros((8, 128), F32)
        for d in range(dims):
            lever = jnp.zeros((8, 128), F32)
            for r in range(0, nodes, 16):
                wide = shapes_ref[d, r : r + 16, lanes].astype(F32)
                weighted = wide * mass_scr[r : r + 16, :]
                square = weighted * wide
                lever += weighted[:8] + weighted[8:]
                general += square[:8] + square[8:]
            out_ref[d : d + 1, lanes] = jnp.sum(lever, axis=0, keepdims=True)
        out_ref[dims : dims + 1, lanes] = jnp.sum(general, axis=0, keepdims=True)


def local_kernel(table_ref, shapes_ref, local_ref, rim_ref, own_scr):
    dims, nodes, block = shapes_ref.shape
    comps = table_ref.shape[0]
    slots = table_ref.shape[1] // (dims + 1)
    rim = rim_ref.shape[1] // (2 * dims)
    span = nodes + rim
    step = 32

    @pl.loop(0, comps // step)
    def _(t):
        rows = pl.ds(pl.multiple_of(t * step, step), step)
        table = table_ref[rows, :]
        code = lax.broadcasted_iota(jnp.int32, (step, span), 1).astype(F32)
        total = [jnp.zeros((step, span), F32) for _ in range(dims)]
        for s in range(slots):
            hit = table[:, slots * dims + s : slots * dims + s + 1] == code
            for d in range(dims):
                value = table[:, s * dims + d : s * dims + d + 1]
                total[d] = total[d] + jnp.where(hit, value, 0.0)
        for d in range(dims):
            high = total[d].astype(BF16)
            low = (total[d] - high.astype(F32)).astype(BF16)
            own_scr[rows, d * nodes : (d + 1) * nodes] = high[:, :nodes]
            own_scr[rows, (dims + d) * nodes : (dims + d + 1) * nodes] = low[:, :nodes]
            rim_ref[rows, d * rim : (d + 1) * rim] = high[:, nodes:]
            rim_ref[rows, (dims + d) * rim : (dims + d + 1) * rim] = low[:, nodes:]

    wide = 256

    @pl.loop(0, block // wide)
    def _(t):
        lanes = pl.ds(pl.multiple_of(t * wide, wide), wide)
        total = jnp.zeros((comps, wide), F32)
        for half in range(2):
            for d in range(dims):
                at = (half * dims + d) * nodes
                total += jnp.dot(
                    own_scr[:, at : at + nodes], shapes_ref[d, :, lanes], preferred_element_type=F32
                )
        local_ref[:, lanes] = total


def mode_rows(freq, rate):
    alpha = rate * freq
    inverse = 1.0 / jnp.sqrt(alpha)
    return (freq * freq * inverse, inverse, 2.0 * alpha, 2.0 * (freq / rate))


def rho_kernel(place_ref, freq_ref, rate_ref, diag_ref, mate_ref, far_ref, col_scr, row_scr):
    block = diag_ref.shape[0]
    half = block // 2
    tile = block // 4
    own, mate, far, parity = place_ref[0], place_ref[1], place_ref[2], place_ref[3]
    pad = jnp.zeros((4, block), F32)
    for which, group in enumerate((own, mate, far)):
        lanes = pl.ds(pl.multiple_of(group * block, block), block)
        rows = jnp.concatenate(list(mode_rows(freq_ref[:, lanes], rate_ref[:, lanes])) + [pad], axis=0)
        row_scr[which * 8 : which * 8 + 8, :] = rows
        if which < 2:
            col_scr[which * block : (which + 1) * block, 0:8] = rows.T

    def fill(out_ref, lead, out_row, out_col, side_row, count, cols_at, col_off, width):
        cols = [
            jnp.broadcast_to(row_scr[cols_at + q : cols_at + q + 1, pl.ds(col_off, width)], (8, width))
            for q in range(4)
        ]

        @pl.loop(0, count // 8, unroll=2)
        def _(t):
            at = pl.multiple_of(t * 8, 8)
            side = col_scr[pl.ds(side_row + at, 8), 0:8]
            high, low, alpha, zeta = (side[:, q : q + 1] for q in range(4))
            spread = high * cols[1] - low * cols[0]
            pair = alpha + cols[2]
            bottom = spread * spread + pair * (zeta + cols[3])
            value = pair / bottom
            spot = pl.ds(out_row + at, 8)
            if lead is None:
                out_ref[spot, pl.ds(out_col, width)] = value
            else:
                out_ref[lead, spot, pl.ds(out_col, width)] = value

    for j in range(4):
        fill(diag_ref, None, 0, j * tile, 0, (j + 1) * tile, 0, j * tile, tile)
    for i in range(2):
        off = pl.multiple_of((i ^ parity) * half, half)
        fill(mate_ref, i, 0, 0, i * half, half, 8, off, half)
    for c in range(0, block, half):
        fill(far_ref, None, 0, c, 0, 2 * block, 16, c, half)


def forces_kernel(
    place_ref, rim_ref, low_ref, high_ref, local_ref, stats_ref, spectral_ref, freq_ref, rate_ref,
    all_ref, part_ref, rim_scr,
):
    comps, block = local_ref.shape
    dims = spectral_ref.shape[0]
    width = low_ref.shape[0] // dims
    part = comps // 2
    own, other = place_ref[0], place_ref[5]
    lanes = pl.ds(pl.multiple_of(own * block, block), block)
    scale = 2.0 * jnp.sqrt(freq_ref[:, lanes] / rate_ref[:, lanes])
    amps = stats_ref[:dims, :] / stats_ref[dims : dims + 1, :] * spectral_ref[:, lanes] * scale
    top = amps.astype(BF16)
    rest = amps - top.astype(F32)
    middle = rest.astype(BF16)
    last = (rest - middle.astype(F32)).astype(BF16)
    fill = jnp.zeros((AMP_ROWS - 3 * dims, block), F32)
    stacked = jnp.concatenate(
        [top.astype(F32), middle.astype(F32), last.astype(F32), fill], axis=0
    ).astype(BF16)
    all_ref[comps:, :] = stacked
    part_ref[part:, :] = stacked
    for d in range(dims):
        for copy in range(2):
            at = (copy * dims + d) * 2 * width
            rim_scr[at : at + width, :] = low_ref[d * width : (d + 1) * width, :]
            rim_scr[at + width : at + 2 * width, :] = high_ref[d * width : (d + 1) * width, :]
    wide = 256

    @pl.loop(0, block // wide)
    def _(t):
        spot = pl.ds(pl.multiple_of(t * wide, wide), wide)
        total = local_ref[:, spot] + jnp.dot(rim_ref[...], rim_scr[:, spot], preferred_element_type=F32)
        all_ref[:comps, spot] = total.astype(BF16)

    part_ref[:part, :] = all_ref[pl.ds(pl.multiple_of(other * part, part), part), :]


def read_amps(ref, base, dims):
    rows = ref[base : base + AMP_ROWS, :].astype(F32)
    amps = rows[:dims] + rows[dims : 2 * dims] + rows[2 * dims : 3 * dims]
    return jnp.concatenate([amps, jnp.zeros((8 - dims, amps.shape[1]), F32)], axis=0)


def fold(value):
    total = value[:, :128]
    for c in range(128, value.shape[1], 128):
        total = total + value[:, c : c + 128]
    return total


def to_row(total):
    ones = jnp.ones((8, total.shape[1]), F32)
    return lax.dot_general(
        ones, total, (((1,), (1,)), ((), ())),
        precision=lax.Precision.HIGHEST, preferred_element_type=F32,
    )[0:1]


def weigh(rho, side, cols, dims):
    pair = side[:, 0:1] * cols[0:1]
    for d in range(1, dims):
        pair = pair + side[:, d : d + 1] * cols[d : d + 1]
    return (rho * pair).astype(BF16)


def near_kernel(dims, place_ref, own_ref, mate_ref, diag_ref, cross_ref, out_ref, acc, side_scr, row_scr, w_scr):
    comps, block = out_ref.shape[1], own_ref.shape[1]
    tile = block // 4
    half = block // 2
    parity = place_ref[3]
    own = read_amps(own_ref, comps, dims)
    row_scr[0:8, :] = own
    row_scr[8:16, :] = read_amps(mate_ref, comps, dims)
    side_scr[:, 0:8] = own.T
    turn = 0
    for j in range(4):
        cols = row_scr[0:8, j * tile : (j + 1) * tile]
        for i in range(j + 1):
            side = side_scr[i * tile : (i + 1) * tile, 0:8]
            side = side * 2.0 if i < j else side
            rho = diag_ref[i * tile : (i + 1) * tile, j * tile : (j + 1) * tile]
            w_scr[turn, i * tile : (i + 1) * tile, :] = weigh(rho, side, cols, dims)
        depth = (j + 1) * tile
        got = jnp.dot(own_ref[:comps, :depth], w_scr[turn, :depth, :], preferred_element_type=F32)
        got = fold(got * own_ref[:comps, j * tile : (j + 1) * tile].astype(F32))
        acc[...] = got if j == 0 else acc[...] + got
        turn = 1 - turn
    for i in range(2):
        for j in range(half // tile):
            at = pl.multiple_of((i ^ parity) * half + j * tile, tile)
            cols = row_scr[8:16, pl.ds(at, tile)]
            side = side_scr[i * half : (i + 1) * half, 0:8] * 2.0
            rho = cross_ref[i, :, j * tile : (j + 1) * tile]
            w_scr[turn, :half, :] = weigh(rho, side, cols, dims)
            got = jnp.dot(
                own_ref[:comps, i * half : (i + 1) * half], w_scr[turn, :half, :], preferred_element_type=F32
            )
            acc[...] += fold(got * mate_ref[:comps, pl.ds(at, tile)].astype(F32))
            turn = 1 - turn
    out_ref[...] = to_row(acc[...])


def far_kernel(dims, place_ref, own_ref, mate_ref, far_ref, rho_ref, near_ref, out_ref, acc, side_scr, w_scr):
    comps, block = out_ref.shape[1], own_ref.shape[1]
    part = comps // 2
    tile = block // 4
    here = place_ref[4]
    rows = pl.ds(pl.multiple_of(here * part, part), part)
    side_scr[:block, 0:8] = read_amps(own_ref, comps, dims).T * 2.0
    side_scr[block:, 0:8] = read_amps(mate_ref, comps, dims).T * 2.0
    far = read_amps(far_ref, part, dims)
    for j in range(4):
        turn = j % 2
        spot = slice(j * tile, (j + 1) * tile)
        cols = far[:, spot]
        for i in range(2 * block // tile):
            side = side_scr[i * tile : (i + 1) * tile, 0:8]
            w_scr[turn, i * tile : (i + 1) * tile, :] = weigh(
                rho_ref[i * tile : (i + 1) * tile, spot], side, cols, dims
            )
        got = jnp.dot(own_ref[rows, :], w_scr[turn, :block, :], preferred_element_type=F32)
        got = got + jnp.dot(mate_ref[rows, :], w_scr[turn, block:, :], preferred_element_type=F32)
        got = fold(got * far_ref[:part, spot].astype(F32))
        acc[...] = got if j == 0 else acc[...] + got
    cross = to_row(acc[...])
    out_ref[...] = near_ref[...]
    lanes = pl.ds(pl.multiple_of(here * part, part), part)
    out_ref[:, lanes] = near_ref[:, lanes] + cross


def four_groups(
    shapes, masses, spectral, frequencies, damping, recovery, connectivity, node_count, shared
):
    dims, nodes, block = shapes.shape
    elems, slots = connectivity.shape
    per_elem = recovery.shape[1]
    comps = elems * per_elem
    part = comps // 2
    width = shared.shape[1]
    parts = lax.axis_size("dom")
    group = lax.axis_index("mode").astype(jnp.int32)
    place = jnp.stack(
        [group, group ^ 1, group ^ 2, group & 1, group >> 1, 1 - (group >> 1)]
    ).astype(jnp.int32)
    sds = jax.ShapeDtypeStruct

    picked = jnp.concatenate([shared[1], shared[0]]).reshape(1, 2 * width)
    up, down = call(
        gather_kernel,
        (sds((dims * width, block), BF16), sds((dims * width, block), BF16)),
        (picked, shapes), 2 * 2 * width * nodes * dims * block, 2 * dims * nodes * block,
    )
    ahead = [(i, i + 1) for i in range(parts - 1)]
    back = [(i + 1, i) for i in range(parts - 1)]
    low = lax.ppermute(up, "dom", ahead)
    high = lax.ppermute(down, "dom", back)

    stats = call(
        stats_kernel, sds((dims + 1, block), F32), (masses.reshape(1, nodes), shapes),
        5 * dims * nodes * block, 2 * dims * nodes * block,
        scratch=[pltpu.VMEM((nodes, 128), F32)],
    )
    if parts & (parts - 1):
        stats = lax.psum(stats, "dom")
    else:
        reach = 1
        while reach < parts:
            stats = stats + lax.ppermute(stats, "dom", [(i, i ^ reach) for i in range(parts)])
            reach *= 2

    used = jnp.where(jnp.arange(slots)[None, :] < node_count[:, None], connectivity, -1)
    used = jnp.broadcast_to(used[:, None, :], (elems, per_elem, slots)).astype(F32)
    table = jnp.concatenate(
        [recovery.reshape(elems, per_elem, slots * dims).astype(F32), used], axis=-1
    ).reshape(comps, slots * (dims + 1))
    local, rim = call(
        local_kernel,
        (sds((comps, block), F32), sds((comps, 2 * dims * 2 * width), BF16)),
        (table, shapes), 4 * comps * dims * nodes * block, 6 * dims * nodes * block,
        scratch=[pltpu.VMEM((comps, 2 * dims * nodes), BF16)],
    )
    freq = frequencies.reshape(1, -1)
    rate = damping.reshape(1, -1)
    rho_diag, rho_mate, rho_far = call(
        rho_kernel,
        (sds((block, block), F32), sds((2, block // 2, block // 2), F32), sds((2 * block, block), F32)),
        (place, freq, rate), 60 * block * block, 14 * block * block, smem=(0,),
        scratch=[pltpu.VMEM((2 * block, 128), F32), pltpu.VMEM((24, block), F32)],
    )
    forces, sent = call(
        forces_kernel,
        (sds((comps + AMP_ROWS, block), BF16), sds((part + AMP_ROWS, block), BF16)),
        (place, rim, low, high, local, stats, spectral, freq, rate),
        8 * comps * dims * width * block, 8 * comps * block, smem=(0,),
        scratch=[pltpu.VMEM((2 * dims * 2 * width, block), BF16)],
    )
    far = lax.ppermute(sent, "mode", [(i, i ^ 2) for i in range(4)])
    mate = lax.ppermute(forces, "mode", [(i, i ^ 1) for i in range(4)])
    near = call(
        functools.partial(near_kernel, dims), sds((1, comps), F32),
        (place, forces, mate, rho_diag, rho_mate), 2 * comps * block * block, 6 * block * block,
        smem=(0,),
        scratch=[
            pltpu.VMEM((comps, 128), F32), pltpu.VMEM((block, 128), F32),
            pltpu.VMEM((16, block), F32), pltpu.VMEM((2, block, block // 4), BF16),
        ],
    )
    value = call(
        functools.partial(far_kernel, dims), sds((1, comps), F32),
        (place, forces, mate, far, rho_far, near), 2 * comps * block * block, 8 * block * block,
        smem=(0,),
        scratch=[
            pltpu.VMEM((part, 128), F32), pltpu.VMEM((2 * block, 128), F32),
            pltpu.VMEM((2, 2 * block, block // 4), BF16),
        ],
    )
    return lax.psum(value.reshape(comps), "mode")


def extended_2(block, sides, width):
    for axis, dim in sides:
        count = lax.axis_size(axis)
        forward = [(i, i + 1) for i in range(count - 1)]
        backward = [(target, source) for source, target in forward]
        low = lax.ppermute(
            lax.slice_in_dim(block, block.shape[dim] - width, None, axis=dim), axis, forward
        )
        high = lax.ppermute(lax.slice_in_dim(block, 0, width, axis=dim), axis, backward)
        block = jnp.concatenate([low, block, high], axis=dim)
    return block


def shifted(value, axis, steps):
    count = lax.axis_size(axis)
    pairs = [(source, (source + steps) % count) for source in range(count)]
    return lax.ppermute(value, axis, pairs)


def correlation_block(freq_rows, freq_cols, rate_rows, rate_cols):
    ratio = freq_cols[None, :] / freq_rows[:, None]
    ratio_sq = ratio * ratio
    rate_row = rate_rows[:, None]
    rate_col = rate_cols[None, :]
    top_part = (
        8.0
        * jnp.sqrt(rate_row * rate_col)
        * (rate_row + ratio * rate_col)
        * ratio
        * jnp.sqrt(ratio)
    )
    spread = 1.0 - ratio_sq
    bottom_part = (
        spread * spread
        + 4.0 * rate_row * rate_col * ratio * (1.0 + ratio_sq)
        + 4.0 * (rate_row * rate_row + rate_col * rate_col) * ratio_sq
    )
    return top_part / bottom_part


def block_terms(own_forces, own_start, far_forces, far_start, amplitudes, frequencies, damping):
    row_count = own_forces.shape[1]
    col_count = far_forces.shape[1]
    freq_rows = lax.dynamic_slice_in_dim(frequencies, own_start, row_count)
    freq_cols = lax.dynamic_slice_in_dim(frequencies, far_start, col_count)
    rate_rows = lax.dynamic_slice_in_dim(damping, own_start, row_count)
    rate_cols = lax.dynamic_slice_in_dim(damping, far_start, col_count)
    correlation = correlation_block(freq_rows, freq_cols, rate_rows, rate_cols)
    amp_rows = lax.dynamic_slice_in_dim(amplitudes, own_start, row_count, 1)
    amp_cols = lax.dynamic_slice_in_dim(amplitudes, far_start, col_count, 1)
    weights = (amp_rows.T[:, :, None] * correlation[:, None, :] * amp_cols[None, :, :]).astype(
        jnp.bfloat16
    )
    weights = weights.reshape(row_count, 3 * col_count)
    projected = jnp.dot(own_forces, weights, preferred_element_type=jnp.float32)
    projected = projected.reshape(own_forces.shape[0], 3, col_count)
    far_wide = far_forces.astype(jnp.float32)
    return jnp.sum(projected * far_wide[:, None, :], axis=(1, 2))


def any_groups(
    shapes, masses, spectral, frequencies, damping, recovery, connectivity, node_count, shared
):
    rim_width = shared.shape[1]
    block_width = shapes.shape[2]
    elem_count = connectivity.shape[0]
    slot_count = connectivity.shape[1]
    mode_index = lax.axis_index("mode")
    own_start = mode_index * block_width
    shape_wide = shapes.astype(jnp.float32)
    weighted = masses[None, :, None] * shape_wide
    lever_arm = jnp.sum(weighted, axis=1)
    general = jnp.sum(weighted * shape_wide, axis=(0, 1))
    lever_sum, general_sum = lax.psum((lever_arm, general), "dom")
    own_spectral = lax.dynamic_slice_in_dim(spectral, own_start, block_width, 1)
    local_amps = lever_sum / general_sum[None, :] * own_spectral
    amplitudes = lax.all_gather(local_amps, "mode", axis=1, tiled=True)
    outgoing = jnp.concatenate(
        [jnp.take(shapes, shared[0], axis=1), jnp.take(shapes, shared[1], axis=1)], axis=1
    )
    extended = extended_2(outgoing, (("dom", 1),), rim_width)
    node_table = jnp.concatenate(
        [shapes, extended[:, :rim_width], extended[:, 3 * rim_width :]], axis=1
    )
    gathered = jnp.take(node_table, connectivity.reshape(-1), axis=1).reshape(
        3, elem_count, slot_count, block_width
    )
    slot_live = (jnp.arange(slot_count)[None, :] < node_count[:, None]).astype(jnp.bfloat16)
    masked = recovery * slot_live[:, None, :, None]
    forces = jnp.einsum("ekna,aenm->ekm", masked, gathered, preferred_element_type=jnp.float32)
    forces = forces.astype(jnp.bfloat16).reshape(elem_count * recovery.shape[1], block_width)
    groups = lax.axis_size("mode")
    half_count = groups // 2
    partial_value = block_terms(
        forces, own_start, forces, own_start, amplitudes, frequencies, damping
    )

    def advance(turn_index, carried):
        incoming, summed = carried
        incoming = shifted(incoming, "mode", 1)
        source = (mode_index - turn_index) % groups * block_width
        factor = jnp.where(turn_index == half_count, jnp.float32(1.0), jnp.float32(2.0))
        summed = summed + factor * block_terms(
            forces, own_start, incoming, source, amplitudes, frequencies, damping
        )
        return (incoming, summed)

    carried = lax.fori_loop(1, half_count + 1, advance, (forces, partial_value))
    partial_value = carried[1]
    return lax.psum(partial_value, "mode")


def solution(mesh):
    in_specs = (
        P(None, "dom", "mode"),
        P("dom"),
        P(),
        P(),
        P(),
        P("dom", None, None, None),
        P("dom", None),
        P("dom"),
        P(None, "dom"),
    )
    out_specs = P("dom")
    step = four_groups if mesh.shape["mode"] == 4 else any_groups
    return jax.shard_map(
        step, mesh=mesh, in_specs=in_specs, out_specs=out_specs, check_vma=False
    )
```

```python
import functools
import jax
import jax.numpy as jnp
from jax import lax
from jax.experimental import pallas as pl
from jax.experimental.pallas import tpu as pltpu
from jax.sharding import PartitionSpec as P

F32 = jnp.float32
BF16 = jnp.bfloat16
VMEM = pl.BlockSpec(memory_space=pltpu.VMEM)
SMEM = pl.BlockSpec(memory_space=pltpu.SMEM)
AMP_ROWS = 16


def call(kernel, out_shape, args, flops, nbytes, smem=(), scratch=(), vmem=24 << 20, after=()):
    count = len(args)
    specs = [SMEM if i in smem else VMEM for i in range(count)]
    specs += [pl.BlockSpec(memory_space=pl.ANY)] * len(after)
    many = isinstance(out_shape, (tuple, list))

    def body(*refs):
        kernel(*refs[:count], *refs[count + len(after) :])

    return pl.pallas_call(
        body,
        out_shape=out_shape,
        in_specs=specs,
        out_specs=[VMEM] * len(out_shape) if many else VMEM,
        scratch_shapes=list(scratch),
        cost_estimate=pl.CostEstimate(flops=flops, bytes_accessed=nbytes, transcendentals=0),
        compiler_params=pltpu.CompilerParams(vmem_limit_bytes=vmem),
        name=getattr(kernel, "func", kernel).__name__,
    )(*args, *after)


def gather_kernel(rows_ref, shapes_ref, up_ref, down_ref):
    dims, nodes, _ = shapes_ref.shape
    width = up_ref.shape[0] // dims
    count = rows_ref.shape[1]
    node = lax.broadcasted_iota(jnp.int32, (nodes, count), 0)
    pick = jnp.where(node == rows_ref[...], 1.0, 0.0).astype(F32).T.astype(BF16)
    for d in range(dims):
        got = jnp.dot(pick, shapes_ref[d], preferred_element_type=F32).astype(BF16)
        up_ref[d * width : (d + 1) * width, :] = got[:width]
        down_ref[d * width : (d + 1) * width, :] = got[width:]


def stats_kernel(mass_ref, shapes_ref, out_ref, mass_scr):
    dims, nodes, block = shapes_ref.shape
    column = jnp.broadcast_to(mass_ref[...], (8, nodes)).T
    mass_scr[...] = jnp.broadcast_to(column[:, 0:1], (nodes, 128))

    @pl.loop(0, block // 128)
    def _(t):
        lanes = pl.ds(pl.multiple_of(t * 128, 128), 128)
        general = jnp.zeros((8, 128), F32)
        for d in range(dims):
            lever = jnp.zeros((8, 128), F32)
            for r in range(0, nodes, 16):
                wide = shapes_ref[d, r : r + 16, lanes].astype(F32)
                weighted = wide * mass_scr[r : r + 16, :]
                square = weighted * wide
                lever += weighted[:8] + weighted[8:]
                general += square[:8] + square[8:]
            out_ref[d : d + 1, lanes] = jnp.sum(lever, axis=0, keepdims=True)
        out_ref[dims : dims + 1, lanes] = jnp.sum(general, axis=0, keepdims=True)


def local_kernel(dims, table_ref, shapes_ref, local_ref, rim_ref, own_scr):
    nodes, block = shapes_ref.shape[0] // dims, shapes_ref.shape[1]
    comps = table_ref.shape[0]
    slots = table_ref.shape[1] // (dims + 1)
    rim = rim_ref.shape[1] // (2 * dims)
    span = nodes + rim
    step = 32

    @pl.loop(0, comps // step, unroll=2)
    def _(t):
        rows = pl.ds(pl.multiple_of(t * step, step), step)
        table = table_ref[rows, :]
        code = lax.broadcasted_iota(jnp.int32, (step, span), 1).astype(F32)
        total = [jnp.zeros((step, span), F32) for _ in range(dims)]
        for s in range(slots):
            hit = table[:, slots * dims + s : slots * dims + s + 1] == code
            for d in range(dims):
                value = table[:, s * dims + d : s * dims + d + 1]
                total[d] = total[d] + jnp.where(hit, value, 0.0)
        for d in range(dims):
            high = total[d].astype(BF16)
            low = (total[d] - high.astype(F32)).astype(BF16)
            own_scr[0, rows, d * nodes : (d + 1) * nodes] = high[:, :nodes]
            own_scr[1, rows, d * nodes : (d + 1) * nodes] = low[:, :nodes]
            rim_ref[rows, d * rim : (d + 1) * rim] = high[:, nodes:]
            rim_ref[rows, (dims + d) * rim : (dims + d + 1) * rim] = low[:, nodes:]

    wide = 256
    for c in range(0, block, wide):
        total = jnp.dot(own_scr[0], shapes_ref[:, c : c + wide], preferred_element_type=F32)
        total = total + jnp.dot(own_scr[1], shapes_ref[:, c : c + wide], preferred_element_type=F32)
        local_ref[:, c : c + wide] = total


def mode_rows(freq, rate):
    alpha = rate * freq
    inverse = 1.0 / jnp.sqrt(alpha)
    return (freq * freq * inverse, inverse, 2.0 * alpha, 2.0 * (freq / rate))


def place_modes(freq_ref, rate_ref, row_scr, col_scr, groups, sides, block):
    for which, group in enumerate(groups):
        lanes = pl.ds(pl.multiple_of(group * block, block), block)
        rows = jnp.concatenate(list(mode_rows(freq_ref[:, lanes], rate_ref[:, lanes])) * 2, axis=0)
        row_scr[which * 8 : which * 8 + 8, :] = rows
        if which < sides:
            turned = rows.T
            for q in range(4):
                col_scr[q, which * block : (which + 1) * block, :] = jnp.broadcast_to(
                    turned[:, q : q + 1], (block, 128)
                )


def fill_rho(row_scr, col_scr, out_ref, out_col, side_row, count, cols_at, col_off, tile):
    step = 64
    cols = [
        jnp.broadcast_to(row_scr[cols_at + q : cols_at + q + 1, pl.ds(col_off, tile)], (8, tile))
        for q in range(4)
    ]

    @pl.loop(0, count // step)
    def _(t):
        for k in range(0, step, 8):
            at = pl.multiple_of(t * step, step) + k
            high, low, alpha, zeta = (col_scr[q, pl.ds(side_row + at, 8), :] for q in range(4))
            for c in range(0, tile, 128):
                col = [value[:, c : c + 128] for value in cols]
                spread = high * col[1] - low * col[0]
                pair = alpha + col[2]
                bottom = spread * spread + pair * (zeta + col[3])
                out_ref[pl.ds(at, 8), out_col + c : out_col + c + 128] = pair / bottom


def rho_near_kernel(place_ref, freq_ref, rate_ref, diag_ref, mate_ref, col_scr, row_scr):
    block = diag_ref.shape[0]
    half = block // 2
    tile = block // 4
    own, mate, parity = place_ref[0], place_ref[1], place_ref[3]
    place_modes(freq_ref, rate_ref, row_scr, col_scr, (own, mate), 1, block)
    for j in range(4):
        fill_rho(row_scr, col_scr, diag_ref, j * tile, 0, (j + 1) * tile, 0, j * tile, tile)
    for i in range(2):
        for j in range(2):
            off = pl.multiple_of((i ^ parity) * half + j * tile, tile)
            fill_rho(row_scr, col_scr, mate_ref.at[i], j * tile, i * half, half, 8, off, tile)


def rho_far_kernel(place_ref, freq_ref, rate_ref, far_ref, col_scr, row_scr):
    block = far_ref.shape[1]
    tile = block // 4
    own, mate, far = place_ref[0], place_ref[1], place_ref[2]
    place_modes(freq_ref, rate_ref, row_scr, col_scr, (own, mate, far), 2, block)
    for j in range(4):
        fill_rho(row_scr, col_scr, far_ref, j * tile, 0, 2 * block, 16, j * tile, tile)


def forces_kernel(
    place_ref, rim_ref, low_ref, high_ref, local_ref, stats_ref, spectral_ref, freq_ref, rate_ref,
    all_ref, part_ref, rim_scr,
):
    comps, block = local_ref.shape
    dims = spectral_ref.shape[0]
    width = low_ref.shape[0] // dims
    part = comps // 2
    own, other = place_ref[0], place_ref[5]
    lanes = pl.ds(pl.multiple_of(own * block, block), block)
    scale = 2.0 * jnp.sqrt(freq_ref[:, lanes] / rate_ref[:, lanes])
    amps = stats_ref[:dims, :] / stats_ref[dims : dims + 1, :] * spectral_ref[:, lanes] * scale
    top = amps.astype(BF16)
    rest = amps - top.astype(F32)
    middle = rest.astype(BF16)
    last = (rest - middle.astype(F32)).astype(BF16)
    fill = jnp.zeros((AMP_ROWS - 3 * dims, block), F32)
    stacked = jnp.concatenate(
        [top.astype(F32), middle.astype(F32), last.astype(F32), fill], axis=0
    ).astype(BF16)
    all_ref[comps:, :] = stacked
    part_ref[part:, :] = stacked
    for d in range(dims):
        for copy in range(2):
            at = (copy * dims + d) * 2 * width
            rim_scr[at : at + width, :] = low_ref[d * width : (d + 1) * width, :]
            rim_scr[at + width : at + 2 * width, :] = high_ref[d * width : (d + 1) * width, :]
    wide = 256
    for c in range(0, block, wide):
        spot = slice(c, c + wide)
        total = local_ref[:, spot] + jnp.dot(rim_ref[...], rim_scr[:, spot], preferred_element_type=F32)
        all_ref[:comps, spot] = total.astype(BF16)

    part_ref[:part, :] = all_ref[pl.ds(pl.multiple_of(other * part, part), part), :]


def read_amps(ref, base, dims):
    rows = ref[base : base + AMP_ROWS, :].astype(F32)
    amps = rows[:dims] + rows[dims : 2 * dims] + rows[2 * dims : 3 * dims]
    return jnp.concatenate([amps, jnp.zeros((8 - dims, amps.shape[1]), F32)], axis=0)


def fold(value):
    total = value[:, :128]
    for c in range(128, value.shape[1], 128):
        total = total + value[:, c : c + 128]
    return total


def to_row(total):
    ones = jnp.ones((8, total.shape[1]), F32)
    return lax.dot_general(
        ones, total, (((1,), (1,)), ((), ())),
        precision=lax.Precision.HIGHEST, preferred_element_type=F32,
    )[0:1]


def spread_sides(side_scr, at, amps, dims):
    sides = amps.T
    for d in range(dims):
        side_scr[d, at : at + amps.shape[1], :] = jnp.broadcast_to(sides[:, d : d + 1], (amps.shape[1], 128))


def weigh(w_scr, turn, at, rho, side_scr, side_at, cols, dims, factor):
    for c in range(0, rho.shape[1], 128):
        col = [jnp.broadcast_to(cols[d : d + 1, c : c + 128] * factor, (16, 128)) for d in range(dims)]
        for r in range(0, rho.shape[0], 16):
            pair = side_scr[0, side_at + r : side_at + r + 16, :] * col[0]
            for d in range(1, dims):
                pair = pair + side_scr[d, side_at + r : side_at + r + 16, :] * col[d]
            w_scr[turn, at + r : at + r + 16, c : c + 128] = (rho[r : r + 16, c : c + 128] * pair).astype(BF16)


def near_kernel(dims, place_ref, own_ref, mate_ref, diag_ref, cross_ref, out_ref, acc, side_scr, row_scr, w_scr):
    comps, block = out_ref.shape[1], own_ref.shape[1]
    tile = block // 4
    half = block // 2
    parity = place_ref[3]
    own = read_amps(own_ref, comps, dims)
    row_scr[0:8, :] = own
    row_scr[8:16, :] = read_amps(mate_ref, comps, dims)
    spread_sides(side_scr, 0, own, dims)
    turn = 0
    for j in range(4):
        cols = row_scr[0:8, j * tile : (j + 1) * tile]
        for i in range(j + 1):
            rho = diag_ref.at[i * tile : (i + 1) * tile, j * tile : (j + 1) * tile]
            weigh(w_scr, turn, i * tile, rho, side_scr, i * tile, cols, dims, 2.0 if i < j else 1.0)
        depth = (j + 1) * tile
        got = jnp.dot(own_ref[:comps, :depth], w_scr[turn, :depth, :], preferred_element_type=F32)
        got = fold(got * own_ref[:comps, j * tile : (j + 1) * tile].astype(F32))
        acc[...] = got if j == 0 else acc[...] + got
        turn = 1 - turn
    for i in range(2):
        for j in range(half // tile):
            at = pl.multiple_of((i ^ parity) * half + j * tile, tile)
            cols = row_scr[8:16, pl.ds(at, tile)]
            rho = cross_ref.at[i, :, j * tile : (j + 1) * tile]
            weigh(w_scr, turn, 0, rho, side_scr, i * half, cols, dims, 2.0)
            got = jnp.dot(
                own_ref[:comps, i * half : (i + 1) * half], w_scr[turn, :half, :], preferred_element_type=F32
            )
            acc[...] += fold(got * mate_ref[:comps, pl.ds(at, tile)].astype(F32))
            turn = 1 - turn
    out_ref[...] = to_row(acc[...])


def far_kernel(dims, place_ref, own_ref, mate_ref, far_ref, rho_ref, near_ref, out_ref, acc, side_scr, w_scr):
    comps, block = out_ref.shape[1], own_ref.shape[1]
    part = comps // 2
    tile = block // 4
    here = place_ref[4]
    rows = pl.ds(pl.multiple_of(here * part, part), part)
    spread_sides(side_scr, 0, read_amps(own_ref, comps, dims), dims)
    spread_sides(side_scr, block, read_amps(mate_ref, comps, dims), dims)
    far = read_amps(far_ref, part, dims)
    for j in range(4):
        turn = j % 2
        spot = slice(j * tile, (j + 1) * tile)
        cols = far[:, spot]
        weigh(w_scr, turn, 0, rho_ref.at[:, spot], side_scr, 0, cols, dims, 2.0)
        got = jnp.dot(own_ref[rows, :], w_scr[turn, :block, :], preferred_element_type=F32)
        got = got + jnp.dot(mate_ref[rows, :], w_scr[turn, block:, :], preferred_element_type=F32)
        got = fold(got * far_ref[:part, spot].astype(F32))
        acc[...] = got if j == 0 else acc[...] + got
    cross = to_row(acc[...])
    out_ref[...] = near_ref[...]
    lanes = pl.ds(pl.multiple_of(here * part, part), part)
    out_ref[:, lanes] = near_ref[:, lanes] + cross


def four_groups(
    shapes, masses, spectral, frequencies, damping, recovery, connectivity, node_count, shared
):
    dims, nodes, block = shapes.shape
    elems, slots = connectivity.shape
    per_elem = recovery.shape[1]
    comps = elems * per_elem
    part = comps // 2
    width = shared.shape[1]
    parts = lax.axis_size("dom")
    group = lax.axis_index("mode").astype(jnp.int32)
    place = jnp.stack(
        [group, group ^ 1, group ^ 2, group & 1, group >> 1, 1 - (group >> 1)]
    ).astype(jnp.int32)
    sds = jax.ShapeDtypeStruct

    picked = jnp.concatenate([shared[1], shared[0]]).reshape(1, 2 * width)
    up, down = call(
        gather_kernel,
        (sds((dims * width, block), BF16), sds((dims * width, block), BF16)),
        (picked, shapes), 2 * 2 * width * nodes * dims * block, 2 * dims * nodes * block,
    )
    ahead = [(i, i + 1) for i in range(parts - 1)]
    back = [(i + 1, i) for i in range(parts - 1)]
    low = lax.ppermute(up, "dom", ahead)
    high = lax.ppermute(down, "dom", back)

    stats = call(
        stats_kernel, sds((dims + 1, block), F32), (masses.reshape(1, nodes), shapes),
        5 * dims * nodes * block, 2 * dims * nodes * block,
        scratch=[pltpu.VMEM((nodes, 128), F32)], after=(up,),
    )
    steps = [stats]
    if parts & (parts - 1):
        stats = lax.psum(stats, "dom")
        steps += [stats, stats]
    else:
        reach = 1
        while reach < parts:
            stats = stats + lax.ppermute(stats, "dom", [(i, i ^ reach) for i in range(parts)])
            steps.append(stats)
            reach *= 2
    steps += [stats] * 2

    used = jnp.where(jnp.arange(slots)[None, :] < node_count[:, None], connectivity, -1)
    used = jnp.broadcast_to(used[:, None, :], (elems, per_elem, slots)).astype(F32)
    table = jnp.concatenate(
        [recovery.reshape(elems, per_elem, slots * dims).astype(F32), used], axis=-1
    ).reshape(comps, slots * (dims + 1))
    local, rim = call(
        functools.partial(local_kernel, dims),
        (sds((comps, block), F32), sds((comps, 2 * dims * 2 * width), BF16)),
        (table, shapes.reshape(dims * nodes, block)), 4 * comps * dims * nodes * block, 6 * dims * nodes * block,
        scratch=[pltpu.VMEM((2, comps, dims * nodes), BF16)],
    )
    freq = frequencies.reshape(1, -1)
    rate = damping.reshape(1, -1)
    rho_diag, rho_mate = call(
        rho_near_kernel,
        (sds((block, block), F32), sds((2, block // 2, block // 2), F32)),
        (place, freq, rate), 20 * block * block, 5 * block * block, smem=(0,),
        scratch=[pltpu.VMEM((4, block, 128), F32), pltpu.VMEM((16, block), F32)],
        after=(steps[1],),
    )
    rho_far = call(
        rho_far_kernel, sds((2 * block, block), F32), (place, freq, rate),
        40 * block * block, 8 * block * block, smem=(0,),
        scratch=[pltpu.VMEM((4, 2 * block, 128), F32), pltpu.VMEM((24, block), F32)],
        after=(steps[2],),
    )
    forces, sent = call(
        forces_kernel,
        (sds((comps + AMP_ROWS, block), BF16), sds((part + AMP_ROWS, block), BF16)),
        (place, rim, low, high, local, stats, spectral, freq, rate),
        8 * comps * dims * width * block, 8 * comps * block, smem=(0,),
        scratch=[pltpu.VMEM((2 * dims * 2 * width, block), BF16)], after=(rho_diag, rho_far),
    )
    far = lax.ppermute(sent, "mode", [(i, i ^ 2) for i in range(4)])
    mate = lax.ppermute(forces, "mode", [(i, i ^ 1) for i in range(4)])
    near = call(
        functools.partial(near_kernel, dims), sds((1, comps), F32),
        (place, forces, mate, rho_diag, rho_mate), 2 * comps * block * block, 6 * block * block,
        smem=(0,),
        scratch=[
            pltpu.VMEM((comps, 128), F32), pltpu.VMEM((dims, block, 128), F32),
            pltpu.VMEM((16, block), F32), pltpu.VMEM((2, block, block // 4), BF16),
        ],
    )
    value = call(
        functools.partial(far_kernel, dims), sds((1, comps), F32),
        (place, forces, mate, far, rho_far, near), 2 * comps * block * block, 8 * block * block,
        smem=(0,),
        scratch=[
            pltpu.VMEM((part, 128), F32), pltpu.VMEM((dims, 2 * block, 128), F32),
            pltpu.VMEM((2, 2 * block, block // 4), BF16),
        ],
    )
    return lax.psum(value.reshape(comps), "mode")


def extended_2(block, sides, width):
    for axis, dim in sides:
        count = lax.axis_size(axis)
        forward = [(i, i + 1) for i in range(count - 1)]
        backward = [(target, source) for source, target in forward]
        low = lax.ppermute(
            lax.slice_in_dim(block, block.shape[dim] - width, None, axis=dim), axis, forward
        )
        high = lax.ppermute(lax.slice_in_dim(block, 0, width, axis=dim), axis, backward)
        block = jnp.concatenate([low, block, high], axis=dim)
    return block


def shifted(value, axis, steps):
    count = lax.axis_size(axis)
    pairs = [(source, (source + steps) % count) for source in range(count)]
    return lax.ppermute(value, axis, pairs)


def correlation_block(freq_rows, freq_cols, rate_rows, rate_cols):
    ratio = freq_cols[None, :] / freq_rows[:, None]
    ratio_sq = ratio * ratio
    rate_row = rate_rows[:, None]
    rate_col = rate_cols[None, :]
    top_part = (
        8.0
        * jnp.sqrt(rate_row * rate_col)
        * (rate_row + ratio * rate_col)
        * ratio
        * jnp.sqrt(ratio)
    )
    spread = 1.0 - ratio_sq
    bottom_part = (
        spread * spread
        + 4.0 * rate_row * rate_col * ratio * (1.0 + ratio_sq)
        + 4.0 * (rate_row * rate_row + rate_col * rate_col) * ratio_sq
    )
    return top_part / bottom_part


def block_terms(own_forces, own_start, far_forces, far_start, amplitudes, frequencies, damping):
    row_count = own_forces.shape[1]
    col_count = far_forces.shape[1]
    freq_rows = lax.dynamic_slice_in_dim(frequencies, own_start, row_count)
    freq_cols = lax.dynamic_slice_in_dim(frequencies, far_start, col_count)
    rate_rows = lax.dynamic_slice_in_dim(damping, own_start, row_count)
    rate_cols = lax.dynamic_slice_in_dim(damping, far_start, col_count)
    correlation = correlation_block(freq_rows, freq_cols, rate_rows, rate_cols)
    amp_rows = lax.dynamic_slice_in_dim(amplitudes, own_start, row_count, 1)
    amp_cols = lax.dynamic_slice_in_dim(amplitudes, far_start, col_count, 1)
    weights = (amp_rows.T[:, :, None] * correlation[:, None, :] * amp_cols[None, :, :]).astype(
        jnp.bfloat16
    )
    weights = weights.reshape(row_count, 3 * col_count)
    projected = jnp.dot(own_forces, weights, preferred_element_type=jnp.float32)
    projected = projected.reshape(own_forces.shape[0], 3, col_count)
    far_wide = far_forces.astype(jnp.float32)
    return jnp.sum(projected * far_wide[:, None, :], axis=(1, 2))


def any_groups(
    shapes, masses, spectral, frequencies, damping, recovery, connectivity, node_count, shared
):
    rim_width = shared.shape[1]
    block_width = shapes.shape[2]
    elem_count = connectivity.shape[0]
    slot_count = connectivity.shape[1]
    mode_index = lax.axis_index("mode")
    own_start = mode_index * block_width
    shape_wide = shapes.astype(jnp.float32)
    weighted = masses[None, :, None] * shape_wide
    lever_arm = jnp.sum(weighted, axis=1)
    general = jnp.sum(weighted * shape_wide, axis=(0, 1))
    lever_sum, general_sum = lax.psum((lever_arm, general), "dom")
    own_spectral = lax.dynamic_slice_in_dim(spectral, own_start, block_width, 1)
    local_amps = lever_sum / general_sum[None, :] * own_spectral
    amplitudes = lax.all_gather(local_amps, "mode", axis=1, tiled=True)
    outgoing = jnp.concatenate(
        [jnp.take(shapes, shared[0], axis=1), jnp.take(shapes, shared[1], axis=1)], axis=1
    )
    extended = extended_2(outgoing, (("dom", 1),), rim_width)
    node_table = jnp.concatenate(
        [shapes, extended[:, :rim_width], extended[:, 3 * rim_width :]], axis=1
    )
    gathered = jnp.take(node_table, connectivity.reshape(-1), axis=1).reshape(
        3, elem_count, slot_count, block_width
    )
    slot_live = (jnp.arange(slot_count)[None, :] < node_count[:, None]).astype(jnp.bfloat16)
    masked = recovery * slot_live[:, None, :, None]
    forces = jnp.einsum("ekna,aenm->ekm", masked, gathered, preferred_element_type=jnp.float32)
    forces = forces.astype(jnp.bfloat16).reshape(elem_count * recovery.shape[1], block_width)
    groups = lax.axis_size("mode")
    half_count = groups // 2
    partial_value = block_terms(
        forces, own_start, forces, own_start, amplitudes, frequencies, damping
    )

    def advance(turn_index, carried):
        incoming, summed = carried
        incoming = shifted(incoming, "mode", 1)
        source = (mode_index - turn_index) % groups * block_width
        factor = jnp.where(turn_index == half_count, jnp.float32(1.0), jnp.float32(2.0))
        summed = summed + factor * block_terms(
            forces, own_start, incoming, source, amplitudes, frequencies, damping
        )
        return (incoming, summed)

    carried = lax.fori_loop(1, half_count + 1, advance, (forces, partial_value))
    partial_value = carried[1]
    return lax.psum(partial_value, "mode")


def solution(mesh):
    in_specs = (
        P(None, "dom", "mode"),
        P("dom"),
        P(),
        P(),
        P(),
        P("dom", None, None, None),
        P("dom", None),
        P("dom"),
        P(None, "dom"),
    )
    out_specs = P("dom")
    step = four_groups if mesh.shape["mode"] == 4 else any_groups
    return jax.shard_map(
        step, mesh=mesh, in_specs=in_specs, out_specs=out_specs, check_vma=False
    )
```

```python
import functools
import jax
import jax.numpy as jnp
from jax import lax
from jax.experimental import pallas as pl
from jax.experimental.pallas import tpu as pltpu
from jax.sharding import PartitionSpec as P

F32 = jnp.float32
BF16 = jnp.bfloat16
VMEM = pl.BlockSpec(memory_space=pltpu.VMEM)
HBM = pl.BlockSpec(memory_space=pltpu.HBM)
ANY = pl.BlockSpec(memory_space=pl.ANY)
SMEM = pl.BlockSpec(memory_space=pltpu.SMEM)


def call(kernel, out_shape, args, flops, nbytes, smem=(), hbm=(), scratch=(), vmem=24 << 20, after=()):
    count = len(args)
    specs = [SMEM if i in smem else HBM if i in hbm else VMEM for i in range(count)]
    specs += [ANY] * len(after)
    many = isinstance(out_shape, (tuple, list))

    def body(*refs):
        kernel(*refs[:count], *refs[count + len(after) :])

    return pl.pallas_call(
        body,
        out_shape=out_shape,
        in_specs=specs,
        out_specs=[VMEM] * len(out_shape) if many else VMEM,
        scratch_shapes=list(scratch),
        cost_estimate=pl.CostEstimate(flops=flops, bytes_accessed=nbytes, transcendentals=0),
        compiler_params=pltpu.CompilerParams(vmem_limit_bytes=vmem),
        name=getattr(kernel, "func", kernel).__name__,
    )(*args, *after)


def add_kernel(left_ref, right_ref, out_ref):
    out_ref[...] = left_ref[...] + right_ref[...]


def gather_kernel(at, shared_ref, shapes_ref, up_ref, down_ref, buf, sem):
    dims, nodes, chunk = buf.shape
    width = shared_ref.shape[1]
    load = pltpu.make_async_copy(shapes_ref.at[:, :, at : at + chunk], buf, sem)
    load.start()
    node = lax.broadcasted_iota(jnp.int32, (nodes, 2 * width), 0)
    wanted = jnp.concatenate([shared_ref[1:2, :], shared_ref[0:1, :]], axis=1)
    pick = jnp.where(node == wanted, 1.0, 0.0).astype(F32).T.astype(BF16)
    load.wait()
    for d in range(dims):
        got = jnp.dot(pick, buf[d], preferred_element_type=F32).astype(BF16)
        up_ref[d * width : (d + 1) * width, :] = got[:width]
        down_ref[d * width : (d + 1) * width, :] = got[width:]


def stats_kernel(chunks, mass_ref, *refs):
    shapes_refs, (out_ref, mass_scr) = refs[:chunks], refs[chunks:]
    dims, nodes, chunk = shapes_refs[0].shape
    column = jnp.broadcast_to(mass_ref[...], (8, nodes)).T
    mass_scr[...] = jnp.broadcast_to(column[:, 0:1], (nodes, 128))
    for c, shapes_ref in enumerate(shapes_refs):
        for at in range(0, chunk, 128):
            lanes = slice(c * chunk + at, c * chunk + at + 128)
            general = jnp.zeros((8, 128), F32)
            for d in range(dims):
                lever = jnp.zeros((8, 128), F32)
                for r in range(0, nodes, 16):
                    wide = shapes_ref[d, r : r + 16, at : at + 128].astype(F32)
                    weighted = wide * mass_scr[r : r + 16, :]
                    square = weighted * wide
                    lever += weighted[:8] + weighted[8:]
                    general += square[:8] + square[8:]
                out_ref[d : d + 1, lanes] = jnp.sum(lever, axis=0, keepdims=True)
            out_ref[dims : dims + 1, lanes] = jnp.sum(general, axis=0, keepdims=True)


def table_kernel(codes_ref, count_ref, recovery_ref, pick_ref, force_ref):
    slots, elems = codes_ref.shape
    per_elem, dims = recovery_ref.shape[0], recovery_ref.shape[1]
    span = pick_ref.shape[1]
    node = lax.broadcasted_iota(jnp.int32, (span, elems), 0)
    for s in range(0, slots, 2):
        picks = []
        for q in range(s, min(s + 2, slots)):
            code = jnp.where(q < count_ref[...], codes_ref[q : q + 1, :], -1)
            picks.append(jnp.where(node == code, 1.0, 0.0).astype(F32))
        pick_ref[s * elems : s * elems + len(picks) * elems, :] = (
            jnp.concatenate(picks, axis=1).T.astype(BF16)
        )
    row = lax.broadcasted_iota(jnp.int32, (elems, 2 * elems), 0)
    column = lax.broadcasted_iota(jnp.int32, (elems, 2 * elems), 1)
    same = (column == row) | (column == row + elems)
    for k in range(per_elem):
        for d in range(dims):
            value = recovery_ref[k, d].astype(F32)
            for s in range(0, slots, 2):
                pair = jnp.concatenate([value[s : s + 1], value[s + 1 : s + 2]], axis=1)
                at = (d * slots + s) * elems
                force_ref[k * elems : (k + 1) * elems, at : at + 2 * elems] = jnp.where(
                    same, pair, 0.0
                ).astype(BF16)


def mode_rows(freq, rate):
    alpha = rate * freq
    inverse = 1.0 / jnp.sqrt(alpha)
    return (freq * freq * inverse, inverse, 2.0 * alpha, 2.0 * (freq / rate))


def place_modes(freq_ref, rate_ref, row_scr, col_scr, groups, sides, block):
    for which, group in enumerate(groups):
        lanes = pl.ds(pl.multiple_of(group * block, block), block)
        rows = jnp.concatenate(list(mode_rows(freq_ref[:, lanes], rate_ref[:, lanes])) * 2, axis=0)
        row_scr[which * 8 : which * 8 + 8, :] = rows
        if which < sides:
            turned = rows.T
            for q in range(4):
                col_scr[q, which * block : (which + 1) * block, :] = jnp.broadcast_to(
                    turned[:, q : q + 1], (block, 128)
                )


def fill_rho(row_scr, col_scr, out_ref, out_col, side_row, count, cols_at, col_off, tile):
    step = min(count, 256)
    cols = [
        jnp.broadcast_to(row_scr[cols_at + q : cols_at + q + 1, pl.ds(col_off, tile)], (8, tile))
        for q in range(4)
    ]

    @pl.loop(0, count // step)
    def _(t):
        for k in range(0, step, 8):
            at = pl.multiple_of(t * step, step) + k
            high, low, alpha, zeta = (col_scr[q, pl.ds(side_row + at, 8), :] for q in range(4))
            for c in range(0, tile, 128):
                col = [value[:, c : c + 128] for value in cols]
                spread = high * col[1] - low * col[0]
                pair = alpha + col[2]
                bottom = spread * spread + pair * (zeta + col[3])
                out_ref[pl.ds(at, 8), out_col + c : out_col + c + 128] = pair / bottom


def rho_near_kernel(place_ref, freq_ref, rate_ref, diag_ref, mate_ref, col_scr, row_scr):
    block = diag_ref.shape[0]
    half = block // 2
    tile = block // 4
    own, mate, parity = place_ref[0], place_ref[1], place_ref[3]
    place_modes(freq_ref, rate_ref, row_scr, col_scr, (own, mate), 1, block)
    for j in range(4):
        fill_rho(row_scr, col_scr, diag_ref, j * tile, 0, (j + 1) * tile, 0, j * tile, tile)
    for i in range(2):
        for j in range(2):
            off = pl.multiple_of((i ^ parity) * half + j * tile, tile)
            fill_rho(row_scr, col_scr, mate_ref.at[i], j * tile, i * half, half, 8, off, tile)


def rho_far_kernel(place_ref, freq_ref, rate_ref, far_ref, col_scr, row_scr):
    block = far_ref.shape[1]
    tile = block // 4
    own, mate, far = place_ref[0], place_ref[1], place_ref[2]
    place_modes(freq_ref, rate_ref, row_scr, col_scr, (own, mate, far), 2, block)
    for j in range(4):
        fill_rho(row_scr, col_scr, far_ref, j * tile, 0, 2 * block, 16, j * tile, tile)


def forces_kernel(
    place_ref, pick_ref, force_ref, shapes_ref, low_ref, high_ref, all_ref, part_ref, rim_scr, got_scr
):
    dims, nodes, _ = shapes_ref.shape
    comps, chunk = all_ref.shape
    width = low_ref.shape[0] // dims
    taken = pick_ref.shape[0]
    part = comps // 2
    other = place_ref[5]
    for d in range(dims):
        rim_scr[d, :width, :] = low_ref[d * width : (d + 1) * width, :]
        rim_scr[d, width:, :] = high_ref[d * width : (d + 1) * width, :]
    wide = 256
    for c in range(0, chunk, wide):
        for d in range(dims):
            got = jnp.dot(
                pick_ref[:, :nodes], shapes_ref[d, :, c : c + wide], preferred_element_type=F32
            )
            got = got + jnp.dot(
                pick_ref[:, nodes:], rim_scr[d, :, c : c + wide], preferred_element_type=F32
            )
            got_scr[d * taken : (d + 1) * taken, c : c + wide] = got.astype(BF16)
        total = jnp.dot(force_ref[...], got_scr[:, c : c + wide], preferred_element_type=F32)
        all_ref[:, c : c + wide] = total.astype(BF16)
    part_ref[...] = all_ref[pl.ds(pl.multiple_of(other * part, part), part), :]


def amps_kernel(place_ref, stats_ref, extra_ref, spectral_ref, freq_ref, rate_ref, out_ref):
    dims, block = spectral_ref.shape[0], stats_ref.shape[1]
    lanes = pl.ds(pl.multiple_of(place_ref[0] * block, block), block)
    total = stats_ref[...] + extra_ref[...]
    scale = 2.0 * jnp.sqrt(freq_ref[:, lanes] / rate_ref[:, lanes])
    amps = total[:dims] / total[dims : dims + 1] * spectral_ref[:, lanes] * scale
    out_ref[...] = jnp.concatenate([amps, jnp.zeros((8 - dims, block), F32)], axis=0)


def fold(value):
    total = value[:, :128]
    for c in range(128, value.shape[1], 128):
        total = total + value[:, c : c + 128]
    return total


def to_row(acc, turned, per_elem):
    elems = acc.shape[0] // per_elem
    for k in range(per_elem):
        turned[pl.ds(k, elems, stride=per_elem), :] = acc[k * elems : (k + 1) * elems, :]
    ones = jnp.ones((8, acc.shape[1]), F32)
    return lax.dot_general(
        ones, turned[...], (((1,), (1,)), ((), ())),
        precision=lax.Precision.HIGHEST, preferred_element_type=F32,
    )[0:1]


def spread_sides(side_scr, at, amps, dims):
    sides = amps.T
    for d in range(dims):
        side_scr[d, at : at + amps.shape[1], :] = jnp.broadcast_to(sides[:, d : d + 1], (amps.shape[1], 128))


def weigh(out, rho, side_scr, side_at, cols, dims, factor):
    for c in range(0, rho.shape[1], 128):
        col = [jnp.broadcast_to(cols[d : d + 1, c : c + 128] * factor, (16, 128)) for d in range(dims)]
        for r in range(0, rho.shape[0], 16):
            pair = side_scr[0, side_at + r : side_at + r + 16, :] * col[0]
            for d in range(1, dims):
                pair = pair + side_scr[d, side_at + r : side_at + r + 16, :] * col[d]
            out[r : r + 16, c : c + 128] = (rho[r : r + 16, c : c + 128] * pair).astype(BF16)


def near_kernel(dims, chunks, *refs):
    place_ref, own_amps_ref, mate_amps_ref, diag_ref, cross_ref = refs[:5]
    own_refs, mate_refs = refs[5 : 5 + chunks], refs[5 + chunks : 5 + 2 * chunks]
    acc, side_scr, w_scr = refs[5 + 2 * chunks :]
    comps, chunk = own_refs[0].shape
    block = diag_ref.shape[0]
    tile = block // 4
    half = block // 2
    parity = place_ref[3]

    def part(parts, at, size):
        return parts[at // chunk][:, at % chunk : at % chunk + size]

    def product(w, at, depth):
        total = None
        for c in range(at, at + depth, min(chunk, depth)):
            size = min(chunk, at + depth - c)
            got = jnp.dot(part(own_refs, c, size), w[c - at : c - at + size, :], preferred_element_type=F32)
            total = got if total is None else total + got
        return total

    spread_sides(side_scr, 0, own_amps_ref[...], dims)
    turn = 0
    for j in range(4):
        cols = own_amps_ref[:, j * tile : (j + 1) * tile]
        for i in range(j + 1):
            rho = diag_ref.at[i * tile : (i + 1) * tile, j * tile : (j + 1) * tile]
            out = w_scr.at[turn, i * tile : (i + 1) * tile, :]
            weigh(out, rho, side_scr, i * tile, cols, dims, 2.0 if i < j else 1.0)
        got = product(w_scr.at[turn], 0, (j + 1) * tile)
        got = fold(got * part(own_refs, j * tile, tile).astype(F32))
        acc[...] = got if j == 0 else acc[...] + got
        turn = 1 - turn
    for i in range(2):
        for j in range(half // tile):
            here, there = i * half + j * tile, (1 - i) * half + j * tile
            straight = parity == 0
            cols = jnp.where(
                straight, mate_amps_ref[:, here : here + tile], mate_amps_ref[:, there : there + tile]
            )
            rho = cross_ref.at[i, :, j * tile : (j + 1) * tile]
            weigh(w_scr.at[turn, :half, :], rho, side_scr, i * half, cols, dims, 2.0)
            got = product(w_scr.at[turn], i * half, half)
            other = jnp.where(
                straight, part(mate_refs, here, tile).astype(F32), part(mate_refs, there, tile).astype(F32)
            )
            acc[...] += fold(got * other)
            turn = 1 - turn


def weights_kernel(dims, own_amps_ref, mate_amps_ref, far_amps_ref, rho_ref, out_ref, side_scr):
    block = rho_ref.shape[1]
    tile = block // 4
    spread_sides(side_scr, 0, own_amps_ref[...], dims)
    spread_sides(side_scr, block, mate_amps_ref[...], dims)

    @pl.loop(0, 2 * block // tile)
    def _(t):
        rows = pl.ds(pl.multiple_of(t * tile, tile), tile)
        sides = side_scr.at[:, rows, :]
        weigh(out_ref.at[rows, :], rho_ref.at[rows, :], sides, 0, far_amps_ref[...], dims, 2.0)


def far_kernel(at, chunks, per_elem, place_ref, near_ref, w_ref, far_ref, *refs):
    own_refs, mate_refs = refs[:chunks], refs[chunks : 2 * chunks]
    if len(refs) == 2 * chunks + 1:
        acc, last = refs[-1], False
    else:
        (out_ref, acc, turned), last = refs[2 * chunks :], True
    comps, chunk = own_refs[0].shape
    block = w_ref.shape[1]
    part = comps // 2
    tile = min(256, chunk)
    here = pl.multiple_of(place_ref[4] * part, part)
    rows = pl.ds(here, part)
    total = near_ref[rows, :]
    for c in range(0, chunk, tile):
        spot = slice(at + c, at + c + tile)
        got = None
        for which, parts in enumerate((own_refs, mate_refs)):
            for q in range(chunks):
                base = which * block + q * chunk
                piece = jnp.dot(
                    parts[q][rows, :], w_ref[base : base + chunk, spot], preferred_element_type=F32
                )
                got = piece if got is None else got + piece
        total = total + fold(got * far_ref[:, c : c + tile].astype(F32))
    acc[...] = near_ref[...]
    acc[rows, :] = total
    if last:
        out_ref[...] = to_row(acc, turned, per_elem)


CHUNKS = 1


def four_groups(
    shapes, masses, spectral, frequencies, damping, recovery, connectivity, node_count, shared
):
    dims, nodes, block = shapes.shape
    elems, slots = connectivity.shape
    per_elem = recovery.shape[1]
    comps = elems * per_elem
    part = comps // 2
    width = shared.shape[1]
    parts = lax.axis_size("dom")
    group = lax.axis_index("mode").astype(jnp.int32)
    place = jnp.stack(
        [group, group ^ 1, group ^ 2, group & 1, group >> 1, 1 - (group >> 1)]
    ).astype(jnp.int32)
    sds = jax.ShapeDtypeStruct
    chunk = block // CHUNKS
    ahead = [(i, i + 1) for i in range(parts - 1)]
    back = [(i + 1, i) for i in range(parts - 1)]
    freq = frequencies.reshape(1, -1)
    rate = damping.reshape(1, -1)

    def moved(name, value, axis, pairs):
        with jax.named_scope(name):
            return lax.ppermute(value, axis, pairs)

    def gathered(c, after):
        return call(
            functools.partial(gather_kernel, c * chunk),
            (sds((dims * width, chunk), BF16), sds((dims * width, chunk), BF16), sds((dims, nodes, chunk), BF16)),
            (shared, shapes), 4 * width * nodes * dims * chunk, 2 * dims * nodes * chunk, hbm=(1,),
            scratch=[pltpu.SemaphoreType.DMA], after=after,
        )

    halos, held = [], []
    after = ()
    for c in range(CHUNKS):
        up, down, kept = gathered(c, after)
        held.append(kept)
        after = (up,)
        halos.append((moved("up%d" % c, up, "dom", ahead), moved("down%d" % c, down, "dom", back)))

    stats = call(
        functools.partial(stats_kernel, CHUNKS), sds((dims + 1, block), F32), (masses.reshape(1, nodes), *held),
        5 * dims * nodes * block, 2 * dims * nodes * block,
        scratch=[pltpu.VMEM((nodes, 128), F32)], after=after,
    )
    pick, force = call(
        table_kernel, (sds((slots * elems, nodes + 2 * width), BF16), sds((comps, dims * slots * elems), BF16)),
        (connectivity.T, node_count.reshape(1, elems), recovery.transpose(1, 3, 2, 0)),
        4 * comps * slots * elems, 4 * comps * slots * elems, after=(stats,),
    )
    rho_diag, rho_mate = call(
        rho_near_kernel,
        (sds((block, block), F32), sds((2, block // 2, block // 2), F32)),
        (place, freq, rate), 20 * block * block, 5 * block * block, smem=(0,),
        scratch=[pltpu.VMEM((4, block, 128), F32), pltpu.VMEM((16, block), F32)], after=(pick,),
    )
    rho_far = call(
        rho_far_kernel, sds((2 * block, block), F32), (place, freq, rate),
        40 * block * block, 8 * block * block, smem=(0,),
        scratch=[pltpu.VMEM((4, 2 * block, 128), F32), pltpu.VMEM((24, block), F32)],
        after=(rho_diag,),
    )
    first = ()
    if parts & (parts - 1) or parts == 1:
        stats = lax.psum(stats, "dom")
        extra = jnp.zeros_like(stats)
    else:
        reach = 1
        waits = (rho_far,)
        while True:
            extra = moved("stage%d" % reach, stats, "dom", [(i, i ^ reach) for i in range(parts)])
            reach *= 2
            if reach == parts:
                break
            stats = call(
                add_kernel, sds(stats.shape, F32), (stats, extra), stats.size, 12 * stats.size, after=waits
            )
            waits = ()
            first = first or (stats,)
    amps = call(
        amps_kernel, sds((8, block), F32), (place, stats, extra, spectral, freq, rate),
        20 * block, 60 * block, smem=(0,),
    )
    mate_amps = moved("amps_mate", amps, "mode", [(i, i ^ 1) for i in range(4)])
    far_amps = moved("amps_far", amps, "mode", [(i, i ^ 2) for i in range(4)])

    own, mate, far = [], [], []
    for c in range(CHUNKS):
        forces, sent = call(
            forces_kernel,
            (sds((comps, chunk), BF16), sds((part, chunk), BF16)),
            (place, pick, force, held[c]) + halos[c],
            4 * comps * dims * nodes * chunk, 8 * comps * chunk, smem=(0,),
            scratch=[
                pltpu.VMEM((dims, 2 * width, chunk), BF16), pltpu.VMEM((dims * slots * elems, chunk), BF16)
            ],
            after=first,
        )
        own.append(forces)
        far.append(moved("far%d" % c, sent, "mode", [(i, i ^ 2) for i in range(4)]))
        mate.append(moved("mate%d" % c, forces, "mode", [(i, i ^ 1) for i in range(4)]))
    near = call(
        functools.partial(near_kernel, dims, CHUNKS), sds((comps, 128), F32),
        (place, amps, mate_amps, rho_diag, rho_mate, *own, *mate),
        2 * comps * block * block, 6 * block * block, smem=(0,),
        scratch=[pltpu.VMEM((dims, block, 128), F32), pltpu.VMEM((2, block, block // 4), BF16)],
    )
    weights = call(
        functools.partial(weights_kernel, dims), sds((2 * block, block), BF16),
        (amps, mate_amps, far_amps, rho_far), 14 * block * block, 12 * block * block,
        scratch=[pltpu.VMEM((dims, 2 * block, 128), F32)],
    )
    value = near
    for c in range(CHUNKS):
        last = c == CHUNKS - 1
        value = call(
            functools.partial(far_kernel, c * chunk, CHUNKS, per_elem),
            sds((1, comps) if last else (comps, 128), F32),
            (place, value, weights, far[c], *own, *mate), 2 * comps * block * chunk, 8 * block * chunk,
            smem=(0,), scratch=[pltpu.VMEM((comps, 128), F32)] * 2 if last else (),
        )
    value = value.reshape(comps)
    for reach in (1, 2):
        value = value + moved("sum%d" % reach, value, "mode", [(i, i ^ reach) for i in range(4)])
    return value


def extended_2(block, sides, width):
    for axis, dim in sides:
        count = lax.axis_size(axis)
        forward = [(i, i + 1) for i in range(count - 1)]
        backward = [(target, source) for source, target in forward]
        low = lax.ppermute(
            lax.slice_in_dim(block, block.shape[dim] - width, None, axis=dim), axis, forward
        )
        high = lax.ppermute(lax.slice_in_dim(block, 0, width, axis=dim), axis, backward)
        block = jnp.concatenate([low, block, high], axis=dim)
    return block


def shifted(value, axis, steps):
    count = lax.axis_size(axis)
    pairs = [(source, (source + steps) % count) for source in range(count)]
    return lax.ppermute(value, axis, pairs)


def correlation_block(freq_rows, freq_cols, rate_rows, rate_cols):
    ratio = freq_cols[None, :] / freq_rows[:, None]
    ratio_sq = ratio * ratio
    rate_row = rate_rows[:, None]
    rate_col = rate_cols[None, :]
    top_part = (
        8.0
        * jnp.sqrt(rate_row * rate_col)
        * (rate_row + ratio * rate_col)
        * ratio
        * jnp.sqrt(ratio)
    )
    spread = 1.0 - ratio_sq
    bottom_part = (
        spread * spread
        + 4.0 * rate_row * rate_col * ratio * (1.0 + ratio_sq)
        + 4.0 * (rate_row * rate_row + rate_col * rate_col) * ratio_sq
    )
    return top_part / bottom_part


def block_terms(own_forces, own_start, far_forces, far_start, amplitudes, frequencies, damping):
    row_count = own_forces.shape[1]
    col_count = far_forces.shape[1]
    freq_rows = lax.dynamic_slice_in_dim(frequencies, own_start, row_count)
    freq_cols = lax.dynamic_slice_in_dim(frequencies, far_start, col_count)
    rate_rows = lax.dynamic_slice_in_dim(damping, own_start, row_count)
    rate_cols = lax.dynamic_slice_in_dim(damping, far_start, col_count)
    correlation = correlation_block(freq_rows, freq_cols, rate_rows, rate_cols)
    amp_rows = lax.dynamic_slice_in_dim(amplitudes, own_start, row_count, 1)
    amp_cols = lax.dynamic_slice_in_dim(amplitudes, far_start, col_count, 1)
    weights = (amp_rows.T[:, :, None] * correlation[:, None, :] * amp_cols[None, :, :]).astype(
        jnp.bfloat16
    )
    weights = weights.reshape(row_count, 3 * col_count)
    projected = jnp.dot(own_forces, weights, preferred_element_type=jnp.float32)
    projected = projected.reshape(own_forces.shape[0], 3, col_count)
    far_wide = far_forces.astype(jnp.float32)
    return jnp.sum(projected * far_wide[:, None, :], axis=(1, 2))


def any_groups(
    shapes, masses, spectral, frequencies, damping, recovery, connectivity, node_count, shared
):
    rim_width = shared.shape[1]
    block_width = shapes.shape[2]
    elem_count = connectivity.shape[0]
    slot_count = connectivity.shape[1]
    mode_index = lax.axis_index("mode")
    own_start = mode_index * block_width
    shape_wide = shapes.astype(jnp.float32)
    weighted = masses[None, :, None] * shape_wide
    lever_arm = jnp.sum(weighted, axis=1)
    general = jnp.sum(weighted * shape_wide, axis=(0, 1))
    lever_sum, general_sum = lax.psum((lever_arm, general), "dom")
    own_spectral = lax.dynamic_slice_in_dim(spectral, own_start, block_width, 1)
    local_amps = lever_sum / general_sum[None, :] * own_spectral
    amplitudes = lax.all_gather(local_amps, "mode", axis=1, tiled=True)
    outgoing = jnp.concatenate(
        [jnp.take(shapes, shared[0], axis=1), jnp.take(shapes, shared[1], axis=1)], axis=1
    )
    extended = extended_2(outgoing, (("dom", 1),), rim_width)
    node_table = jnp.concatenate(
        [shapes, extended[:, :rim_width], extended[:, 3 * rim_width :]], axis=1
    )
    gathered = jnp.take(node_table, connectivity.reshape(-1), axis=1).reshape(
        3, elem_count, slot_count, block_width
    )
    slot_live = (jnp.arange(slot_count)[None, :] < node_count[:, None]).astype(jnp.bfloat16)
    masked = recovery * slot_live[:, None, :, None]
    forces = jnp.einsum("ekna,aenm->ekm", masked, gathered, preferred_element_type=jnp.float32)
    forces = forces.astype(jnp.bfloat16).reshape(elem_count * recovery.shape[1], block_width)
    groups = lax.axis_size("mode")
    half_count = groups // 2
    partial_value = block_terms(
        forces, own_start, forces, own_start, amplitudes, frequencies, damping
    )

    def advance(turn_index, carried):
        incoming, summed = carried
        incoming = shifted(incoming, "mode", 1)
        source = (mode_index - turn_index) % groups * block_width
        factor = jnp.where(turn_index == half_count, jnp.float32(1.0), jnp.float32(2.0))
        summed = summed + factor * block_terms(
            forces, own_start, incoming, source, amplitudes, frequencies, damping
        )
        return (incoming, summed)

    carried = lax.fori_loop(1, half_count + 1, advance, (forces, partial_value))
    partial_value = carried[1]
    return lax.psum(partial_value, "mode")


def solution(mesh):
    in_specs = (
        P(None, "dom", "mode"),
        P("dom"),
        P(),
        P(),
        P(),
        P("dom", None, None, None),
        P("dom", None),
        P("dom"),
        P(None, "dom"),
    )
    out_specs = P("dom")
    step = four_groups if mesh.shape["mode"] == 4 else any_groups
    return jax.shard_map(
        step, mesh=mesh, in_specs=in_specs, out_specs=out_specs, check_vma=False
    )
```

```python
import functools
import jax
import jax.numpy as jnp
from jax import lax
from jax.experimental import pallas as pl
from jax.experimental.pallas import tpu as pltpu
from jax.sharding import PartitionSpec as P


F32 = jnp.float32
BF16 = jnp.bfloat16
VMEM = pl.BlockSpec(memory_space=pltpu.VMEM)
HBM = pl.BlockSpec(memory_space=pltpu.HBM)
ANY = pl.BlockSpec(memory_space=pl.ANY)
SMEM = pl.BlockSpec(memory_space=pltpu.SMEM)


def call(kernel, out_shape, args, cost, smem=(), hbm=(), scratch=(), vmem=14 << 20, after=()):
    count = len(args)
    specs = [SMEM if i in smem else HBM if i in hbm else VMEM for i in range(count)]
    specs += [ANY] * len(after)
    many = isinstance(out_shape, (tuple, list))

    def body(*refs):
        kernel(*refs[:count], *refs[count + len(after) :])

    return pl.pallas_call(
        body,
        out_shape=out_shape,
        in_specs=specs,
        out_specs=[VMEM] * len(out_shape) if many else VMEM,
        scratch_shapes=list(scratch),
        cost_estimate=pl.CostEstimate(flops=int(1.1e9 * cost), bytes_accessed=0, transcendentals=0),
        compiler_params=pltpu.CompilerParams(vmem_limit_bytes=vmem),
    )(*args, *after)


def add_kernel(left_ref, right_ref, out_ref):
    out_ref[...] = left_ref[...] + right_ref[...]


def gather_kernel(at, shared_ref, shapes_ref, up_ref, down_ref, buf, sem):
    dims, nodes, chunk = buf.shape
    width = shared_ref.shape[1]
    load = pltpu.make_async_copy(shapes_ref.at[:, :, at : at + chunk], buf, sem)
    load.start()
    node = lax.broadcasted_iota(jnp.int32, (nodes, 2 * width), 0)
    wanted = jnp.concatenate([shared_ref[1:2, :], shared_ref[0:1, :]], axis=1)
    pick = jnp.where(node == wanted, 1.0, 0.0).astype(F32).T.astype(BF16)
    load.wait()
    for d in range(dims):
        got = jnp.dot(pick, buf[d], preferred_element_type=F32).astype(BF16)
        up_ref[d * width : (d + 1) * width, :] = got[:width]
        down_ref[d * width : (d + 1) * width, :] = got[width:]


def stats_kernel(chunks, mass_ref, *refs):
    shapes_refs, (out_ref, mass_scr) = refs[:chunks], refs[chunks:]
    dims, nodes, chunk = shapes_refs[0].shape
    column = jnp.broadcast_to(mass_ref[...], (8, nodes)).T
    mass_scr[...] = jnp.broadcast_to(column[:, 0:1], (nodes, 128))
    for c, shapes_ref in enumerate(shapes_refs):
        for at in range(0, chunk, 128):
            lanes = slice(c * chunk + at, c * chunk + at + 128)
            general = jnp.zeros((8, 128), F32)
            for d in range(dims):
                lever = jnp.zeros((8, 128), F32)
                for r in range(0, nodes, 16):
                    wide = shapes_ref[d, r : r + 16, at : at + 128].astype(F32)
                    weighted = wide * mass_scr[r : r + 16, :]
                    square = weighted * wide
                    lever += weighted[:8] + weighted[8:]
                    general += square[:8] + square[8:]
                out_ref[d : d + 1, lanes] = jnp.sum(lever, axis=0, keepdims=True)
            out_ref[dims : dims + 1, lanes] = jnp.sum(general, axis=0, keepdims=True)


def table_kernel(codes_ref, count_ref, recovery_ref, pick_ref, force_ref):
    slots, elems = codes_ref.shape
    per_elem, dims = recovery_ref.shape[0], recovery_ref.shape[1]
    span = pick_ref.shape[1]
    node = lax.broadcasted_iota(jnp.int32, (span, elems), 0)
    for s in range(0, slots, 2):
        picks = []
        for q in range(s, min(s + 2, slots)):
            code = jnp.where(q < count_ref[...], codes_ref[q : q + 1, :], -1)
            picks.append(jnp.where(node == code, 1.0, 0.0).astype(F32))
        pick_ref[s * elems : s * elems + len(picks) * elems, :] = (
            jnp.concatenate(picks, axis=1).T.astype(BF16)
        )
    row = lax.broadcasted_iota(jnp.int32, (elems, 2 * elems), 0)
    column = lax.broadcasted_iota(jnp.int32, (elems, 2 * elems), 1)
    same = (column == row) | (column == row + elems)
    for k in range(per_elem):
        for d in range(dims):
            value = recovery_ref[k, d].astype(F32)
            for s in range(0, slots, 2):
                pair = jnp.concatenate([value[s : s + 1], value[s + 1 : s + 2]], axis=1)
                at = (d * slots + s) * elems
                force_ref[k * elems : (k + 1) * elems, at : at + 2 * elems] = jnp.where(
                    same, pair, 0.0
                ).astype(BF16)


def mode_rows(freq, rate):
    alpha = rate * freq
    inverse = 1.0 / jnp.sqrt(alpha)
    return (freq * freq * inverse, inverse, 2.0 * alpha, 2.0 * (freq / rate))


def place_modes(freq_ref, rate_ref, row_scr, col_scr, groups, sides, block):
    for which, group in enumerate(groups):
        lanes = pl.ds(pl.multiple_of(group * block, block), block)
        rows = jnp.concatenate(list(mode_rows(freq_ref[:, lanes], rate_ref[:, lanes])) * 2, axis=0)
        row_scr[which * 8 : which * 8 + 8, :] = rows
        if which < sides:
            turned = rows.T
            for q in range(4):
                col_scr[q, which * block : (which + 1) * block, :] = jnp.broadcast_to(
                    turned[:, q : q + 1], (block, 128)
                )


def fill_rho(row_scr, col_scr, out_ref, out_col, side_row, count, cols_at, col_off, tile):
    step = min(count, 256)
    cols = [
        jnp.broadcast_to(row_scr[cols_at + q : cols_at + q + 1, pl.ds(col_off, tile)], (8, tile))
        for q in range(4)
    ]

    @pl.loop(0, count // step)
    def _(t):
        for k in range(0, step, 8):
            at = pl.multiple_of(t * step, step) + k
            high, low, alpha, zeta = (col_scr[q, pl.ds(side_row + at, 8), :] for q in range(4))
            for c in range(0, tile, 128):
                col = [value[:, c : c + 128] for value in cols]
                spread = high * col[1] - low * col[0]
                pair = alpha + col[2]
                bottom = spread * spread + pair * (zeta + col[3])
                out_ref[pl.ds(at, 8), out_col + c : out_col + c + 128] = pair / bottom


def rho_near_kernel(place_ref, freq_ref, rate_ref, diag_ref, mate_ref, col_scr, row_scr):
    block = diag_ref.shape[0]
    half = block // 2
    tile = block // 4
    own, mate, parity = place_ref[0], place_ref[1], place_ref[3]
    place_modes(freq_ref, rate_ref, row_scr, col_scr, (own, mate), 1, block)
    for j in range(4):
        fill_rho(row_scr, col_scr, diag_ref, j * tile, 0, (j + 1) * tile, 0, j * tile, tile)
    for i in range(2):
        for j in range(2):
            off = pl.multiple_of((i ^ parity) * half + j * tile, tile)
            fill_rho(row_scr, col_scr, mate_ref.at[i], j * tile, i * half, half, 8, off, tile)


def rho_far_kernel(place_ref, freq_ref, rate_ref, far_ref, col_scr, row_scr):
    block = far_ref.shape[1]
    tile = block // 4
    own, mate, far = place_ref[0], place_ref[1], place_ref[2]
    place_modes(freq_ref, rate_ref, row_scr, col_scr, (own, mate, far), 2, block)
    for j in range(4):
        fill_rho(row_scr, col_scr, far_ref, j * tile, 0, 2 * block, 16, j * tile, tile)


def forces_kernel(
    place_ref, pick_ref, force_ref, shapes_ref, low_ref, high_ref, all_ref, part_ref, rim_scr, got_scr
):
    dims, nodes, _ = shapes_ref.shape
    comps, chunk = all_ref.shape
    width = low_ref.shape[0] // dims
    taken = pick_ref.shape[0]
    part = comps // 2
    other = place_ref[5]
    for d in range(dims):
        rim_scr[d, :width, :] = low_ref[d * width : (d + 1) * width, :]
        rim_scr[d, width:, :] = high_ref[d * width : (d + 1) * width, :]
    wide = 256
    for c in range(0, chunk, wide):
        for d in range(dims):
            got = jnp.dot(
                pick_ref[:, :nodes], shapes_ref[d, :, c : c + wide], preferred_element_type=F32
            )
            got = got + jnp.dot(
                pick_ref[:, nodes:], rim_scr[d, :, c : c + wide], preferred_element_type=F32
            )
            got_scr[d * taken : (d + 1) * taken, c : c + wide] = got.astype(BF16)
        total = jnp.dot(force_ref[...], got_scr[:, c : c + wide], preferred_element_type=F32)
        all_ref[:, c : c + wide] = total.astype(BF16)
    part_ref[...] = all_ref[pl.ds(pl.multiple_of(other * part, part), part), :]


def amps_kernel(place_ref, stats_ref, extra_ref, spectral_ref, freq_ref, rate_ref, out_ref):
    dims, block = spectral_ref.shape[0], stats_ref.shape[1]
    lanes = pl.ds(pl.multiple_of(place_ref[0] * block, block), block)
    total = stats_ref[...] + extra_ref[...]
    scale = 2.0 * jnp.sqrt(freq_ref[:, lanes] / rate_ref[:, lanes])
    amps = total[:dims] / total[dims : dims + 1] * spectral_ref[:, lanes] * scale
    out_ref[...] = jnp.concatenate([amps, jnp.zeros((8 - dims, block), F32)], axis=0)


def fold(value):
    total = value[:, :128]
    for c in range(128, value.shape[1], 128):
        total = total + value[:, c : c + 128]
    return total


def to_row(acc, turned, per_elem):
    elems = acc.shape[0] // per_elem
    for k in range(per_elem):
        turned[pl.ds(k, elems, stride=per_elem), :] = acc[k * elems : (k + 1) * elems, :]
    ones = jnp.ones((8, acc.shape[1]), F32)
    return lax.dot_general(
        ones, turned[...], (((1,), (1,)), ((), ())),
        precision=lax.Precision.HIGHEST, preferred_element_type=F32,
    )[0:1]


def spread_sides(side_scr, at, amps, dims):
    sides = amps.T
    for d in range(dims):
        side_scr[d, at : at + amps.shape[1], :] = jnp.broadcast_to(sides[:, d : d + 1], (amps.shape[1], 128))


def weigh(out, rho, side_scr, side_at, cols, dims, factor):
    for c in range(0, rho.shape[1], 128):
        col = [jnp.broadcast_to(cols[d : d + 1, c : c + 128] * factor, (16, 128)) for d in range(dims)]
        for r in range(0, rho.shape[0], 16):
            pair = side_scr[0, side_at + r : side_at + r + 16, :] * col[0]
            for d in range(1, dims):
                pair = pair + side_scr[d, side_at + r : side_at + r + 16, :] * col[d]
            out[r : r + 16, c : c + 128] = (rho[r : r + 16, c : c + 128] * pair).astype(BF16)


def near_kernel(dims, chunks, *refs):
    place_ref, own_amps_ref, mate_amps_ref, diag_ref, cross_ref = refs[:5]
    own_refs, mate_refs = refs[5 : 5 + chunks], refs[5 + chunks : 5 + 2 * chunks]
    acc, side_scr, w_scr = refs[5 + 2 * chunks :]
    _, chunk = own_refs[0].shape
    block = diag_ref.shape[0]
    tile = block // 4
    half = block // 2
    parity = place_ref[3]

    def part(parts, at, size):
        return parts[at // chunk][:, at % chunk : at % chunk + size]

    def product(w, at, depth):
        total = None
        for c in range(at, at + depth, min(chunk, depth)):
            size = min(chunk, at + depth - c)
            got = jnp.dot(part(own_refs, c, size), w[c - at : c - at + size, :], preferred_element_type=F32)
            total = got if total is None else total + got
        return total

    spread_sides(side_scr, 0, own_amps_ref[...], dims)
    turn = 0
    for j in range(4):
        cols = own_amps_ref[:, j * tile : (j + 1) * tile]
        for i in range(j + 1):
            rho = diag_ref.at[i * tile : (i + 1) * tile, j * tile : (j + 1) * tile]
            out = w_scr.at[turn, i * tile : (i + 1) * tile, :]
            weigh(out, rho, side_scr, i * tile, cols, dims, 2.0 if i < j else 1.0)
        got = product(w_scr.at[turn], 0, (j + 1) * tile)
        got = fold(got * part(own_refs, j * tile, tile).astype(F32))
        acc[...] = got if j == 0 else acc[...] + got
        turn = 1 - turn
    for i in range(2):
        for j in range(half // tile):
            here, there = i * half + j * tile, (1 - i) * half + j * tile
            straight = parity == 0
            cols = jnp.where(
                straight, mate_amps_ref[:, here : here + tile], mate_amps_ref[:, there : there + tile]
            )
            rho = cross_ref.at[i, :, j * tile : (j + 1) * tile]
            weigh(w_scr.at[turn, :half, :], rho, side_scr, i * half, cols, dims, 2.0)
            got = product(w_scr.at[turn], i * half, half)
            other = jnp.where(
                straight, part(mate_refs, here, tile).astype(F32), part(mate_refs, there, tile).astype(F32)
            )
            acc[...] += fold(got * other)
            turn = 1 - turn


def weights_kernel(dims, own_amps_ref, mate_amps_ref, far_amps_ref, rho_ref, out_ref, side_scr):
    block = rho_ref.shape[1]
    tile = block // 4
    spread_sides(side_scr, 0, own_amps_ref[...], dims)
    spread_sides(side_scr, block, mate_amps_ref[...], dims)

    @pl.loop(0, 2 * block // tile)
    def _(t):
        rows = pl.ds(pl.multiple_of(t * tile, tile), tile)
        sides = side_scr.at[:, rows, :]
        weigh(out_ref.at[rows, :], rho_ref.at[rows, :], sides, 0, far_amps_ref[...], dims, 2.0)


def far_kernel(at, chunks, per_elem, place_ref, near_ref, w_ref, far_ref, *refs):
    own_refs, mate_refs = refs[:chunks], refs[chunks : 2 * chunks]
    if len(refs) == 2 * chunks + 1:
        acc, last = refs[-1], False
    else:
        (out_ref, acc, turned), last = refs[2 * chunks :], True
    comps, chunk = own_refs[0].shape
    block = w_ref.shape[1]
    part = comps // 2
    tile = min(256, chunk)
    here = pl.multiple_of(place_ref[4] * part, part)
    rows = pl.ds(here, part)
    total = near_ref[rows, :]
    for c in range(0, chunk, tile):
        spot = slice(at + c, at + c + tile)
        got = None
        for which, parts in enumerate((own_refs, mate_refs)):
            for q in range(chunks):
                base = which * block + q * chunk
                piece = jnp.dot(
                    parts[q][rows, :], w_ref[base : base + chunk, spot], preferred_element_type=F32
                )
                got = piece if got is None else got + piece
        total = total + fold(got * far_ref[:, c : c + tile].astype(F32))
    acc[...] = near_ref[...]
    acc[rows, :] = total
    if last:
        out_ref[...] = to_row(acc, turned, per_elem)


CHUNKS = 1


def four_groups(*args):
    return combined(*args)


def combined(
    shapes, masses, spectral, frequencies, damping, recovery, connectivity, node_count, shared
):
    dims, nodes, block = shapes.shape
    elems, slots = connectivity.shape
    per_elem = recovery.shape[1]
    comps = elems * per_elem
    part = comps // 2
    width = shared.shape[1]
    parts = lax.axis_size("dom")
    group = lax.axis_index("mode").astype(jnp.int32)
    place = jnp.stack(
        [group, group ^ 1, group ^ 2, group & 1, group >> 1, 1 - (group >> 1)]
    ).astype(jnp.int32)
    sds = jax.ShapeDtypeStruct
    chunk = block // CHUNKS
    ahead = [(i, i + 1) for i in range(parts - 1)]
    back = [(i + 1, i) for i in range(parts - 1)]
    freq = frequencies.reshape(1, -1)
    rate = damping.reshape(1, -1)

    def gathered(c, after):
        return call(
            functools.partial(gather_kernel, c * chunk),
            (sds((dims * width, chunk), BF16), sds((dims * width, chunk), BF16), sds((dims, nodes, chunk), BF16)),
            (shared, shapes), 2.0 / CHUNKS, hbm=(1,),
            scratch=[pltpu.SemaphoreType.DMA], after=after,
        )

    halos, held = [], []
    after = ()
    for c in range(CHUNKS):
        up, down, kept = gathered(c, after)
        held.append(kept)
        after = (up,)
        halos.append((lax.ppermute(up, "dom", ahead), lax.ppermute(down, "dom", back)))

    stats = call(
        functools.partial(stats_kernel, CHUNKS), sds((dims + 1, block), F32), (masses.reshape(1, nodes), *held), 0.8,
        scratch=[pltpu.VMEM((nodes, 128), F32)], after=after,
    )
    pick, force = call(
        table_kernel, (sds((slots * elems, nodes + 2 * width), BF16), sds((comps, dims * slots * elems), BF16)),
        (connectivity.T, node_count.reshape(1, elems), recovery.transpose(1, 3, 2, 0)),
        0.5, after=(stats,),
    )
    order = [1 << q for q in range(1, parts.bit_length() - 1)] + [1]
    if parts & (parts - 1) or parts == 1:
        stats = lax.psum(stats, "dom")
        order = []
    extra = jnp.zeros_like(stats)
    for q, reach in enumerate(order):
        if q:
            stats = call(add_kernel, sds(stats.shape, F32), (stats, extra), 0.5)
        extra = lax.ppermute(stats, "dom", [(i, i ^ reach) for i in range(parts)])
    rho_diag, rho_mate = call(
        rho_near_kernel,
        (sds((block, block), F32), sds((2, block // 2, block // 2), F32)),
        (place, freq, rate), 3.0, smem=(0,),
        scratch=[pltpu.VMEM((4, block, 128), F32), pltpu.VMEM((16, block), F32)], after=(pick,),
    )
    rho_far = call(
        rho_far_kernel, sds((2 * block, block), F32), (place, freq, rate),
        5.0, smem=(0,),
        scratch=[pltpu.VMEM((4, 2 * block, 128), F32), pltpu.VMEM((24, block), F32)],
        after=(rho_diag,),
    )
    amps = call(
        amps_kernel, sds((8, block), F32), (place, stats, extra, spectral, freq, rate),
        0.6, smem=(0,), after=(rho_far,),
    )
    mate_amps = lax.ppermute(amps, "mode", [(i, i ^ 1) for i in range(4)])
    far_amps = lax.ppermute(amps, "mode", [(i, i ^ 2) for i in range(4)])

    own, mate, far = [], [], []
    for c in range(CHUNKS):
        forces, sent = call(
            forces_kernel,
            (sds((comps, chunk), BF16), sds((part, chunk), BF16)),
            (place, pick, force, held[c]) + halos[c],
            2.6 / CHUNKS, smem=(0,),
            scratch=[
                pltpu.VMEM((dims, 2 * width, chunk), BF16), pltpu.VMEM((dims * slots * elems, chunk), BF16)
            ],
            after=(amps,),
        )
        own.append(forces)
        far.append(lax.ppermute(sent, "mode", [(i, i ^ 2) for i in range(4)]))
        mate.append(lax.ppermute(forces, "mode", [(i, i ^ 1) for i in range(4)]))
    near = call(
        functools.partial(near_kernel, dims, CHUNKS), sds((comps, 128), F32),
        (place, amps, mate_amps, rho_diag, rho_mate, *own, *mate),
        3.4, smem=(0,),
        scratch=[pltpu.VMEM((dims, block, 128), F32), pltpu.VMEM((2, block, block // 4), BF16)],
    )
    weights = call(
        functools.partial(weights_kernel, dims), sds((2 * block, block), BF16),
        (amps, mate_amps, far_amps, rho_far), 3.3,
        scratch=[pltpu.VMEM((dims, 2 * block, 128), F32)],
    )
    value = near
    for c in range(CHUNKS):
        last = c == CHUNKS - 1
        value = call(
            functools.partial(far_kernel, c * chunk, CHUNKS, per_elem),
            sds((1, comps) if last else (comps, 128), F32),
            (place, value, weights, far[c], *own, *mate), 2.1 / CHUNKS,
            smem=(0,), scratch=[pltpu.VMEM((comps, 128), F32)] * 2 if last else (),
        )
    value = value.reshape(comps)
    for reach in (1, 2):
        value = value + lax.ppermute(value, "mode", [(i, i ^ reach) for i in range(4)])
    return value


def extended_2(block, sides, width):
    for axis, dim in sides:
        count = lax.axis_size(axis)
        forward = [(i, i + 1) for i in range(count - 1)]
        backward = [(target, source) for source, target in forward]
        low = lax.ppermute(
            lax.slice_in_dim(block, block.shape[dim] - width, None, axis=dim), axis, forward
        )
        high = lax.ppermute(lax.slice_in_dim(block, 0, width, axis=dim), axis, backward)
        block = jnp.concatenate([low, block, high], axis=dim)
    return block


def shifted(value, axis, steps):
    count = lax.axis_size(axis)
    pairs = [(source, (source + steps) % count) for source in range(count)]
    return lax.ppermute(value, axis, pairs)


def correlation_block(freq_rows, freq_cols, rate_rows, rate_cols):
    ratio = freq_cols[None, :] / freq_rows[:, None]
    ratio_sq = ratio * ratio
    rate_row = rate_rows[:, None]
    rate_col = rate_cols[None, :]
    top_part = (
        8.0
        * jnp.sqrt(rate_row * rate_col)
        * (rate_row + ratio * rate_col)
        * ratio
        * jnp.sqrt(ratio)
    )
    spread = 1.0 - ratio_sq
    bottom_part = (
        spread * spread
        + 4.0 * rate_row * rate_col * ratio * (1.0 + ratio_sq)
        + 4.0 * (rate_row * rate_row + rate_col * rate_col) * ratio_sq
    )
    return top_part / bottom_part


def block_terms(own_forces, own_start, far_forces, far_start, amplitudes, frequencies, damping):
    row_count = own_forces.shape[1]
    col_count = far_forces.shape[1]
    freq_rows = lax.dynamic_slice_in_dim(frequencies, own_start, row_count)
    freq_cols = lax.dynamic_slice_in_dim(frequencies, far_start, col_count)
    rate_rows = lax.dynamic_slice_in_dim(damping, own_start, row_count)
    rate_cols = lax.dynamic_slice_in_dim(damping, far_start, col_count)
    correlation = correlation_block(freq_rows, freq_cols, rate_rows, rate_cols)
    amp_rows = lax.dynamic_slice_in_dim(amplitudes, own_start, row_count, 1)
    amp_cols = lax.dynamic_slice_in_dim(amplitudes, far_start, col_count, 1)
    weights = (amp_rows.T[:, :, None] * correlation[:, None, :] * amp_cols[None, :, :]).astype(
        jnp.bfloat16
    )
    weights = weights.reshape(row_count, 3 * col_count)
    projected = jnp.dot(own_forces, weights, preferred_element_type=jnp.float32)
    projected = projected.reshape(own_forces.shape[0], 3, col_count)
    far_wide = far_forces.astype(jnp.float32)
    return jnp.sum(projected * far_wide[:, None, :], axis=(1, 2))


def any_groups(
    shapes, masses, spectral, frequencies, damping, recovery, connectivity, node_count, shared
):
    rim_width = shared.shape[1]
    block_width = shapes.shape[2]
    elem_count = connectivity.shape[0]
    slot_count = connectivity.shape[1]
    mode_index = lax.axis_index("mode")
    own_start = mode_index * block_width
    shape_wide = shapes.astype(jnp.float32)
    weighted = masses[None, :, None] * shape_wide
    lever_arm = jnp.sum(weighted, axis=1)
    general = jnp.sum(weighted * shape_wide, axis=(0, 1))
    lever_sum, general_sum = lax.psum((lever_arm, general), "dom")
    own_spectral = lax.dynamic_slice_in_dim(spectral, own_start, block_width, 1)
    local_amps = lever_sum / general_sum[None, :] * own_spectral
    amplitudes = lax.all_gather(local_amps, "mode", axis=1, tiled=True)
    outgoing = jnp.concatenate(
        [jnp.take(shapes, shared[0], axis=1), jnp.take(shapes, shared[1], axis=1)], axis=1
    )
    extended = extended_2(outgoing, (("dom", 1),), rim_width)
    node_table = jnp.concatenate(
        [shapes, extended[:, :rim_width], extended[:, 3 * rim_width :]], axis=1
    )
    gathered = jnp.take(node_table, connectivity.reshape(-1), axis=1).reshape(
        3, elem_count, slot_count, block_width
    )
    slot_live = (jnp.arange(slot_count)[None, :] < node_count[:, None]).astype(jnp.bfloat16)
    masked = recovery * slot_live[:, None, :, None]
    forces = jnp.einsum("ekna,aenm->ekm", masked, gathered, preferred_element_type=jnp.float32)
    forces = forces.astype(jnp.bfloat16).reshape(elem_count * recovery.shape[1], block_width)
    groups = lax.axis_size("mode")
    half_count = groups // 2
    partial_value = block_terms(
        forces, own_start, forces, own_start, amplitudes, frequencies, damping
    )

    def advance(turn_index, carried):
        incoming, summed = carried
        incoming = shifted(incoming, "mode", 1)
        source = (mode_index - turn_index) % groups * block_width
        factor = jnp.where(turn_index == half_count, jnp.float32(1.0), jnp.float32(2.0))
        summed = summed + factor * block_terms(
            forces, own_start, incoming, source, amplitudes, frequencies, damping
        )
        return (incoming, summed)

    carried = lax.fori_loop(1, half_count + 1, advance, (forces, partial_value))
    partial_value = carried[1]
    return lax.psum(partial_value, "mode")


def solution(mesh):
    in_specs = (
        P(None, "dom", "mode"),
        P("dom"),
        P(),
        P(),
        P(),
        P("dom", None, None, None),
        P("dom", None),
        P("dom"),
        P(None, "dom"),
    )
    out_specs = P("dom")
    special = mesh.shape["mode"] == 4
    step = four_groups if special else any_groups
    step = jax.shard_map(
        step, mesh=mesh, in_specs=in_specs, out_specs=out_specs, check_vma=False
    )
    return step
```

```python
import functools
import jax
import jax.numpy as jnp
from jax import lax
from jax.experimental import pallas as pl
from jax.experimental.pallas import tpu as pltpu
from jax.sharding import PartitionSpec as P


F32 = jnp.float32
BF16 = jnp.bfloat16
VMEM = pl.BlockSpec(memory_space=pltpu.VMEM)
HBM = pl.BlockSpec(memory_space=pltpu.HBM)
ANY = pl.BlockSpec(memory_space=pl.ANY)
SMEM = pl.BlockSpec(memory_space=pltpu.SMEM)


def call(kernel, out_shape, args, cost, smem=(), hbm=(), scratch=(), vmem=14 << 20, after=()):
    count = len(args)
    specs = [SMEM if i in smem else HBM if i in hbm else VMEM for i in range(count)]
    specs += [ANY] * len(after)
    many = isinstance(out_shape, (tuple, list))

    def body(*refs):
        kernel(*refs[:count], *refs[count + len(after) :])

    return pl.pallas_call(
        body,
        out_shape=out_shape,
        in_specs=specs,
        out_specs=[VMEM] * len(out_shape) if many else VMEM,
        scratch_shapes=list(scratch),
        cost_estimate=pl.CostEstimate(flops=int(1.1e9 * cost), bytes_accessed=0, transcendentals=0),
        compiler_params=pltpu.CompilerParams(vmem_limit_bytes=vmem),
    )(*args, *after)


def add_kernel(left_ref, right_ref, out_ref):
    out_ref[...] = left_ref[...] + right_ref[...]


def gather_kernel(at, shared_ref, shapes_ref, up_ref, down_ref, buf, sem):
    dims, nodes, chunk = buf.shape
    width = shared_ref.shape[1]
    load = pltpu.make_async_copy(shapes_ref.at[:, :, at : at + chunk], buf, sem)
    load.start()
    node = lax.broadcasted_iota(jnp.int32, (nodes, 2 * width), 0)
    wanted = jnp.concatenate([shared_ref[1:2, :], shared_ref[0:1, :]], axis=1)
    pick = jnp.where(node == wanted, 1.0, 0.0).astype(F32).T.astype(BF16)
    load.wait()
    for d in range(dims):
        got = jnp.dot(pick, buf[d], preferred_element_type=F32).astype(BF16)
        up_ref[d * width : (d + 1) * width, :] = got[:width]
        down_ref[d * width : (d + 1) * width, :] = got[width:]


def stats_kernel(chunks, mass_ref, *refs):
    shapes_refs, (out_ref, mass_scr) = refs[:chunks], refs[chunks:]
    dims, nodes, chunk = shapes_refs[0].shape
    column = jnp.broadcast_to(mass_ref[...], (8, nodes)).T
    mass_scr[...] = jnp.broadcast_to(column[:, 0:1], (nodes, 128))
    for c, shapes_ref in enumerate(shapes_refs):
        for at in range(0, chunk, 128):
            lanes = slice(c * chunk + at, c * chunk + at + 128)
            general = jnp.zeros((8, 128), F32)
            for d in range(dims):
                lever = jnp.zeros((8, 128), F32)
                for r in range(0, nodes, 16):
                    wide = shapes_ref[d, r : r + 16, at : at + 128].astype(F32)
                    weighted = wide * mass_scr[r : r + 16, :]
                    square = weighted * wide
                    lever += weighted[:8] + weighted[8:]
                    general += square[:8] + square[8:]
                out_ref[d : d + 1, lanes] = jnp.sum(lever, axis=0, keepdims=True)
            out_ref[dims : dims + 1, lanes] = jnp.sum(general, axis=0, keepdims=True)


def table_kernel(codes_ref, count_ref, recovery_ref, pick_ref, force_ref):
    slots, elems = codes_ref.shape
    per_elem, dims = recovery_ref.shape[0], recovery_ref.shape[1]
    span = pick_ref.shape[1]
    node = lax.broadcasted_iota(jnp.int32, (span, elems), 0)
    for s in range(0, slots, 2):
        picks = []
        for q in range(s, min(s + 2, slots)):
            code = jnp.where(q < count_ref[...], codes_ref[q : q + 1, :], -1)
            picks.append(jnp.where(node == code, 1.0, 0.0).astype(F32))
        pick_ref[s * elems : s * elems + len(picks) * elems, :] = (
            jnp.concatenate(picks, axis=1).T.astype(BF16)
        )
    row = lax.broadcasted_iota(jnp.int32, (elems, 2 * elems), 0)
    column = lax.broadcasted_iota(jnp.int32, (elems, 2 * elems), 1)
    same = (column == row) | (column == row + elems)
    for k in range(per_elem):
        for d in range(dims):
            value = recovery_ref[k, d].astype(F32)
            for s in range(0, slots, 2):
                pair = jnp.concatenate([value[s : s + 1], value[s + 1 : s + 2]], axis=1)
                at = (d * slots + s) * elems
                force_ref[k * elems : (k + 1) * elems, at : at + 2 * elems] = jnp.where(
                    same, pair, 0.0
                ).astype(BF16)


def mode_rows(freq, rate):
    alpha = rate * freq
    inverse = 1.0 / jnp.sqrt(alpha)
    return (freq * freq * inverse, inverse, 2.0 * alpha, 2.0 * (freq / rate))


def place_modes(freq_ref, rate_ref, row_scr, col_scr, groups, sides, block):
    for which, group in enumerate(groups):
        lanes = pl.ds(pl.multiple_of(group * block, block), block)
        rows = jnp.concatenate(list(mode_rows(freq_ref[:, lanes], rate_ref[:, lanes])) * 2, axis=0)
        row_scr[which * 8 : which * 8 + 8, :] = rows
        if which < sides:
            turned = rows.T
            for q in range(4):
                col_scr[q, which * block : (which + 1) * block, :] = jnp.broadcast_to(
                    turned[:, q : q + 1], (block, 128)
                )


def fill_rho(row_scr, col_scr, out_ref, out_col, side_row, count, cols_at, col_off, tile):
    step = min(count, 256)
    cols = [
        jnp.broadcast_to(row_scr[cols_at + q : cols_at + q + 1, pl.ds(col_off, tile)], (8, tile))
        for q in range(4)
    ]

    @pl.loop(0, count // step)
    def _(t):
        for k in range(0, step, 8):
            at = pl.multiple_of(t * step, step) + k
            high, low, alpha, zeta = (col_scr[q, pl.ds(side_row + at, 8), :] for q in range(4))
            for c in range(0, tile, 128):
                col = [value[:, c : c + 128] for value in cols]
                spread = high * col[1] - low * col[0]
                pair = alpha + col[2]
                bottom = spread * spread + pair * (zeta + col[3])
                out_ref[pl.ds(at, 8), out_col + c : out_col + c + 128] = pair / bottom


def rho_near_kernel(place_ref, freq_ref, rate_ref, diag_ref, mate_ref, col_scr, row_scr):
    block = diag_ref.shape[0]
    half = block // 2
    tile = block // 4
    own, mate, parity = place_ref[0], place_ref[1], place_ref[3]
    place_modes(freq_ref, rate_ref, row_scr, col_scr, (own, mate), 1, block)
    for j in range(4):
        fill_rho(row_scr, col_scr, diag_ref, j * tile, 0, (j + 1) * tile, 0, j * tile, tile)
    for i in range(2):
        for j in range(2):
            off = pl.multiple_of((i ^ parity) * half + j * tile, tile)
            fill_rho(row_scr, col_scr, mate_ref.at[i], j * tile, i * half, half, 8, off, tile)


def rho_far_kernel(place_ref, freq_ref, rate_ref, far_ref, col_scr, row_scr):
    block = far_ref.shape[1]
    tile = block // 4
    own, mate, far = place_ref[0], place_ref[1], place_ref[2]
    place_modes(freq_ref, rate_ref, row_scr, col_scr, (own, mate, far), 2, block)
    for j in range(4):
        fill_rho(row_scr, col_scr, far_ref, j * tile, 0, 2 * block, 16, j * tile, tile)


def forces_kernel(
    place_ref, pick_ref, force_ref, shapes_ref, low_ref, high_ref, all_ref, part_ref, rim_scr, got_scr
):
    dims, nodes, _ = shapes_ref.shape
    comps, chunk = all_ref.shape
    width = low_ref.shape[0] // dims
    taken = pick_ref.shape[0]
    part = comps // 2
    other = place_ref[5]
    for d in range(dims):
        rim_scr[d, :width, :] = low_ref[d * width : (d + 1) * width, :]
        rim_scr[d, width:, :] = high_ref[d * width : (d + 1) * width, :]
    wide = 256
    for c in range(0, chunk, wide):
        for d in range(dims):
            got = jnp.dot(
                pick_ref[:, :nodes], shapes_ref[d, :, c : c + wide], preferred_element_type=F32
            )
            got = got + jnp.dot(
                pick_ref[:, nodes:], rim_scr[d, :, c : c + wide], preferred_element_type=F32
            )
            got_scr[d * taken : (d + 1) * taken, c : c + wide] = got.astype(BF16)
        total = jnp.dot(force_ref[...], got_scr[:, c : c + wide], preferred_element_type=F32)
        all_ref[:, c : c + wide] = total.astype(BF16)
    part_ref[...] = all_ref[pl.ds(pl.multiple_of(other * part, part), part), :]


def join_kernel(*refs):
    out_ref = refs[-1]
    size = refs[0].shape[0]
    for q, ref in enumerate(refs[:-1]):
        out_ref[q * size : (q + 1) * size, :] = ref[...]


def amps_kernel(place_ref, stats_ref, extra_ref, spectral_ref, freq_ref, rate_ref, *out_refs):
    dims, block = spectral_ref.shape[0], stats_ref.shape[1]
    for q, out_ref in enumerate(out_refs):
        lanes = pl.ds(pl.multiple_of(place_ref[q] * block, block), block)
        rows = slice(q * (dims + 1), (q + 1) * (dims + 1))
        total = stats_ref[rows, :] + extra_ref[rows, :]
        scale = 2.0 * jnp.sqrt(freq_ref[:, lanes] / rate_ref[:, lanes])
        amps = total[:dims] / total[dims : dims + 1] * spectral_ref[:, lanes] * scale
        out_ref[...] = jnp.concatenate([amps, jnp.zeros((8 - dims, block), F32)], axis=0)


def fold(value):
    total = value[:, :128]
    for c in range(128, value.shape[1], 128):
        total = total + value[:, c : c + 128]
    return total


def to_row(acc, turned, per_elem):
    elems = acc.shape[0] // per_elem
    for k in range(per_elem):
        turned[pl.ds(k, elems, stride=per_elem), :] = acc[k * elems : (k + 1) * elems, :]
    ones = jnp.ones((8, acc.shape[1]), F32)
    return lax.dot_general(
        ones, turned[...], (((1,), (1,)), ((), ())),
        precision=lax.Precision.HIGHEST, preferred_element_type=F32,
    )[0:1]


def spread_sides(side_scr, at, amps, dims):
    sides = amps.T
    for d in range(dims):
        side_scr[d, at : at + amps.shape[1], :] = jnp.broadcast_to(sides[:, d : d + 1], (amps.shape[1], 128))


def weigh(out, rho, side_scr, side_at, cols, dims, factor):
    span = min(512, rho.shape[1])
    for base in range(0, rho.shape[1], span):
        lanes = range(base, base + span, 128)
        col = [
            [jnp.broadcast_to(cols[d : d + 1, c : c + 128] * factor, (16, 128)) for d in range(dims)]
            for c in lanes
        ]
        for r in range(0, rho.shape[0], 16):
            side = [side_scr[d, side_at + r : side_at + r + 16, :] for d in range(dims)]
            for c, own in zip(lanes, col):
                pair = side[0] * own[0]
                for d in range(1, dims):
                    pair = pair + side[d] * own[d]
                out[r : r + 16, c : c + 128] = (rho[r : r + 16, c : c + 128] * pair).astype(BF16)


def near_kernel(dims, chunks, *refs):
    place_ref, own_amps_ref, mate_amps_ref, diag_ref, cross_ref = refs[:5]
    own_refs, mate_refs = refs[5 : 5 + chunks], refs[5 + chunks : 5 + 2 * chunks]
    acc, side_scr, w_scr = refs[5 + 2 * chunks :]
    _, chunk = own_refs[0].shape
    block = diag_ref.shape[0]
    tile = block // 4
    half = block // 2
    parity = place_ref[3]

    def part(parts, at, size):
        return parts[at // chunk][:, at % chunk : at % chunk + size]

    def product(w, at, depth):
        total = None
        for c in range(at, at + depth, min(chunk, depth)):
            size = min(chunk, at + depth - c)
            got = jnp.dot(part(own_refs, c, size), w[c - at : c - at + size, :], preferred_element_type=F32)
            total = got if total is None else total + got
        return total

    spread_sides(side_scr, 0, own_amps_ref[...], dims)
    turn = 0
    for j in range(4):
        cols = own_amps_ref[:, j * tile : (j + 1) * tile]
        for i in range(j + 1):
            rho = diag_ref.at[i * tile : (i + 1) * tile, j * tile : (j + 1) * tile]
            out = w_scr.at[turn, i * tile : (i + 1) * tile, :]
            weigh(out, rho, side_scr, i * tile, cols, dims, 2.0 if i < j else 1.0)
        got = product(w_scr.at[turn], 0, (j + 1) * tile)
        got = fold(got * part(own_refs, j * tile, tile).astype(F32))
        acc[...] = got if j == 0 else acc[...] + got
        turn = 1 - turn
    for i in range(2):
        for j in range(half // tile):
            here, there = i * half + j * tile, (1 - i) * half + j * tile
            straight = parity == 0
            cols = jnp.where(
                straight, mate_amps_ref[:, here : here + tile], mate_amps_ref[:, there : there + tile]
            )
            rho = cross_ref.at[i, :, j * tile : (j + 1) * tile]
            weigh(w_scr.at[turn, :half, :], rho, side_scr, i * half, cols, dims, 2.0)
            got = product(w_scr.at[turn], i * half, half)
            other = jnp.where(
                straight, part(mate_refs, here, tile).astype(F32), part(mate_refs, there, tile).astype(F32)
            )
            acc[...] += fold(got * other)
            turn = 1 - turn


def weights_kernel(dims, own_amps_ref, mate_amps_ref, far_amps_ref, rho_ref, out_ref, side_scr):
    block = rho_ref.shape[1]
    tile = block // 4
    spread_sides(side_scr, 0, own_amps_ref[...], dims)
    spread_sides(side_scr, block, mate_amps_ref[...], dims)

    @pl.loop(0, 2 * block // tile)
    def _(t):
        rows = pl.ds(pl.multiple_of(t * tile, tile), tile)
        sides = side_scr.at[:, rows, :]
        weigh(out_ref.at[rows, :], rho_ref.at[rows, :], sides, 0, far_amps_ref[...], dims, 2.0)


def far_kernel(at, chunks, per_elem, place_ref, near_ref, w_ref, far_ref, *refs):
    own_refs, mate_refs = refs[:chunks], refs[chunks : 2 * chunks]
    if len(refs) == 2 * chunks + 1:
        acc, last = refs[-1], False
    else:
        (out_ref, acc, turned), last = refs[2 * chunks :], True
    comps, chunk = own_refs[0].shape
    block = w_ref.shape[1]
    part = comps // 2
    tile = min(256, chunk)
    here = pl.multiple_of(place_ref[4] * part, part)
    rows = pl.ds(here, part)
    total = near_ref[rows, :]
    for c in range(0, chunk, tile):
        spot = slice(at + c, at + c + tile)
        got = None
        for which, parts in enumerate((own_refs, mate_refs)):
            for q in range(chunks):
                base = which * block + q * chunk
                piece = jnp.dot(
                    parts[q][rows, :], w_ref[base : base + chunk, spot], preferred_element_type=F32
                )
                got = piece if got is None else got + piece
        total = total + fold(got * far_ref[:, c : c + tile].astype(F32))
    acc[...] = near_ref[...]
    acc[rows, :] = total
    if last:
        out_ref[...] = to_row(acc, turned, per_elem)


CHUNKS = 1


def four_groups(*args):
    return combined(*args)


def combined(
    shapes, masses, spectral, frequencies, damping, recovery, connectivity, node_count, shared
):
    dims, nodes, block = shapes.shape
    elems, slots = connectivity.shape
    per_elem = recovery.shape[1]
    comps = elems * per_elem
    part = comps // 2
    width = shared.shape[1]
    parts = lax.axis_size("dom")
    group = lax.axis_index("mode").astype(jnp.int32)
    place = jnp.stack(
        [group, group ^ 1, group ^ 2, group & 1, group >> 1, 1 - (group >> 1)]
    ).astype(jnp.int32)
    sds = jax.ShapeDtypeStruct
    chunk = block // CHUNKS
    ahead = [(i, i + 1) for i in range(parts - 1)]
    back = [(i + 1, i) for i in range(parts - 1)]
    freq = frequencies.reshape(1, -1)
    rate = damping.reshape(1, -1)

    def gathered(c, after):
        return call(
            functools.partial(gather_kernel, c * chunk),
            (sds((dims * width, chunk), BF16), sds((dims * width, chunk), BF16), sds((dims, nodes, chunk), BF16)),
            (shared, shapes), 2.0 / CHUNKS, hbm=(1,),
            scratch=[pltpu.SemaphoreType.DMA], after=after,
        )

    halos, held = [], []
    after = ()
    for c in range(CHUNKS):
        up, down, kept = gathered(c, after)
        held.append(kept)
        after = (up,)
        halos.append((lax.ppermute(up, "dom", ahead), lax.ppermute(down, "dom", back)))

    stats = call(
        functools.partial(stats_kernel, CHUNKS), sds((dims + 1, block), F32), (masses.reshape(1, nodes), *held), 0.8,
        scratch=[pltpu.VMEM((nodes, 128), F32)], after=after,
    )
    pick, force = call(
        table_kernel, (sds((slots * elems, nodes + 2 * width), BF16), sds((comps, dims * slots * elems), BF16)),
        (connectivity.T, node_count.reshape(1, elems), recovery.transpose(1, 3, 2, 0)),
        0.5, after=(stats,),
    )
    rho_diag, rho_mate = call(
        rho_near_kernel,
        (sds((block, block), F32), sds((2, block // 2, block // 2), F32)),
        (place, freq, rate), 3.0, smem=(0,),
        scratch=[pltpu.VMEM((4, block, 128), F32), pltpu.VMEM((16, block), F32)], after=(pick,),
    )
    rho_far = call(
        rho_far_kernel, sds((2 * block, block), F32), (place, freq, rate),
        5.0, smem=(0,),
        scratch=[pltpu.VMEM((4, 2 * block, 128), F32), pltpu.VMEM((24, block), F32)],
        after=(rho_diag,),
    )
    given = [stats] + [lax.ppermute(stats, "mode", [(i, i ^ q) for i in range(4)]) for q in (1, 2)]
    stats = call(join_kernel, sds((3 * (dims + 1), block), F32), given, 0.5, after=(pick,))
    first = stats
    order = [1 << q for q in range(1, parts.bit_length() - 1)] + [1]
    if parts & (parts - 1) or parts == 1:
        stats = lax.psum(stats, "dom")
        order = []
    extra = jnp.zeros_like(stats)
    for q, reach in enumerate(order):
        if q:
            stats = call(
                add_kernel, sds(stats.shape, F32), (stats, extra), 0.5, after=(rho_far,) if q == 1 else ()
            )
            first = stats if q == 1 else first
        extra = lax.ppermute(stats, "dom", [(i, i ^ reach) for i in range(parts)])
    amps, mate_amps, far_amps = call(
        amps_kernel, [sds((8, block), F32)] * 3, (place, stats, extra, spectral, freq, rate), 0.8, smem=(0,)
    )

    own, mate, far = [], [], []
    for c in range(CHUNKS):
        forces, sent = call(
            forces_kernel,
            (sds((comps, chunk), BF16), sds((part, chunk), BF16)),
            (place, pick, force, held[c]) + halos[c],
            2.6 / CHUNKS, smem=(0,),
            scratch=[
                pltpu.VMEM((dims, 2 * width, chunk), BF16), pltpu.VMEM((dims * slots * elems, chunk), BF16)
            ],
            after=(first,),
        )
        own.append(forces)
        far.append(lax.ppermute(sent, "mode", [(i, i ^ 2) for i in range(4)]))
        mate.append(lax.ppermute(forces, "mode", [(i, i ^ 1) for i in range(4)]))
    near = call(
        functools.partial(near_kernel, dims, CHUNKS), sds((comps, 128), F32),
        (place, amps, mate_amps, rho_diag, rho_mate, *own, *mate),
        3.4, smem=(0,),
        scratch=[pltpu.VMEM((dims, block, 128), F32), pltpu.VMEM((2, block, block // 4), BF16)],
    )
    weights = call(
        functools.partial(weights_kernel, dims), sds((2 * block, block), BF16),
        (amps, mate_amps, far_amps, rho_far), 3.3,
        scratch=[pltpu.VMEM((dims, 2 * block, 128), F32)],
    )
    value = near
    for c in range(CHUNKS):
        last = c == CHUNKS - 1
        value = call(
            functools.partial(far_kernel, c * chunk, CHUNKS, per_elem),
            sds((1, comps) if last else (comps, 128), F32),
            (place, value, weights, far[c], *own, *mate), 2.1 / CHUNKS,
            smem=(0,), scratch=[pltpu.VMEM((comps, 128), F32)] * 2 if last else (),
        )
    value = value.reshape(comps)
    for reach in (1, 2):
        value = value + lax.ppermute(value, "mode", [(i, i ^ reach) for i in range(4)])
    return value


def extended_2(block, sides, width):
    for axis, dim in sides:
        count = lax.axis_size(axis)
        forward = [(i, i + 1) for i in range(count - 1)]
        backward = [(target, source) for source, target in forward]
        low = lax.ppermute(
            lax.slice_in_dim(block, block.shape[dim] - width, None, axis=dim), axis, forward
        )
        high = lax.ppermute(lax.slice_in_dim(block, 0, width, axis=dim), axis, backward)
        block = jnp.concatenate([low, block, high], axis=dim)
    return block


def shifted(value, axis, steps):
    count = lax.axis_size(axis)
    pairs = [(source, (source + steps) % count) for source in range(count)]
    return lax.ppermute(value, axis, pairs)


def correlation_block(freq_rows, freq_cols, rate_rows, rate_cols):
    ratio = freq_cols[None, :] / freq_rows[:, None]
    ratio_sq = ratio * ratio
    rate_row = rate_rows[:, None]
    rate_col = rate_cols[None, :]
    top_part = (
        8.0
        * jnp.sqrt(rate_row * rate_col)
        * (rate_row + ratio * rate_col)
        * ratio
        * jnp.sqrt(ratio)
    )
    spread = 1.0 - ratio_sq
    bottom_part = (
        spread * spread
        + 4.0 * rate_row * rate_col * ratio * (1.0 + ratio_sq)
        + 4.0 * (rate_row * rate_row + rate_col * rate_col) * ratio_sq
    )
    return top_part / bottom_part


def block_terms(own_forces, own_start, far_forces, far_start, amplitudes, frequencies, damping):
    row_count = own_forces.shape[1]
    col_count = far_forces.shape[1]
    freq_rows = lax.dynamic_slice_in_dim(frequencies, own_start, row_count)
    freq_cols = lax.dynamic_slice_in_dim(frequencies, far_start, col_count)
    rate_rows = lax.dynamic_slice_in_dim(damping, own_start, row_count)
    rate_cols = lax.dynamic_slice_in_dim(damping, far_start, col_count)
    correlation = correlation_block(freq_rows, freq_cols, rate_rows, rate_cols)
    amp_rows = lax.dynamic_slice_in_dim(amplitudes, own_start, row_count, 1)
    amp_cols = lax.dynamic_slice_in_dim(amplitudes, far_start, col_count, 1)
    weights = (amp_rows.T[:, :, None] * correlation[:, None, :] * amp_cols[None, :, :]).astype(
        jnp.bfloat16
    )
    weights = weights.reshape(row_count, 3 * col_count)
    projected = jnp.dot(own_forces, weights, preferred_element_type=jnp.float32)
    projected = projected.reshape(own_forces.shape[0], 3, col_count)
    far_wide = far_forces.astype(jnp.float32)
    return jnp.sum(projected * far_wide[:, None, :], axis=(1, 2))


def any_groups(
    shapes, masses, spectral, frequencies, damping, recovery, connectivity, node_count, shared
):
    rim_width = shared.shape[1]
    block_width = shapes.shape[2]
    elem_count = connectivity.shape[0]
    slot_count = connectivity.shape[1]
    mode_index = lax.axis_index("mode")
    own_start = mode_index * block_width
    shape_wide = shapes.astype(jnp.float32)
    weighted = masses[None, :, None] * shape_wide
    lever_arm = jnp.sum(weighted, axis=1)
    general = jnp.sum(weighted * shape_wide, axis=(0, 1))
    lever_sum, general_sum = lax.psum((lever_arm, general), "dom")
    own_spectral = lax.dynamic_slice_in_dim(spectral, own_start, block_width, 1)
    local_amps = lever_sum / general_sum[None, :] * own_spectral
    amplitudes = lax.all_gather(local_amps, "mode", axis=1, tiled=True)
    outgoing = jnp.concatenate(
        [jnp.take(shapes, shared[0], axis=1), jnp.take(shapes, shared[1], axis=1)], axis=1
    )
    extended = extended_2(outgoing, (("dom", 1),), rim_width)
    node_table = jnp.concatenate(
        [shapes, extended[:, :rim_width], extended[:, 3 * rim_width :]], axis=1
    )
    gathered = jnp.take(node_table, connectivity.reshape(-1), axis=1).reshape(
        3, elem_count, slot_count, block_width
    )
    slot_live = (jnp.arange(slot_count)[None, :] < node_count[:, None]).astype(jnp.bfloat16)
    masked = recovery * slot_live[:, None, :, None]
    forces = jnp.einsum("ekna,aenm->ekm", masked, gathered, preferred_element_type=jnp.float32)
    forces = forces.astype(jnp.bfloat16).reshape(elem_count * recovery.shape[1], block_width)
    groups = lax.axis_size("mode")
    half_count = groups // 2
    partial_value = block_terms(
        forces, own_start, forces, own_start, amplitudes, frequencies, damping
    )

    def advance(turn_index, carried):
        incoming, summed = carried
        incoming = shifted(incoming, "mode", 1)
        source = (mode_index - turn_index) % groups * block_width
        factor = jnp.where(turn_index == half_count, jnp.float32(1.0), jnp.float32(2.0))
        summed = summed + factor * block_terms(
            forces, own_start, incoming, source, amplitudes, frequencies, damping
        )
        return (incoming, summed)

    carried = lax.fori_loop(1, half_count + 1, advance, (forces, partial_value))
    partial_value = carried[1]
    return lax.psum(partial_value, "mode")


def solution(mesh):
    in_specs = (
        P(None, "dom", "mode"),
        P("dom"),
        P(),
        P(),
        P(),
        P("dom", None, None, None),
        P("dom", None),
        P("dom"),
        P(None, "dom"),
    )
    out_specs = P("dom")
    special = mesh.shape["mode"] == 4
    step = four_groups if special else any_groups
    step = jax.shard_map(
        step, mesh=mesh, in_specs=in_specs, out_specs=out_specs, check_vma=False
    )
    return step
```

```python
import functools
import jax
import jax.numpy as jnp
from jax import lax
from jax.experimental import pallas as pl
from jax.experimental.pallas import tpu as pltpu
from jax.sharding import PartitionSpec as P


F32 = jnp.float32
BF16 = jnp.bfloat16
VMEM = pl.BlockSpec(memory_space=pltpu.VMEM)
HBM = pl.BlockSpec(memory_space=pltpu.HBM)
ANY = pl.BlockSpec(memory_space=pl.ANY)
SMEM = pl.BlockSpec(memory_space=pltpu.SMEM)


def call(kernel, out_shape, args, cost, smem=(), hbm=(), scratch=(), vmem=14 << 20, after=()):
    count = len(args)
    specs = [SMEM if i in smem else HBM if i in hbm else VMEM for i in range(count)]
    specs += [ANY] * len(after)
    many = isinstance(out_shape, (tuple, list))

    def body(*refs):
        kernel(*refs[:count], *refs[count + len(after) :])

    return pl.pallas_call(
        body,
        out_shape=out_shape,
        in_specs=specs,
        out_specs=[VMEM] * len(out_shape) if many else VMEM,
        scratch_shapes=list(scratch),
        cost_estimate=pl.CostEstimate(flops=int(1.1e9 * cost), bytes_accessed=0, transcendentals=0),
        compiler_params=pltpu.CompilerParams(vmem_limit_bytes=vmem),
    )(*args, *after)


def add_kernel(left_ref, right_ref, out_ref):
    out_ref[...] = left_ref[...] + right_ref[...]


def gather_kernel(at, shared_ref, shapes_ref, up_ref, down_ref, buf, sem):
    dims, nodes, chunk = buf.shape
    width = shared_ref.shape[1]
    load = pltpu.make_async_copy(shapes_ref.at[:, :, at : at + chunk], buf, sem)
    load.start()
    node = lax.broadcasted_iota(jnp.int32, (nodes, 2 * width), 0)
    wanted = jnp.concatenate([shared_ref[1:2, :], shared_ref[0:1, :]], axis=1)
    pick = jnp.where(node == wanted, 1.0, 0.0).astype(F32).T.astype(BF16)
    load.wait()
    for d in range(dims):
        got = jnp.dot(pick, buf[d], preferred_element_type=F32).astype(BF16)
        up_ref[d * width : (d + 1) * width, :] = got[:width]
        down_ref[d * width : (d + 1) * width, :] = got[width:]


def stats_kernel(chunks, mass_ref, *refs):
    shapes_refs, (out_ref, mass_scr) = refs[:chunks], refs[chunks:]
    dims, nodes, chunk = shapes_refs[0].shape
    column = jnp.broadcast_to(mass_ref[...], (8, nodes)).T
    mass_scr[...] = jnp.broadcast_to(column[:, 0:1], (nodes, 128))
    for c, shapes_ref in enumerate(shapes_refs):
        for at in range(0, chunk, 128):
            lanes = slice(c * chunk + at, c * chunk + at + 128)
            general = jnp.zeros((8, 128), F32)
            for d in range(dims):
                lever = jnp.zeros((8, 128), F32)
                for r in range(0, nodes, 16):
                    wide = shapes_ref[d, r : r + 16, at : at + 128].astype(F32)
                    weighted = wide * mass_scr[r : r + 16, :]
                    square = weighted * wide
                    lever += weighted[:8] + weighted[8:]
                    general += square[:8] + square[8:]
                out_ref[d : d + 1, lanes] = jnp.sum(lever, axis=0, keepdims=True)
            out_ref[dims : dims + 1, lanes] = jnp.sum(general, axis=0, keepdims=True)


def table_kernel(codes_ref, count_ref, recovery_ref, pick_ref, force_ref):
    slots, elems = codes_ref.shape
    per_elem, dims = recovery_ref.shape[0], recovery_ref.shape[1]
    span = pick_ref.shape[1]
    node = lax.broadcasted_iota(jnp.int32, (span, elems), 0)
    for s in range(0, slots, 2):
        picks = []
        for q in range(s, min(s + 2, slots)):
            code = jnp.where(q < count_ref[...], codes_ref[q : q + 1, :], -1)
            picks.append(jnp.where(node == code, 1.0, 0.0).astype(F32))
        pick_ref[s * elems : s * elems + len(picks) * elems, :] = (
            jnp.concatenate(picks, axis=1).T.astype(BF16)
        )
    row = lax.broadcasted_iota(jnp.int32, (elems, 2 * elems), 0)
    column = lax.broadcasted_iota(jnp.int32, (elems, 2 * elems), 1)
    same = (column == row) | (column == row + elems)
    for k in range(per_elem):
        for d in range(dims):
            value = recovery_ref[k, d].astype(F32)
            for s in range(0, slots, 2):
                pair = jnp.concatenate([value[s : s + 1], value[s + 1 : s + 2]], axis=1)
                at = (d * slots + s) * elems
                force_ref[k * elems : (k + 1) * elems, at : at + 2 * elems] = jnp.where(
                    same, pair, 0.0
                ).astype(BF16)


def mode_rows(freq, rate):
    alpha = rate * freq
    inverse = 1.0 / jnp.sqrt(alpha)
    return (freq * freq * inverse, inverse, 2.0 * alpha, 2.0 * (freq / rate))


def turn_rows(rows):
    pieces = [rows[:, c : c + 128] for c in range(0, rows.shape[1], 128)]
    while len(pieces) * 8 % 128:
        pieces.append(jnp.zeros((8, 128), F32))
    return [jnp.concatenate(pieces[c : c + 16], axis=0).T for c in range(0, len(pieces), 16)]


def place_modes(freq_ref, rate_ref, row_scr, col_scr, groups, sides, block):
    side_rows = []
    for which, group in enumerate(groups):
        lanes = pl.ds(pl.multiple_of(group * block, block), block)
        rows = jnp.concatenate(list(mode_rows(freq_ref[:, lanes], rate_ref[:, lanes])) * 2, axis=0)
        row_scr[which * 8 : which * 8 + 8, :] = rows
        if which < sides:
            side_rows.append(rows)
    turned = turn_rows(jnp.concatenate(side_rows, axis=1))
    for t in range(sides * block // 128):
        for q in range(4):
            lane = t % 16 * 8 + q
            col_scr[q, t * 128 : (t + 1) * 128, :] = jnp.broadcast_to(
                turned[t // 16][:, lane : lane + 1], (128, 128)
            )


def fill_rho(row_scr, col_scr, out_ref, out_col, side_row, count, cols_at, col_off, tile):
    step = min(count, 256)
    cols = [
        jnp.broadcast_to(row_scr[cols_at + q : cols_at + q + 1, pl.ds(col_off, tile)], (8, tile))
        for q in range(4)
    ]

    @pl.loop(0, count // step)
    def _(t):
        for k in range(0, step, 8):
            at = pl.multiple_of(t * step, step) + k
            high, low, alpha, zeta = (col_scr[q, pl.ds(side_row + at, 8), :] for q in range(4))
            for c in range(0, tile, 128):
                col = [value[:, c : c + 128] for value in cols]
                spread = high * col[1] - low * col[0]
                pair = alpha + col[2]
                bottom = spread * spread + pair * (zeta + col[3])
                out_ref[pl.ds(at, 8), out_col + c : out_col + c + 128] = pair / bottom


def rho_near_kernel(place_ref, freq_ref, rate_ref, diag_ref, mate_ref, col_scr, row_scr):
    block = diag_ref.shape[0]
    half = block // 2
    tile = block // 4
    own, mate, parity = place_ref[0], place_ref[1], place_ref[3]
    place_modes(freq_ref, rate_ref, row_scr, col_scr, (own, mate), 1, block)
    for j in range(4):
        fill_rho(row_scr, col_scr, diag_ref, j * tile, 0, (j + 1) * tile, 0, j * tile, tile)
    for i in range(2):
        for j in range(2):
            off = pl.multiple_of((i ^ parity) * half + j * tile, tile)
            fill_rho(row_scr, col_scr, mate_ref.at[i], j * tile, i * half, half, 8, off, tile)


def rho_far_kernel(place_ref, freq_ref, rate_ref, far_ref, col_scr, row_scr):
    block = far_ref.shape[1]
    tile = block // 4
    own, mate, far = place_ref[0], place_ref[1], place_ref[2]
    place_modes(freq_ref, rate_ref, row_scr, col_scr, (own, mate, far), 2, block)
    for j in range(4):
        fill_rho(row_scr, col_scr, far_ref, j * tile, 0, 2 * block, 16, j * tile, tile)


def forces_kernel(
    place_ref, pick_ref, force_ref, shapes_ref, low_ref, high_ref, all_ref, part_ref, rim_scr, got_scr
):
    dims, nodes, _ = shapes_ref.shape
    comps, chunk = all_ref.shape
    width = low_ref.shape[0] // dims
    taken = pick_ref.shape[0]
    part = comps // 2
    other = place_ref[5]
    for d in range(dims):
        rim_scr[d, :width, :] = low_ref[d * width : (d + 1) * width, :]
        rim_scr[d, width:, :] = high_ref[d * width : (d + 1) * width, :]
    wide = 256
    for c in range(0, chunk, wide):
        for d in range(dims):
            got = jnp.dot(
                pick_ref[:, :nodes], shapes_ref[d, :, c : c + wide], preferred_element_type=F32
            )
            got = got + jnp.dot(
                pick_ref[:, nodes:], rim_scr[d, :, c : c + wide], preferred_element_type=F32
            )
            got_scr[d * taken : (d + 1) * taken, c : c + wide] = got.astype(BF16)
        total = jnp.dot(force_ref[...], got_scr[:, c : c + wide], preferred_element_type=F32)
        all_ref[:, c : c + wide] = total.astype(BF16)
    part_ref[...] = all_ref[pl.ds(pl.multiple_of(other * part, part), part), :]


def join_kernel(*refs):
    out_ref = refs[-1]
    size = refs[0].shape[0]
    for q, ref in enumerate(refs[:-1]):
        out_ref[q * size : (q + 1) * size, :] = ref[...]


def amps_kernel(place_ref, stats_ref, extra_ref, spectral_ref, freq_ref, rate_ref, *out_refs):
    dims, block = spectral_ref.shape[0], stats_ref.shape[1]
    for q, out_ref in enumerate(out_refs):
        lanes = pl.ds(pl.multiple_of(place_ref[q] * block, block), block)
        rows = slice(q * (dims + 1), (q + 1) * (dims + 1))
        total = stats_ref[rows, :] + extra_ref[rows, :]
        scale = 2.0 * jnp.sqrt(freq_ref[:, lanes] / rate_ref[:, lanes])
        amps = total[:dims] / total[dims : dims + 1] * spectral_ref[:, lanes] * scale
        out_ref[...] = jnp.concatenate([amps, jnp.zeros((8 - dims, block), F32)], axis=0)


def fold(value):
    total = value[:, :128]
    for c in range(128, value.shape[1], 128):
        total = total + value[:, c : c + 128]
    return total


def to_row(acc, turned, per_elem):
    elems = acc.shape[0] // per_elem
    for k in range(per_elem):
        turned[pl.ds(k, elems, stride=per_elem), :] = acc[k * elems : (k + 1) * elems, :]
    ones = jnp.ones((8, acc.shape[1]), F32)
    return lax.dot_general(
        ones, turned[...], (((1,), (1,)), ((), ())),
        precision=lax.Precision.HIGHEST, preferred_element_type=F32,
    )[0:1]


def split(value):
    top = value.astype(BF16).astype(F32)
    rest = value - top
    middle = rest.astype(BF16).astype(F32)
    return top, middle, rest - middle


def side_terms(out_scr, at, amps, dims):
    top, middle, last = split(amps[:dims])
    rows = jnp.concatenate([top, top, middle, middle, top, last], axis=0)
    rows = jnp.concatenate([rows, jnp.zeros((32 - rows.shape[0], rows.shape[1]), F32)], axis=0)
    for c in range(0, amps.shape[1], 512):
        stack = [rows[:, c + q : c + q + 128] for q in range(0, 512, 128)]
        turned = jnp.concatenate(stack, axis=0).T
        for q in range(4):
            out_scr[at + c + q * 128 : at + c + (q + 1) * 128, :] = turned[:, q * 32 : (q + 1) * 32].astype(BF16)


def col_terms(amps, dims, factor):
    top, middle, last = split(amps[:dims] * factor)
    rows = jnp.concatenate([top, middle, top, middle, last, top], axis=0)
    rows = jnp.concatenate([rows, jnp.zeros((32 - rows.shape[0], rows.shape[1]), F32)], axis=0)
    return rows.astype(BF16)


def weigh(rho, side, cols):
    return (rho * jnp.dot(side, cols, preferred_element_type=F32)).astype(BF16)


def near_kernel(dims, chunks, *refs):
    place_ref, own_amps_ref, mate_amps_ref, diag_ref, cross_ref = refs[:5]
    own_refs, mate_refs = refs[5 : 5 + chunks], refs[5 + chunks : 5 + 2 * chunks]
    acc, side_scr, w_scr = refs[5 + 2 * chunks :]
    _, chunk = own_refs[0].shape
    block = diag_ref.shape[0]
    tile = block // 4
    half = block // 2
    parity = place_ref[3]

    def part(parts, at, size):
        return parts[at // chunk][:, at % chunk : at % chunk + size]

    def product(w, at, depth):
        total = None
        for c in range(at, at + depth, min(chunk, depth)):
            size = min(chunk, at + depth - c)
            got = jnp.dot(part(own_refs, c, size), w[c - at : c - at + size, :], preferred_element_type=F32)
            total = got if total is None else total + got
        return total

    side_terms(side_scr, 0, own_amps_ref[...], dims)
    once, twice = (col_terms(own_amps_ref[...], dims, factor) for factor in (1.0, 2.0))
    straight = parity == 0
    turn = 0
    for j in range(4):
        spot = slice(j * tile, (j + 1) * tile)
        for i in range(j + 1):
            rows = slice(i * tile, (i + 1) * tile)
            cols = twice if i < j else once
            w_scr[turn, rows, :] = weigh(diag_ref[rows, spot], side_scr[rows, :], cols[:, spot])
        got = product(w_scr.at[turn], 0, (j + 1) * tile)
        got = fold(got * part(own_refs, j * tile, tile).astype(F32))
        acc[...] = got if j == 0 else acc[...] + got
        turn = 1 - turn
    for i in range(2):
        for j in range(half // tile):
            here, there = i * half + j * tile, (1 - i) * half + j * tile
            cols = jnp.where(
                straight, mate_amps_ref[:, here : here + tile], mate_amps_ref[:, there : there + tile]
            )
            w_scr[turn, :half, :] = weigh(
                cross_ref[i, :, j * tile : (j + 1) * tile],
                side_scr[i * half : (i + 1) * half, :], col_terms(cols, dims, 2.0),
            )
            got = product(w_scr.at[turn], i * half, half)
            other = jnp.where(
                straight, part(mate_refs, here, tile).astype(F32), part(mate_refs, there, tile).astype(F32)
            )
            acc[...] += fold(got * other)
            turn = 1 - turn


def weights_kernel(dims, own_amps_ref, mate_amps_ref, far_amps_ref, rho_ref, out_ref, side_scr):
    block = rho_ref.shape[1]
    tile = block // 4
    side_terms(side_scr, 0, own_amps_ref[...], dims)
    side_terms(side_scr, block, mate_amps_ref[...], dims)
    cols = col_terms(far_amps_ref[...], dims, 2.0)
    for at in range(0, 2 * block, tile):
        rows = slice(at, at + tile)
        for c in range(0, block, tile):
            spot = slice(c, c + tile)
            out_ref[rows, spot] = weigh(rho_ref[rows, spot], side_scr[rows, :], cols[:, spot])


def far_kernel(at, chunks, per_elem, place_ref, near_ref, w_ref, far_ref, *refs):
    own_refs, mate_refs = refs[:chunks], refs[chunks : 2 * chunks]
    if len(refs) == 2 * chunks + 1:
        acc, last = refs[-1], False
    else:
        (out_ref, acc, turned), last = refs[2 * chunks :], True
    comps, chunk = own_refs[0].shape
    block = w_ref.shape[1]
    part = comps // 2
    tile = min(256, chunk)
    here = pl.multiple_of(place_ref[4] * part, part)
    rows = pl.ds(here, part)
    total = near_ref[rows, :]
    for c in range(0, chunk, tile):
        spot = slice(at + c, at + c + tile)
        got = None
        for which, parts in enumerate((own_refs, mate_refs)):
            for q in range(chunks):
                base = which * block + q * chunk
                piece = jnp.dot(
                    parts[q][rows, :], w_ref[base : base + chunk, spot], preferred_element_type=F32
                )
                got = piece if got is None else got + piece
        total = total + fold(got * far_ref[:, c : c + tile].astype(F32))
    acc[...] = near_ref[...]
    acc[rows, :] = total
    if last:
        out_ref[...] = to_row(acc, turned, per_elem)


CHUNKS = 1


def four_groups(*args):
    return combined(*args)


def combined(
    shapes, masses, spectral, frequencies, damping, recovery, connectivity, node_count, shared
):
    dims, nodes, block = shapes.shape
    elems, slots = connectivity.shape
    per_elem = recovery.shape[1]
    comps = elems * per_elem
    part = comps // 2
    width = shared.shape[1]
    parts = lax.axis_size("dom")
    group = lax.axis_index("mode").astype(jnp.int32)
    place = jnp.stack(
        [group, group ^ 1, group ^ 2, group & 1, group >> 1, 1 - (group >> 1)]
    ).astype(jnp.int32)
    sds = jax.ShapeDtypeStruct
    chunk = block // CHUNKS
    ahead = [(i, i + 1) for i in range(parts - 1)]
    back = [(i + 1, i) for i in range(parts - 1)]
    freq = frequencies.reshape(1, -1)
    rate = damping.reshape(1, -1)

    def gathered(c, after):
        return call(
            functools.partial(gather_kernel, c * chunk),
            (sds((dims * width, chunk), BF16), sds((dims * width, chunk), BF16), sds((dims, nodes, chunk), BF16)),
            (shared, shapes), 2.0 / CHUNKS, hbm=(1,), vmem=60 << 20,
            scratch=[pltpu.SemaphoreType.DMA], after=after,
        )

    halos, held = [], []
    after = ()
    for c in range(CHUNKS):
        up, down, kept = gathered(c, after)
        held.append(kept)
        after = (up,)
        halos.append((lax.ppermute(up, "dom", ahead), lax.ppermute(down, "dom", back)))

    stats = call(
        functools.partial(stats_kernel, CHUNKS), sds((dims + 1, block), F32), (masses.reshape(1, nodes), *held), 0.8,
        scratch=[pltpu.VMEM((nodes, 128), F32)],
    )
    rho_diag, rho_mate = call(
        rho_near_kernel,
        (sds((block, block), F32), sds((2, block // 2, block // 2), F32)),
        (place, freq, rate), 3.0, smem=(0,),
        scratch=[pltpu.VMEM((4, block, 128), F32), pltpu.VMEM((16, block), F32)], after=(stats,),
    )
    pick, force = call(
        table_kernel, (sds((slots * elems, nodes + 2 * width), BF16), sds((comps, dims * slots * elems), BF16)),
        (connectivity.T, node_count.reshape(1, elems), recovery.transpose(1, 3, 2, 0)),
        0.5, after=(rho_diag,),
    )
    rho_far = call(
        rho_far_kernel, sds((2 * block, block), F32), (place, freq, rate),
        5.0, smem=(0,),
        scratch=[pltpu.VMEM((4, 2 * block, 128), F32), pltpu.VMEM((24, block), F32)],
        after=(rho_diag,),
    )
    given = [stats] + [lax.ppermute(stats, "mode", [(i, i ^ q) for i in range(4)]) for q in (1, 2)]
    stats = call(join_kernel, sds((3 * (dims + 1), block), F32), given, 0.5)
    first = stats
    order = [1 << q for q in range(1, parts.bit_length() - 1)] + [1]
    if parts & (parts - 1) or parts == 1:
        stats = lax.psum(stats, "dom")
        order = []
    extra = jnp.zeros_like(stats)
    for q, reach in enumerate(order):
        if q:
            stats = call(
                add_kernel, sds(stats.shape, F32), (stats, extra), 0.5, after=(rho_diag,) if q == 1 else ()
            )
            first = stats if q == 1 else first
        extra = lax.ppermute(stats, "dom", [(i, i ^ reach) for i in range(parts)])
    amps, mate_amps, far_amps = call(
        amps_kernel, [sds((8, block), F32)] * 3, (place, stats, extra, spectral, freq, rate), 0.8, smem=(0,)
    )

    own, mate, far = [], [], []
    for c in range(CHUNKS):
        forces, sent = call(
            forces_kernel,
            (sds((comps, chunk), BF16), sds((part, chunk), BF16)),
            (place, pick, force, held[c]) + halos[c],
            2.6 / CHUNKS, smem=(0,),
            scratch=[
                pltpu.VMEM((dims, 2 * width, chunk), BF16), pltpu.VMEM((dims * slots * elems, chunk), BF16)
            ],
            after=(first,),
        )
        own.append(forces)
        far.append(lax.ppermute(sent, "mode", [(i, i ^ 2) for i in range(4)]))
        mate.append(lax.ppermute(forces, "mode", [(i, i ^ 1) for i in range(4)]))
    near = call(
        functools.partial(near_kernel, dims, CHUNKS), sds((comps, 128), F32),
        (place, amps, mate_amps, rho_diag, rho_mate, *own, *mate),
        3.4, smem=(0,),
        scratch=[pltpu.VMEM((block, 32), BF16), pltpu.VMEM((2, block, block // 4), BF16)],
    )
    weights = call(
        functools.partial(weights_kernel, dims), sds((2 * block, block), BF16),
        (amps, mate_amps, far_amps, rho_far), 3.3,
        scratch=[pltpu.VMEM((2 * block, 32), BF16)],
    )
    value = near
    for c in range(CHUNKS):
        last = c == CHUNKS - 1
        value = call(
            functools.partial(far_kernel, c * chunk, CHUNKS, per_elem),
            sds((1, comps) if last else (comps, 128), F32),
            (place, value, weights, far[c], *own, *mate), 2.1 / CHUNKS,
            smem=(0,), scratch=[pltpu.VMEM((comps, 128), F32)] * 2 if last else (),
        )
    value = value.reshape(comps)
    for reach in (1, 2):
        value = value + lax.ppermute(value, "mode", [(i, i ^ reach) for i in range(4)])
    return value


def extended_2(block, sides, width):
    for axis, dim in sides:
        count = lax.axis_size(axis)
        forward = [(i, i + 1) for i in range(count - 1)]
        backward = [(target, source) for source, target in forward]
        low = lax.ppermute(
            lax.slice_in_dim(block, block.shape[dim] - width, None, axis=dim), axis, forward
        )
        high = lax.ppermute(lax.slice_in_dim(block, 0, width, axis=dim), axis, backward)
        block = jnp.concatenate([low, block, high], axis=dim)
    return block


def shifted(value, axis, steps):
    count = lax.axis_size(axis)
    pairs = [(source, (source + steps) % count) for source in range(count)]
    return lax.ppermute(value, axis, pairs)


def correlation_block(freq_rows, freq_cols, rate_rows, rate_cols):
    ratio = freq_cols[None, :] / freq_rows[:, None]
    ratio_sq = ratio * ratio
    rate_row = rate_rows[:, None]
    rate_col = rate_cols[None, :]
    top_part = (
        8.0
        * jnp.sqrt(rate_row * rate_col)
        * (rate_row + ratio * rate_col)
        * ratio
        * jnp.sqrt(ratio)
    )
    spread = 1.0 - ratio_sq
    bottom_part = (
        spread * spread
        + 4.0 * rate_row * rate_col * ratio * (1.0 + ratio_sq)
        + 4.0 * (rate_row * rate_row + rate_col * rate_col) * ratio_sq
    )
    return top_part / bottom_part


def block_terms(own_forces, own_start, far_forces, far_start, amplitudes, frequencies, damping):
    row_count = own_forces.shape[1]
    col_count = far_forces.shape[1]
    freq_rows = lax.dynamic_slice_in_dim(frequencies, own_start, row_count)
    freq_cols = lax.dynamic_slice_in_dim(frequencies, far_start, col_count)
    rate_rows = lax.dynamic_slice_in_dim(damping, own_start, row_count)
    rate_cols = lax.dynamic_slice_in_dim(damping, far_start, col_count)
    correlation = correlation_block(freq_rows, freq_cols, rate_rows, rate_cols)
    amp_rows = lax.dynamic_slice_in_dim(amplitudes, own_start, row_count, 1)
    amp_cols = lax.dynamic_slice_in_dim(amplitudes, far_start, col_count, 1)
    weights = (amp_rows.T[:, :, None] * correlation[:, None, :] * amp_cols[None, :, :]).astype(
        jnp.bfloat16
    )
    weights = weights.reshape(row_count, 3 * col_count)
    projected = jnp.dot(own_forces, weights, preferred_element_type=jnp.float32)
    projected = projected.reshape(own_forces.shape[0], 3, col_count)
    far_wide = far_forces.astype(jnp.float32)
    return jnp.sum(projected * far_wide[:, None, :], axis=(1, 2))


def any_groups(
    shapes, masses, spectral, frequencies, damping, recovery, connectivity, node_count, shared
):
    rim_width = shared.shape[1]
    block_width = shapes.shape[2]
    elem_count = connectivity.shape[0]
    slot_count = connectivity.shape[1]
    mode_index = lax.axis_index("mode")
    own_start = mode_index * block_width
    shape_wide = shapes.astype(jnp.float32)
    weighted = masses[None, :, None] * shape_wide
    lever_arm = jnp.sum(weighted, axis=1)
    general = jnp.sum(weighted * shape_wide, axis=(0, 1))
    lever_sum, general_sum = lax.psum((lever_arm, general), "dom")
    own_spectral = lax.dynamic_slice_in_dim(spectral, own_start, block_width, 1)
    local_amps = lever_sum / general_sum[None, :] * own_spectral
    amplitudes = lax.all_gather(local_amps, "mode", axis=1, tiled=True)
    outgoing = jnp.concatenate(
        [jnp.take(shapes, shared[0], axis=1), jnp.take(shapes, shared[1], axis=1)], axis=1
    )
    extended = extended_2(outgoing, (("dom", 1),), rim_width)
    node_table = jnp.concatenate(
        [shapes, extended[:, :rim_width], extended[:, 3 * rim_width :]], axis=1
    )
    gathered = jnp.take(node_table, connectivity.reshape(-1), axis=1).reshape(
        3, elem_count, slot_count, block_width
    )
    slot_live = (jnp.arange(slot_count)[None, :] < node_count[:, None]).astype(jnp.bfloat16)
    masked = recovery * slot_live[:, None, :, None]
    forces = jnp.einsum("ekna,aenm->ekm", masked, gathered, preferred_element_type=jnp.float32)
    forces = forces.astype(jnp.bfloat16).reshape(elem_count * recovery.shape[1], block_width)
    groups = lax.axis_size("mode")
    half_count = groups // 2
    partial_value = block_terms(
        forces, own_start, forces, own_start, amplitudes, frequencies, damping
    )

    def advance(turn_index, carried):
        incoming, summed = carried
        incoming = shifted(incoming, "mode", 1)
        source = (mode_index - turn_index) % groups * block_width
        factor = jnp.where(turn_index == half_count, jnp.float32(1.0), jnp.float32(2.0))
        summed = summed + factor * block_terms(
            forces, own_start, incoming, source, amplitudes, frequencies, damping
        )
        return (incoming, summed)

    carried = lax.fori_loop(1, half_count + 1, advance, (forces, partial_value))
    partial_value = carried[1]
    return lax.psum(partial_value, "mode")


def solution(mesh):
    in_specs = (
        P(None, "dom", "mode"),
        P("dom"),
        P(),
        P(),
        P(),
        P("dom", None, None, None),
        P("dom", None),
        P("dom"),
        P(None, "dom"),
    )
    out_specs = P("dom")
    special = mesh.shape["mode"] == 4
    step = four_groups if special else any_groups
    step = jax.shard_map(
        step, mesh=mesh, in_specs=in_specs, out_specs=out_specs, check_vma=False
    )
    return step
```

```python
import functools
import jax
import jax.numpy as jnp
from jax import lax
from jax.experimental import pallas as pl
from jax.experimental.pallas import tpu as pltpu
from jax.sharding import PartitionSpec as P


F32 = jnp.float32
BF16 = jnp.bfloat16
VMEM = pl.BlockSpec(memory_space=pltpu.VMEM)
HBM = pl.BlockSpec(memory_space=pltpu.HBM)
ANY = pl.BlockSpec(memory_space=pl.ANY)
SMEM = pl.BlockSpec(memory_space=pltpu.SMEM)


def call(kernel, out_shape, args, cost, smem=(), hbm=(), scratch=(), vmem=14 << 20, after=()):
    count = len(args)
    specs = [SMEM if i in smem else HBM if i in hbm else VMEM for i in range(count)]
    specs += [ANY] * len(after)
    many = isinstance(out_shape, (tuple, list))

    def body(*refs):
        kernel(*refs[:count], *refs[count + len(after) :])

    return pl.pallas_call(
        body,
        out_shape=out_shape,
        in_specs=specs,
        out_specs=[VMEM] * len(out_shape) if many else VMEM,
        scratch_shapes=list(scratch),
        cost_estimate=pl.CostEstimate(flops=int(1.1e9 * cost), bytes_accessed=0, transcendentals=0),
        compiler_params=pltpu.CompilerParams(vmem_limit_bytes=vmem),
    )(*args, *after)


def add_kernel(left_ref, right_ref, out_ref):
    out_ref[...] = left_ref[...] + right_ref[...]


def gather_kernel(shared_ref, shapes_ref, up_ref, down_ref, ids, buf, sems):
    dims, nodes, _ = buf.shape
    width = shared_ref.shape[1]
    listed = pltpu.make_async_copy(shared_ref, ids, sems.at[dims])
    listed.start()
    loads = [pltpu.make_async_copy(shapes_ref.at[d], buf.at[d], sems.at[d]) for d in range(dims)]
    for load in loads:
        load.start()
    listed.wait()
    node = lax.broadcasted_iota(jnp.int32, (nodes, 2 * width), 0)
    wanted = jnp.concatenate([ids[1:2, :], ids[0:1, :]], axis=1)
    pick = jnp.where(node == wanted, 1.0, 0.0).astype(F32).T.astype(BF16)
    for d in range(dims):
        loads[d].wait()
        got = jnp.dot(pick, buf[d], preferred_element_type=F32).astype(BF16)
        up_ref[d * width : (d + 1) * width, :] = got[:width]
        down_ref[d * width : (d + 1) * width, :] = got[width:]


def stats_kernel(mass_ref, shapes_ref, out_ref, mass_scr, total_scr, buf, sems):
    dims, nodes, block = buf.shape
    loads = [pltpu.make_async_copy(shapes_ref.at[d], buf.at[d], sems.at[d]) for d in range(dims)]
    for load in loads:
        load.start()
    column = jnp.broadcast_to(mass_ref[...], (8, nodes)).T
    mass_scr[...] = jnp.broadcast_to(column[:, 0:1], (nodes, 128))
    for d in range(dims):
        loads[d].wait()
        for at in range(0, block, 128):
            lanes = slice(at, at + 128)
            lever = jnp.zeros((8, 128), F32)
            general = jnp.zeros((8, 128), F32) if d == 0 else total_scr[:, lanes]
            for r in range(0, nodes, 16):
                wide = buf[d, r : r + 16, lanes].astype(F32)
                weighted = wide * mass_scr[r : r + 16, :]
                square = weighted * wide
                lever += weighted[:8] + weighted[8:]
                general += square[:8] + square[8:]
            out_ref[d : d + 1, lanes] = jnp.sum(lever, axis=0, keepdims=True)
            total_scr[:, lanes] = general
    out_ref[dims : dims + 1, :] = jnp.sum(total_scr[...], axis=0, keepdims=True)


def local_kernel(codes_ref, count_ref, recovery_ref, shapes_ref, local_ref, rim_ref, pick_ref, force_ref, got_scr):
    slots, elems = codes_ref.shape
    per_elem, dims = recovery_ref.shape[0], recovery_ref.shape[1]
    nodes, block = shapes_ref.shape[1], shapes_ref.shape[2]
    taken = slots * elems
    span = pick_ref.shape[1]
    node = lax.broadcasted_iota(jnp.int32, (span, elems), 0)
    for s in range(0, slots, 2):
        picks = []
        for q in range(s, min(s + 2, slots)):
            code = jnp.where(q < count_ref[...], codes_ref[q : q + 1, :], -1)
            picks.append(jnp.where(node == code, 1.0, 0.0).astype(F32))
        pick_ref[s * elems : s * elems + len(picks) * elems, :] = (
            jnp.concatenate(picks, axis=1).T.astype(BF16)
        )
    row = lax.broadcasted_iota(jnp.int32, (elems, 2 * elems), 0)
    column = lax.broadcasted_iota(jnp.int32, (elems, 2 * elems), 1)
    same = (column == row) | (column == row + elems)
    for k in range(per_elem):
        for d in range(dims):
            value = recovery_ref[k, d].astype(F32)
            for s in range(0, slots, 2):
                pair = jnp.concatenate([value[s : s + 1], value[s + 1 : s + 2]], axis=1)
                at = (d * slots + s) * elems
                force_ref[k * elems : (k + 1) * elems, at : at + 2 * elems] = jnp.where(
                    same, pair, 0.0
                ).astype(BF16)
    rim = span - nodes
    for d in range(dims):
        rows = slice(d * taken, (d + 1) * taken)
        value = jnp.dot(force_ref[:, rows], pick_ref[:, nodes:], preferred_element_type=F32)
        high = value.astype(BF16)
        rim_ref[:, d * rim : (d + 1) * rim] = high
        rim_ref[:, (dims + d) * rim : (dims + d + 1) * rim] = (value - high.astype(F32)).astype(BF16)
        got = jnp.dot(pick_ref[:, :nodes], shapes_ref[d], preferred_element_type=F32)
        got_scr[rows, :] = got.astype(BF16)
    for c in range(0, block, 256):
        local_ref[:, c : c + 256] = jnp.dot(
            force_ref[...], got_scr[:, c : c + 256], preferred_element_type=F32
        )


def mode_rows(freq, rate):
    alpha = rate * freq
    inverse = 1.0 / jnp.sqrt(alpha)
    return (freq * freq * inverse, inverse, 2.0 * alpha, 2.0 * (freq / rate))


def turn_rows(rows):
    pieces = [rows[:, c : c + 128] for c in range(0, rows.shape[1], 128)]
    while len(pieces) * 8 % 128:
        pieces.append(jnp.zeros((8, 128), F32))
    return [jnp.concatenate(pieces[c : c + 16], axis=0).T for c in range(0, len(pieces), 16)]


def place_modes(freq_ref, rate_ref, row_scr, col_scr, groups, side, block):
    side_rows = []
    for which, group in enumerate(groups):
        lanes = pl.ds(pl.multiple_of(group * block, block), block)
        rows = jnp.concatenate(list(mode_rows(freq_ref[:, lanes], rate_ref[:, lanes])) * 2, axis=0)
        row_scr[which * 8 : which * 8 + 8, :] = rows
        if which == side:
            side_rows.append(rows)
    turned = turn_rows(jnp.concatenate(side_rows, axis=1))
    for t in range(block // 128):
        for q in range(4):
            lane = t % 16 * 8 + q
            col_scr[q, t * 128 : (t + 1) * 128, :] = jnp.broadcast_to(
                turned[t // 16][:, lane : lane + 1], (128, 128)
            )


def fill_rho(row_scr, col_scr, out_ref, out_col, side_row, count, cols_at, col_off, tile):
    step = min(count, 256)
    cols = [
        jnp.broadcast_to(row_scr[cols_at + q : cols_at + q + 1, pl.ds(col_off, tile)], (8, tile))
        for q in range(4)
    ]

    @pl.loop(0, count // step)
    def _(t):
        for k in range(0, step, 8):
            at = pl.multiple_of(t * step, step) + k
            high, low, alpha, zeta = (col_scr[q, pl.ds(side_row + at, 8), :] for q in range(4))
            for c in range(0, tile, 128):
                col = [value[:, c : c + 128] for value in cols]
                spread = high * col[1] - low * col[0]
                pair = alpha + col[2]
                bottom = spread * spread + pair * (zeta + col[3])
                out_ref[pl.ds(at, 8), out_col + c : out_col + c + 128] = pair / bottom


def rho_near_kernel(place_ref, freq_ref, rate_ref, diag_ref, mate_ref, col_scr, row_scr):
    block = diag_ref.shape[0]
    half = block // 2
    tile = block // 4
    own, mate, parity = place_ref[0], place_ref[1], place_ref[3]
    place_modes(freq_ref, rate_ref, row_scr, col_scr, (own, mate), 0, block)
    for j in range(4):
        fill_rho(row_scr, col_scr, diag_ref, j * tile, 0, (j + 1) * tile, 0, j * tile, tile)
    for i in range(2):
        for j in range(2):
            off = pl.multiple_of((i ^ parity) * half + j * tile, tile)
            fill_rho(row_scr, col_scr, mate_ref.at[i], j * tile, i * half, half, 8, off, tile)


def rho_far_kernel(place_ref, freq_ref, rate_ref, own_side_ref, far_ref, col_scr, row_scr):
    block = far_ref.shape[1]
    tile = block // 4
    mate, far = place_ref[1], place_ref[2]
    place_modes(freq_ref, rate_ref, row_scr, col_scr, (mate, far), 0, block)
    for q, side_ref in enumerate((own_side_ref, col_scr)):
        rows = far_ref.at[q * block : (q + 1) * block, :]
        for j in range(4):
            fill_rho(row_scr, side_ref, rows, j * tile, 0, block, 8, j * tile, tile)


def forces_kernel(at, dims, place_ref, rim_ref, low_ref, high_ref, local_ref, all_ref, part_ref, rim_scr):
    comps, chunk = all_ref.shape
    width = low_ref.shape[0] // dims
    part = comps // 2
    other = place_ref[5]
    lanes = slice(at, at + chunk)
    for copy in range(2):
        for d in range(dims):
            base = (copy * dims + d) * 2 * width
            rim_scr[base : base + width, :] = low_ref[d * width : (d + 1) * width, lanes]
            rim_scr[base + width : base + 2 * width, :] = high_ref[d * width : (d + 1) * width, lanes]
    for c in range(0, chunk, 256):
        total = jnp.dot(rim_ref[...], rim_scr[:, c : c + 256], preferred_element_type=F32)
        all_ref[:, c : c + 256] = (local_ref[:, at + c : at + c + 256] + total).astype(BF16)
    part_ref[...] = all_ref[pl.ds(pl.multiple_of(other * part, part), part), :]


def join_kernel(*refs):
    out_ref = refs[-1]
    size = refs[0].shape[0]
    for q, ref in enumerate(refs[:-1]):
        out_ref[q * size : (q + 1) * size, :] = ref[...]


def amps_kernel(place_ref, stats_ref, extra_ref, spectral_ref, freq_ref, rate_ref, *out_refs):
    dims, block = spectral_ref.shape[0], stats_ref.shape[1]
    for q, out_ref in enumerate(out_refs):
        lanes = pl.ds(pl.multiple_of(place_ref[q] * block, block), block)
        rows = slice(q * (dims + 1), (q + 1) * (dims + 1))
        total = stats_ref[rows, :] + extra_ref[rows, :]
        scale = 2.0 * jnp.sqrt(freq_ref[:, lanes] / rate_ref[:, lanes])
        amps = total[:dims] / total[dims : dims + 1] * spectral_ref[:, lanes] * scale
        out_ref[...] = jnp.concatenate([amps, jnp.zeros((8 - dims, block), F32)], axis=0)


def fold(value):
    total = value[:, :128]
    for c in range(128, value.shape[1], 128):
        total = total + value[:, c : c + 128]
    return total


def to_row(acc, turned, per_elem):
    elems = acc.shape[0] // per_elem
    for k in range(per_elem):
        turned[pl.ds(k, elems, stride=per_elem), :] = acc[k * elems : (k + 1) * elems, :]
    ones = jnp.ones((8, acc.shape[1]), F32)
    return lax.dot_general(
        ones, turned[...], (((1,), (1,)), ((), ())),
        precision=lax.Precision.HIGHEST, preferred_element_type=F32,
    )[0:1]


def split(value):
    top = value.astype(BF16).astype(F32)
    rest = value - top
    middle = rest.astype(BF16).astype(F32)
    return top, middle, rest - middle


def side_terms(out_scr, at, amps, dims):
    top, middle, last = split(amps[:dims])
    rows = jnp.concatenate([top, top, middle, middle, top, last], axis=0)
    rows = jnp.concatenate([rows, jnp.zeros((32 - rows.shape[0], rows.shape[1]), F32)], axis=0)
    for c in range(0, amps.shape[1], 512):
        stack = [rows[:, c + q : c + q + 128] for q in range(0, 512, 128)]
        turned = jnp.concatenate(stack, axis=0).T
        for q in range(4):
            out_scr[at + c + q * 128 : at + c + (q + 1) * 128, :] = turned[:, q * 32 : (q + 1) * 32].astype(BF16)


def col_terms(amps, dims, factor):
    top, middle, last = split(amps[:dims] * factor)
    rows = jnp.concatenate([top, middle, top, middle, last, top], axis=0)
    rows = jnp.concatenate([rows, jnp.zeros((32 - rows.shape[0], rows.shape[1]), F32)], axis=0)
    return rows.astype(BF16)


def weigh(rho, side, cols):
    return (rho * jnp.dot(side, cols, preferred_element_type=F32)).astype(BF16)


def near_kernel(dims, chunks, *refs):
    place_ref, own_amps_ref, mate_amps_ref, diag_ref, cross_ref = refs[:5]
    own_refs, mate_refs = refs[5 : 5 + chunks], refs[5 + chunks : 5 + 2 * chunks]
    acc, side_scr, w_scr = refs[5 + 2 * chunks :]
    _, chunk = own_refs[0].shape
    block = diag_ref.shape[0]
    tile = block // 4
    half = block // 2
    parity = place_ref[3]

    def part(parts, at, size):
        return parts[at // chunk][:, at % chunk : at % chunk + size]

    def product(w, at, depth):
        total = None
        for c in range(at, at + depth, min(chunk, depth)):
            size = min(chunk, at + depth - c)
            got = jnp.dot(part(own_refs, c, size), w[c - at : c - at + size, :], preferred_element_type=F32)
            total = got if total is None else total + got
        return total

    side_terms(side_scr, 0, own_amps_ref[...], dims)
    once, twice = (col_terms(own_amps_ref[...], dims, factor) for factor in (1.0, 2.0))
    straight = parity == 0
    turn = 0
    for j in range(4):
        spot = slice(j * tile, (j + 1) * tile)
        for i in range(j + 1):
            rows = slice(i * tile, (i + 1) * tile)
            cols = twice if i < j else once
            w_scr[turn, rows, :] = weigh(diag_ref[rows, spot], side_scr[rows, :], cols[:, spot])
        got = product(w_scr.at[turn], 0, (j + 1) * tile)
        got = fold(got * part(own_refs, j * tile, tile).astype(F32))
        acc[...] = got if j == 0 else acc[...] + got
        turn = 1 - turn
    for i in range(2):
        for j in range(half // tile):
            here, there = i * half + j * tile, (1 - i) * half + j * tile
            cols = jnp.where(
                straight, mate_amps_ref[:, here : here + tile], mate_amps_ref[:, there : there + tile]
            )
            w_scr[turn, :half, :] = weigh(
                cross_ref[i, :, j * tile : (j + 1) * tile],
                side_scr[i * half : (i + 1) * half, :], col_terms(cols, dims, 2.0),
            )
            got = product(w_scr.at[turn], i * half, half)
            other = jnp.where(
                straight, part(mate_refs, here, tile).astype(F32), part(mate_refs, there, tile).astype(F32)
            )
            acc[...] += fold(got * other)
            turn = 1 - turn


def weights_kernel(dims, own_amps_ref, mate_amps_ref, far_amps_ref, rho_ref, out_ref, side_scr):
    block = rho_ref.shape[1]
    tile = block // 4
    side_terms(side_scr, 0, own_amps_ref[...], dims)
    side_terms(side_scr, block, mate_amps_ref[...], dims)
    cols = col_terms(far_amps_ref[...], dims, 2.0)
    for at in range(0, 2 * block, tile):
        rows = slice(at, at + tile)
        for c in range(0, block, tile):
            spot = slice(c, c + tile)
            out_ref[rows, spot] = weigh(rho_ref[rows, spot], side_scr[rows, :], cols[:, spot])


def far_kernel(at, chunks, per_elem, place_ref, near_ref, w_ref, far_ref, *refs):
    own_refs, mate_refs = refs[:chunks], refs[chunks : 2 * chunks]
    if len(refs) == 2 * chunks + 1:
        acc, last = refs[-1], False
    else:
        (out_ref, acc, turned), last = refs[2 * chunks :], True
    comps, chunk = own_refs[0].shape
    block = w_ref.shape[1]
    part = comps // 2
    tile = min(256, chunk)
    here = pl.multiple_of(place_ref[4] * part, part)
    rows = pl.ds(here, part)
    total = near_ref[rows, :]
    for c in range(0, chunk, tile):
        spot = slice(at + c, at + c + tile)
        got = None
        for which, parts in enumerate((own_refs, mate_refs)):
            for q in range(chunks):
                base = which * block + q * chunk
                piece = jnp.dot(
                    parts[q][rows, :], w_ref[base : base + chunk, spot], preferred_element_type=F32
                )
                got = piece if got is None else got + piece
        total = total + fold(got * far_ref[:, c : c + tile].astype(F32))
    acc[...] = near_ref[...]
    acc[rows, :] = total
    if last:
        out_ref[...] = to_row(acc, turned, per_elem)


CHUNKS = 2


def four_groups(*args):
    return combined(*args)


def combined(
    shapes, masses, spectral, frequencies, damping, recovery, connectivity, node_count, shared
):
    dims, nodes, block = shapes.shape
    elems, slots = connectivity.shape
    per_elem = recovery.shape[1]
    comps = elems * per_elem
    part = comps // 2
    width = shared.shape[1]
    parts = lax.axis_size("dom")
    group = lax.axis_index("mode").astype(jnp.int32)
    place = jnp.stack(
        [group, group ^ 1, group ^ 2, group & 1, group >> 1, 1 - (group >> 1)]
    ).astype(jnp.int32)
    sds = jax.ShapeDtypeStruct
    chunk = block // CHUNKS
    ahead = [(i, i + 1) for i in range(parts - 1)]
    back = [(i + 1, i) for i in range(parts - 1)]
    freq = frequencies.reshape(1, -1)
    rate = damping.reshape(1, -1)

    up, down = call(
        gather_kernel, [sds((dims * width, block), BF16)] * 2, (shared, shapes), 2.0, hbm=(0, 1),
        scratch=[
            pltpu.VMEM(shared.shape, jnp.int32), pltpu.VMEM(shapes.shape, BF16),
            pltpu.SemaphoreType.DMA((dims + 1,)),
        ],
        vmem=60 << 20,
    )
    low, high = lax.ppermute(up, "dom", ahead), lax.ppermute(down, "dom", back)
    stats = call(
        stats_kernel, sds((dims + 1, block), F32), (masses.reshape(1, nodes), shapes), 1.5, hbm=(1,),
        scratch=[
            pltpu.VMEM((nodes, 128), F32), pltpu.VMEM((8, block), F32),
            pltpu.VMEM(shapes.shape, BF16), pltpu.SemaphoreType.DMA((dims,)),
        ],
        vmem=60 << 20, after=(up,),
    )
    taken = slots * elems
    local, rim = call(
        local_kernel, (sds((comps, block), F32), sds((comps, 4 * dims * width), BF16)),
        (connectivity.T, node_count.reshape(1, elems), recovery.transpose(1, 3, 2, 0), shapes),
        2.3,
        scratch=[
            pltpu.VMEM((taken, nodes + 2 * width), BF16), pltpu.VMEM((comps, dims * taken), BF16),
            pltpu.VMEM((dims * taken, block), BF16),
        ],
    )
    rho_diag, rho_mate, sides = call(
        rho_near_kernel,
        (sds((block, block), F32), sds((2, block // 2, block // 2), F32), sds((4, block, 128), F32)),
        (place, freq, rate), 3.0, smem=(0,),
        scratch=[pltpu.VMEM((16, block), F32)], after=(rim,),
    )
    rho_far = call(
        rho_far_kernel, sds((2 * block, block), F32), (place, freq, rate, sides),
        4.5, smem=(0,),
        scratch=[pltpu.VMEM((4, block, 128), F32), pltpu.VMEM((16, block), F32)],
    )
    given = [stats] + [lax.ppermute(stats, "mode", [(i, i ^ q) for i in range(4)]) for q in (1, 2)]
    stats = call(join_kernel, sds((3 * (dims + 1), block), F32), given, 0.5)
    first = stats
    order = [1 << q for q in range(1, parts.bit_length() - 1)] + [1]
    if parts & (parts - 1) or parts == 1:
        stats = lax.psum(stats, "dom")
        order = []
    extra = jnp.zeros_like(stats)
    for q, reach in enumerate(order):
        if q:
            stats = call(
                add_kernel, sds(stats.shape, F32), (stats, extra), 0.5, after=(rho_diag,) if q == 1 else ()
            )
            first = stats if q == 1 else first
        extra = lax.ppermute(stats, "dom", [(i, i ^ reach) for i in range(parts)])
    amps, mate_amps, far_amps = call(
        amps_kernel, [sds((8, block), F32)] * 3, (place, stats, extra, spectral, freq, rate), 0.8, smem=(0,)
    )

    own, mate, far = [], [], []
    for c in range(CHUNKS):
        forces, sent = call(
            functools.partial(forces_kernel, c * chunk, dims),
            (sds((comps, chunk), BF16), sds((part, chunk), BF16)),
            (place, rim, low, high, local), 1.4 / CHUNKS, smem=(0,),
            scratch=[pltpu.VMEM((4 * dims * width, chunk), BF16)], after=(own[-1] if own else first,),
        )
        own.append(forces)
        far.append(lax.ppermute(sent, "mode", [(i, i ^ 2) for i in range(4)]))
        mate.append(lax.ppermute(forces, "mode", [(i, i ^ 1) for i in range(4)]))
    near = call(
        functools.partial(near_kernel, dims, CHUNKS), sds((comps, 128), F32),
        (place, amps, mate_amps, rho_diag, rho_mate, *own, *mate),
        3.4, smem=(0,),
        scratch=[pltpu.VMEM((block, 32), BF16), pltpu.VMEM((2, block, block // 4), BF16)],
    )
    weights = call(
        functools.partial(weights_kernel, dims), sds((2 * block, block), BF16),
        (amps, mate_amps, far_amps, rho_far), 3.3,
        scratch=[pltpu.VMEM((2 * block, 32), BF16)],
    )
    value = near
    for c in range(CHUNKS):
        last = c == CHUNKS - 1
        value = call(
            functools.partial(far_kernel, c * chunk, CHUNKS, per_elem),
            sds((1, comps) if last else (comps, 128), F32),
            (place, value, weights, far[c], *own, *mate), 2.1 / CHUNKS,
            smem=(0,), scratch=[pltpu.VMEM((comps, 128), F32)] * 2 if last else (),
        )
    value = value.reshape(comps)
    for reach in (1, 2):
        value = value + lax.ppermute(value, "mode", [(i, i ^ reach) for i in range(4)])
    return value


def extended_2(block, sides, width):
    for axis, dim in sides:
        count = lax.axis_size(axis)
        forward = [(i, i + 1) for i in range(count - 1)]
        backward = [(target, source) for source, target in forward]
        low = lax.ppermute(
            lax.slice_in_dim(block, block.shape[dim] - width, None, axis=dim), axis, forward
        )
        high = lax.ppermute(lax.slice_in_dim(block, 0, width, axis=dim), axis, backward)
        block = jnp.concatenate([low, block, high], axis=dim)
    return block


def shifted(value, axis, steps):
    count = lax.axis_size(axis)
    pairs = [(source, (source + steps) % count) for source in range(count)]
    return lax.ppermute(value, axis, pairs)


def correlation_block(freq_rows, freq_cols, rate_rows, rate_cols):
    ratio = freq_cols[None, :] / freq_rows[:, None]
    ratio_sq = ratio * ratio
    rate_row = rate_rows[:, None]
    rate_col = rate_cols[None, :]
    top_part = (
        8.0
        * jnp.sqrt(rate_row * rate_col)
        * (rate_row + ratio * rate_col)
        * ratio
        * jnp.sqrt(ratio)
    )
    spread = 1.0 - ratio_sq
    bottom_part = (
        spread * spread
        + 4.0 * rate_row * rate_col * ratio * (1.0 + ratio_sq)
        + 4.0 * (rate_row * rate_row + rate_col * rate_col) * ratio_sq
    )
    return top_part / bottom_part


def block_terms(own_forces, own_start, far_forces, far_start, amplitudes, frequencies, damping):
    row_count = own_forces.shape[1]
    col_count = far_forces.shape[1]
    freq_rows = lax.dynamic_slice_in_dim(frequencies, own_start, row_count)
    freq_cols = lax.dynamic_slice_in_dim(frequencies, far_start, col_count)
    rate_rows = lax.dynamic_slice_in_dim(damping, own_start, row_count)
    rate_cols = lax.dynamic_slice_in_dim(damping, far_start, col_count)
    correlation = correlation_block(freq_rows, freq_cols, rate_rows, rate_cols)
    amp_rows = lax.dynamic_slice_in_dim(amplitudes, own_start, row_count, 1)
    amp_cols = lax.dynamic_slice_in_dim(amplitudes, far_start, col_count, 1)
    weights = (amp_rows.T[:, :, None] * correlation[:, None, :] * amp_cols[None, :, :]).astype(
        jnp.bfloat16
    )
    weights = weights.reshape(row_count, 3 * col_count)
    projected = jnp.dot(own_forces, weights, preferred_element_type=jnp.float32)
    projected = projected.reshape(own_forces.shape[0], 3, col_count)
    far_wide = far_forces.astype(jnp.float32)
    return jnp.sum(projected * far_wide[:, None, :], axis=(1, 2))


def any_groups(
    shapes, masses, spectral, frequencies, damping, recovery, connectivity, node_count, shared
):
    rim_width = shared.shape[1]
    block_width = shapes.shape[2]
    elem_count = connectivity.shape[0]
    slot_count = connectivity.shape[1]
    mode_index = lax.axis_index("mode")
    own_start = mode_index * block_width
    shape_wide = shapes.astype(jnp.float32)
    weighted = masses[None, :, None] * shape_wide
    lever_arm = jnp.sum(weighted, axis=1)
    general = jnp.sum(weighted * shape_wide, axis=(0, 1))
    lever_sum, general_sum = lax.psum((lever_arm, general), "dom")
    own_spectral = lax.dynamic_slice_in_dim(spectral, own_start, block_width, 1)
    local_amps = lever_sum / general_sum[None, :] * own_spectral
    amplitudes = lax.all_gather(local_amps, "mode", axis=1, tiled=True)
    outgoing = jnp.concatenate(
        [jnp.take(shapes, shared[0], axis=1), jnp.take(shapes, shared[1], axis=1)], axis=1
    )
    extended = extended_2(outgoing, (("dom", 1),), rim_width)
    node_table = jnp.concatenate(
        [shapes, extended[:, :rim_width], extended[:, 3 * rim_width :]], axis=1
    )
    gathered = jnp.take(node_table, connectivity.reshape(-1), axis=1).reshape(
        3, elem_count, slot_count, block_width
    )
    slot_live = (jnp.arange(slot_count)[None, :] < node_count[:, None]).astype(jnp.bfloat16)
    masked = recovery * slot_live[:, None, :, None]
    forces = jnp.einsum("ekna,aenm->ekm", masked, gathered, preferred_element_type=jnp.float32)
    forces = forces.astype(jnp.bfloat16).reshape(elem_count * recovery.shape[1], block_width)
    groups = lax.axis_size("mode")
    half_count = groups // 2
    partial_value = block_terms(
        forces, own_start, forces, own_start, amplitudes, frequencies, damping
    )

    def advance(turn_index, carried):
        incoming, summed = carried
        incoming = shifted(incoming, "mode", 1)
        source = (mode_index - turn_index) % groups * block_width
        factor = jnp.where(turn_index == half_count, jnp.float32(1.0), jnp.float32(2.0))
        summed = summed + factor * block_terms(
            forces, own_start, incoming, source, amplitudes, frequencies, damping
        )
        return (incoming, summed)

    carried = lax.fori_loop(1, half_count + 1, advance, (forces, partial_value))
    partial_value = carried[1]
    return lax.psum(partial_value, "mode")


def solution(mesh):
    in_specs = (
        P(None, "dom", "mode"),
        P("dom"),
        P(),
        P(),
        P(),
        P("dom", None, None, None),
        P("dom", None),
        P("dom"),
        P(None, "dom"),
    )
    out_specs = P("dom")
    special = mesh.shape["mode"] == 4
    step = four_groups if special else any_groups
    step = jax.shard_map(
        step, mesh=mesh, in_specs=in_specs, out_specs=out_specs, check_vma=False
    )
    return step
```

```python
import functools
import jax
import jax.numpy as jnp
from jax import lax
from jax.experimental import pallas as pl
from jax.experimental.pallas import tpu as pltpu
from jax.sharding import PartitionSpec as P


F32 = jnp.float32
BF16 = jnp.bfloat16
VMEM = pl.BlockSpec(memory_space=pltpu.VMEM)
HBM = pl.BlockSpec(memory_space=pltpu.HBM)
ANY = pl.BlockSpec(memory_space=pl.ANY)
SMEM = pl.BlockSpec(memory_space=pltpu.SMEM)


def call(kernel, out_shape, args, cost, smem=(), hbm=(), scratch=(), vmem=14 << 20, after=()):
    count = len(args)
    specs = [SMEM if i in smem else HBM if i in hbm else VMEM for i in range(count)]
    specs += [ANY] * len(after)
    many = isinstance(out_shape, (tuple, list))

    def body(*refs):
        kernel(*refs[:count], *refs[count + len(after) :])

    return pl.pallas_call(
        body,
        out_shape=out_shape,
        in_specs=specs,
        out_specs=[VMEM] * len(out_shape) if many else VMEM,
        scratch_shapes=list(scratch),
        cost_estimate=pl.CostEstimate(flops=int(1.1e9 * cost), bytes_accessed=0, transcendentals=0),
        compiler_params=pltpu.CompilerParams(vmem_limit_bytes=vmem),
    )(*args, *after)


def add_kernel(left_ref, right_ref, out_ref):
    out_ref[...] = left_ref[...] + right_ref[...]


def gather_kernel(shared_ref, shapes_ref, up_ref, down_ref, held_ref, sem):
    dims, nodes, _ = held_ref.shape
    width = shared_ref.shape[1]
    load = pltpu.make_async_copy(shapes_ref, held_ref, sem)
    load.start()
    node = lax.broadcasted_iota(jnp.int32, (nodes, 2 * width), 0)
    wanted = jnp.concatenate([shared_ref[1:2, :], shared_ref[0:1, :]], axis=1)
    pick = jnp.where(node == wanted, 1.0, 0.0).astype(F32).T.astype(BF16)
    load.wait()
    for d in range(dims):
        got = jnp.dot(pick, held_ref[d], preferred_element_type=F32).astype(BF16)
        up_ref[d * width : (d + 1) * width, :] = got[:width]
        down_ref[d * width : (d + 1) * width, :] = got[width:]


def stats_kernel(mass_ref, shapes_ref, out_ref, mass_scr):
    dims, nodes, block = shapes_ref.shape
    column = jnp.broadcast_to(mass_ref[...], (8, nodes)).T
    mass_scr[...] = jnp.broadcast_to(column[:, 0:1], (nodes, 128))
    for at in range(0, block, 128):
        lanes = slice(at, at + 128)
        general = jnp.zeros((8, 128), F32)
        for d in range(dims):
            lever = jnp.zeros((8, 128), F32)
            for r in range(0, nodes, 16):
                wide = shapes_ref[d, r : r + 16, lanes].astype(F32)
                weighted = wide * mass_scr[r : r + 16, :]
                square = weighted * wide
                lever += weighted[:8] + weighted[8:]
                general += square[:8] + square[8:]
            out_ref[d : d + 1, lanes] = jnp.sum(lever, axis=0, keepdims=True)
        out_ref[dims : dims + 1, lanes] = jnp.sum(general, axis=0, keepdims=True)


def local_kernel(codes_ref, count_ref, recovery_ref, shapes_ref, local_ref, rim_ref, pick_ref, force_ref, got_scr):
    slots, elems = codes_ref.shape
    per_elem, dims = recovery_ref.shape[0], recovery_ref.shape[1]
    nodes, block = shapes_ref.shape[1], shapes_ref.shape[2]
    taken = slots * elems
    span = pick_ref.shape[1]
    node = lax.broadcasted_iota(jnp.int32, (span, elems), 0)
    for s in range(0, slots, 2):
        picks = []
        for q in range(s, min(s + 2, slots)):
            code = jnp.where(q < count_ref[...], codes_ref[q : q + 1, :], -1)
            picks.append(jnp.where(node == code, 1.0, 0.0).astype(F32))
        pick_ref[s * elems : s * elems + len(picks) * elems, :] = (
            jnp.concatenate(picks, axis=1).T.astype(BF16)
        )
    row = lax.broadcasted_iota(jnp.int32, (elems, 2 * elems), 0)
    column = lax.broadcasted_iota(jnp.int32, (elems, 2 * elems), 1)
    same = (column == row) | (column == row + elems)
    for k in range(per_elem):
        for d in range(dims):
            value = recovery_ref[k, d].astype(F32)
            for s in range(0, slots, 2):
                pair = jnp.concatenate([value[s : s + 1], value[s + 1 : s + 2]], axis=1)
                at = (d * slots + s) * elems
                force_ref[k * elems : (k + 1) * elems, at : at + 2 * elems] = jnp.where(
                    same, pair, 0.0
                ).astype(BF16)
    rim = span - nodes
    for d in range(dims):
        rows = slice(d * taken, (d + 1) * taken)
        value = jnp.dot(force_ref[:, rows], pick_ref[:, nodes:], preferred_element_type=F32)
        high = value.astype(BF16)
        rim_ref[:, d * rim : (d + 1) * rim] = high
        rim_ref[:, (dims + d) * rim : (dims + d + 1) * rim] = (value - high.astype(F32)).astype(BF16)
        got = jnp.dot(pick_ref[:, :nodes], shapes_ref[d], preferred_element_type=F32)
        got_scr[rows, :] = got.astype(BF16)
    for c in range(0, block, 256):
        local_ref[:, c : c + 256] = jnp.dot(
            force_ref[...], got_scr[:, c : c + 256], preferred_element_type=F32
        )


def mode_rows(freq, rate):
    alpha = rate * freq
    inverse = 1.0 / jnp.sqrt(alpha)
    return (freq * freq * inverse, inverse, 2.0 * alpha, 2.0 * (freq / rate))


def turn_rows(rows):
    pieces = [rows[:, c : c + 128] for c in range(0, rows.shape[1], 128)]
    while len(pieces) * 8 % 128:
        pieces.append(jnp.zeros((8, 128), F32))
    return [jnp.concatenate(pieces[c : c + 16], axis=0).T for c in range(0, len(pieces), 16)]


def place_modes(freq_ref, rate_ref, row_scr, col_scr, groups, side, block):
    side_rows = []
    for which, group in enumerate(groups):
        lanes = pl.ds(pl.multiple_of(group * block, block), block)
        rows = jnp.concatenate(list(mode_rows(freq_ref[:, lanes], rate_ref[:, lanes])) * 2, axis=0)
        row_scr[which * 8 : which * 8 + 8, :] = rows
        if which == side:
            side_rows.append(rows)
    if side is None:
        return
    turned = turn_rows(jnp.concatenate(side_rows, axis=1))
    for t in range(block // 128):
        for q in range(4):
            lane = t % 16 * 8 + q
            col_scr[q, t * 128 : (t + 1) * 128, :] = jnp.broadcast_to(
                turned[t // 16][:, lane : lane + 1], (128, 128)
            )


def fill_rho(row_scr, col_scr, out_ref, out_col, side_row, count, cols_at, col_off, tile):
    step = min(count, 256)
    cols = [
        jnp.broadcast_to(row_scr[cols_at + q : cols_at + q + 1, pl.ds(col_off, tile)], (8, tile))
        for q in range(4)
    ]

    @pl.loop(0, count // step)
    def _(t):
        for k in range(0, step, 8):
            at = pl.multiple_of(t * step, step) + k
            high, low, alpha, zeta = (col_scr[q, pl.ds(side_row + at, 8), :] for q in range(4))
            for c in range(0, tile, 128):
                col = [value[:, c : c + 128] for value in cols]
                spread = high * col[1] - low * col[0]
                pair = alpha + col[2]
                bottom = spread * spread + pair * (zeta + col[3])
                out_ref[pl.ds(at, 8), out_col + c : out_col + c + 128] = pair / bottom


def rho_near_kernel(place_ref, freq_ref, rate_ref, diag_ref, mate_ref, col_scr, row_scr):
    block = diag_ref.shape[0]
    half = block // 2
    tile = block // 4
    own, mate, parity = place_ref[0], place_ref[1], place_ref[3]
    place_modes(freq_ref, rate_ref, row_scr, col_scr, (own, mate), 0, block)
    for j in range(4):
        fill_rho(row_scr, col_scr, diag_ref, j * tile, 0, (j + 1) * tile, 0, j * tile, tile)
    for i in range(2):
        for j in range(2):
            off = pl.multiple_of((i ^ parity) * half + j * tile, tile)
            fill_rho(row_scr, col_scr, mate_ref.at[i], j * tile, i * half, half, 8, off, tile)


def rho_own_kernel(place_ref, freq_ref, rate_ref, side_ref, out_ref, row_scr):
    block = out_ref.shape[0]
    tile = block // 4
    place_modes(freq_ref, rate_ref, row_scr, None, (place_ref[2],), None, block)
    for j in range(4):
        fill_rho(row_scr, side_ref, out_ref, j * tile, 0, block, 0, j * tile, tile)


def rho_mate_kernel(place_ref, freq_ref, rate_ref, out_ref, col_scr, row_scr):
    block = out_ref.shape[0]
    tile = block // 4
    place_modes(freq_ref, rate_ref, row_scr, col_scr, (place_ref[1], place_ref[2]), 0, block)
    for j in range(4):
        fill_rho(row_scr, col_scr, out_ref, j * tile, 0, block, 8, j * tile, tile)


def forces_kernel(at, dims, place_ref, rim_ref, low_ref, high_ref, local_ref, all_ref, part_ref, rim_scr):
    comps, chunk = all_ref.shape
    width = low_ref.shape[0] // dims
    part = comps // 2
    other = place_ref[5]
    lanes = slice(at, at + chunk)
    for copy in range(2):
        for d in range(dims):
            base = (copy * dims + d) * 2 * width
            rim_scr[base : base + width, :] = low_ref[d * width : (d + 1) * width, lanes]
            rim_scr[base + width : base + 2 * width, :] = high_ref[d * width : (d + 1) * width, lanes]
    for c in range(0, chunk, 256):
        total = jnp.dot(rim_ref[...], rim_scr[:, c : c + 256], preferred_element_type=F32)
        all_ref[:, c : c + 256] = (local_ref[:, at + c : at + c + 256] + total).astype(BF16)
    part_ref[...] = all_ref[pl.ds(pl.multiple_of(other * part, part), part), :]


def join_kernel(*refs):
    out_ref = refs[-1]
    size = refs[0].shape[0]
    for q, ref in enumerate(refs[:-1]):
        out_ref[q * size : (q + 1) * size, :] = ref[...]


def amps_kernel(place_ref, stats_ref, extra_ref, spectral_ref, freq_ref, rate_ref, *out_refs):
    dims, block = spectral_ref.shape[0], stats_ref.shape[1]
    for q, out_ref in enumerate(out_refs):
        lanes = pl.ds(pl.multiple_of(place_ref[q] * block, block), block)
        rows = slice(q * (dims + 1), (q + 1) * (dims + 1))
        total = stats_ref[rows, :] + extra_ref[rows, :]
        scale = 2.0 * jnp.sqrt(freq_ref[:, lanes] / rate_ref[:, lanes])
        amps = total[:dims] / total[dims : dims + 1] * spectral_ref[:, lanes] * scale
        out_ref[...] = jnp.concatenate([amps, jnp.zeros((8 - dims, block), F32)], axis=0)


def fold(value):
    total = value[:, :128]
    for c in range(128, value.shape[1], 128):
        total = total + value[:, c : c + 128]
    return total


def to_row(acc, turned, per_elem):
    elems = acc.shape[0] // per_elem
    for k in range(per_elem):
        turned[pl.ds(k, elems, stride=per_elem), :] = acc[k * elems : (k + 1) * elems, :]
    ones = jnp.ones((8, acc.shape[1]), F32)
    return lax.dot_general(
        ones, turned[...], (((1,), (1,)), ((), ())),
        precision=lax.Precision.HIGHEST, preferred_element_type=F32,
    )[0:1]


def split(value):
    top = value.astype(BF16).astype(F32)
    rest = value - top
    middle = rest.astype(BF16).astype(F32)
    return top, middle, rest - middle


def side_terms(out_scr, at, amps, dims):
    top, middle, last = split(amps[:dims])
    rows = jnp.concatenate([top, top, middle, middle, top, last], axis=0)
    rows = jnp.concatenate([rows, jnp.zeros((32 - rows.shape[0], rows.shape[1]), F32)], axis=0)
    for c in range(0, amps.shape[1], 512):
        stack = [rows[:, c + q : c + q + 128] for q in range(0, 512, 128)]
        turned = jnp.concatenate(stack, axis=0).T
        for q in range(4):
            out_scr[at + c + q * 128 : at + c + (q + 1) * 128, :] = turned[:, q * 32 : (q + 1) * 32].astype(BF16)


def col_terms(amps, dims, factor):
    top, middle, last = split(amps[:dims] * factor)
    rows = jnp.concatenate([top, middle, top, middle, last, top], axis=0)
    rows = jnp.concatenate([rows, jnp.zeros((32 - rows.shape[0], rows.shape[1]), F32)], axis=0)
    return rows.astype(BF16)


def weigh(rho, side, cols):
    return (rho * jnp.dot(side, cols, preferred_element_type=F32)).astype(BF16)


def near_kernel(dims, chunks, *refs):
    place_ref, own_amps_ref, mate_amps_ref, diag_ref, cross_ref = refs[:5]
    own_refs, mate_refs = refs[5 : 5 + chunks], refs[5 + chunks : 5 + 2 * chunks]
    acc, side_scr, w_scr = refs[5 + 2 * chunks :]
    _, chunk = own_refs[0].shape
    block = diag_ref.shape[0]
    tile = block // 4
    half = block // 2
    parity = place_ref[3]

    def part(parts, at, size):
        return parts[at // chunk][:, at % chunk : at % chunk + size]

    def product(w, at, depth):
        total = None
        for c in range(at, at + depth, min(chunk, depth)):
            size = min(chunk, at + depth - c)
            got = jnp.dot(part(own_refs, c, size), w[c - at : c - at + size, :], preferred_element_type=F32)
            total = got if total is None else total + got
        return total

    side_terms(side_scr, 0, own_amps_ref[...], dims)
    once, twice = (col_terms(own_amps_ref[...], dims, factor) for factor in (1.0, 2.0))
    straight = parity == 0
    turn = 0
    for j in range(4):
        spot = slice(j * tile, (j + 1) * tile)
        for i in range(j + 1):
            rows = slice(i * tile, (i + 1) * tile)
            cols = twice if i < j else once
            w_scr[turn, rows, :] = weigh(diag_ref[rows, spot], side_scr[rows, :], cols[:, spot])
        got = product(w_scr.at[turn], 0, (j + 1) * tile)
        got = fold(got * part(own_refs, j * tile, tile).astype(F32))
        acc[...] = got if j == 0 else acc[...] + got
        turn = 1 - turn
    for i in range(2):
        for j in range(half // tile):
            here, there = i * half + j * tile, (1 - i) * half + j * tile
            cols = jnp.where(
                straight, mate_amps_ref[:, here : here + tile], mate_amps_ref[:, there : there + tile]
            )
            w_scr[turn, :half, :] = weigh(
                cross_ref[i, :, j * tile : (j + 1) * tile],
                side_scr[i * half : (i + 1) * half, :], col_terms(cols, dims, 2.0),
            )
            got = product(w_scr.at[turn], i * half, half)
            other = jnp.where(
                straight, part(mate_refs, here, tile).astype(F32), part(mate_refs, there, tile).astype(F32)
            )
            acc[...] += fold(got * other)
            turn = 1 - turn


def weights_kernel(dims, own_amps_ref, mate_amps_ref, far_amps_ref, own_ref, mate_ref, out_ref, side_scr):
    block = own_ref.shape[1]
    tile = block // 4
    cols = col_terms(far_amps_ref[...], dims, 2.0)
    for q, (amps_ref, rho_ref) in enumerate(((own_amps_ref, own_ref), (mate_amps_ref, mate_ref))):
        side_terms(side_scr, q * block, amps_ref[...], dims)
        for at in range(0, block, tile):
            base = q * block + at
            for c in range(0, block, tile):
                spot = slice(c, c + tile)
                out_ref[base : base + tile, spot] = weigh(
                    rho_ref[at : at + tile, spot], side_scr[base : base + tile, :], cols[:, spot]
                )


def far_kernel(at, chunks, per_elem, place_ref, near_ref, w_ref, far_ref, *refs):
    own_refs, mate_refs = refs[:chunks], refs[chunks : 2 * chunks]
    if len(refs) == 2 * chunks + 1:
        acc, last = refs[-1], False
    else:
        (out_ref, acc, turned), last = refs[2 * chunks :], True
    comps, chunk = own_refs[0].shape
    block = w_ref.shape[1]
    part = comps // 2
    tile = min(256, chunk)
    here = pl.multiple_of(place_ref[4] * part, part)
    rows = pl.ds(here, part)
    total = near_ref[rows, :]
    for c in range(0, chunk, tile):
        spot = slice(at + c, at + c + tile)
        got = None
        for which, parts in enumerate((own_refs, mate_refs)):
            for q in range(chunks):
                base = which * block + q * chunk
                piece = jnp.dot(
                    parts[q][rows, :], w_ref[base : base + chunk, spot], preferred_element_type=F32
                )
                got = piece if got is None else got + piece
        total = total + fold(got * far_ref[:, c : c + tile].astype(F32))
    acc[...] = near_ref[...]
    acc[rows, :] = total
    if last:
        out_ref[...] = to_row(acc, turned, per_elem)


CHUNKS = 1


def four_groups(*args):
    return combined(*args)


def combined(
    shapes, masses, spectral, frequencies, damping, recovery, connectivity, node_count, shared
):
    dims, nodes, block = shapes.shape
    elems, slots = connectivity.shape
    per_elem = recovery.shape[1]
    comps = elems * per_elem
    part = comps // 2
    width = shared.shape[1]
    parts = lax.axis_size("dom")
    group = lax.axis_index("mode").astype(jnp.int32)
    place = jnp.stack(
        [group, group ^ 1, group ^ 2, group & 1, group >> 1, 1 - (group >> 1)]
    ).astype(jnp.int32)
    sds = jax.ShapeDtypeStruct
    chunk = block // CHUNKS
    ahead = [(i, i + 1) for i in range(parts - 1)]
    back = [(i + 1, i) for i in range(parts - 1)]
    freq = frequencies.reshape(1, -1)
    rate = damping.reshape(1, -1)

    up, down, held = call(
        gather_kernel, [sds((dims * width, block), BF16)] * 2 + [sds(shapes.shape, BF16)], (shared, shapes),
        2.0, hbm=(1,), scratch=[pltpu.SemaphoreType.DMA],
    )
    low, high = lax.ppermute(up, "dom", ahead), lax.ppermute(down, "dom", back)
    stats = call(
        stats_kernel, sds((dims + 1, block), F32), (masses.reshape(1, nodes), held), 0.8,
        scratch=[pltpu.VMEM((nodes, 128), F32)],
    )
    rho_diag, rho_mate, sides = call(
        rho_near_kernel,
        (sds((block, block), F32), sds((2, block // 2, block // 2), F32), sds((4, block, 128), F32)),
        (place, freq, rate), 3.0, smem=(0,),
        scratch=[pltpu.VMEM((16, block), F32)], after=(stats,),
    )
    far_own = call(
        rho_own_kernel, sds((block, block), F32), (place, freq, rate, sides), 1.9, smem=(0,),
        scratch=[pltpu.VMEM((8, block), F32)],
    )
    taken = slots * elems
    local, rim = call(
        local_kernel, (sds((comps, block), F32), sds((comps, 4 * dims * width), BF16)),
        (connectivity.T, node_count.reshape(1, elems), recovery.transpose(1, 3, 2, 0), held),
        1.8, after=(far_own,),
        scratch=[
            pltpu.VMEM((taken, nodes + 2 * width), BF16), pltpu.VMEM((comps, dims * taken), BF16),
            pltpu.VMEM((dims * taken, block), BF16),
        ],
    )
    far_mate = call(
        rho_mate_kernel, sds((block, block), F32), (place, freq, rate), 2.5, smem=(0,),
        scratch=[pltpu.VMEM((4, block, 128), F32), pltpu.VMEM((16, block), F32)],
    )
    given = [stats] + [lax.ppermute(stats, "mode", [(i, i ^ q) for i in range(4)]) for q in (1, 2)]
    stats = call(join_kernel, sds((3 * (dims + 1), block), F32), given, 0.5)
    first = stats
    order = [1 << q for q in range(1, parts.bit_length() - 1)] + [1]
    if parts & (parts - 1) or parts == 1:
        stats = lax.psum(stats, "dom")
        order = []
    extra = jnp.zeros_like(stats)
    for q, reach in enumerate(order):
        if q:
            stats = call(
                add_kernel, sds(stats.shape, F32), (stats, extra), 0.5, after=(rim,) if q == 1 else ()
            )
            first = stats if q == 1 else first
        extra = lax.ppermute(stats, "dom", [(i, i ^ reach) for i in range(parts)])
    amps, mate_amps, far_amps = call(
        amps_kernel, [sds((8, block), F32)] * 3, (place, stats, extra, spectral, freq, rate), 0.8, smem=(0,)
    )

    own, mate, far = [], [], []
    for c in range(CHUNKS):
        forces, sent = call(
            functools.partial(forces_kernel, c * chunk, dims),
            (sds((comps, chunk), BF16), sds((part, chunk), BF16)),
            (place, rim, low, high, local), 1.4 / CHUNKS, smem=(0,),
            scratch=[pltpu.VMEM((4 * dims * width, chunk), BF16)], after=(own[-1] if own else first,),
        )
        own.append(forces)
        far.append(lax.ppermute(sent, "mode", [(i, i ^ 2) for i in range(4)]))
        mate.append(lax.ppermute(forces, "mode", [(i, i ^ 1) for i in range(4)]))
    near = call(
        functools.partial(near_kernel, dims, CHUNKS), sds((comps, 128), F32),
        (place, amps, mate_amps, rho_diag, rho_mate, *own, *mate),
        3.4, smem=(0,),
        scratch=[pltpu.VMEM((block, 32), BF16), pltpu.VMEM((2, block, block // 4), BF16)],
    )
    weights = call(
        functools.partial(weights_kernel, dims), sds((2 * block, block), BF16),
        (amps, mate_amps, far_amps, far_own, far_mate), 1.4,
        scratch=[pltpu.VMEM((2 * block, 32), BF16)],
    )
    value = near
    for c in range(CHUNKS):
        last = c == CHUNKS - 1
        value = call(
            functools.partial(far_kernel, c * chunk, CHUNKS, per_elem),
            sds((1, comps) if last else (comps, 128), F32),
            (place, value, weights, far[c], *own, *mate), 2.1 / CHUNKS,
            smem=(0,), scratch=[pltpu.VMEM((comps, 128), F32)] * 2 if last else (),
        )
    value = value.reshape(comps)
    for reach in (1, 2):
        value = value + lax.ppermute(value, "mode", [(i, i ^ reach) for i in range(4)])
    return value


def extended_2(block, sides, width):
    for axis, dim in sides:
        count = lax.axis_size(axis)
        forward = [(i, i + 1) for i in range(count - 1)]
        backward = [(target, source) for source, target in forward]
        low = lax.ppermute(
            lax.slice_in_dim(block, block.shape[dim] - width, None, axis=dim), axis, forward
        )
        high = lax.ppermute(lax.slice_in_dim(block, 0, width, axis=dim), axis, backward)
        block = jnp.concatenate([low, block, high], axis=dim)
    return block


def shifted(value, axis, steps):
    count = lax.axis_size(axis)
    pairs = [(source, (source + steps) % count) for source in range(count)]
    return lax.ppermute(value, axis, pairs)


def correlation_block(freq_rows, freq_cols, rate_rows, rate_cols):
    ratio = freq_cols[None, :] / freq_rows[:, None]
    ratio_sq = ratio * ratio
    rate_row = rate_rows[:, None]
    rate_col = rate_cols[None, :]
    top_part = (
        8.0
        * jnp.sqrt(rate_row * rate_col)
        * (rate_row + ratio * rate_col)
        * ratio
        * jnp.sqrt(ratio)
    )
    spread = 1.0 - ratio_sq
    bottom_part = (
        spread * spread
        + 4.0 * rate_row * rate_col * ratio * (1.0 + ratio_sq)
        + 4.0 * (rate_row * rate_row + rate_col * rate_col) * ratio_sq
    )
    return top_part / bottom_part


def block_terms(own_forces, own_start, far_forces, far_start, amplitudes, frequencies, damping):
    row_count = own_forces.shape[1]
    col_count = far_forces.shape[1]
    freq_rows = lax.dynamic_slice_in_dim(frequencies, own_start, row_count)
    freq_cols = lax.dynamic_slice_in_dim(frequencies, far_start, col_count)
    rate_rows = lax.dynamic_slice_in_dim(damping, own_start, row_count)
    rate_cols = lax.dynamic_slice_in_dim(damping, far_start, col_count)
    correlation = correlation_block(freq_rows, freq_cols, rate_rows, rate_cols)
    amp_rows = lax.dynamic_slice_in_dim(amplitudes, own_start, row_count, 1)
    amp_cols = lax.dynamic_slice_in_dim(amplitudes, far_start, col_count, 1)
    weights = (amp_rows.T[:, :, None] * correlation[:, None, :] * amp_cols[None, :, :]).astype(
        jnp.bfloat16
    )
    weights = weights.reshape(row_count, 3 * col_count)
    projected = jnp.dot(own_forces, weights, preferred_element_type=jnp.float32)
    projected = projected.reshape(own_forces.shape[0], 3, col_count)
    far_wide = far_forces.astype(jnp.float32)
    return jnp.sum(projected * far_wide[:, None, :], axis=(1, 2))


def any_groups(
    shapes, masses, spectral, frequencies, damping, recovery, connectivity, node_count, shared
):
    rim_width = shared.shape[1]
    block_width = shapes.shape[2]
    elem_count = connectivity.shape[0]
    slot_count = connectivity.shape[1]
    mode_index = lax.axis_index("mode")
    own_start = mode_index * block_width
    shape_wide = shapes.astype(jnp.float32)
    weighted = masses[None, :, None] * shape_wide
    lever_arm = jnp.sum(weighted, axis=1)
    general = jnp.sum(weighted * shape_wide, axis=(0, 1))
    lever_sum, general_sum = lax.psum((lever_arm, general), "dom")
    own_spectral = lax.dynamic_slice_in_dim(spectral, own_start, block_width, 1)
    local_amps = lever_sum / general_sum[None, :] * own_spectral
    amplitudes = lax.all_gather(local_amps, "mode", axis=1, tiled=True)
    outgoing = jnp.concatenate(
        [jnp.take(shapes, shared[0], axis=1), jnp.take(shapes, shared[1], axis=1)], axis=1
    )
    extended = extended_2(outgoing, (("dom", 1),), rim_width)
    node_table = jnp.concatenate(
        [shapes, extended[:, :rim_width], extended[:, 3 * rim_width :]], axis=1
    )
    gathered = jnp.take(node_table, connectivity.reshape(-1), axis=1).reshape(
        3, elem_count, slot_count, block_width
    )
    slot_live = (jnp.arange(slot_count)[None, :] < node_count[:, None]).astype(jnp.bfloat16)
    masked = recovery * slot_live[:, None, :, None]
    forces = jnp.einsum("ekna,aenm->ekm", masked, gathered, preferred_element_type=jnp.float32)
    forces = forces.astype(jnp.bfloat16).reshape(elem_count * recovery.shape[1], block_width)
    groups = lax.axis_size("mode")
    half_count = groups // 2
    partial_value = block_terms(
        forces, own_start, forces, own_start, amplitudes, frequencies, damping
    )

    def advance(turn_index, carried):
        incoming, summed = carried
        incoming = shifted(incoming, "mode", 1)
        source = (mode_index - turn_index) % groups * block_width
        factor = jnp.where(turn_index == half_count, jnp.float32(1.0), jnp.float32(2.0))
        summed = summed + factor * block_terms(
            forces, own_start, incoming, source, amplitudes, frequencies, damping
        )
        return (incoming, summed)

    carried = lax.fori_loop(1, half_count + 1, advance, (forces, partial_value))
    partial_value = carried[1]
    return lax.psum(partial_value, "mode")


def solution(mesh):
    in_specs = (
        P(None, "dom", "mode"),
        P("dom"),
        P(),
        P(),
        P(),
        P("dom", None, None, None),
        P("dom", None),
        P("dom"),
        P(None, "dom"),
    )
    out_specs = P("dom")
    special = mesh.shape["mode"] == 4
    step = four_groups if special else any_groups
    step = jax.shard_map(
        step, mesh=mesh, in_specs=in_specs, out_specs=out_specs, check_vma=False
    )
    return step
```

```python
import functools
import jax
import jax.numpy as jnp
from jax import lax
from jax.experimental import pallas as pl
from jax.experimental.pallas import tpu as pltpu
from jax.sharding import PartitionSpec as P


F32 = jnp.float32
BF16 = jnp.bfloat16
VMEM = pl.BlockSpec(memory_space=pltpu.VMEM)
HBM = pl.BlockSpec(memory_space=pltpu.HBM)
ANY = pl.BlockSpec(memory_space=pl.ANY)
SMEM = pl.BlockSpec(memory_space=pltpu.SMEM)


def call(kernel, out_shape, args, cost, smem=(), hbm=(), scratch=(), vmem=14 << 20, after=()):
    count = len(args)
    specs = [SMEM if i in smem else HBM if i in hbm else VMEM for i in range(count)]
    specs += [ANY] * len(after)
    many = isinstance(out_shape, (tuple, list))

    def body(*refs):
        kernel(*refs[:count], *refs[count + len(after) :])

    return pl.pallas_call(
        body,
        out_shape=out_shape,
        in_specs=specs,
        out_specs=[VMEM] * len(out_shape) if many else VMEM,
        scratch_shapes=list(scratch),
        cost_estimate=pl.CostEstimate(flops=int(1.1e9 * cost), bytes_accessed=0, transcendentals=0),
        compiler_params=pltpu.CompilerParams(vmem_limit_bytes=vmem),
    )(*args, *after)


def place():
    group = lax.axis_index("mode")
    return (group, group ^ 1, group ^ 2, group & 1, group >> 1, 1 - (group >> 1))


def add_kernel(left_ref, right_ref, out_ref):
    out_ref[...] = left_ref[...] + right_ref[...]


def gather_kernel(shared_ref, shapes_ref, up_ref, down_ref, held_ref, sem):
    dims, nodes, _ = held_ref.shape
    width = shared_ref.shape[1]
    load = pltpu.make_async_copy(shapes_ref, held_ref, sem)
    load.start()
    node = lax.broadcasted_iota(jnp.int32, (nodes, 2 * width), 0)
    wanted = jnp.concatenate([shared_ref[1:2, :], shared_ref[0:1, :]], axis=1)
    pick = jnp.where(node == wanted, 1.0, 0.0).astype(F32).T.astype(BF16)
    load.wait()
    for d in range(dims):
        got = jnp.dot(pick, held_ref[d], preferred_element_type=F32).astype(BF16)
        up_ref[d * width : (d + 1) * width, :] = got[:width]
        down_ref[d * width : (d + 1) * width, :] = got[width:]


def stats_kernel(mass_ref, shapes_ref, out_ref, mass_scr):
    dims, nodes, block = shapes_ref.shape
    column = jnp.broadcast_to(mass_ref[...], (8, nodes)).T
    mass_scr[...] = jnp.broadcast_to(column[:, 0:1], (nodes, 128))
    for at in range(0, block, 128):
        lanes = slice(at, at + 128)
        general = jnp.zeros((8, 128), F32)
        for d in range(dims):
            lever = jnp.zeros((8, 128), F32)
            for r in range(0, nodes, 16):
                wide = shapes_ref[d, r : r + 16, lanes].astype(F32)
                weighted = wide * mass_scr[r : r + 16, :]
                square = weighted * wide
                lever += weighted[:8] + weighted[8:]
                general += square[:8] + square[8:]
            out_ref[d : d + 1, lanes] = jnp.sum(lever, axis=0, keepdims=True)
        out_ref[dims : dims + 1, lanes] = jnp.sum(general, axis=0, keepdims=True)


def local_kernel(codes_ref, count_ref, recovery_ref, shapes_ref, local_ref, rim_ref, pick_ref, force_ref, got_scr):
    slots, elems = codes_ref.shape
    per_elem, dims = recovery_ref.shape[0], recovery_ref.shape[1]
    nodes, block = shapes_ref.shape[1], shapes_ref.shape[2]
    taken = slots * elems
    span = pick_ref.shape[1]
    node = lax.broadcasted_iota(jnp.int32, (span, elems), 0)
    for s in range(0, slots, 2):
        picks = []
        for q in range(s, min(s + 2, slots)):
            code = jnp.where(q < count_ref[...], codes_ref[q : q + 1, :], -1)
            picks.append(jnp.where(node == code, 1.0, 0.0).astype(F32))
        pick_ref[s * elems : s * elems + len(picks) * elems, :] = (
            jnp.concatenate(picks, axis=1).T.astype(BF16)
        )
    row = lax.broadcasted_iota(jnp.int32, (elems, 2 * elems), 0)
    column = lax.broadcasted_iota(jnp.int32, (elems, 2 * elems), 1)
    same = (column == row) | (column == row + elems)
    for k in range(per_elem):
        for d in range(dims):
            value = recovery_ref[k, d].astype(F32)
            for s in range(0, slots, 2):
                pair = jnp.concatenate([value[s : s + 1], value[s + 1 : s + 2]], axis=1)
                at = (d * slots + s) * elems
                force_ref[k * elems : (k + 1) * elems, at : at + 2 * elems] = jnp.where(
                    same, pair, 0.0
                ).astype(BF16)
    rim = span - nodes
    for d in range(dims):
        rows = slice(d * taken, (d + 1) * taken)
        value = jnp.dot(force_ref[:, rows], pick_ref[:, nodes:], preferred_element_type=F32)
        high = value.astype(BF16)
        rim_ref[:, d * rim : (d + 1) * rim] = high
        rim_ref[:, (dims + d) * rim : (dims + d + 1) * rim] = (value - high.astype(F32)).astype(BF16)
        got = jnp.dot(pick_ref[:, :nodes], shapes_ref[d], preferred_element_type=F32)
        got_scr[rows, :] = got.astype(BF16)
    for c in range(0, block, 256):
        local_ref[:, c : c + 256] = jnp.dot(
            force_ref[...], got_scr[:, c : c + 256], preferred_element_type=F32
        )


def mode_rows(freq, rate):
    alpha = rate * freq
    inverse = 1.0 / jnp.sqrt(alpha)
    return (freq * freq * inverse, inverse, 2.0 * alpha, 2.0 * (freq / rate))


def turn_rows(rows):
    pieces = [rows[:, c : c + 128] for c in range(0, rows.shape[1], 128)]
    while len(pieces) * 8 % 128:
        pieces.append(jnp.zeros((8, 128), F32))
    return [jnp.concatenate(pieces[c : c + 16], axis=0).T for c in range(0, len(pieces), 16)]


def place_modes(freq_ref, rate_ref, row_scr, col_scr, groups, side, block):
    side_rows = []
    for which, group in enumerate(groups):
        lanes = pl.ds(pl.multiple_of(group * block, block), block)
        rows = jnp.concatenate(list(mode_rows(freq_ref[:, lanes], rate_ref[:, lanes])) * 2, axis=0)
        row_scr[which * 8 : which * 8 + 8, :] = rows
        if which == side:
            side_rows.append(rows)
    if side is None:
        return
    turned = turn_rows(jnp.concatenate(side_rows, axis=1))
    for t in range(block // 128):
        for q in range(4):
            lane = t % 16 * 8 + q
            col_scr[q, t * 128 : (t + 1) * 128, :] = jnp.broadcast_to(
                turned[t // 16][:, lane : lane + 1], (128, 128)
            )


def fill_rho(row_scr, col_scr, out_ref, out_col, side_row, count, cols_at, col_off, tile):
    step = min(count, 256)
    cols = [
        jnp.broadcast_to(row_scr[cols_at + q : cols_at + q + 1, pl.ds(col_off, tile)], (8, tile))
        for q in range(4)
    ]

    @pl.loop(0, count // step)
    def _(t):
        for k in range(0, step, 8):
            at = pl.multiple_of(t * step, step) + k
            high, low, alpha, zeta = (col_scr[q, pl.ds(side_row + at, 8), :] for q in range(4))
            for c in range(0, tile, 128):
                col = [value[:, c : c + 128] for value in cols]
                spread = high * col[1] - low * col[0]
                pair = alpha + col[2]
                bottom = spread * spread + pair * (zeta + col[3])
                out_ref[pl.ds(at, 8), out_col + c : out_col + c + 128] = pair / bottom


def rho_near_kernel(freq_ref, rate_ref, diag_ref, mate_ref, col_scr, row_scr):
    block = diag_ref.shape[0]
    half = block // 2
    tile = block // 4
    own, mate, parity = place()[0], place()[1], place()[3]
    place_modes(freq_ref, rate_ref, row_scr, col_scr, (own, mate), 0, block)
    for j in range(4):
        fill_rho(row_scr, col_scr, diag_ref, j * tile, 0, (j + 1) * tile, 0, j * tile, tile)
    for i in range(2):
        for j in range(2):
            off = pl.multiple_of((i ^ parity) * half + j * tile, tile)
            fill_rho(row_scr, col_scr, mate_ref.at[i], j * tile, i * half, half, 8, off, tile)


def rho_own_kernel(freq_ref, rate_ref, side_ref, out_ref, row_scr):
    block = out_ref.shape[0]
    tile = block // 4
    place_modes(freq_ref, rate_ref, row_scr, None, (place()[2],), None, block)
    for j in range(4):
        fill_rho(row_scr, side_ref, out_ref, j * tile, 0, block, 0, j * tile, tile)


def rho_mate_kernel(freq_ref, rate_ref, out_ref, col_scr, row_scr):
    block = out_ref.shape[0]
    tile = block // 4
    place_modes(freq_ref, rate_ref, row_scr, col_scr, (place()[1], place()[2]), 0, block)
    for j in range(4):
        fill_rho(row_scr, col_scr, out_ref, j * tile, 0, block, 8, j * tile, tile)


def forces_kernel(dims, rim_ref, low_ref, high_ref, local_ref, all_ref, *refs):
    part_refs, rim_scr = refs[:-1], refs[-1]
    comps, block = all_ref.shape
    width = low_ref.shape[0] // dims
    part = comps // 2
    rows = pl.ds(pl.multiple_of(place()[5] * part, part), part)
    for copy in range(2):
        for d in range(dims):
            base = (copy * dims + d) * 2 * width
            rim_scr[base : base + width, :] = low_ref[d * width : (d + 1) * width, :]
            rim_scr[base + width : base + 2 * width, :] = high_ref[d * width : (d + 1) * width, :]
    for c in range(0, block, 256):
        total = jnp.dot(rim_ref[...], rim_scr[:, c : c + 256], preferred_element_type=F32)
        all_ref[:, c : c + 256] = (local_ref[:, c : c + 256] + total).astype(BF16)
    at = 0
    for part_ref in part_refs:
        part_ref[...] = all_ref[rows, at : at + part_ref.shape[1]]
        at += part_ref.shape[1]


def join_kernel(*refs):
    out_ref = refs[-1]
    size = refs[0].shape[0]
    for q, ref in enumerate(refs[:-1]):
        out_ref[q * size : (q + 1) * size, :] = ref[...]


def amps_kernel(stats_ref, extra_ref, spectral_ref, freq_ref, rate_ref, *out_refs):
    dims, block = spectral_ref.shape[0], stats_ref.shape[1]
    for q, out_ref in enumerate(out_refs):
        lanes = pl.ds(pl.multiple_of(place()[q] * block, block), block)
        rows = slice(q * (dims + 1), (q + 1) * (dims + 1))
        total = stats_ref[rows, :] + extra_ref[rows, :]
        scale = 2.0 * jnp.sqrt(freq_ref[:, lanes] / rate_ref[:, lanes])
        amps = total[:dims] / total[dims : dims + 1] * spectral_ref[:, lanes] * scale
        out_ref[...] = jnp.concatenate([amps, jnp.zeros((8 - dims, block), F32)], axis=0)


def fold(value):
    total = value[:, :128]
    for c in range(128, value.shape[1], 128):
        total = total + value[:, c : c + 128]
    return total


def to_row(acc, turned, per_elem):
    elems = acc.shape[0] // per_elem
    for k in range(per_elem):
        turned[pl.ds(k, elems, stride=per_elem), :] = acc[k * elems : (k + 1) * elems, :]
    ones = jnp.ones((8, acc.shape[1]), F32)
    return lax.dot_general(
        ones, turned[...], (((1,), (1,)), ((), ())),
        precision=lax.Precision.HIGHEST, preferred_element_type=F32,
    )[0:1]


def split(value):
    top = value.astype(BF16).astype(F32)
    rest = value - top
    middle = rest.astype(BF16).astype(F32)
    return top, middle, rest - middle


def side_terms(out_scr, at, amps, dims):
    top, middle, last = split(amps[:dims])
    rows = jnp.concatenate([top, top, middle, middle, top, last], axis=0)
    rows = jnp.concatenate([rows, jnp.zeros((32 - rows.shape[0], rows.shape[1]), F32)], axis=0)
    for c in range(0, amps.shape[1], 512):
        stack = [rows[:, c + q : c + q + 128] for q in range(0, 512, 128)]
        turned = jnp.concatenate(stack, axis=0).T
        for q in range(4):
            out_scr[at + c + q * 128 : at + c + (q + 1) * 128, :] = turned[:, q * 32 : (q + 1) * 32].astype(BF16)


def col_terms(amps, dims, factor):
    top, middle, last = split(amps[:dims] * factor)
    rows = jnp.concatenate([top, middle, top, middle, last, top], axis=0)
    rows = jnp.concatenate([rows, jnp.zeros((32 - rows.shape[0], rows.shape[1]), F32)], axis=0)
    return rows.astype(BF16)


def weigh(rho, side, cols):
    return (rho * jnp.dot(side, cols, preferred_element_type=F32)).astype(BF16)


def near_kernel(dims, chunks, *refs):
    own_amps_ref, mate_amps_ref, diag_ref, cross_ref = refs[:4]
    own_refs, mate_refs = refs[4 : 4 + chunks], refs[4 + chunks : 4 + 2 * chunks]
    acc, side_scr, w_scr = refs[4 + 2 * chunks :]
    _, chunk = own_refs[0].shape
    block = diag_ref.shape[0]
    tile = block // 4
    half = block // 2
    parity = place()[3]

    def part(parts, at, size):
        return parts[at // chunk][:, at % chunk : at % chunk + size]

    def product(w, at, depth):
        total = None
        for c in range(at, at + depth, min(chunk, depth)):
            size = min(chunk, at + depth - c)
            got = jnp.dot(part(own_refs, c, size), w[c - at : c - at + size, :], preferred_element_type=F32)
            total = got if total is None else total + got
        return total

    side_terms(side_scr, 0, own_amps_ref[...], dims)
    once, twice = (col_terms(own_amps_ref[...], dims, factor) for factor in (1.0, 2.0))
    straight = parity == 0
    turn = 0
    for j in range(4):
        spot = slice(j * tile, (j + 1) * tile)
        for i in range(j + 1):
            rows = slice(i * tile, (i + 1) * tile)
            cols = twice if i < j else once
            w_scr[turn, rows, :] = weigh(diag_ref[rows, spot], side_scr[rows, :], cols[:, spot])
        got = product(w_scr.at[turn], 0, (j + 1) * tile)
        got = fold(got * part(own_refs, j * tile, tile).astype(F32))
        acc[...] = got if j == 0 else acc[...] + got
        turn = 1 - turn
    for i in range(2):
        for j in range(half // tile):
            here, there = i * half + j * tile, (1 - i) * half + j * tile
            cols = jnp.where(
                straight, mate_amps_ref[:, here : here + tile], mate_amps_ref[:, there : there + tile]
            )
            w_scr[turn, :half, :] = weigh(
                cross_ref[i, :, j * tile : (j + 1) * tile],
                side_scr[i * half : (i + 1) * half, :], col_terms(cols, dims, 2.0),
            )
            got = product(w_scr.at[turn], i * half, half)
            other = jnp.where(
                straight, part(mate_refs, here, tile).astype(F32), part(mate_refs, there, tile).astype(F32)
            )
            acc[...] += fold(got * other)
            turn = 1 - turn


def weights_kernel(dims, own_amps_ref, mate_amps_ref, far_amps_ref, own_ref, mate_ref, out_ref, side_scr):
    block = own_ref.shape[1]
    tile = block // 4
    cols = col_terms(far_amps_ref[...], dims, 2.0)
    for q, (amps_ref, rho_ref) in enumerate(((own_amps_ref, own_ref), (mate_amps_ref, mate_ref))):
        side_terms(side_scr, q * block, amps_ref[...], dims)
        for at in range(0, block, tile):
            base = q * block + at
            for c in range(0, block, tile):
                spot = slice(c, c + tile)
                out_ref[base : base + tile, spot] = weigh(
                    rho_ref[at : at + tile, spot], side_scr[base : base + tile, :], cols[:, spot]
                )


def far_kernel(at, per_elem, near_ref, w_ref, far_ref, own_ref, mate_ref, out_ref, *scratch):
    _, block = own_ref.shape
    part, chunk = far_ref.shape
    tile = min(256, chunk)
    rows = pl.ds(pl.multiple_of(place()[4] * part, part), part)
    total = near_ref[rows, :]
    for c in range(0, chunk, tile):
        spot = slice(at + c, at + c + tile)
        got = jnp.dot(own_ref[rows, :], w_ref[:block, spot], preferred_element_type=F32)
        got = got + jnp.dot(mate_ref[rows, :], w_ref[block:, spot], preferred_element_type=F32)
        total = total + fold(got * far_ref[:, c : c + tile].astype(F32))
    acc = scratch[0] if scratch else out_ref
    acc[...] = near_ref[...]
    acc[rows, :] = total
    if scratch:
        out_ref[...] = to_row(acc, scratch[1], per_elem)


def four_groups(*args):
    return combined(*args)


def combined(
    shapes, masses, spectral, frequencies, damping, recovery, connectivity, node_count, shared
):
    dims, nodes, block = shapes.shape
    elems, slots = connectivity.shape
    per_elem = recovery.shape[1]
    comps = elems * per_elem
    part = comps // 2
    width = shared.shape[1]
    parts = lax.axis_size("dom")
    sds = jax.ShapeDtypeStruct
    ahead = [(i, i + 1) for i in range(parts - 1)]
    back = [(i + 1, i) for i in range(parts - 1)]
    freq = frequencies.reshape(1, -1)
    rate = damping.reshape(1, -1)

    up, down, held = call(
        gather_kernel, [sds((dims * width, block), BF16)] * 2 + [sds(shapes.shape, BF16)], (shared, shapes),
        2.0, hbm=(1,), scratch=[pltpu.SemaphoreType.DMA],
    )
    low, high = lax.ppermute(up, "dom", ahead), lax.ppermute(down, "dom", back)
    stats = call(
        stats_kernel, sds((dims + 1, block), F32), (masses.reshape(1, nodes), held), 0.8,
        scratch=[pltpu.VMEM((nodes, 128), F32)],
    )
    rho_diag, rho_mate, sides = call(
        rho_near_kernel,
        (sds((block, block), F32), sds((2, block // 2, block // 2), F32), sds((4, block, 128), F32)),
        (freq, rate), 3.0,
        scratch=[pltpu.VMEM((16, block), F32)], after=(stats,),
    )
    far_own = call(
        rho_own_kernel, sds((block, block), F32), (freq, rate, sides), 1.9,
        scratch=[pltpu.VMEM((8, block), F32)],
    )
    taken = slots * elems
    local, rim = call(
        local_kernel, (sds((comps, block), F32), sds((comps, 4 * dims * width), BF16)),
        (connectivity.T, node_count.reshape(1, elems), recovery.transpose(1, 3, 2, 0), held),
        1.8, after=(far_own,),
        scratch=[
            pltpu.VMEM((taken, nodes + 2 * width), BF16), pltpu.VMEM((comps, dims * taken), BF16),
            pltpu.VMEM((dims * taken, block), BF16),
        ],
    )
    far_mate = call(
        rho_mate_kernel, sds((block, block), F32), (freq, rate), 2.5,
        scratch=[pltpu.VMEM((4, block, 128), F32), pltpu.VMEM((16, block), F32)],
    )
    given = [stats] + [lax.ppermute(stats, "mode", [(i, i ^ q) for i in range(4)]) for q in (1, 2)]
    stats = call(join_kernel, sds((3 * (dims + 1), block), F32), given, 0.5)
    first = stats
    order = [1 << q for q in range(1, parts.bit_length() - 1)] + [1]
    if parts & (parts - 1) or parts == 1:
        stats = lax.psum(stats, "dom")
        order = []
    extra = jnp.zeros_like(stats)
    for q, reach in enumerate(order):
        if q:
            stats = call(
                add_kernel, sds(stats.shape, F32), (stats, extra), 0.5, after=(rim,) if q == 1 else ()
            )
            first = stats if q == 1 else first
        extra = lax.ppermute(stats, "dom", [(i, i ^ reach) for i in range(parts)])
    amps, mate_amps, far_amps = call(
        amps_kernel, [sds((8, block), F32)] * 3, (stats, extra, spectral, freq, rate), 0.8,
    )

    cuts = [block - block // 4, block // 4]
    forces, *sent = call(
        functools.partial(forces_kernel, dims),
        [sds((comps, block), BF16)] + [sds((part, cut), BF16) for cut in cuts],
        (rim, low, high, local), 1.4,
        scratch=[pltpu.VMEM((4 * dims * width, block), BF16)], after=(first,),
    )
    far = [lax.ppermute(value, "mode", [(i, i ^ 2) for i in range(4)]) for value in sent]
    mate = lax.ppermute(forces, "mode", [(i, i ^ 1) for i in range(4)])
    near = call(
        functools.partial(near_kernel, dims, 1), sds((comps, 128), F32),
        (amps, mate_amps, rho_diag, rho_mate, forces, mate),
        3.4,
        scratch=[pltpu.VMEM((block, 32), BF16), pltpu.VMEM((2, block, block // 4), BF16)],
    )
    weights = call(
        functools.partial(weights_kernel, dims), sds((2 * block, block), BF16),
        (amps, mate_amps, far_amps, far_own, far_mate), 1.4,
        scratch=[pltpu.VMEM((2 * block, 32), BF16)],
    )
    value = near
    at = 0
    for c, cut in enumerate(cuts):
        last = c == len(cuts) - 1
        value = call(
            functools.partial(far_kernel, at, per_elem), sds((1, comps) if last else (comps, 128), F32),
            (value, weights, far[c], forces, mate), 2.1 * cut / block,
            scratch=[pltpu.VMEM((comps, 128), F32)] * 2 if last else (),
        )
        at += cut
    value = value.reshape(comps)
    for reach in (1, 2):
        value = value + lax.ppermute(value, "mode", [(i, i ^ reach) for i in range(4)])
    return value


def extended_2(block, sides, width):
    for axis, dim in sides:
        count = lax.axis_size(axis)
        forward = [(i, i + 1) for i in range(count - 1)]
        backward = [(target, source) for source, target in forward]
        low = lax.ppermute(
            lax.slice_in_dim(block, block.shape[dim] - width, None, axis=dim), axis, forward
        )
        high = lax.ppermute(lax.slice_in_dim(block, 0, width, axis=dim), axis, backward)
        block = jnp.concatenate([low, block, high], axis=dim)
    return block


def shifted(value, axis, steps):
    count = lax.axis_size(axis)
    pairs = [(source, (source + steps) % count) for source in range(count)]
    return lax.ppermute(value, axis, pairs)


def correlation_block(freq_rows, freq_cols, rate_rows, rate_cols):
    ratio = freq_cols[None, :] / freq_rows[:, None]
    ratio_sq = ratio * ratio
    rate_row = rate_rows[:, None]
    rate_col = rate_cols[None, :]
    top_part = (
        8.0
        * jnp.sqrt(rate_row * rate_col)
        * (rate_row + ratio * rate_col)
        * ratio
        * jnp.sqrt(ratio)
    )
    spread = 1.0 - ratio_sq
    bottom_part = (
        spread * spread
        + 4.0 * rate_row * rate_col * ratio * (1.0 + ratio_sq)
        + 4.0 * (rate_row * rate_row + rate_col * rate_col) * ratio_sq
    )
    return top_part / bottom_part


def block_terms(own_forces, own_start, far_forces, far_start, amplitudes, frequencies, damping):
    row_count = own_forces.shape[1]
    col_count = far_forces.shape[1]
    freq_rows = lax.dynamic_slice_in_dim(frequencies, own_start, row_count)
    freq_cols = lax.dynamic_slice_in_dim(frequencies, far_start, col_count)
    rate_rows = lax.dynamic_slice_in_dim(damping, own_start, row_count)
    rate_cols = lax.dynamic_slice_in_dim(damping, far_start, col_count)
    correlation = correlation_block(freq_rows, freq_cols, rate_rows, rate_cols)
    amp_rows = lax.dynamic_slice_in_dim(amplitudes, own_start, row_count, 1)
    amp_cols = lax.dynamic_slice_in_dim(amplitudes, far_start, col_count, 1)
    weights = (amp_rows.T[:, :, None] * correlation[:, None, :] * amp_cols[None, :, :]).astype(
        jnp.bfloat16
    )
    weights = weights.reshape(row_count, 3 * col_count)
    projected = jnp.dot(own_forces, weights, preferred_element_type=jnp.float32)
    projected = projected.reshape(own_forces.shape[0], 3, col_count)
    far_wide = far_forces.astype(jnp.float32)
    return jnp.sum(projected * far_wide[:, None, :], axis=(1, 2))


def any_groups(
    shapes, masses, spectral, frequencies, damping, recovery, connectivity, node_count, shared
):
    rim_width = shared.shape[1]
    block_width = shapes.shape[2]
    elem_count = connectivity.shape[0]
    slot_count = connectivity.shape[1]
    mode_index = lax.axis_index("mode")
    own_start = mode_index * block_width
    shape_wide = shapes.astype(jnp.float32)
    weighted = masses[None, :, None] * shape_wide
    lever_arm = jnp.sum(weighted, axis=1)
    general = jnp.sum(weighted * shape_wide, axis=(0, 1))
    lever_sum, general_sum = lax.psum((lever_arm, general), "dom")
    own_spectral = lax.dynamic_slice_in_dim(spectral, own_start, block_width, 1)
    local_amps = lever_sum / general_sum[None, :] * own_spectral
    amplitudes = lax.all_gather(local_amps, "mode", axis=1, tiled=True)
    outgoing = jnp.concatenate(
        [jnp.take(shapes, shared[0], axis=1), jnp.take(shapes, shared[1], axis=1)], axis=1
    )
    extended = extended_2(outgoing, (("dom", 1),), rim_width)
    node_table = jnp.concatenate(
        [shapes, extended[:, :rim_width], extended[:, 3 * rim_width :]], axis=1
    )
    gathered = jnp.take(node_table, connectivity.reshape(-1), axis=1).reshape(
        3, elem_count, slot_count, block_width
    )
    slot_live = (jnp.arange(slot_count)[None, :] < node_count[:, None]).astype(jnp.bfloat16)
    masked = recovery * slot_live[:, None, :, None]
    forces = jnp.einsum("ekna,aenm->ekm", masked, gathered, preferred_element_type=jnp.float32)
    forces = forces.astype(jnp.bfloat16).reshape(elem_count * recovery.shape[1], block_width)
    groups = lax.axis_size("mode")
    half_count = groups // 2
    partial_value = block_terms(
        forces, own_start, forces, own_start, amplitudes, frequencies, damping
    )

    def advance(turn_index, carried):
        incoming, summed = carried
        incoming = shifted(incoming, "mode", 1)
        source = (mode_index - turn_index) % groups * block_width
        factor = jnp.where(turn_index == half_count, jnp.float32(1.0), jnp.float32(2.0))
        summed = summed + factor * block_terms(
            forces, own_start, incoming, source, amplitudes, frequencies, damping
        )
        return (incoming, summed)

    carried = lax.fori_loop(1, half_count + 1, advance, (forces, partial_value))
    partial_value = carried[1]
    return lax.psum(partial_value, "mode")


def solution(mesh):
    in_specs = (
        P(None, "dom", "mode"),
        P("dom"),
        P(),
        P(),
        P(),
        P("dom", None, None, None),
        P("dom", None),
        P("dom"),
        P(None, "dom"),
    )
    out_specs = P("dom")
    special = mesh.shape["mode"] == 4
    step = four_groups if special else any_groups
    step = jax.shard_map(
        step, mesh=mesh, in_specs=in_specs, out_specs=out_specs, check_vma=False
    )
    return step
```

```python
import functools
import jax
import jax.numpy as jnp
from jax import lax
from jax.experimental import pallas as pl
from jax.experimental.pallas import tpu as pltpu
from jax.sharding import PartitionSpec as P


F32 = jnp.float32
BF16 = jnp.bfloat16
VMEM = pl.BlockSpec(memory_space=pltpu.VMEM)
HBM = pl.BlockSpec(memory_space=pltpu.HBM)
ANY = pl.BlockSpec(memory_space=pl.ANY)
SMEM = pl.BlockSpec(memory_space=pltpu.SMEM)


def call(kernel, out_shape, args, cost, smem=(), hbm=(), scratch=(), vmem=14 << 20, after=()):
    count = len(args)
    specs = [SMEM if i in smem else HBM if i in hbm else VMEM for i in range(count)]
    specs += [ANY] * len(after)
    many = isinstance(out_shape, (tuple, list))

    def body(*refs):
        kernel(*refs[:count], *refs[count + len(after) :])

    return pl.pallas_call(
        body,
        out_shape=out_shape,
        in_specs=specs,
        out_specs=[VMEM] * len(out_shape) if many else VMEM,
        scratch_shapes=list(scratch),
        cost_estimate=pl.CostEstimate(flops=int(1.1e9 * cost), bytes_accessed=0, transcendentals=0),
        compiler_params=pltpu.CompilerParams(vmem_limit_bytes=vmem),
    )(*args, *after)


def place():
    group = lax.axis_index("mode")
    return (group, group ^ 1, group ^ 2, group & 1, group >> 1, 1 - (group >> 1))


def add_kernel(left_ref, right_ref, out_ref):
    out_ref[...] = left_ref[...] + right_ref[...]


def gather_kernel(shared_ref, shapes_ref, first_ref, second_ref, held_ref, sem):
    dims, nodes, _ = held_ref.shape
    width = shared_ref.shape[1]
    load = pltpu.make_async_copy(shapes_ref, held_ref, sem)
    load.start()
    node = lax.broadcasted_iota(jnp.int32, (nodes, 2 * width), 0)
    odd = lax.axis_index("dom") & 1
    wanted = jnp.concatenate([shared_ref[pl.ds(1 - odd, 1), :], shared_ref[pl.ds(odd, 1), :]], axis=1)
    pick = jnp.where(node == wanted, 1.0, 0.0).astype(F32).T.astype(BF16)
    load.wait()
    for d in range(dims):
        got = jnp.dot(pick, held_ref[d], preferred_element_type=F32).astype(BF16)
        first_ref[d * width : (d + 1) * width, :] = got[:width]
        second_ref[d * width : (d + 1) * width, :] = got[width:]


def stats_kernel(mass_ref, shapes_ref, out_ref, mass_scr):
    dims, nodes, block = shapes_ref.shape
    column = jnp.broadcast_to(mass_ref[...], (8, nodes)).T
    mass_scr[...] = jnp.broadcast_to(column[:, 0:1], (nodes, 128))
    for at in range(0, block, 128):
        lanes = slice(at, at + 128)
        general = jnp.zeros((8, 128), F32)
        for d in range(dims):
            lever = jnp.zeros((8, 128), F32)
            for r in range(0, nodes, 16):
                wide = shapes_ref[d, r : r + 16, lanes].astype(F32)
                weighted = wide * mass_scr[r : r + 16, :]
                square = weighted * wide
                lever += weighted[:8] + weighted[8:]
                general += square[:8] + square[8:]
            out_ref[d : d + 1, lanes] = jnp.sum(lever, axis=0, keepdims=True)
        out_ref[dims : dims + 1, lanes] = jnp.sum(general, axis=0, keepdims=True)


def local_kernel(codes_ref, count_ref, recovery_ref, shapes_ref, local_ref, rim_ref, pick_ref, force_ref, got_scr):
    slots, elems = codes_ref.shape
    per_elem, dims = recovery_ref.shape[0], recovery_ref.shape[1]
    nodes, block = shapes_ref.shape[1], shapes_ref.shape[2]
    taken = slots * elems
    span = pick_ref.shape[1]
    node = lax.broadcasted_iota(jnp.int32, (span, elems), 0)
    width = (span - nodes) // 2
    even = 1 - (lax.axis_index("dom") & 1)
    swapped = jnp.where(node < nodes + width, node + width, node - width)
    node = jnp.where((node >= nodes) & (even == 1), swapped, node)
    for s in range(0, slots, 2):
        picks = []
        for q in range(s, min(s + 2, slots)):
            code = jnp.where(q < count_ref[...], codes_ref[q : q + 1, :], -1)
            picks.append(jnp.where(node == code, 1.0, 0.0).astype(F32))
        pick_ref[s * elems : s * elems + len(picks) * elems, :] = (
            jnp.concatenate(picks, axis=1).T.astype(BF16)
        )
    row = lax.broadcasted_iota(jnp.int32, (elems, 2 * elems), 0)
    column = lax.broadcasted_iota(jnp.int32, (elems, 2 * elems), 1)
    same = (column == row) | (column == row + elems)
    for k in range(per_elem):
        for d in range(dims):
            value = recovery_ref[k, d].astype(F32)
            for s in range(0, slots, 2):
                pair = jnp.concatenate([value[s : s + 1], value[s + 1 : s + 2]], axis=1)
                at = (d * slots + s) * elems
                force_ref[k * elems : (k + 1) * elems, at : at + 2 * elems] = jnp.where(
                    same, pair, 0.0
                ).astype(BF16)
    rim = span - nodes
    for d in range(dims):
        rows = slice(d * taken, (d + 1) * taken)
        value = jnp.dot(force_ref[:, rows], pick_ref[:, nodes:], preferred_element_type=F32)
        high = value.astype(BF16)
        rim_ref[:, d * rim : (d + 1) * rim] = high
        rim_ref[:, (dims + d) * rim : (dims + d + 1) * rim] = (value - high.astype(F32)).astype(BF16)
        got = jnp.dot(pick_ref[:, :nodes], shapes_ref[d], preferred_element_type=F32)
        got_scr[rows, :] = got.astype(BF16)
    for c in range(0, block, 256):
        local_ref[:, c : c + 256] = jnp.dot(
            force_ref[...], got_scr[:, c : c + 256], preferred_element_type=F32
        )


def mode_rows(freq, rate):
    alpha = rate * freq
    inverse = 1.0 / jnp.sqrt(alpha)
    return (freq * freq * inverse, inverse, 2.0 * alpha, 2.0 * (freq / rate))


def turn_rows(rows):
    pieces = [rows[:, c : c + 128] for c in range(0, rows.shape[1], 128)]
    while len(pieces) * 8 % 128:
        pieces.append(jnp.zeros((8, 128), F32))
    return [jnp.concatenate(pieces[c : c + 16], axis=0).T for c in range(0, len(pieces), 16)]


def place_modes(freq_ref, rate_ref, row_scr, col_scr, groups, side, block):
    side_rows = []
    for which, group in enumerate(groups):
        lanes = pl.ds(pl.multiple_of(group * block, block), block)
        rows = jnp.concatenate(list(mode_rows(freq_ref[:, lanes], rate_ref[:, lanes])) * 2, axis=0)
        row_scr[which * 8 : which * 8 + 8, :] = rows
        if which == side:
            side_rows.append(rows)
    if side is None:
        return
    turned = turn_rows(jnp.concatenate(side_rows, axis=1))
    for t in range(block // 128):
        for q in range(4):
            lane = t % 16 * 8 + q
            col_scr[q, t * 128 : (t + 1) * 128, :] = jnp.broadcast_to(
                turned[t // 16][:, lane : lane + 1], (128, 128)
            )


def fill_rho(row_scr, col_scr, out_ref, out_col, side_row, count, cols_at, col_off, tile):
    step = min(count, 256)
    cols = [
        jnp.broadcast_to(row_scr[cols_at + q : cols_at + q + 1, pl.ds(col_off, tile)], (8, tile))
        for q in range(4)
    ]

    @pl.loop(0, count // step)
    def _(t):
        for k in range(0, step, 8):
            at = pl.multiple_of(t * step, step) + k
            high, low, alpha, zeta = (col_scr[q, pl.ds(side_row + at, 8), :] for q in range(4))
            for c in range(0, tile, 128):
                col = [value[:, c : c + 128] for value in cols]
                spread = high * col[1] - low * col[0]
                pair = alpha + col[2]
                bottom = spread * spread + pair * (zeta + col[3])
                out_ref[pl.ds(at, 8), out_col + c : out_col + c + 128] = pair / bottom


def rho_near_kernel(freq_ref, rate_ref, diag_ref, mate_ref, col_scr, row_scr):
    block = diag_ref.shape[0]
    half = block // 2
    tile = block // 4
    own, mate, parity = place()[0], place()[1], place()[3]
    place_modes(freq_ref, rate_ref, row_scr, col_scr, (own, mate), 0, block)
    for j in range(4):
        fill_rho(row_scr, col_scr, diag_ref, j * tile, 0, (j + 1) * tile, 0, j * tile, tile)
    for i in range(2):
        for j in range(2):
            off = pl.multiple_of((i ^ parity) * half + j * tile, tile)
            fill_rho(row_scr, col_scr, mate_ref.at[i], j * tile, i * half, half, 8, off, tile)


def rho_own_kernel(freq_ref, rate_ref, side_ref, out_ref, row_scr):
    block = out_ref.shape[0]
    tile = block // 4
    place_modes(freq_ref, rate_ref, row_scr, None, (place()[2],), None, block)
    for j in range(4):
        fill_rho(row_scr, side_ref, out_ref, j * tile, 0, block, 0, j * tile, tile)


def rho_mate_kernel(freq_ref, rate_ref, out_ref, col_scr, row_scr):
    block = out_ref.shape[0]
    tile = block // 4
    place_modes(freq_ref, rate_ref, row_scr, col_scr, (place()[1], place()[2]), 0, block)
    for j in range(4):
        fill_rho(row_scr, col_scr, out_ref, j * tile, 0, block, 8, j * tile, tile)


def forces_kernel(dims, rim_ref, first_ref, second_ref, local_ref, all_ref, *refs):
    part_refs, rim_scr = refs[:-1], refs[-1]
    comps, block = all_ref.shape
    width = first_ref.shape[0] // dims
    part = comps // 2
    rows = pl.ds(pl.multiple_of(place()[5] * part, part), part)
    for copy in range(2):
        for d in range(dims):
            base = (copy * dims + d) * 2 * width
            rim_scr[base : base + width, :] = first_ref[d * width : (d + 1) * width, :]
            rim_scr[base + width : base + 2 * width, :] = second_ref[d * width : (d + 1) * width, :]
    for c in range(0, block, 256):
        total = jnp.dot(rim_ref[...], rim_scr[:, c : c + 256], preferred_element_type=F32)
        all_ref[:, c : c + 256] = (local_ref[:, c : c + 256] + total).astype(BF16)
    at = 0
    for part_ref in part_refs:
        part_ref[...] = all_ref[rows, at : at + part_ref.shape[1]]
        at += part_ref.shape[1]


def join_kernel(*refs):
    out_ref = refs[-1]
    size = refs[0].shape[0]
    for q, ref in enumerate(refs[:-1]):
        out_ref[q * size : (q + 1) * size, :] = ref[...]


def amps_kernel(stats_ref, extra_ref, spectral_ref, freq_ref, rate_ref, *out_refs):
    dims, block = spectral_ref.shape[0], stats_ref.shape[1]
    for q, out_ref in enumerate(out_refs):
        lanes = pl.ds(pl.multiple_of(place()[q] * block, block), block)
        rows = slice(q * (dims + 1), (q + 1) * (dims + 1))
        total = stats_ref[rows, :] + extra_ref[rows, :]
        scale = 2.0 * jnp.sqrt(freq_ref[:, lanes] / rate_ref[:, lanes])
        amps = total[:dims] / total[dims : dims + 1] * spectral_ref[:, lanes] * scale
        out_ref[...] = jnp.concatenate([amps, jnp.zeros((8 - dims, block), F32)], axis=0)


def fold(value):
    total = value[:, :128]
    for c in range(128, value.shape[1], 128):
        total = total + value[:, c : c + 128]
    return total


def to_row(acc, turned, per_elem):
    elems = acc.shape[0] // per_elem
    for k in range(per_elem):
        turned[pl.ds(k, elems, stride=per_elem), :] = acc[k * elems : (k + 1) * elems, :]
    pieces = jnp.concatenate([piece.astype(BF16) for piece in split(turned[...])], axis=1)
    return lax.dot_general(
        jnp.ones((8, pieces.shape[1]), BF16), pieces, (((1,), (1,)), ((), ())), preferred_element_type=F32
    )[0:1]


def split(value):
    top = value.astype(BF16).astype(F32)
    rest = value - top
    middle = rest.astype(BF16).astype(F32)
    return top, middle, rest - middle


def side_terms(out_scr, at, amps, dims):
    top, middle, last = split(amps[:dims])
    rows = jnp.concatenate([top, top, middle, middle, top, last], axis=0)
    rows = jnp.concatenate([rows, jnp.zeros((32 - rows.shape[0], rows.shape[1]), F32)], axis=0)
    for c in range(0, amps.shape[1], 512):
        stack = [rows[:, c + q : c + q + 128] for q in range(0, 512, 128)]
        turned = jnp.concatenate(stack, axis=0).T
        for q in range(4):
            out_scr[at + c + q * 128 : at + c + (q + 1) * 128, :] = turned[:, q * 32 : (q + 1) * 32].astype(BF16)


def col_terms(amps, dims, factor):
    top, middle, last = split(amps[:dims] * factor)
    rows = jnp.concatenate([top, middle, top, middle, last, top], axis=0)
    rows = jnp.concatenate([rows, jnp.zeros((32 - rows.shape[0], rows.shape[1]), F32)], axis=0)
    return rows.astype(BF16)


def weigh(rho, side, cols):
    return (rho * jnp.dot(side, cols, preferred_element_type=F32)).astype(BF16)


def near_kernel(dims, chunks, *refs):
    own_amps_ref, mate_amps_ref, diag_ref, cross_ref = refs[:4]
    own_refs, mate_refs = refs[4 : 4 + chunks], refs[4 + chunks : 4 + 2 * chunks]
    acc, side_scr, w_scr = refs[4 + 2 * chunks :]
    _, chunk = own_refs[0].shape
    block = diag_ref.shape[0]
    tile = block // 4
    half = block // 2
    parity = place()[3]

    def part(parts, at, size):
        return parts[at // chunk][:, at % chunk : at % chunk + size]

    def product(w, at, depth):
        total = None
        for c in range(at, at + depth, min(chunk, depth)):
            size = min(chunk, at + depth - c)
            got = jnp.dot(part(own_refs, c, size), w[c - at : c - at + size, :], preferred_element_type=F32)
            total = got if total is None else total + got
        return total

    side_terms(side_scr, 0, own_amps_ref[...], dims)
    once, twice = (col_terms(own_amps_ref[...], dims, factor) for factor in (1.0, 2.0))
    straight = parity == 0
    turn = 0
    for j in range(4):
        spot = slice(j * tile, (j + 1) * tile)
        for i in range(j + 1):
            rows = slice(i * tile, (i + 1) * tile)
            cols = twice if i < j else once
            w_scr[turn, rows, :] = weigh(diag_ref[rows, spot], side_scr[rows, :], cols[:, spot])
        got = product(w_scr.at[turn], 0, (j + 1) * tile)
        got = fold(got * part(own_refs, j * tile, tile).astype(F32))
        acc[...] = got if j == 0 else acc[...] + got
        turn = 1 - turn
    for i in range(2):
        for j in range(half // tile):
            here, there = i * half + j * tile, (1 - i) * half + j * tile
            cols = jnp.where(
                straight, mate_amps_ref[:, here : here + tile], mate_amps_ref[:, there : there + tile]
            )
            w_scr[turn, :half, :] = weigh(
                cross_ref[i, :, j * tile : (j + 1) * tile],
                side_scr[i * half : (i + 1) * half, :], col_terms(cols, dims, 2.0),
            )
            got = product(w_scr.at[turn], i * half, half)
            other = jnp.where(
                straight, part(mate_refs, here, tile).astype(F32), part(mate_refs, there, tile).astype(F32)
            )
            acc[...] += fold(got * other)
            turn = 1 - turn


def weights_kernel(dims, own_amps_ref, mate_amps_ref, far_amps_ref, own_ref, mate_ref, out_ref, side_scr):
    block = own_ref.shape[1]
    tile = block // 4
    cols = col_terms(far_amps_ref[...], dims, 2.0)
    for q, (amps_ref, rho_ref) in enumerate(((own_amps_ref, own_ref), (mate_amps_ref, mate_ref))):
        side_terms(side_scr, q * block, amps_ref[...], dims)
        for at in range(0, block, tile):
            base = q * block + at
            for c in range(0, block, tile):
                spot = slice(c, c + tile)
                out_ref[base : base + tile, spot] = weigh(
                    rho_ref[at : at + tile, spot], side_scr[base : base + tile, :], cols[:, spot]
                )


def far_kernel(at, per_elem, near_ref, w_ref, far_ref, own_ref, mate_ref, out_ref, *scratch):
    _, block = own_ref.shape
    part, chunk = far_ref.shape
    tile = min(256, chunk)
    rows = pl.ds(pl.multiple_of(place()[4] * part, part), part)
    total = near_ref[rows, :]
    for c in range(0, chunk, tile):
        spot = slice(at + c, at + c + tile)
        got = jnp.dot(own_ref[rows, :], w_ref[:block, spot], preferred_element_type=F32)
        got = got + jnp.dot(mate_ref[rows, :], w_ref[block:, spot], preferred_element_type=F32)
        total = total + fold(got * far_ref[:, c : c + tile].astype(F32))
    acc = scratch[0] if scratch else out_ref
    acc[...] = near_ref[...]
    acc[rows, :] = total
    if scratch:
        out_ref[...] = to_row(acc, scratch[1], per_elem)


def four_groups(*args):
    return combined(*args)


def combined(
    shapes, masses, spectral, frequencies, damping, recovery, connectivity, node_count, shared
):
    dims, nodes, block = shapes.shape
    elems, slots = connectivity.shape
    per_elem = recovery.shape[1]
    comps = elems * per_elem
    part = comps // 2
    width = shared.shape[1]
    parts = lax.axis_size("dom")
    sds = jax.ShapeDtypeStruct
    halves = [[], []]
    for i in range(parts - 1):
        halves[i % 2] += [(i, i + 1), (i + 1, i)]
    freq = frequencies.reshape(1, -1)
    rate = damping.reshape(1, -1)

    outgoing, other, held = call(
        gather_kernel, [sds((dims * width, block), BF16)] * 2 + [sds(shapes.shape, BF16)], (shared, shapes),
        2.0, hbm=(1,), scratch=[pltpu.SemaphoreType.DMA],
    )
    rims = (lax.ppermute(outgoing, "dom", halves[0]), lax.ppermute(other, "dom", halves[1]))
    stats = call(
        stats_kernel, sds((dims + 1, block), F32), (masses.reshape(1, nodes), held), 0.8,
        scratch=[pltpu.VMEM((nodes, 128), F32)],
    )
    rho_diag, rho_mate, sides = call(
        rho_near_kernel,
        (sds((block, block), F32), sds((2, block // 2, block // 2), F32), sds((4, block, 128), F32)),
        (freq, rate), 3.0,
        scratch=[pltpu.VMEM((16, block), F32)], after=(stats,),
    )
    far_own = call(
        rho_own_kernel, sds((block, block), F32), (freq, rate, sides), 1.9,
        scratch=[pltpu.VMEM((8, block), F32)],
    )
    taken = slots * elems
    local, rim = call(
        local_kernel, (sds((comps, block), F32), sds((comps, 4 * dims * width), BF16)),
        (connectivity.T, node_count.reshape(1, elems), recovery.transpose(1, 3, 2, 0), held),
        1.8, after=(far_own,),
        scratch=[
            pltpu.VMEM((taken, nodes + 2 * width), BF16), pltpu.VMEM((comps, dims * taken), BF16),
            pltpu.VMEM((dims * taken, block), BF16),
        ],
    )
    far_mate = call(
        rho_mate_kernel, sds((block, block), F32), (freq, rate), 2.5,
        scratch=[pltpu.VMEM((4, block, 128), F32), pltpu.VMEM((16, block), F32)],
    )
    given = [stats] + [lax.ppermute(stats, "mode", [(i, i ^ q) for i in range(4)]) for q in (1, 2)]
    stats = call(join_kernel, sds((3 * (dims + 1), block), F32), given, 0.5)
    first = stats
    order = [1 << q for q in range(1, parts.bit_length() - 1)] + [1]
    if parts & (parts - 1) or parts == 1:
        stats = lax.psum(stats, "dom")
        order = []
    extra = jnp.zeros_like(stats)
    for q, reach in enumerate(order):
        if q:
            stats = call(
                add_kernel, sds(stats.shape, F32), (stats, extra), 0.5, after=(rim,) if q == 1 else ()
            )
            first = stats if q == 1 else first
        extra = lax.ppermute(stats, "dom", [(i, i ^ reach) for i in range(parts)])
    amps, mate_amps, far_amps = call(
        amps_kernel, [sds((8, block), F32)] * 3, (stats, extra, spectral, freq, rate), 0.8,
    )

    cuts = [block - block // 4, block // 4]
    forces, *sent = call(
        functools.partial(forces_kernel, dims),
        [sds((comps, block), BF16)] + [sds((part, cut), BF16) for cut in cuts],
        (rim, *rims, local), 1.4,
        scratch=[pltpu.VMEM((4 * dims * width, block), BF16)], after=(first,),
    )
    far = [lax.ppermute(value, "mode", [(i, i ^ 2) for i in range(4)]) for value in sent]
    mate = lax.ppermute(forces, "mode", [(i, i ^ 1) for i in range(4)])
    near = call(
        functools.partial(near_kernel, dims, 1), sds((comps, 128), F32),
        (amps, mate_amps, rho_diag, rho_mate, forces, mate),
        3.4,
        scratch=[pltpu.VMEM((block, 32), BF16), pltpu.VMEM((2, block, block // 4), BF16)],
    )
    weights = call(
        functools.partial(weights_kernel, dims), sds((2 * block, block), BF16),
        (amps, mate_amps, far_amps, far_own, far_mate), 1.4,
        scratch=[pltpu.VMEM((2 * block, 32), BF16)],
    )
    value = near
    at = 0
    for c, cut in enumerate(cuts):
        last = c == len(cuts) - 1
        value = call(
            functools.partial(far_kernel, at, per_elem), sds((1, comps) if last else (comps, 128), F32),
            (value, weights, far[c], forces, mate), 2.1 * cut / block,
            scratch=[pltpu.VMEM((comps, 128), F32)] * 2 if last else (),
        )
        at += cut
    value = value.reshape(comps)
    for reach in (1, 2):
        value = value + lax.ppermute(value, "mode", [(i, i ^ reach) for i in range(4)])
    return value


def extended_2(block, sides, width):
    for axis, dim in sides:
        count = lax.axis_size(axis)
        forward = [(i, i + 1) for i in range(count - 1)]
        backward = [(target, source) for source, target in forward]
        low = lax.ppermute(
            lax.slice_in_dim(block, block.shape[dim] - width, None, axis=dim), axis, forward
        )
        high = lax.ppermute(lax.slice_in_dim(block, 0, width, axis=dim), axis, backward)
        block = jnp.concatenate([low, block, high], axis=dim)
    return block


def shifted(value, axis, steps):
    count = lax.axis_size(axis)
    pairs = [(source, (source + steps) % count) for source in range(count)]
    return lax.ppermute(value, axis, pairs)


def correlation_block(freq_rows, freq_cols, rate_rows, rate_cols):
    ratio = freq_cols[None, :] / freq_rows[:, None]
    ratio_sq = ratio * ratio
    rate_row = rate_rows[:, None]
    rate_col = rate_cols[None, :]
    top_part = (
        8.0
        * jnp.sqrt(rate_row * rate_col)
        * (rate_row + ratio * rate_col)
        * ratio
        * jnp.sqrt(ratio)
    )
    spread = 1.0 - ratio_sq
    bottom_part = (
        spread * spread
        + 4.0 * rate_row * rate_col * ratio * (1.0 + ratio_sq)
        + 4.0 * (rate_row * rate_row + rate_col * rate_col) * ratio_sq
    )
    return top_part / bottom_part


def block_terms(own_forces, own_start, far_forces, far_start, amplitudes, frequencies, damping):
    row_count = own_forces.shape[1]
    col_count = far_forces.shape[1]
    freq_rows = lax.dynamic_slice_in_dim(frequencies, own_start, row_count)
    freq_cols = lax.dynamic_slice_in_dim(frequencies, far_start, col_count)
    rate_rows = lax.dynamic_slice_in_dim(damping, own_start, row_count)
    rate_cols = lax.dynamic_slice_in_dim(damping, far_start, col_count)
    correlation = correlation_block(freq_rows, freq_cols, rate_rows, rate_cols)
    amp_rows = lax.dynamic_slice_in_dim(amplitudes, own_start, row_count, 1)
    amp_cols = lax.dynamic_slice_in_dim(amplitudes, far_start, col_count, 1)
    weights = (amp_rows.T[:, :, None] * correlation[:, None, :] * amp_cols[None, :, :]).astype(
        jnp.bfloat16
    )
    weights = weights.reshape(row_count, 3 * col_count)
    projected = jnp.dot(own_forces, weights, preferred_element_type=jnp.float32)
    projected = projected.reshape(own_forces.shape[0], 3, col_count)
    far_wide = far_forces.astype(jnp.float32)
    return jnp.sum(projected * far_wide[:, None, :], axis=(1, 2))


def any_groups(
    shapes, masses, spectral, frequencies, damping, recovery, connectivity, node_count, shared
):
    rim_width = shared.shape[1]
    block_width = shapes.shape[2]
    elem_count = connectivity.shape[0]
    slot_count = connectivity.shape[1]
    mode_index = lax.axis_index("mode")
    own_start = mode_index * block_width
    shape_wide = shapes.astype(jnp.float32)
    weighted = masses[None, :, None] * shape_wide
    lever_arm = jnp.sum(weighted, axis=1)
    general = jnp.sum(weighted * shape_wide, axis=(0, 1))
    lever_sum, general_sum = lax.psum((lever_arm, general), "dom")
    own_spectral = lax.dynamic_slice_in_dim(spectral, own_start, block_width, 1)
    local_amps = lever_sum / general_sum[None, :] * own_spectral
    amplitudes = lax.all_gather(local_amps, "mode", axis=1, tiled=True)
    outgoing = jnp.concatenate(
        [jnp.take(shapes, shared[0], axis=1), jnp.take(shapes, shared[1], axis=1)], axis=1
    )
    extended = extended_2(outgoing, (("dom", 1),), rim_width)
    node_table = jnp.concatenate(
        [shapes, extended[:, :rim_width], extended[:, 3 * rim_width :]], axis=1
    )
    gathered = jnp.take(node_table, connectivity.reshape(-1), axis=1).reshape(
        3, elem_count, slot_count, block_width
    )
    slot_live = (jnp.arange(slot_count)[None, :] < node_count[:, None]).astype(jnp.bfloat16)
    masked = recovery * slot_live[:, None, :, None]
    forces = jnp.einsum("ekna,aenm->ekm", masked, gathered, preferred_element_type=jnp.float32)
    forces = forces.astype(jnp.bfloat16).reshape(elem_count * recovery.shape[1], block_width)
    groups = lax.axis_size("mode")
    half_count = groups // 2
    partial_value = block_terms(
        forces, own_start, forces, own_start, amplitudes, frequencies, damping
    )

    def advance(turn_index, carried):
        incoming, summed = carried
        incoming = shifted(incoming, "mode", 1)
        source = (mode_index - turn_index) % groups * block_width
        factor = jnp.where(turn_index == half_count, jnp.float32(1.0), jnp.float32(2.0))
        summed = summed + factor * block_terms(
            forces, own_start, incoming, source, amplitudes, frequencies, damping
        )
        return (incoming, summed)

    carried = lax.fori_loop(1, half_count + 1, advance, (forces, partial_value))
    partial_value = carried[1]
    return lax.psum(partial_value, "mode")


def solution(mesh):
    in_specs = (
        P(None, "dom", "mode"),
        P("dom"),
        P(),
        P(),
        P(),
        P("dom", None, None, None),
        P("dom", None),
        P("dom"),
        P(None, "dom"),
    )
    out_specs = P("dom")
    special = mesh.shape["mode"] == 4
    step = four_groups if special else any_groups
    step = jax.shard_map(
        step, mesh=mesh, in_specs=in_specs, out_specs=out_specs, check_vma=False
    )
    return step
```

```python
import functools
import jax
import jax.numpy as jnp
from jax import lax
from jax.experimental import pallas as pl
from jax.experimental.pallas import tpu as pltpu
from jax.sharding import PartitionSpec as P


F32 = jnp.float32
BF16 = jnp.bfloat16
VMEM = pl.BlockSpec(memory_space=pltpu.VMEM)
HBM = pl.BlockSpec(memory_space=pltpu.HBM)
ANY = pl.BlockSpec(memory_space=pl.ANY)
SMEM = pl.BlockSpec(memory_space=pltpu.SMEM)


def call(kernel, out_shape, args, cost, smem=(), hbm=(), scratch=(), vmem=14 << 20, after=()):
    count = len(args)
    specs = [SMEM if i in smem else HBM if i in hbm else VMEM for i in range(count)]
    specs += [ANY] * len(after)
    many = isinstance(out_shape, (tuple, list))

    def body(*refs):
        kernel(*refs[:count], *refs[count + len(after) :])

    return pl.pallas_call(
        body,
        out_shape=out_shape,
        in_specs=specs,
        out_specs=[VMEM] * len(out_shape) if many else VMEM,
        scratch_shapes=list(scratch),
        cost_estimate=pl.CostEstimate(flops=int(1.1e9 * cost), bytes_accessed=0, transcendentals=0),
        compiler_params=pltpu.CompilerParams(vmem_limit_bytes=vmem),
    )(*args, *after)


def place():
    group = lax.axis_index("mode")
    return (group, group ^ 1, group ^ 2, group & 1, group >> 1, 1 - (group >> 1))


def add_kernel(left_ref, right_ref, out_ref):
    out_ref[...] = left_ref[...] + right_ref[...]


def gather_kernel(shared_ref, shapes_ref, first_ref, *refs):
    second_refs, (held_ref, sem) = refs[:-2], refs[-2:]
    dims, nodes, _ = held_ref.shape
    width = shared_ref.shape[1]
    load = pltpu.make_async_copy(shapes_ref, held_ref, sem)
    load.start()
    node = lax.broadcasted_iota(jnp.int32, (nodes, 2 * width), 0)
    odd = lax.axis_index("dom") & 1
    wanted = jnp.concatenate([shared_ref[pl.ds(1 - odd, 1), :], shared_ref[pl.ds(odd, 1), :]], axis=1)
    pick = jnp.where(node == wanted, 1.0, 0.0).astype(F32).T.astype(BF16)
    load.wait()
    for d in range(dims):
        got = jnp.dot(pick, held_ref[d], preferred_element_type=F32).astype(BF16)
        first_ref[d * width : (d + 1) * width, :] = got[:width]
        at = 0
        for second_ref in second_refs:
            lanes = slice(at, at + second_ref.shape[1])
            second_ref[d * width : (d + 1) * width, :] = got[width:, lanes]
            at = lanes.stop


def stats_kernel(mass_ref, shapes_ref, out_ref, mass_scr):
    dims, nodes, block = shapes_ref.shape
    column = jnp.broadcast_to(mass_ref[...], (8, nodes)).T
    mass_scr[...] = jnp.broadcast_to(column[:, 0:1], (nodes, 128))
    for at in range(0, block, 128):
        lanes = slice(at, at + 128)
        general = jnp.zeros((8, 128), F32)
        for d in range(dims):
            lever = jnp.zeros((8, 128), F32)
            for r in range(0, nodes, 16):
                wide = shapes_ref[d, r : r + 16, lanes].astype(F32)
                weighted = wide * mass_scr[r : r + 16, :]
                square = weighted * wide
                lever += weighted[:8] + weighted[8:]
                general += square[:8] + square[8:]
            out_ref[d : d + 1, lanes] = jnp.sum(lever, axis=0, keepdims=True)
        out_ref[dims : dims + 1, lanes] = jnp.sum(general, axis=0, keepdims=True)


def local_kernel(codes_ref, count_ref, recovery_ref, shapes_ref, local_ref, rim_ref, pick_ref, force_ref, got_scr):
    slots, elems = codes_ref.shape
    per_elem, dims = recovery_ref.shape[0], recovery_ref.shape[1]
    nodes, block = shapes_ref.shape[1], shapes_ref.shape[2]
    taken = slots * elems
    span = pick_ref.shape[1]
    node = lax.broadcasted_iota(jnp.int32, (span, elems), 0)
    width = (span - nodes) // 2
    even = 1 - (lax.axis_index("dom") & 1)
    swapped = jnp.where(node < nodes + width, node + width, node - width)
    node = jnp.where((node >= nodes) & (even == 1), swapped, node)
    for s in range(0, slots, 2):
        picks = []
        for q in range(s, min(s + 2, slots)):
            code = jnp.where(q < count_ref[...], codes_ref[q : q + 1, :], -1)
            picks.append(jnp.where(node == code, 1.0, 0.0).astype(F32))
        pick_ref[s * elems : s * elems + len(picks) * elems, :] = (
            jnp.concatenate(picks, axis=1).T.astype(BF16)
        )
    row = lax.broadcasted_iota(jnp.int32, (elems, 2 * elems), 0)
    column = lax.broadcasted_iota(jnp.int32, (elems, 2 * elems), 1)
    same = (column == row) | (column == row + elems)
    for k in range(per_elem):
        for d in range(dims):
            value = recovery_ref[k, d].astype(F32)
            for s in range(0, slots, 2):
                pair = jnp.concatenate([value[s : s + 1], value[s + 1 : s + 2]], axis=1)
                at = (d * slots + s) * elems
                force_ref[k * elems : (k + 1) * elems, at : at + 2 * elems] = jnp.where(
                    same, pair, 0.0
                ).astype(BF16)
    rim = span - nodes
    for d in range(dims):
        rows = slice(d * taken, (d + 1) * taken)
        value = jnp.dot(force_ref[:, rows], pick_ref[:, nodes:], preferred_element_type=F32)
        high = value.astype(BF16)
        rim_ref[:, d * rim : (d + 1) * rim] = high
        rim_ref[:, (dims + d) * rim : (dims + d + 1) * rim] = (value - high.astype(F32)).astype(BF16)
        got = jnp.dot(pick_ref[:, :nodes], shapes_ref[d], preferred_element_type=F32)
        got_scr[rows, :] = got.astype(BF16)
    for c in range(0, block, 256):
        local_ref[:, c : c + 256] = jnp.dot(
            force_ref[...], got_scr[:, c : c + 256], preferred_element_type=F32
        )


def mode_rows(freq, rate):
    alpha = rate * freq
    inverse = 1.0 / jnp.sqrt(alpha)
    return (freq * freq * inverse, inverse, 2.0 * alpha, 2.0 * (freq / rate))


def turn_rows(rows):
    pieces = [rows[:, c : c + 128] for c in range(0, rows.shape[1], 128)]
    while len(pieces) * 8 % 128:
        pieces.append(jnp.zeros((8, 128), F32))
    return [jnp.concatenate(pieces[c : c + 16], axis=0).T for c in range(0, len(pieces), 16)]


def place_modes(freq_ref, rate_ref, row_scr, col_scr, groups, side, block):
    side_rows = []
    for which, group in enumerate(groups):
        lanes = pl.ds(pl.multiple_of(group * block, block), block)
        rows = jnp.concatenate(list(mode_rows(freq_ref[:, lanes], rate_ref[:, lanes])) * 2, axis=0)
        row_scr[which * 8 : which * 8 + 8, :] = rows
        if which == side:
            side_rows.append(rows)
    if side is None:
        return
    turned = turn_rows(jnp.concatenate(side_rows, axis=1))
    for t in range(block // 128):
        for q in range(4):
            lane = t % 16 * 8 + q
            col_scr[q, t * 128 : (t + 1) * 128, :] = jnp.broadcast_to(
                turned[t // 16][:, lane : lane + 1], (128, 128)
            )


def fill_rho(row_scr, col_scr, out_ref, out_col, side_row, count, cols_at, col_off, tile):
    step = min(count, 256)
    cols = [
        jnp.broadcast_to(row_scr[cols_at + q : cols_at + q + 1, pl.ds(col_off, tile)], (8, tile))
        for q in range(4)
    ]

    @pl.loop(0, count // step)
    def _(t):
        for k in range(0, step, 8):
            at = pl.multiple_of(t * step, step) + k
            high, low, alpha, zeta = (col_scr[q, pl.ds(side_row + at, 8), :] for q in range(4))
            for c in range(0, tile, 128):
                col = [value[:, c : c + 128] for value in cols]
                spread = high * col[1] - low * col[0]
                pair = alpha + col[2]
                bottom = spread * spread + pair * (zeta + col[3])
                out_ref[pl.ds(at, 8), out_col + c : out_col + c + 128] = pair / bottom


def rho_near_kernel(freq_ref, rate_ref, diag_ref, mate_ref, col_scr, row_scr):
    block = diag_ref.shape[0]
    half = block // 2
    tile = block // 4
    own, mate, parity = place()[0], place()[1], place()[3]
    place_modes(freq_ref, rate_ref, row_scr, col_scr, (own, mate), 0, block)
    for j in range(4):
        fill_rho(row_scr, col_scr, diag_ref, j * tile, 0, (j + 1) * tile, 0, j * tile, tile)
    for i in range(2):
        for j in range(2):
            off = pl.multiple_of((i ^ parity) * half + j * tile, tile)
            fill_rho(row_scr, col_scr, mate_ref.at[i], j * tile, i * half, half, 8, off, tile)


def rho_own_kernel(freq_ref, rate_ref, side_ref, out_ref, row_scr):
    block = out_ref.shape[0]
    tile = block // 4
    place_modes(freq_ref, rate_ref, row_scr, None, (place()[2],), None, block)
    for j in range(4):
        fill_rho(row_scr, side_ref, out_ref, j * tile, 0, block, 0, j * tile, tile)


def rho_mate_kernel(freq_ref, rate_ref, out_ref, col_scr, row_scr):
    block = out_ref.shape[0]
    tile = block // 4
    place_modes(freq_ref, rate_ref, row_scr, col_scr, (place()[1], place()[2]), 0, block)
    for j in range(4):
        fill_rho(row_scr, col_scr, out_ref, j * tile, 0, block, 8, j * tile, tile)


def forces_kernel(at, dims, rim_ref, first_ref, second_ref, local_ref, all_ref, part_ref, rim_scr):
    comps, chunk = all_ref.shape
    width = first_ref.shape[0] // dims
    part = comps // 2
    lanes = slice(at, at + chunk)
    for copy in range(2):
        for d in range(dims):
            base = (copy * dims + d) * 2 * width
            rim_scr[base : base + width, :] = first_ref[d * width : (d + 1) * width, lanes]
            rim_scr[base + width : base + 2 * width, :] = second_ref[d * width : (d + 1) * width, :]
    for c in range(0, chunk, 256):
        total = jnp.dot(rim_ref[...], rim_scr[:, c : c + 256], preferred_element_type=F32)
        all_ref[:, c : c + 256] = (local_ref[:, at + c : at + c + 256] + total).astype(BF16)
    part_ref[...] = all_ref[pl.ds(pl.multiple_of(place()[5] * part, part), part), :]


def join_kernel(*refs):
    out_ref = refs[-1]
    size = refs[0].shape[0]
    for q, ref in enumerate(refs[:-1]):
        out_ref[q * size : (q + 1) * size, :] = ref[...]


def amps_kernel(stats_ref, extra_ref, spectral_ref, freq_ref, rate_ref, *out_refs):
    dims, block = spectral_ref.shape[0], stats_ref.shape[1]
    for q, out_ref in enumerate(out_refs):
        lanes = pl.ds(pl.multiple_of(place()[q] * block, block), block)
        rows = slice(q * (dims + 1), (q + 1) * (dims + 1))
        total = stats_ref[rows, :] + extra_ref[rows, :]
        scale = 2.0 * jnp.sqrt(freq_ref[:, lanes] / rate_ref[:, lanes])
        amps = total[:dims] / total[dims : dims + 1] * spectral_ref[:, lanes] * scale
        out_ref[...] = jnp.concatenate([amps, jnp.zeros((8 - dims, block), F32)], axis=0)


def fold(value):
    total = value[:, :128]
    for c in range(128, value.shape[1], 128):
        total = total + value[:, c : c + 128]
    return total


def to_row(acc, turned, per_elem):
    elems = acc.shape[0] // per_elem
    for k in range(per_elem):
        turned[pl.ds(k, elems, stride=per_elem), :] = acc[k * elems : (k + 1) * elems, :]
    pieces = jnp.concatenate([piece.astype(BF16) for piece in split(turned[...])], axis=1)
    return lax.dot_general(
        jnp.ones((8, pieces.shape[1]), BF16), pieces, (((1,), (1,)), ((), ())), preferred_element_type=F32
    )[0:1]


def split(value):
    top = value.astype(BF16).astype(F32)
    rest = value - top
    middle = rest.astype(BF16).astype(F32)
    return top, middle, rest - middle


def side_terms(out_scr, at, amps, dims):
    top, middle, last = split(amps[:dims])
    rows = jnp.concatenate([top, top, middle, middle, top, last], axis=0)
    rows = jnp.concatenate([rows, jnp.zeros((32 - rows.shape[0], rows.shape[1]), F32)], axis=0)
    for c in range(0, amps.shape[1], 512):
        stack = [rows[:, c + q : c + q + 128] for q in range(0, 512, 128)]
        turned = jnp.concatenate(stack, axis=0).T
        for q in range(4):
            out_scr[at + c + q * 128 : at + c + (q + 1) * 128, :] = turned[:, q * 32 : (q + 1) * 32].astype(BF16)


def col_terms(amps, dims, factor):
    top, middle, last = split(amps[:dims] * factor)
    rows = jnp.concatenate([top, middle, top, middle, last, top], axis=0)
    rows = jnp.concatenate([rows, jnp.zeros((32 - rows.shape[0], rows.shape[1]), F32)], axis=0)
    return rows.astype(BF16)


def weigh(rho, side, cols):
    return (rho * jnp.dot(side, cols, preferred_element_type=F32)).astype(BF16)


def near_kernel(dims, chunks, *refs):
    own_amps_ref, mate_amps_ref, diag_ref, cross_ref = refs[:4]
    own_refs, mate_refs = refs[4 : 4 + chunks], refs[4 + chunks : 4 + 2 * chunks]
    acc, side_scr, w_scr = refs[4 + 2 * chunks :]
    _, chunk = own_refs[0].shape
    block = diag_ref.shape[0]
    tile = block // 4
    half = block // 2
    parity = place()[3]

    def part(parts, at, size):
        return parts[at // chunk][:, at % chunk : at % chunk + size]

    def product(w, at, depth):
        total = None
        for c in range(at, at + depth, min(chunk, depth)):
            size = min(chunk, at + depth - c)
            got = jnp.dot(part(own_refs, c, size), w[c - at : c - at + size, :], preferred_element_type=F32)
            total = got if total is None else total + got
        return total

    side_terms(side_scr, 0, own_amps_ref[...], dims)
    once, twice = (col_terms(own_amps_ref[...], dims, factor) for factor in (1.0, 2.0))
    straight = parity == 0
    turn = 0
    for j in range(4):
        spot = slice(j * tile, (j + 1) * tile)
        for i in range(j + 1):
            rows = slice(i * tile, (i + 1) * tile)
            cols = twice if i < j else once
            w_scr[turn, rows, :] = weigh(diag_ref[rows, spot], side_scr[rows, :], cols[:, spot])
        got = product(w_scr.at[turn], 0, (j + 1) * tile)
        got = fold(got * part(own_refs, j * tile, tile).astype(F32))
        acc[...] = got if j == 0 else acc[...] + got
        turn = 1 - turn
    for i in range(2):
        for j in range(half // tile):
            here, there = i * half + j * tile, (1 - i) * half + j * tile
            cols = jnp.where(
                straight, mate_amps_ref[:, here : here + tile], mate_amps_ref[:, there : there + tile]
            )
            w_scr[turn, :half, :] = weigh(
                cross_ref[i, :, j * tile : (j + 1) * tile],
                side_scr[i * half : (i + 1) * half, :], col_terms(cols, dims, 2.0),
            )
            got = product(w_scr.at[turn], i * half, half)
            other = jnp.where(
                straight, part(mate_refs, here, tile).astype(F32), part(mate_refs, there, tile).astype(F32)
            )
            acc[...] += fold(got * other)
            turn = 1 - turn


def weights_kernel(dims, own_amps_ref, mate_amps_ref, far_amps_ref, own_ref, mate_ref, out_ref, side_scr):
    block = own_ref.shape[1]
    tile = block // 4
    cols = col_terms(far_amps_ref[...], dims, 2.0)
    for q, (amps_ref, rho_ref) in enumerate(((own_amps_ref, own_ref), (mate_amps_ref, mate_ref))):
        side_terms(side_scr, q * block, amps_ref[...], dims)
        for at in range(0, block, tile):
            base = q * block + at
            for c in range(0, block, tile):
                spot = slice(c, c + tile)
                out_ref[base : base + tile, spot] = weigh(
                    rho_ref[at : at + tile, spot], side_scr[base : base + tile, :], cols[:, spot]
                )


def far_kernel(at, per_elem, chunks, near_ref, w_ref, far_ref, *refs):
    sides, (out_ref, *scratch) = refs[: 2 * chunks], refs[2 * chunks :]
    _, chunk = sides[0].shape
    part = far_ref.shape[0]
    tile = min(256, chunk)
    rows = pl.ds(pl.multiple_of(place()[4] * part, part), part)
    total = near_ref[rows, :]
    for c in range(0, chunk, tile):
        spot = slice(at + c, at + c + tile)
        got = None
        for q, side_ref in enumerate(sides):
            w = w_ref[q * chunk : (q + 1) * chunk, spot]
            piece = jnp.dot(side_ref[rows, :], w, preferred_element_type=F32)
            got = piece if got is None else got + piece
        total = total + fold(got * far_ref[:, c : c + tile].astype(F32))
    acc = scratch[0] if scratch else out_ref
    acc[...] = near_ref[...]
    acc[rows, :] = total
    if scratch:
        out_ref[...] = to_row(acc, scratch[1], per_elem)


CHUNKS = 2


def four_groups(*args):
    return combined(*args)


def combined(
    shapes, masses, spectral, frequencies, damping, recovery, connectivity, node_count, shared
):
    dims, nodes, block = shapes.shape
    elems, slots = connectivity.shape
    per_elem = recovery.shape[1]
    comps = elems * per_elem
    part = comps // 2
    width = shared.shape[1]
    parts = lax.axis_size("dom")
    sds = jax.ShapeDtypeStruct
    halves = [[], []]
    for i in range(parts - 1):
        halves[i % 2] += [(i, i + 1), (i + 1, i)]
    freq = frequencies.reshape(1, -1)
    rate = damping.reshape(1, -1)

    chunk = block // CHUNKS
    outgoing, *others, held = call(
        gather_kernel,
        [sds((dims * width, size), BF16) for size in [block] + [chunk] * CHUNKS] + [sds(shapes.shape, BF16)],
        (shared, shapes),
        2.0, hbm=(1,), scratch=[pltpu.SemaphoreType.DMA],
    )
    first_rim = lax.ppermute(outgoing, "dom", halves[0])
    rims = [lax.ppermute(other, "dom", halves[1]) for other in others]
    stats = call(
        stats_kernel, sds((dims + 1, block), F32), (masses.reshape(1, nodes), held), 0.8,
        scratch=[pltpu.VMEM((nodes, 128), F32)],
    )
    rho_diag, rho_mate, sides = call(
        rho_near_kernel,
        (sds((block, block), F32), sds((2, block // 2, block // 2), F32), sds((4, block, 128), F32)),
        (freq, rate), 3.0,
        scratch=[pltpu.VMEM((16, block), F32)], after=(stats,),
    )
    far_own = call(
        rho_own_kernel, sds((block, block), F32), (freq, rate, sides), 1.9,
        scratch=[pltpu.VMEM((8, block), F32)],
    )
    taken = slots * elems
    local, rim = call(
        local_kernel, (sds((comps, block), F32), sds((comps, 4 * dims * width), BF16)),
        (connectivity.T, node_count.reshape(1, elems), recovery.transpose(1, 3, 2, 0), held),
        1.8, after=(far_own,),
        scratch=[
            pltpu.VMEM((taken, nodes + 2 * width), BF16), pltpu.VMEM((comps, dims * taken), BF16),
            pltpu.VMEM((dims * taken, block), BF16),
        ],
    )
    far_mate = call(
        rho_mate_kernel, sds((block, block), F32), (freq, rate), 2.5,
        scratch=[pltpu.VMEM((4, block, 128), F32), pltpu.VMEM((16, block), F32)],
    )
    given = [stats] + [lax.ppermute(stats, "mode", [(i, i ^ q) for i in range(4)]) for q in (1, 2)]
    stats = call(join_kernel, sds((3 * (dims + 1), block), F32), given, 0.5)
    order = [1 << q for q in range(1, parts.bit_length() - 1)] + [1]
    if parts & (parts - 1) or parts == 1:
        stats = lax.psum(stats, "dom")
        order = []
    extra = jnp.zeros_like(stats)
    for q, reach in enumerate(order):
        if q:
            stats = call(
                add_kernel, sds(stats.shape, F32), (stats, extra), 0.5, after=(rim,) if q == 1 else ()
            )
        extra = lax.ppermute(stats, "dom", [(i, i ^ reach) for i in range(parts)])
    amps, mate_amps, far_amps = call(
        amps_kernel, [sds((8, block), F32)] * 3, (stats, extra, spectral, freq, rate), 0.8,
    )

    own, mate, far = [], [], []
    for c in range(CHUNKS):
        forces, sent = call(
            functools.partial(forces_kernel, c * chunk, dims),
            [sds((comps, chunk), BF16), sds((part, chunk), BF16)],
            (rim, first_rim, rims[c], local), 0.8,
            scratch=[pltpu.VMEM((4 * dims * width, chunk), BF16)],
        )
        own.append(forces)
        far.append(lax.ppermute(sent, "mode", [(i, i ^ 2) for i in range(4)]))
        mate.append(lax.ppermute(forces, "mode", [(i, i ^ 1) for i in range(4)]))
    near = call(
        functools.partial(near_kernel, dims, CHUNKS), sds((comps, 128), F32),
        (amps, mate_amps, rho_diag, rho_mate, *own, *mate),
        3.4,
        scratch=[pltpu.VMEM((block, 32), BF16), pltpu.VMEM((2, block, block // 4), BF16)],
    )
    weights = call(
        functools.partial(weights_kernel, dims), sds((2 * block, block), BF16),
        (amps, mate_amps, far_amps, far_own, far_mate), 1.4,
        scratch=[pltpu.VMEM((2 * block, 32), BF16)],
    )
    value = near
    for c in range(CHUNKS):
        last = c == CHUNKS - 1
        value = call(
            functools.partial(far_kernel, c * chunk, per_elem, CHUNKS),
            sds((1, comps) if last else (comps, 128), F32),
            (value, weights, far[c], *own, *mate), 1.0,
            scratch=[pltpu.VMEM((comps, 128), F32)] * 2 if last else (),
        )
    value = value.reshape(comps)
    for reach in (1, 2):
        value = value + lax.ppermute(value, "mode", [(i, i ^ reach) for i in range(4)])
    return value


def extended_2(block, sides, width):
    for axis, dim in sides:
        count = lax.axis_size(axis)
        forward = [(i, i + 1) for i in range(count - 1)]
        backward = [(target, source) for source, target in forward]
        low = lax.ppermute(
            lax.slice_in_dim(block, block.shape[dim] - width, None, axis=dim), axis, forward
        )
        high = lax.ppermute(lax.slice_in_dim(block, 0, width, axis=dim), axis, backward)
        block = jnp.concatenate([low, block, high], axis=dim)
    return block


def shifted(value, axis, steps):
    count = lax.axis_size(axis)
    pairs = [(source, (source + steps) % count) for source in range(count)]
    return lax.ppermute(value, axis, pairs)


def correlation_block(freq_rows, freq_cols, rate_rows, rate_cols):
    ratio = freq_cols[None, :] / freq_rows[:, None]
    ratio_sq = ratio * ratio
    rate_row = rate_rows[:, None]
    rate_col = rate_cols[None, :]
    top_part = (
        8.0
        * jnp.sqrt(rate_row * rate_col)
        * (rate_row + ratio * rate_col)
        * ratio
        * jnp.sqrt(ratio)
    )
    spread = 1.0 - ratio_sq
    bottom_part = (
        spread * spread
        + 4.0 * rate_row * rate_col * ratio * (1.0 + ratio_sq)
        + 4.0 * (rate_row * rate_row + rate_col * rate_col) * ratio_sq
    )
    return top_part / bottom_part


def block_terms(own_forces, own_start, far_forces, far_start, amplitudes, frequencies, damping):
    row_count = own_forces.shape[1]
    col_count = far_forces.shape[1]
    freq_rows = lax.dynamic_slice_in_dim(frequencies, own_start, row_count)
    freq_cols = lax.dynamic_slice_in_dim(frequencies, far_start, col_count)
    rate_rows = lax.dynamic_slice_in_dim(damping, own_start, row_count)
    rate_cols = lax.dynamic_slice_in_dim(damping, far_start, col_count)
    correlation = correlation_block(freq_rows, freq_cols, rate_rows, rate_cols)
    amp_rows = lax.dynamic_slice_in_dim(amplitudes, own_start, row_count, 1)
    amp_cols = lax.dynamic_slice_in_dim(amplitudes, far_start, col_count, 1)
    weights = (amp_rows.T[:, :, None] * correlation[:, None, :] * amp_cols[None, :, :]).astype(
        jnp.bfloat16
    )
    weights = weights.reshape(row_count, 3 * col_count)
    projected = jnp.dot(own_forces, weights, preferred_element_type=jnp.float32)
    projected = projected.reshape(own_forces.shape[0], 3, col_count)
    far_wide = far_forces.astype(jnp.float32)
    return jnp.sum(projected * far_wide[:, None, :], axis=(1, 2))


def any_groups(
    shapes, masses, spectral, frequencies, damping, recovery, connectivity, node_count, shared
):
    rim_width = shared.shape[1]
    block_width = shapes.shape[2]
    elem_count = connectivity.shape[0]
    slot_count = connectivity.shape[1]
    mode_index = lax.axis_index("mode")
    own_start = mode_index * block_width
    shape_wide = shapes.astype(jnp.float32)
    weighted = masses[None, :, None] * shape_wide
    lever_arm = jnp.sum(weighted, axis=1)
    general = jnp.sum(weighted * shape_wide, axis=(0, 1))
    lever_sum, general_sum = lax.psum((lever_arm, general), "dom")
    own_spectral = lax.dynamic_slice_in_dim(spectral, own_start, block_width, 1)
    local_amps = lever_sum / general_sum[None, :] * own_spectral
    amplitudes = lax.all_gather(local_amps, "mode", axis=1, tiled=True)
    outgoing = jnp.concatenate(
        [jnp.take(shapes, shared[0], axis=1), jnp.take(shapes, shared[1], axis=1)], axis=1
    )
    extended = extended_2(outgoing, (("dom", 1),), rim_width)
    node_table = jnp.concatenate(
        [shapes, extended[:, :rim_width], extended[:, 3 * rim_width :]], axis=1
    )
    gathered = jnp.take(node_table, connectivity.reshape(-1), axis=1).reshape(
        3, elem_count, slot_count, block_width
    )
    slot_live = (jnp.arange(slot_count)[None, :] < node_count[:, None]).astype(jnp.bfloat16)
    masked = recovery * slot_live[:, None, :, None]
    forces = jnp.einsum("ekna,aenm->ekm", masked, gathered, preferred_element_type=jnp.float32)
    forces = forces.astype(jnp.bfloat16).reshape(elem_count * recovery.shape[1], block_width)
    groups = lax.axis_size("mode")
    half_count = groups // 2
    partial_value = block_terms(
        forces, own_start, forces, own_start, amplitudes, frequencies, damping
    )

    def advance(turn_index, carried):
        incoming, summed = carried
        incoming = shifted(incoming, "mode", 1)
        source = (mode_index - turn_index) % groups * block_width
        factor = jnp.where(turn_index == half_count, jnp.float32(1.0), jnp.float32(2.0))
        summed = summed + factor * block_terms(
            forces, own_start, incoming, source, amplitudes, frequencies, damping
        )
        return (incoming, summed)

    carried = lax.fori_loop(1, half_count + 1, advance, (forces, partial_value))
    partial_value = carried[1]
    return lax.psum(partial_value, "mode")


def solution(mesh):
    in_specs = (
        P(None, "dom", "mode"),
        P("dom"),
        P(),
        P(),
        P(),
        P("dom", None, None, None),
        P("dom", None),
        P("dom"),
        P(None, "dom"),
    )
    out_specs = P("dom")
    special = mesh.shape["mode"] == 4
    step = four_groups if special else any_groups
    step = jax.shard_map(
        step, mesh=mesh, in_specs=in_specs, out_specs=out_specs, check_vma=False
    )
    return step
```

```python
import functools
import jax
import jax.numpy as jnp
from jax import lax
from jax.experimental import pallas as pl
from jax.experimental.pallas import tpu as pltpu
from jax.sharding import PartitionSpec as P


F32 = jnp.float32
BF16 = jnp.bfloat16
VMEM = pl.BlockSpec(memory_space=pltpu.VMEM)
HBM = pl.BlockSpec(memory_space=pltpu.HBM)
ANY = pl.BlockSpec(memory_space=pl.ANY)
SMEM = pl.BlockSpec(memory_space=pltpu.SMEM)


def call(kernel, out_shape, args, cost, smem=(), hbm=(), scratch=(), vmem=14 << 20, after=()):
    count = len(args)
    specs = [SMEM if i in smem else HBM if i in hbm else VMEM for i in range(count)]
    specs += [ANY] * len(after)
    many = isinstance(out_shape, (tuple, list))

    def body(*refs):
        kernel(*refs[:count], *refs[count + len(after) :])

    return pl.pallas_call(
        body,
        out_shape=out_shape,
        in_specs=specs,
        out_specs=[VMEM] * len(out_shape) if many else VMEM,
        scratch_shapes=list(scratch),
        cost_estimate=pl.CostEstimate(flops=int(1.1e9 * cost), bytes_accessed=0, transcendentals=0),
        compiler_params=pltpu.CompilerParams(vmem_limit_bytes=vmem),
    )(*args, *after)


def place():
    group = lax.axis_index("mode")
    return (group, group ^ 1, group ^ 2, group & 1, group >> 1, 1 - (group >> 1))


def add_kernel(left_ref, right_ref, out_ref):
    out_ref[...] = left_ref[...] + right_ref[...]


def pick_kernel(shared_ref, pick_ref):
    nodes = pick_ref.shape[1]
    odd = lax.axis_index("dom") & 1
    wanted = jnp.concatenate([shared_ref[pl.ds(1 - odd, 1), :], shared_ref[pl.ds(odd, 1), :]], axis=1)
    node = lax.broadcasted_iota(jnp.int32, (nodes, wanted.shape[1]), 0)
    pick_ref[...] = jnp.where(node == wanted, 1.0, 0.0).astype(F32).T.astype(BF16)


def pair_rows_kernel(pick_ref, shapes_ref, out_ref):
    dims = shapes_ref.shape[0]
    width = out_ref.shape[0] // dims
    for d in range(dims):
        got = jnp.dot(pick_ref[:width, :], shapes_ref[d], preferred_element_type=F32)
        out_ref[d * width : (d + 1) * width, :] = got.astype(BF16)


def next_rows_kernel(pick_ref, shapes_ref, out_ref, held_ref, sem):
    dims = held_ref.shape[0]
    width = out_ref.shape[0] // dims
    load = pltpu.make_async_copy(shapes_ref, held_ref, sem)
    load.start()
    load.wait()
    for d in range(dims):
        got = jnp.dot(pick_ref[width:, :], held_ref[d], preferred_element_type=F32)
        out_ref[d * width : (d + 1) * width, :] = got.astype(BF16)


def stats_kernel(mass_ref, shapes_ref, out_ref, mass_scr):
    dims, nodes, block = shapes_ref.shape
    column = jnp.broadcast_to(mass_ref[...], (8, nodes)).T
    mass_scr[...] = jnp.broadcast_to(column[:, 0:1], (nodes, 128))
    for at in range(0, block, 128):
        lanes = slice(at, at + 128)
        general = jnp.zeros((8, 128), F32)
        for d in range(dims):
            lever = jnp.zeros((8, 128), F32)
            for r in range(0, nodes, 16):
                wide = shapes_ref[d, r : r + 16, lanes].astype(F32)
                weighted = wide * mass_scr[r : r + 16, :]
                square = weighted * wide
                lever += weighted[:8] + weighted[8:]
                general += square[:8] + square[8:]
            out_ref[d : d + 1, lanes] = jnp.sum(lever, axis=0, keepdims=True)
        out_ref[dims : dims + 1, lanes] = jnp.sum(general, axis=0, keepdims=True)


def local_kernel(codes_ref, count_ref, recovery_ref, shapes_ref, local_ref, rim_ref, pick_ref, force_ref, got_scr):
    slots, elems = codes_ref.shape
    per_elem, dims = recovery_ref.shape[0], recovery_ref.shape[1]
    nodes, block = shapes_ref.shape[1], shapes_ref.shape[2]
    taken = slots * elems
    span = pick_ref.shape[1]
    node = lax.broadcasted_iota(jnp.int32, (span, elems), 0)
    width = (span - nodes) // 2
    even = 1 - (lax.axis_index("dom") & 1)
    swapped = jnp.where(node < nodes + width, node + width, node - width)
    node = jnp.where((node >= nodes) & (even == 1), swapped, node)
    for s in range(0, slots, 2):
        picks = []
        for q in range(s, min(s + 2, slots)):
            code = jnp.where(q < count_ref[...], codes_ref[q : q + 1, :], -1)
            picks.append(jnp.where(node == code, 1.0, 0.0).astype(F32))
        pick_ref[s * elems : s * elems + len(picks) * elems, :] = (
            jnp.concatenate(picks, axis=1).T.astype(BF16)
        )
    row = lax.broadcasted_iota(jnp.int32, (elems, 2 * elems), 0)
    column = lax.broadcasted_iota(jnp.int32, (elems, 2 * elems), 1)
    same = (column == row) | (column == row + elems)
    for k in range(per_elem):
        for d in range(dims):
            value = recovery_ref[k, d].astype(F32)
            for s in range(0, slots, 2):
                pair = jnp.concatenate([value[s : s + 1], value[s + 1 : s + 2]], axis=1)
                at = (d * slots + s) * elems
                force_ref[k * elems : (k + 1) * elems, at : at + 2 * elems] = jnp.where(
                    same, pair, 0.0
                ).astype(BF16)
    rim = span - nodes
    for d in range(dims):
        rows = slice(d * taken, (d + 1) * taken)
        value = jnp.dot(force_ref[:, rows], pick_ref[:, nodes:], preferred_element_type=F32)
        high = value.astype(BF16)
        rim_ref[:, d * rim : (d + 1) * rim] = high
        rim_ref[:, (dims + d) * rim : (dims + d + 1) * rim] = (value - high.astype(F32)).astype(BF16)
        got = jnp.dot(pick_ref[:, :nodes], shapes_ref[d], preferred_element_type=F32)
        got_scr[rows, :] = got.astype(BF16)
    for c in range(0, block, 256):
        local_ref[:, c : c + 256] = jnp.dot(
            force_ref[...], got_scr[:, c : c + 256], preferred_element_type=F32
        )


def mode_rows(freq, rate):
    alpha = rate * freq
    inverse = 1.0 / jnp.sqrt(alpha)
    return (freq * freq * inverse, inverse, 2.0 * alpha, 2.0 * (freq / rate))


def turn_rows(rows):
    pieces = [rows[:, c : c + 128] for c in range(0, rows.shape[1], 128)]
    while len(pieces) * 8 % 128:
        pieces.append(jnp.zeros((8, 128), F32))
    return [jnp.concatenate(pieces[c : c + 16], axis=0).T for c in range(0, len(pieces), 16)]


def place_modes(freq_ref, rate_ref, row_scr, col_scr, groups, side, block):
    side_rows = []
    for which, group in enumerate(groups):
        lanes = pl.ds(pl.multiple_of(group * block, block), block)
        rows = jnp.concatenate(list(mode_rows(freq_ref[:, lanes], rate_ref[:, lanes])) * 2, axis=0)
        row_scr[which * 8 : which * 8 + 8, :] = rows
        if which == side:
            side_rows.append(rows)
    if side is None:
        return
    turned = turn_rows(jnp.concatenate(side_rows, axis=1))
    for t in range(block // 128):
        for q in range(4):
            lane = t % 16 * 8 + q
            col_scr[q, t * 128 : (t + 1) * 128, :] = jnp.broadcast_to(
                turned[t // 16][:, lane : lane + 1], (128, 128)
            )


def fill_rho(row_scr, col_scr, out_ref, out_col, side_row, count, cols_at, col_off, tile):
    step = min(count, 256)
    cols = [
        jnp.broadcast_to(row_scr[cols_at + q : cols_at + q + 1, pl.ds(col_off, tile)], (8, tile))
        for q in range(4)
    ]

    @pl.loop(0, count // step)
    def _(t):
        for k in range(0, step, 8):
            at = pl.multiple_of(t * step, step) + k
            high, low, alpha, zeta = (col_scr[q, pl.ds(side_row + at, 8), :] for q in range(4))
            for c in range(0, tile, 128):
                col = [value[:, c : c + 128] for value in cols]
                spread = high * col[1] - low * col[0]
                pair = alpha + col[2]
                bottom = spread * spread + pair * (zeta + col[3])
                out_ref[pl.ds(at, 8), out_col + c : out_col + c + 128] = pair / bottom


def rho_near_kernel(freq_ref, rate_ref, diag_ref, mate_ref, col_scr, row_scr):
    block = diag_ref.shape[0]
    half = block // 2
    tile = block // 4
    own, mate, parity = place()[0], place()[1], place()[3]
    place_modes(freq_ref, rate_ref, row_scr, col_scr, (own, mate), 0, block)
    for j in range(4):
        fill_rho(row_scr, col_scr, diag_ref, j * tile, 0, (j + 1) * tile, 0, j * tile, tile)
    for i in range(2):
        for j in range(2):
            off = pl.multiple_of((i ^ parity) * half + j * tile, tile)
            fill_rho(row_scr, col_scr, mate_ref.at[i], j * tile, i * half, half, 8, off, tile)


def rho_own_kernel(freq_ref, rate_ref, side_ref, out_ref, row_scr):
    block = out_ref.shape[0]
    tile = block // 4
    place_modes(freq_ref, rate_ref, row_scr, None, (place()[2],), None, block)
    for j in range(4):
        fill_rho(row_scr, side_ref, out_ref, j * tile, 0, block, 0, j * tile, tile)


def rho_mate_kernel(freq_ref, rate_ref, out_ref, col_scr, row_scr):
    block = out_ref.shape[0]
    tile = block // 4
    place_modes(freq_ref, rate_ref, row_scr, col_scr, (place()[1], place()[2]), 0, block)
    for j in range(4):
        fill_rho(row_scr, col_scr, out_ref, j * tile, 0, block, 8, j * tile, tile)


def forces_kernel(dims, rim_ref, first_ref, second_ref, local_ref, all_ref, *refs):
    part_refs, rim_scr = refs[:-1], refs[-1]
    comps, block = all_ref.shape
    width = first_ref.shape[0] // dims
    part = comps // 2
    rows = pl.ds(pl.multiple_of(place()[5] * part, part), part)
    for copy in range(2):
        for d in range(dims):
            base = (copy * dims + d) * 2 * width
            rim_scr[base : base + width, :] = first_ref[d * width : (d + 1) * width, :]
            rim_scr[base + width : base + 2 * width, :] = second_ref[d * width : (d + 1) * width, :]
    for c in range(0, block, 256):
        total = jnp.dot(rim_ref[...], rim_scr[:, c : c + 256], preferred_element_type=F32)
        all_ref[:, c : c + 256] = (local_ref[:, c : c + 256] + total).astype(BF16)
    at = 0
    for part_ref in part_refs:
        part_ref[...] = all_ref[rows, at : at + part_ref.shape[1]]
        at += part_ref.shape[1]


def join_kernel(*refs):
    out_ref = refs[-1]
    size = refs[0].shape[0]
    for q, ref in enumerate(refs[:-1]):
        out_ref[q * size : (q + 1) * size, :] = ref[...]


def amps_kernel(stats_ref, extra_ref, spectral_ref, freq_ref, rate_ref, *out_refs):
    dims, block = spectral_ref.shape[0], stats_ref.shape[1]
    for q, out_ref in enumerate(out_refs):
        lanes = pl.ds(pl.multiple_of(place()[q] * block, block), block)
        rows = slice(q * (dims + 1), (q + 1) * (dims + 1))
        total = stats_ref[rows, :] + extra_ref[rows, :]
        scale = 2.0 * jnp.sqrt(freq_ref[:, lanes] / rate_ref[:, lanes])
        amps = total[:dims] / total[dims : dims + 1] * spectral_ref[:, lanes] * scale
        out_ref[...] = jnp.concatenate([amps, jnp.zeros((8 - dims, block), F32)], axis=0)


def fold(value):
    total = value[:, :128]
    for c in range(128, value.shape[1], 128):
        total = total + value[:, c : c + 128]
    return total


def to_row(acc, turned, per_elem):
    elems = acc.shape[0] // per_elem
    for k in range(per_elem):
        turned[pl.ds(k, elems, stride=per_elem), :] = acc[k * elems : (k + 1) * elems, :]
    pieces = jnp.concatenate([piece.astype(BF16) for piece in split(turned[...])], axis=1)
    return lax.dot_general(
        jnp.ones((8, pieces.shape[1]), BF16), pieces, (((1,), (1,)), ((), ())), preferred_element_type=F32
    )[0:1]


def split(value):
    top = value.astype(BF16).astype(F32)
    rest = value - top
    middle = rest.astype(BF16).astype(F32)
    return top, middle, rest - middle


def side_terms(out_scr, at, amps, dims):
    top, middle, last = split(amps[:dims])
    rows = jnp.concatenate([top, top, middle, middle, top, last], axis=0)
    rows = jnp.concatenate([rows, jnp.zeros((32 - rows.shape[0], rows.shape[1]), F32)], axis=0)
    for c in range(0, amps.shape[1], 512):
        stack = [rows[:, c + q : c + q + 128] for q in range(0, 512, 128)]
        turned = jnp.concatenate(stack, axis=0).T
        for q in range(4):
            out_scr[at + c + q * 128 : at + c + (q + 1) * 128, :] = turned[:, q * 32 : (q + 1) * 32].astype(BF16)


def col_terms(amps, dims, factor):
    top, middle, last = split(amps[:dims] * factor)
    rows = jnp.concatenate([top, middle, top, middle, last, top], axis=0)
    rows = jnp.concatenate([rows, jnp.zeros((32 - rows.shape[0], rows.shape[1]), F32)], axis=0)
    return rows.astype(BF16)


def weigh(rho, side, cols):
    return (rho * jnp.dot(side, cols, preferred_element_type=F32)).astype(BF16)


def near_kernel(dims, chunks, *refs):
    own_amps_ref, mate_amps_ref, diag_ref, cross_ref = refs[:4]
    own_refs, mate_refs = refs[4 : 4 + chunks], refs[4 + chunks : 4 + 2 * chunks]
    acc, side_scr, w_scr = refs[4 + 2 * chunks :]
    _, chunk = own_refs[0].shape
    block = diag_ref.shape[0]
    tile = block // 4
    half = block // 2
    parity = place()[3]

    def part(parts, at, size):
        return parts[at // chunk][:, at % chunk : at % chunk + size]

    def product(w, at, depth):
        total = None
        for c in range(at, at + depth, min(chunk, depth)):
            size = min(chunk, at + depth - c)
            got = jnp.dot(part(own_refs, c, size), w[c - at : c - at + size, :], preferred_element_type=F32)
            total = got if total is None else total + got
        return total

    side_terms(side_scr, 0, own_amps_ref[...], dims)
    once, twice = (col_terms(own_amps_ref[...], dims, factor) for factor in (1.0, 2.0))
    straight = parity == 0
    turn = 0
    for j in range(4):
        spot = slice(j * tile, (j + 1) * tile)
        for i in range(j + 1):
            rows = slice(i * tile, (i + 1) * tile)
            cols = twice if i < j else once
            w_scr[turn, rows, :] = weigh(diag_ref[rows, spot], side_scr[rows, :], cols[:, spot])
        got = product(w_scr.at[turn], 0, (j + 1) * tile)
        got = fold(got * part(own_refs, j * tile, tile).astype(F32))
        acc[...] = got if j == 0 else acc[...] + got
        turn = 1 - turn
    for i in range(2):
        for j in range(half // tile):
            here, there = i * half + j * tile, (1 - i) * half + j * tile
            cols = jnp.where(
                straight, mate_amps_ref[:, here : here + tile], mate_amps_ref[:, there : there + tile]
            )
            w_scr[turn, :half, :] = weigh(
                cross_ref[i, :, j * tile : (j + 1) * tile],
                side_scr[i * half : (i + 1) * half, :], col_terms(cols, dims, 2.0),
            )
            got = product(w_scr.at[turn], i * half, half)
            other = jnp.where(
                straight, part(mate_refs, here, tile).astype(F32), part(mate_refs, there, tile).astype(F32)
            )
            acc[...] += fold(got * other)
            turn = 1 - turn


def weights_kernel(dims, own_amps_ref, mate_amps_ref, far_amps_ref, own_ref, mate_ref, out_ref, side_scr):
    block = own_ref.shape[1]
    tile = block // 4
    cols = col_terms(far_amps_ref[...], dims, 2.0)
    for q, (amps_ref, rho_ref) in enumerate(((own_amps_ref, own_ref), (mate_amps_ref, mate_ref))):
        side_terms(side_scr, q * block, amps_ref[...], dims)
        for at in range(0, block, tile):
            base = q * block + at
            for c in range(0, block, tile):
                spot = slice(c, c + tile)
                out_ref[base : base + tile, spot] = weigh(
                    rho_ref[at : at + tile, spot], side_scr[base : base + tile, :], cols[:, spot]
                )


def far_kernel(at, per_elem, near_ref, w_ref, far_ref, own_ref, mate_ref, out_ref, *scratch):
    _, block = own_ref.shape
    part, chunk = far_ref.shape
    tile = min(256, chunk)
    rows = pl.ds(pl.multiple_of(place()[4] * part, part), part)
    total = near_ref[rows, :]
    for c in range(0, chunk, tile):
        spot = slice(at + c, at + c + tile)
        got = jnp.dot(own_ref[rows, :], w_ref[:block, spot], preferred_element_type=F32)
        got = got + jnp.dot(mate_ref[rows, :], w_ref[block:, spot], preferred_element_type=F32)
        total = total + fold(got * far_ref[:, c : c + tile].astype(F32))
    acc = scratch[0] if scratch else out_ref
    acc[...] = near_ref[...]
    acc[rows, :] = total
    if scratch:
        out_ref[...] = to_row(acc, scratch[1], per_elem)


def four_groups(*args):
    return combined(*args)


def combined(
    shapes, masses, spectral, frequencies, damping, recovery, connectivity, node_count, shared
):
    dims, nodes, block = shapes.shape
    elems, slots = connectivity.shape
    per_elem = recovery.shape[1]
    comps = elems * per_elem
    part = comps // 2
    width = shared.shape[1]
    parts = lax.axis_size("dom")
    sds = jax.ShapeDtypeStruct
    halves = [[], []]
    for i in range(parts - 1):
        halves[i % 2] += [(i, i + 1), (i + 1, i)]
    freq = frequencies.reshape(1, -1)
    rate = damping.reshape(1, -1)

    picked = call(pick_kernel, sds((2 * width, nodes), BF16), (shared,), 2.0)
    rows = sds((dims * width, block), BF16)
    outgoing = call(pair_rows_kernel, rows, (picked, shapes), 0.4)
    other, held = call(
        next_rows_kernel, [rows, sds(shapes.shape, BF16)], (picked, shapes), 0.7, hbm=(1,),
        scratch=[pltpu.SemaphoreType.DMA],
    )
    rims = (lax.ppermute(outgoing, "dom", halves[0]), lax.ppermute(other, "dom", halves[1]))
    stats = call(
        stats_kernel, sds((dims + 1, block), F32), (masses.reshape(1, nodes), held), 0.8,
        scratch=[pltpu.VMEM((nodes, 128), F32)],
    )
    rho_diag, rho_mate, sides = call(
        rho_near_kernel,
        (sds((block, block), F32), sds((2, block // 2, block // 2), F32), sds((4, block, 128), F32)),
        (freq, rate), 3.0,
        scratch=[pltpu.VMEM((16, block), F32)], after=(stats,),
    )
    far_own = call(
        rho_own_kernel, sds((block, block), F32), (freq, rate, sides), 1.9,
        scratch=[pltpu.VMEM((8, block), F32)],
    )
    taken = slots * elems
    local, rim = call(
        local_kernel, (sds((comps, block), F32), sds((comps, 4 * dims * width), BF16)),
        (connectivity.T, node_count.reshape(1, elems), recovery.transpose(1, 3, 2, 0), held),
        1.8, after=(far_own,),
        scratch=[
            pltpu.VMEM((taken, nodes + 2 * width), BF16), pltpu.VMEM((comps, dims * taken), BF16),
            pltpu.VMEM((dims * taken, block), BF16),
        ],
    )
    far_mate = call(
        rho_mate_kernel, sds((block, block), F32), (freq, rate), 2.5,
        scratch=[pltpu.VMEM((4, block, 128), F32), pltpu.VMEM((16, block), F32)],
    )
    given = [stats] + [lax.ppermute(stats, "mode", [(i, i ^ q) for i in range(4)]) for q in (1, 2)]
    stats = call(join_kernel, sds((3 * (dims + 1), block), F32), given, 0.5)
    order = [1 << q for q in range(1, parts.bit_length() - 1)] + [1]
    if parts & (parts - 1) or parts == 1:
        stats = lax.psum(stats, "dom")
        order = []
    extra = jnp.zeros_like(stats)
    for q, reach in enumerate(order):
        if q:
            stats = call(
                add_kernel, sds(stats.shape, F32), (stats, extra), 0.5, after=(rim,) if q == 1 else ()
            )
        extra = lax.ppermute(stats, "dom", [(i, i ^ reach) for i in range(parts)])
    amps, mate_amps, far_amps = call(
        amps_kernel, [sds((8, block), F32)] * 3, (stats, extra, spectral, freq, rate), 0.8,
    )

    cuts = [block - block // 4, block // 4]
    forces, *sent = call(
        functools.partial(forces_kernel, dims),
        [sds((comps, block), BF16)] + [sds((part, cut), BF16) for cut in cuts],
        (rim, *rims, local), 1.4,
        scratch=[pltpu.VMEM((4 * dims * width, block), BF16)],
    )
    far = [lax.ppermute(value, "mode", [(i, i ^ 2) for i in range(4)]) for value in sent]
    mate = lax.ppermute(forces, "mode", [(i, i ^ 1) for i in range(4)])
    near = call(
        functools.partial(near_kernel, dims, 1), sds((comps, 128), F32),
        (amps, mate_amps, rho_diag, rho_mate, forces, mate),
        3.4,
        scratch=[pltpu.VMEM((block, 32), BF16), pltpu.VMEM((2, block, block // 4), BF16)],
    )
    weights = call(
        functools.partial(weights_kernel, dims), sds((2 * block, block), BF16),
        (amps, mate_amps, far_amps, far_own, far_mate), 1.4,
        scratch=[pltpu.VMEM((2 * block, 32), BF16)],
    )
    value = near
    at = 0
    for c, cut in enumerate(cuts):
        last = c == len(cuts) - 1
        value = call(
            functools.partial(far_kernel, at, per_elem), sds((1, comps) if last else (comps, 128), F32),
            (value, weights, far[c], forces, mate), 2.1 * cut / block,
            scratch=[pltpu.VMEM((comps, 128), F32)] * 2 if last else (),
        )
        at += cut
    value = value.reshape(comps)
    for reach in (1, 2):
        value = value + lax.ppermute(value, "mode", [(i, i ^ reach) for i in range(4)])
    return value


def extended_2(block, sides, width):
    for axis, dim in sides:
        count = lax.axis_size(axis)
        forward = [(i, i + 1) for i in range(count - 1)]
        backward = [(target, source) for source, target in forward]
        low = lax.ppermute(
            lax.slice_in_dim(block, block.shape[dim] - width, None, axis=dim), axis, forward
        )
        high = lax.ppermute(lax.slice_in_dim(block, 0, width, axis=dim), axis, backward)
        block = jnp.concatenate([low, block, high], axis=dim)
    return block


def shifted(value, axis, steps):
    count = lax.axis_size(axis)
    pairs = [(source, (source + steps) % count) for source in range(count)]
    return lax.ppermute(value, axis, pairs)


def correlation_block(freq_rows, freq_cols, rate_rows, rate_cols):
    ratio = freq_cols[None, :] / freq_rows[:, None]
    ratio_sq = ratio * ratio
    rate_row = rate_rows[:, None]
    rate_col = rate_cols[None, :]
    top_part = (
        8.0
        * jnp.sqrt(rate_row * rate_col)
        * (rate_row + ratio * rate_col)
        * ratio
        * jnp.sqrt(ratio)
    )
    spread = 1.0 - ratio_sq
    bottom_part = (
        spread * spread
        + 4.0 * rate_row * rate_col * ratio * (1.0 + ratio_sq)
        + 4.0 * (rate_row * rate_row + rate_col * rate_col) * ratio_sq
    )
    return top_part / bottom_part


def block_terms(own_forces, own_start, far_forces, far_start, amplitudes, frequencies, damping):
    row_count = own_forces.shape[1]
    col_count = far_forces.shape[1]
    freq_rows = lax.dynamic_slice_in_dim(frequencies, own_start, row_count)
    freq_cols = lax.dynamic_slice_in_dim(frequencies, far_start, col_count)
    rate_rows = lax.dynamic_slice_in_dim(damping, own_start, row_count)
    rate_cols = lax.dynamic_slice_in_dim(damping, far_start, col_count)
    correlation = correlation_block(freq_rows, freq_cols, rate_rows, rate_cols)
    amp_rows = lax.dynamic_slice_in_dim(amplitudes, own_start, row_count, 1)
    amp_cols = lax.dynamic_slice_in_dim(amplitudes, far_start, col_count, 1)
    weights = (amp_rows.T[:, :, None] * correlation[:, None, :] * amp_cols[None, :, :]).astype(
        jnp.bfloat16
    )
    weights = weights.reshape(row_count, 3 * col_count)
    projected = jnp.dot(own_forces, weights, preferred_element_type=jnp.float32)
    projected = projected.reshape(own_forces.shape[0], 3, col_count)
    far_wide = far_forces.astype(jnp.float32)
    return jnp.sum(projected * far_wide[:, None, :], axis=(1, 2))


def any_groups(
    shapes, masses, spectral, frequencies, damping, recovery, connectivity, node_count, shared
):
    rim_width = shared.shape[1]
    block_width = shapes.shape[2]
    elem_count = connectivity.shape[0]
    slot_count = connectivity.shape[1]
    mode_index = lax.axis_index("mode")
    own_start = mode_index * block_width
    shape_wide = shapes.astype(jnp.float32)
    weighted = masses[None, :, None] * shape_wide
    lever_arm = jnp.sum(weighted, axis=1)
    general = jnp.sum(weighted * shape_wide, axis=(0, 1))
    lever_sum, general_sum = lax.psum((lever_arm, general), "dom")
    own_spectral = lax.dynamic_slice_in_dim(spectral, own_start, block_width, 1)
    local_amps = lever_sum / general_sum[None, :] * own_spectral
    amplitudes = lax.all_gather(local_amps, "mode", axis=1, tiled=True)
    outgoing = jnp.concatenate(
        [jnp.take(shapes, shared[0], axis=1), jnp.take(shapes, shared[1], axis=1)], axis=1
    )
    extended = extended_2(outgoing, (("dom", 1),), rim_width)
    node_table = jnp.concatenate(
        [shapes, extended[:, :rim_width], extended[:, 3 * rim_width :]], axis=1
    )
    gathered = jnp.take(node_table, connectivity.reshape(-1), axis=1).reshape(
        3, elem_count, slot_count, block_width
    )
    slot_live = (jnp.arange(slot_count)[None, :] < node_count[:, None]).astype(jnp.bfloat16)
    masked = recovery * slot_live[:, None, :, None]
    forces = jnp.einsum("ekna,aenm->ekm", masked, gathered, preferred_element_type=jnp.float32)
    forces = forces.astype(jnp.bfloat16).reshape(elem_count * recovery.shape[1], block_width)
    groups = lax.axis_size("mode")
    half_count = groups // 2
    partial_value = block_terms(
        forces, own_start, forces, own_start, amplitudes, frequencies, damping
    )

    def advance(turn_index, carried):
        incoming, summed = carried
        incoming = shifted(incoming, "mode", 1)
        source = (mode_index - turn_index) % groups * block_width
        factor = jnp.where(turn_index == half_count, jnp.float32(1.0), jnp.float32(2.0))
        summed = summed + factor * block_terms(
            forces, own_start, incoming, source, amplitudes, frequencies, damping
        )
        return (incoming, summed)

    carried = lax.fori_loop(1, half_count + 1, advance, (forces, partial_value))
    partial_value = carried[1]
    return lax.psum(partial_value, "mode")


def solution(mesh):
    in_specs = (
        P(None, "dom", "mode"),
        P("dom"),
        P(),
        P(),
        P(),
        P("dom", None, None, None),
        P("dom", None),
        P("dom"),
        P(None, "dom"),
    )
    out_specs = P("dom")
    special = mesh.shape["mode"] == 4
    step = four_groups if special else any_groups
    step = jax.shard_map(
        step, mesh=mesh, in_specs=in_specs, out_specs=out_specs, check_vma=False
    )
    return step
```

```python
import functools
import jax
import jax.numpy as jnp
from jax import lax
from jax.experimental import pallas as pl
from jax.experimental.pallas import tpu as pltpu
from jax.sharding import PartitionSpec as P


F32 = jnp.float32
BF16 = jnp.bfloat16
VMEM = pl.BlockSpec(memory_space=pltpu.VMEM)
HBM = pl.BlockSpec(memory_space=pltpu.HBM)
ANY = pl.BlockSpec(memory_space=pl.ANY)
SMEM = pl.BlockSpec(memory_space=pltpu.SMEM)


def call(kernel, out_shape, args, cost, smem=(), hbm=(), scratch=(), vmem=14 << 20, after=()):
    count = len(args)
    specs = [SMEM if i in smem else HBM if i in hbm else VMEM for i in range(count)]
    specs += [ANY] * len(after)
    many = isinstance(out_shape, (tuple, list))

    def body(*refs):
        kernel(*refs[:count], *refs[count + len(after) :])

    return pl.pallas_call(
        body,
        out_shape=out_shape,
        in_specs=specs,
        out_specs=[VMEM] * len(out_shape) if many else VMEM,
        scratch_shapes=list(scratch),
        cost_estimate=pl.CostEstimate(flops=int(1.1e9 * cost), bytes_accessed=0, transcendentals=0),
        compiler_params=pltpu.CompilerParams(vmem_limit_bytes=vmem),
    )(*args, *after)


def place():
    group = lax.axis_index("mode")
    return (group, group ^ 1, group ^ 2, group & 1, group >> 1, 1 - (group >> 1))


def add_kernel(left_ref, right_ref, out_ref):
    out_ref[...] = left_ref[...] + right_ref[...]


def pick_kernel(shared_ref, pick_ref):
    nodes = pick_ref.shape[1]
    odd = lax.axis_index("dom") & 1
    wanted = jnp.concatenate([shared_ref[pl.ds(1 - odd, 1), :], shared_ref[pl.ds(odd, 1), :]], axis=1)
    node = lax.broadcasted_iota(jnp.int32, (nodes, wanted.shape[1]), 0)
    pick_ref[...] = jnp.where(node == wanted, 1.0, 0.0).astype(F32).T.astype(BF16)


def pair_rows_kernel(pick_ref, shapes_ref, out_ref):
    dims = shapes_ref.shape[0]
    width = out_ref.shape[0] // dims
    for d in range(dims):
        got = jnp.dot(pick_ref[:width, :], shapes_ref[d], preferred_element_type=F32)
        out_ref[d * width : (d + 1) * width, :] = got.astype(BF16)


def next_rows_kernel(pick_ref, shapes_ref, out_ref, held_ref, sem):
    dims = held_ref.shape[0]
    width = out_ref.shape[0] // dims
    load = pltpu.make_async_copy(shapes_ref, held_ref, sem)
    load.start()
    load.wait()
    for d in range(dims):
        got = jnp.dot(pick_ref[width:, :], held_ref[d], preferred_element_type=F32)
        out_ref[d * width : (d + 1) * width, :] = got.astype(BF16)


def stats_kernel(mass_ref, shapes_ref, out_ref, mass_scr):
    dims, nodes, block = shapes_ref.shape
    column = jnp.broadcast_to(mass_ref[...], (8, nodes)).T
    mass_scr[...] = jnp.broadcast_to(column[:, 0:1], (nodes, 128))
    for at in range(0, block, 128):
        lanes = slice(at, at + 128)
        general = jnp.zeros((8, 128), F32)
        for d in range(dims):
            lever = jnp.zeros((8, 128), F32)
            for r in range(0, nodes, 16):
                wide = shapes_ref[d, r : r + 16, lanes].astype(F32)
                weighted = wide * mass_scr[r : r + 16, :]
                square = weighted * wide
                lever += weighted[:8] + weighted[8:]
                general += square[:8] + square[8:]
            out_ref[d : d + 1, lanes] = jnp.sum(lever, axis=0, keepdims=True)
        out_ref[dims : dims + 1, lanes] = jnp.sum(general, axis=0, keepdims=True)


def local_kernel(codes_ref, count_ref, recovery_ref, shapes_ref, local_ref, rim_ref, pick_ref, force_ref, got_scr):
    slots, elems = codes_ref.shape
    per_elem, dims = recovery_ref.shape[0], recovery_ref.shape[1]
    nodes, block = shapes_ref.shape[1], shapes_ref.shape[2]
    taken = slots * elems
    span = pick_ref.shape[1]
    node = lax.broadcasted_iota(jnp.int32, (span, elems), 0)
    width = (span - nodes) // 2
    even = 1 - (lax.axis_index("dom") & 1)
    swapped = jnp.where(node < nodes + width, node + width, node - width)
    node = jnp.where((node >= nodes) & (even == 1), swapped, node)
    for s in range(0, slots, 2):
        picks = []
        for q in range(s, min(s + 2, slots)):
            code = jnp.where(q < count_ref[...], codes_ref[q : q + 1, :], -1)
            picks.append(jnp.where(node == code, 1.0, 0.0).astype(F32))
        pick_ref[s * elems : s * elems + len(picks) * elems, :] = (
            jnp.concatenate(picks, axis=1).T.astype(BF16)
        )
    row = lax.broadcasted_iota(jnp.int32, (elems, 2 * elems), 0)
    column = lax.broadcasted_iota(jnp.int32, (elems, 2 * elems), 1)
    same = (column == row) | (column == row + elems)
    for k in range(per_elem):
        for d in range(dims):
            value = recovery_ref[k, d].astype(F32)
            for s in range(0, slots, 2):
                pair = jnp.concatenate([value[s : s + 1], value[s + 1 : s + 2]], axis=1)
                at = (d * slots + s) * elems
                force_ref[k * elems : (k + 1) * elems, at : at + 2 * elems] = jnp.where(
                    same, pair, 0.0
                ).astype(BF16)
    rim = span - nodes
    for d in range(dims):
        rows = slice(d * taken, (d + 1) * taken)
        value = jnp.dot(force_ref[:, rows], pick_ref[:, nodes:], preferred_element_type=F32)
        high = value.astype(BF16)
        rim_ref[:, d * rim : (d + 1) * rim] = high
        rim_ref[:, (dims + d) * rim : (dims + d + 1) * rim] = (value - high.astype(F32)).astype(BF16)
        got = jnp.dot(pick_ref[:, :nodes], shapes_ref[d], preferred_element_type=F32)
        got_scr[rows, :] = got.astype(BF16)
    for c in range(0, block, 256):
        local_ref[:, c : c + 256] = jnp.dot(
            force_ref[...], got_scr[:, c : c + 256], preferred_element_type=F32
        )


def mode_rows(freq, rate):
    alpha = rate * freq
    inverse = 1.0 / jnp.sqrt(alpha)
    return (freq * freq * inverse, inverse, 2.0 * alpha, 2.0 * (freq / rate))


def turn_rows(rows):
    pieces = [rows[:, c : c + 128] for c in range(0, rows.shape[1], 128)]
    while len(pieces) * 8 % 128:
        pieces.append(jnp.zeros((8, 128), F32))
    return [jnp.concatenate(pieces[c : c + 16], axis=0).T for c in range(0, len(pieces), 16)]


def place_modes(freq_ref, rate_ref, row_scr, col_scr, groups, side, block):
    side_rows = []
    for which, group in enumerate(groups):
        lanes = pl.ds(pl.multiple_of(group * block, block), block)
        rows = jnp.concatenate(list(mode_rows(freq_ref[:, lanes], rate_ref[:, lanes])) * 2, axis=0)
        row_scr[which * 8 : which * 8 + 8, :] = rows
        if which == side:
            side_rows.append(rows)
    if side is None:
        return
    turned = turn_rows(jnp.concatenate(side_rows, axis=1))
    for t in range(block // 128):
        for q in range(4):
            lane = t % 16 * 8 + q
            col_scr[q, t * 128 : (t + 1) * 128, :] = jnp.broadcast_to(
                turned[t // 16][:, lane : lane + 1], (128, 128)
            )


def fill_rho(row_scr, col_scr, out_ref, out_col, side_row, count, cols_at, col_off, tile):
    step = min(count, 256)
    cols = [
        jnp.broadcast_to(row_scr[cols_at + q : cols_at + q + 1, pl.ds(col_off, tile)], (8, tile))
        for q in range(4)
    ]

    @pl.loop(0, count // step)
    def _(t):
        for k in range(0, step, 8):
            at = pl.multiple_of(t * step, step) + k
            high, low, alpha, zeta = (col_scr[q, pl.ds(side_row + at, 8), :] for q in range(4))
            for c in range(0, tile, 128):
                col = [value[:, c : c + 128] for value in cols]
                spread = high * col[1] - low * col[0]
                pair = alpha + col[2]
                bottom = spread * spread + pair * (zeta + col[3])
                out_ref[pl.ds(at, 8), out_col + c : out_col + c + 128] = pair / bottom


def rho_near_kernel(freq_ref, rate_ref, diag_ref, mate_ref, col_scr, row_scr):
    block = diag_ref.shape[0]
    half = block // 2
    tile = block // 4
    own, mate, parity = place()[0], place()[1], place()[3]
    place_modes(freq_ref, rate_ref, row_scr, col_scr, (own, mate), 0, block)
    for j in range(4):
        fill_rho(row_scr, col_scr, diag_ref, j * tile, 0, (j + 1) * tile, 0, j * tile, tile)
    for i in range(2):
        for j in range(2):
            off = pl.multiple_of((i ^ parity) * half + j * tile, tile)
            fill_rho(row_scr, col_scr, mate_ref.at[i], j * tile, i * half, half, 8, off, tile)


def rho_own_kernel(freq_ref, rate_ref, side_ref, out_ref, row_scr):
    block = out_ref.shape[0]
    tile = block // 4
    place_modes(freq_ref, rate_ref, row_scr, None, (place()[2],), None, block)
    for j in range(4):
        fill_rho(row_scr, side_ref, out_ref, j * tile, 0, block, 0, j * tile, tile)


def rho_mate_kernel(freq_ref, rate_ref, out_ref, col_scr, row_scr):
    block = out_ref.shape[0]
    tile = block // 4
    place_modes(freq_ref, rate_ref, row_scr, col_scr, (place()[1], place()[2]), 0, block)
    for j in range(4):
        fill_rho(row_scr, col_scr, out_ref, j * tile, 0, block, 8, j * tile, tile)


def forces_kernel(at, dims, rim_ref, first_ref, second_ref, local_ref, all_ref, part_ref, rim_scr):
    comps, chunk = all_ref.shape
    width = first_ref.shape[0] // dims
    part = comps // 2
    lanes = slice(at, at + chunk)
    for copy in range(2):
        for d in range(dims):
            base = (copy * dims + d) * 2 * width
            rim_scr[base : base + width, :] = first_ref[d * width : (d + 1) * width, lanes]
            rim_scr[base + width : base + 2 * width, :] = second_ref[d * width : (d + 1) * width, lanes]
    for c in range(0, chunk, 256):
        total = jnp.dot(rim_ref[...], rim_scr[:, c : c + 256], preferred_element_type=F32)
        all_ref[:, c : c + 256] = (local_ref[:, at + c : at + c + 256] + total).astype(BF16)
    part_ref[...] = all_ref[pl.ds(pl.multiple_of(place()[5] * part, part), part), :]


def join_kernel(*refs):
    out_ref = refs[-1]
    size = refs[0].shape[0]
    for q, ref in enumerate(refs[:-1]):
        out_ref[q * size : (q + 1) * size, :] = ref[...]


def amps_kernel(stats_ref, extra_ref, spectral_ref, freq_ref, rate_ref, *out_refs):
    dims, block = spectral_ref.shape[0], stats_ref.shape[1]
    for q, out_ref in enumerate(out_refs):
        lanes = pl.ds(pl.multiple_of(place()[q] * block, block), block)
        rows = slice(q * (dims + 1), (q + 1) * (dims + 1))
        total = stats_ref[rows, :] + extra_ref[rows, :]
        scale = 2.0 * jnp.sqrt(freq_ref[:, lanes] / rate_ref[:, lanes])
        amps = total[:dims] / total[dims : dims + 1] * spectral_ref[:, lanes] * scale
        out_ref[...] = jnp.concatenate([amps, jnp.zeros((8 - dims, block), F32)], axis=0)


def fold(value):
    total = value[:, :128]
    for c in range(128, value.shape[1], 128):
        total = total + value[:, c : c + 128]
    return total


def to_row(acc, turned, per_elem):
    elems = acc.shape[0] // per_elem
    for k in range(per_elem):
        turned[pl.ds(k, elems, stride=per_elem), :] = acc[k * elems : (k + 1) * elems, :]
    pieces = jnp.concatenate([piece.astype(BF16) for piece in split(turned[...])], axis=1)
    return lax.dot_general(
        jnp.ones((8, pieces.shape[1]), BF16), pieces, (((1,), (1,)), ((), ())), preferred_element_type=F32
    )[0:1]


def split(value):
    top = value.astype(BF16).astype(F32)
    rest = value - top
    middle = rest.astype(BF16).astype(F32)
    return top, middle, rest - middle


def side_terms(out_scr, at, amps, dims):
    top, middle, last = split(amps[:dims])
    rows = jnp.concatenate([top, top, middle, middle, top, last], axis=0)
    rows = jnp.concatenate([rows, jnp.zeros((32 - rows.shape[0], rows.shape[1]), F32)], axis=0)
    for c in range(0, amps.shape[1], 512):
        stack = [rows[:, c + q : c + q + 128] for q in range(0, 512, 128)]
        turned = jnp.concatenate(stack, axis=0).T
        for q in range(4):
            out_scr[at + c + q * 128 : at + c + (q + 1) * 128, :] = turned[:, q * 32 : (q + 1) * 32].astype(BF16)


def col_terms(amps, dims, factor):
    top, middle, last = split(amps[:dims] * factor)
    rows = jnp.concatenate([top, middle, top, middle, last, top], axis=0)
    rows = jnp.concatenate([rows, jnp.zeros((32 - rows.shape[0], rows.shape[1]), F32)], axis=0)
    return rows.astype(BF16)


def weigh(rho, side, cols):
    return (rho * jnp.dot(side, cols, preferred_element_type=F32)).astype(BF16)


def near_kernel(dims, chunks, *refs):
    own_amps_ref, mate_amps_ref, diag_ref, cross_ref = refs[:4]
    own_refs, mate_refs = refs[4 : 4 + chunks], refs[4 + chunks : 4 + 2 * chunks]
    acc, side_scr, w_scr = refs[4 + 2 * chunks :]
    _, chunk = own_refs[0].shape
    block = diag_ref.shape[0]
    tile = block // 4
    half = block // 2
    parity = place()[3]

    def part(parts, at, size):
        return parts[at // chunk][:, at % chunk : at % chunk + size]

    def product(w, at, depth):
        total = None
        for c in range(at, at + depth, min(chunk, depth)):
            size = min(chunk, at + depth - c)
            got = jnp.dot(part(own_refs, c, size), w[c - at : c - at + size, :], preferred_element_type=F32)
            total = got if total is None else total + got
        return total

    side_terms(side_scr, 0, own_amps_ref[...], dims)
    once, twice = (col_terms(own_amps_ref[...], dims, factor) for factor in (1.0, 2.0))
    straight = parity == 0
    turn = 0
    for j in range(4):
        spot = slice(j * tile, (j + 1) * tile)
        for i in range(j + 1):
            rows = slice(i * tile, (i + 1) * tile)
            cols = twice if i < j else once
            w_scr[turn, rows, :] = weigh(diag_ref[rows, spot], side_scr[rows, :], cols[:, spot])
        got = product(w_scr.at[turn], 0, (j + 1) * tile)
        got = fold(got * part(own_refs, j * tile, tile).astype(F32))
        acc[...] = got if j == 0 else acc[...] + got
        turn = 1 - turn
    for i in range(2):
        for j in range(half // tile):
            here, there = i * half + j * tile, (1 - i) * half + j * tile
            cols = jnp.where(
                straight, mate_amps_ref[:, here : here + tile], mate_amps_ref[:, there : there + tile]
            )
            w_scr[turn, :half, :] = weigh(
                cross_ref[i, :, j * tile : (j + 1) * tile],
                side_scr[i * half : (i + 1) * half, :], col_terms(cols, dims, 2.0),
            )
            got = product(w_scr.at[turn], i * half, half)
            other = jnp.where(
                straight, part(mate_refs, here, tile).astype(F32), part(mate_refs, there, tile).astype(F32)
            )
            acc[...] += fold(got * other)
            turn = 1 - turn


def weights_kernel(dims, own_amps_ref, mate_amps_ref, far_amps_ref, own_ref, mate_ref, out_ref, side_scr):
    block = own_ref.shape[1]
    tile = block // 4
    cols = col_terms(far_amps_ref[...], dims, 2.0)
    for q, (amps_ref, rho_ref) in enumerate(((own_amps_ref, own_ref), (mate_amps_ref, mate_ref))):
        side_terms(side_scr, q * block, amps_ref[...], dims)
        for at in range(0, block, tile):
            base = q * block + at
            for c in range(0, block, tile):
                spot = slice(c, c + tile)
                out_ref[base : base + tile, spot] = weigh(
                    rho_ref[at : at + tile, spot], side_scr[base : base + tile, :], cols[:, spot]
                )


def far_kernel(at, per_elem, chunks, near_ref, w_ref, far_ref, *refs):
    sides, (out_ref, *scratch) = refs[: 2 * chunks], refs[2 * chunks :]
    _, chunk = sides[0].shape
    part = far_ref.shape[0]
    tile = min(256, chunk)
    rows = pl.ds(pl.multiple_of(place()[4] * part, part), part)
    total = near_ref[rows, :]
    for c in range(0, chunk, tile):
        spot = slice(at + c, at + c + tile)
        got = None
        for q, side_ref in enumerate(sides):
            w = w_ref[q * chunk : (q + 1) * chunk, spot]
            piece = jnp.dot(side_ref[rows, :], w, preferred_element_type=F32)
            got = piece if got is None else got + piece
        total = total + fold(got * far_ref[:, c : c + tile].astype(F32))
    acc = scratch[0] if scratch else out_ref
    acc[...] = near_ref[...]
    acc[rows, :] = total
    if scratch:
        out_ref[...] = to_row(acc, scratch[1], per_elem)


CHUNKS = 2


def four_groups(*args):
    return combined(*args)


def combined(
    shapes, masses, spectral, frequencies, damping, recovery, connectivity, node_count, shared
):
    dims, nodes, block = shapes.shape
    elems, slots = connectivity.shape
    per_elem = recovery.shape[1]
    comps = elems * per_elem
    part = comps // 2
    width = shared.shape[1]
    parts = lax.axis_size("dom")
    sds = jax.ShapeDtypeStruct
    halves = [[], []]
    for i in range(parts - 1):
        halves[i % 2] += [(i, i + 1), (i + 1, i)]
    freq = frequencies.reshape(1, -1)
    rate = damping.reshape(1, -1)

    picked = call(pick_kernel, sds((2 * width, nodes), BF16), (shared,), 2.0)
    rows = sds((dims * width, block), BF16)
    outgoing = call(pair_rows_kernel, rows, (picked, shapes), 0.4)
    other, held = call(
        next_rows_kernel, [rows, sds(shapes.shape, BF16)], (picked, shapes), 0.7, hbm=(1,),
        scratch=[pltpu.SemaphoreType.DMA],
    )
    rims = (lax.ppermute(outgoing, "dom", halves[0]), lax.ppermute(other, "dom", halves[1]))
    stats = call(
        stats_kernel, sds((dims + 1, block), F32), (masses.reshape(1, nodes), held), 0.8,
        scratch=[pltpu.VMEM((nodes, 128), F32)],
    )
    rho_diag, rho_mate, sides = call(
        rho_near_kernel,
        (sds((block, block), F32), sds((2, block // 2, block // 2), F32), sds((4, block, 128), F32)),
        (freq, rate), 3.0,
        scratch=[pltpu.VMEM((16, block), F32)], after=(stats,),
    )
    far_own = call(
        rho_own_kernel, sds((block, block), F32), (freq, rate, sides), 1.9,
        scratch=[pltpu.VMEM((8, block), F32)],
    )
    taken = slots * elems
    local, rim = call(
        local_kernel, (sds((comps, block), F32), sds((comps, 4 * dims * width), BF16)),
        (connectivity.T, node_count.reshape(1, elems), recovery.transpose(1, 3, 2, 0), held),
        1.8, after=(far_own,),
        scratch=[
            pltpu.VMEM((taken, nodes + 2 * width), BF16), pltpu.VMEM((comps, dims * taken), BF16),
            pltpu.VMEM((dims * taken, block), BF16),
        ],
    )
    far_mate = call(
        rho_mate_kernel, sds((block, block), F32), (freq, rate), 2.5,
        scratch=[pltpu.VMEM((4, block, 128), F32), pltpu.VMEM((16, block), F32)],
    )
    given = [stats] + [lax.ppermute(stats, "mode", [(i, i ^ q) for i in range(4)]) for q in (1, 2)]
    stats = call(join_kernel, sds((3 * (dims + 1), block), F32), given, 0.5)
    order = [1 << q for q in range(1, parts.bit_length() - 1)] + [1]
    if parts & (parts - 1) or parts == 1:
        stats = lax.psum(stats, "dom")
        order = []
    extra = jnp.zeros_like(stats)
    for q, reach in enumerate(order):
        if q:
            stats = call(
                add_kernel, sds(stats.shape, F32), (stats, extra), 0.5, after=(rim,) if q == 1 else ()
            )
        extra = lax.ppermute(stats, "dom", [(i, i ^ reach) for i in range(parts)])
    amps, mate_amps, far_amps = call(
        amps_kernel, [sds((8, block), F32)] * 3, (stats, extra, spectral, freq, rate), 0.8,
    )

    chunk = block // CHUNKS
    own, mate, far = [], [], []
    for c in range(CHUNKS):
        forces, sent = call(
            functools.partial(forces_kernel, c * chunk, dims),
            [sds((comps, chunk), BF16), sds((part, chunk), BF16)],
            (rim, *rims, local), 0.6,
            scratch=[pltpu.VMEM((4 * dims * width, chunk), BF16)],
        )
        own.append(forces)
        far.append(lax.ppermute(sent, "mode", [(i, i ^ 2) for i in range(4)]))
        mate.append(lax.ppermute(forces, "mode", [(i, i ^ 1) for i in range(4)]))
    near = call(
        functools.partial(near_kernel, dims, CHUNKS), sds((comps, 128), F32),
        (amps, mate_amps, rho_diag, rho_mate, *own, *mate),
        3.4,
        scratch=[pltpu.VMEM((block, 32), BF16), pltpu.VMEM((2, block, block // 4), BF16)],
    )
    weights = call(
        functools.partial(weights_kernel, dims), sds((2 * block, block), BF16),
        (amps, mate_amps, far_amps, far_own, far_mate), 1.4,
        scratch=[pltpu.VMEM((2 * block, 32), BF16)],
    )
    value = near
    for c in range(CHUNKS):
        last = c == CHUNKS - 1
        value = call(
            functools.partial(far_kernel, c * chunk, per_elem, CHUNKS),
            sds((1, comps) if last else (comps, 128), F32),
            (value, weights, far[c], *own, *mate), 1.0,
            scratch=[pltpu.VMEM((comps, 128), F32)] * 2 if last else (),
        )
    value = value.reshape(comps)
    for reach in (1, 2):
        value = value + lax.ppermute(value, "mode", [(i, i ^ reach) for i in range(4)])
    return value


def extended_2(block, sides, width):
    for axis, dim in sides:
        count = lax.axis_size(axis)
        forward = [(i, i + 1) for i in range(count - 1)]
        backward = [(target, source) for source, target in forward]
        low = lax.ppermute(
            lax.slice_in_dim(block, block.shape[dim] - width, None, axis=dim), axis, forward
        )
        high = lax.ppermute(lax.slice_in_dim(block, 0, width, axis=dim), axis, backward)
        block = jnp.concatenate([low, block, high], axis=dim)
    return block


def shifted(value, axis, steps):
    count = lax.axis_size(axis)
    pairs = [(source, (source + steps) % count) for source in range(count)]
    return lax.ppermute(value, axis, pairs)


def correlation_block(freq_rows, freq_cols, rate_rows, rate_cols):
    ratio = freq_cols[None, :] / freq_rows[:, None]
    ratio_sq = ratio * ratio
    rate_row = rate_rows[:, None]
    rate_col = rate_cols[None, :]
    top_part = (
        8.0
        * jnp.sqrt(rate_row * rate_col)
        * (rate_row + ratio * rate_col)
        * ratio
        * jnp.sqrt(ratio)
    )
    spread = 1.0 - ratio_sq
    bottom_part = (
        spread * spread
        + 4.0 * rate_row * rate_col * ratio * (1.0 + ratio_sq)
        + 4.0 * (rate_row * rate_row + rate_col * rate_col) * ratio_sq
    )
    return top_part / bottom_part


def block_terms(own_forces, own_start, far_forces, far_start, amplitudes, frequencies, damping):
    row_count = own_forces.shape[1]
    col_count = far_forces.shape[1]
    freq_rows = lax.dynamic_slice_in_dim(frequencies, own_start, row_count)
    freq_cols = lax.dynamic_slice_in_dim(frequencies, far_start, col_count)
    rate_rows = lax.dynamic_slice_in_dim(damping, own_start, row_count)
    rate_cols = lax.dynamic_slice_in_dim(damping, far_start, col_count)
    correlation = correlation_block(freq_rows, freq_cols, rate_rows, rate_cols)
    amp_rows = lax.dynamic_slice_in_dim(amplitudes, own_start, row_count, 1)
    amp_cols = lax.dynamic_slice_in_dim(amplitudes, far_start, col_count, 1)
    weights = (amp_rows.T[:, :, None] * correlation[:, None, :] * amp_cols[None, :, :]).astype(
        jnp.bfloat16
    )
    weights = weights.reshape(row_count, 3 * col_count)
    projected = jnp.dot(own_forces, weights, preferred_element_type=jnp.float32)
    projected = projected.reshape(own_forces.shape[0], 3, col_count)
    far_wide = far_forces.astype(jnp.float32)
    return jnp.sum(projected * far_wide[:, None, :], axis=(1, 2))


def any_groups(
    shapes, masses, spectral, frequencies, damping, recovery, connectivity, node_count, shared
):
    rim_width = shared.shape[1]
    block_width = shapes.shape[2]
    elem_count = connectivity.shape[0]
    slot_count = connectivity.shape[1]
    mode_index = lax.axis_index("mode")
    own_start = mode_index * block_width
    shape_wide = shapes.astype(jnp.float32)
    weighted = masses[None, :, None] * shape_wide
    lever_arm = jnp.sum(weighted, axis=1)
    general = jnp.sum(weighted * shape_wide, axis=(0, 1))
    lever_sum, general_sum = lax.psum((lever_arm, general), "dom")
    own_spectral = lax.dynamic_slice_in_dim(spectral, own_start, block_width, 1)
    local_amps = lever_sum / general_sum[None, :] * own_spectral
    amplitudes = lax.all_gather(local_amps, "mode", axis=1, tiled=True)
    outgoing = jnp.concatenate(
        [jnp.take(shapes, shared[0], axis=1), jnp.take(shapes, shared[1], axis=1)], axis=1
    )
    extended = extended_2(outgoing, (("dom", 1),), rim_width)
    node_table = jnp.concatenate(
        [shapes, extended[:, :rim_width], extended[:, 3 * rim_width :]], axis=1
    )
    gathered = jnp.take(node_table, connectivity.reshape(-1), axis=1).reshape(
        3, elem_count, slot_count, block_width
    )
    slot_live = (jnp.arange(slot_count)[None, :] < node_count[:, None]).astype(jnp.bfloat16)
    masked = recovery * slot_live[:, None, :, None]
    forces = jnp.einsum("ekna,aenm->ekm", masked, gathered, preferred_element_type=jnp.float32)
    forces = forces.astype(jnp.bfloat16).reshape(elem_count * recovery.shape[1], block_width)
    groups = lax.axis_size("mode")
    half_count = groups // 2
    partial_value = block_terms(
        forces, own_start, forces, own_start, amplitudes, frequencies, damping
    )

    def advance(turn_index, carried):
        incoming, summed = carried
        incoming = shifted(incoming, "mode", 1)
        source = (mode_index - turn_index) % groups * block_width
        factor = jnp.where(turn_index == half_count, jnp.float32(1.0), jnp.float32(2.0))
        summed = summed + factor * block_terms(
            forces, own_start, incoming, source, amplitudes, frequencies, damping
        )
        return (incoming, summed)

    carried = lax.fori_loop(1, half_count + 1, advance, (forces, partial_value))
    partial_value = carried[1]
    return lax.psum(partial_value, "mode")


def solution(mesh):
    in_specs = (
        P(None, "dom", "mode"),
        P("dom"),
        P(),
        P(),
        P(),
        P("dom", None, None, None),
        P("dom", None),
        P("dom"),
        P(None, "dom"),
    )
    out_specs = P("dom")
    special = mesh.shape["mode"] == 4
    step = four_groups if special else any_groups
    step = jax.shard_map(
        step, mesh=mesh, in_specs=in_specs, out_specs=out_specs, check_vma=False
    )
    return step
```

```python
import functools
import jax
import jax.numpy as jnp
from jax import lax
from jax.experimental import pallas as pl
from jax.experimental.pallas import tpu as pltpu
from jax.sharding import PartitionSpec as P


F32 = jnp.float32
BF16 = jnp.bfloat16
VMEM = pl.BlockSpec(memory_space=pltpu.VMEM)
HBM = pl.BlockSpec(memory_space=pltpu.HBM)
ANY = pl.BlockSpec(memory_space=pl.ANY)
SMEM = pl.BlockSpec(memory_space=pltpu.SMEM)


def call(kernel, out_shape, args, cost, smem=(), hbm=(), scratch=(), vmem=14 << 20, after=()):
    count = len(args)
    specs = [SMEM if i in smem else HBM if i in hbm else VMEM for i in range(count)]
    specs += [ANY] * len(after)
    many = isinstance(out_shape, (tuple, list))

    def body(*refs):
        kernel(*refs[:count], *refs[count + len(after) :])

    return pl.pallas_call(
        body,
        out_shape=out_shape,
        in_specs=specs,
        out_specs=[VMEM] * len(out_shape) if many else VMEM,
        scratch_shapes=list(scratch),
        cost_estimate=pl.CostEstimate(flops=int(1.1e9 * cost), bytes_accessed=0, transcendentals=0),
        compiler_params=pltpu.CompilerParams(vmem_limit_bytes=vmem),
    )(*args, *after)


def place():
    group = lax.axis_index("mode")
    return (group, group ^ 1, group ^ 2, group & 1, group >> 1, 1 - (group >> 1))


def add_kernel(left_ref, right_ref, out_ref):
    out_ref[...] = left_ref[...] + right_ref[...]


def pick_kernel(shared_ref, pick_ref):
    nodes = pick_ref.shape[1]
    odd = lax.axis_index("dom") & 1
    wanted = jnp.concatenate([shared_ref[pl.ds(1 - odd, 1), :], shared_ref[pl.ds(odd, 1), :]], axis=1)
    node = lax.broadcasted_iota(jnp.int32, (nodes, wanted.shape[1]), 0)
    pick_ref[...] = jnp.where(node == wanted, 1.0, 0.0).astype(F32).T.astype(BF16)


def pair_rows_kernel(pick_ref, shapes_ref, out_ref):
    dims = shapes_ref.shape[0]
    width = out_ref.shape[0] // dims
    for d in range(dims):
        got = jnp.dot(pick_ref[:width, :], shapes_ref[d], preferred_element_type=F32)
        out_ref[d * width : (d + 1) * width, :] = got.astype(BF16)


def next_rows_kernel(pick_ref, shapes_ref, out_ref, held_ref, sem):
    dims = held_ref.shape[0]
    width = out_ref.shape[0] // dims
    load = pltpu.make_async_copy(shapes_ref, held_ref, sem)
    load.start()
    load.wait()
    for d in range(dims):
        got = jnp.dot(pick_ref[width:, :], held_ref[d], preferred_element_type=F32)
        out_ref[d * width : (d + 1) * width, :] = got.astype(BF16)


def stats_kernel(mass_ref, shapes_ref, out_ref, mass_scr):
    dims, nodes, block = shapes_ref.shape
    column = jnp.broadcast_to(mass_ref[...], (8, nodes)).T
    mass_scr[...] = jnp.broadcast_to(column[:, 0:1], (nodes, 128))
    for at in range(0, block, 128):
        lanes = slice(at, at + 128)
        general = jnp.zeros((8, 128), F32)
        for d in range(dims):
            lever = jnp.zeros((8, 128), F32)
            for r in range(0, nodes, 16):
                wide = shapes_ref[d, r : r + 16, lanes].astype(F32)
                weighted = wide * mass_scr[r : r + 16, :]
                square = weighted * wide
                lever += weighted[:8] + weighted[8:]
                general += square[:8] + square[8:]
            out_ref[d : d + 1, lanes] = jnp.sum(lever, axis=0, keepdims=True)
        out_ref[dims : dims + 1, lanes] = jnp.sum(general, axis=0, keepdims=True)


def local_kernel(codes_ref, count_ref, recovery_ref, shapes_ref, local_ref, rim_ref, pick_ref, force_ref, got_scr):
    slots, elems = codes_ref.shape
    per_elem, dims = recovery_ref.shape[0], recovery_ref.shape[1]
    nodes, block = shapes_ref.shape[1], shapes_ref.shape[2]
    taken = slots * elems
    span = pick_ref.shape[1]
    node = lax.broadcasted_iota(jnp.int32, (span, elems), 0)
    width = (span - nodes) // 2
    even = 1 - (lax.axis_index("dom") & 1)
    swapped = jnp.where(node < nodes + width, node + width, node - width)
    node = jnp.where((node >= nodes) & (even == 1), swapped, node)
    for s in range(0, slots, 2):
        picks = []
        for q in range(s, min(s + 2, slots)):
            code = jnp.where(q < count_ref[...], codes_ref[q : q + 1, :], -1)
            picks.append(jnp.where(node == code, 1.0, 0.0).astype(F32))
        pick_ref[s * elems : s * elems + len(picks) * elems, :] = (
            jnp.concatenate(picks, axis=1).T.astype(BF16)
        )
    row = lax.broadcasted_iota(jnp.int32, (elems, 2 * elems), 0)
    column = lax.broadcasted_iota(jnp.int32, (elems, 2 * elems), 1)
    same = (column == row) | (column == row + elems)
    for k in range(per_elem):
        for d in range(dims):
            value = recovery_ref[k, d].astype(F32)
            for s in range(0, slots, 2):
                pair = jnp.concatenate([value[s : s + 1], value[s + 1 : s + 2]], axis=1)
                at = (d * slots + s) * elems
                force_ref[k * elems : (k + 1) * elems, at : at + 2 * elems] = jnp.where(
                    same, pair, 0.0
                ).astype(BF16)
    rim = span - nodes
    for d in range(dims):
        rows = slice(d * taken, (d + 1) * taken)
        value = jnp.dot(force_ref[:, rows], pick_ref[:, nodes:], preferred_element_type=F32)
        high = value.astype(BF16)
        rim_ref[:, d * rim : (d + 1) * rim] = high
        rim_ref[:, (dims + d) * rim : (dims + d + 1) * rim] = (value - high.astype(F32)).astype(BF16)
        got = jnp.dot(pick_ref[:, :nodes], shapes_ref[d], preferred_element_type=F32)
        got_scr[rows, :] = got.astype(BF16)
    for c in range(0, block, 256):
        local_ref[:, c : c + 256] = jnp.dot(
            force_ref[...], got_scr[:, c : c + 256], preferred_element_type=F32
        )


def mode_rows(freq, rate):
    alpha = rate * freq
    inverse = 1.0 / jnp.sqrt(alpha)
    return (freq * freq * inverse, inverse, 2.0 * alpha, 2.0 * (freq / rate))


def turn_rows(rows):
    pieces = [rows[:, c : c + 128] for c in range(0, rows.shape[1], 128)]
    while len(pieces) * 8 % 128:
        pieces.append(jnp.zeros((8, 128), F32))
    return [jnp.concatenate(pieces[c : c + 16], axis=0).T for c in range(0, len(pieces), 16)]


def place_modes(freq_ref, rate_ref, row_scr, col_scr, groups, side, block):
    side_rows = []
    for which, group in enumerate(groups):
        lanes = pl.ds(pl.multiple_of(group * block, block), block)
        rows = jnp.concatenate(list(mode_rows(freq_ref[:, lanes], rate_ref[:, lanes])) * 2, axis=0)
        row_scr[which * 8 : which * 8 + 8, :] = rows
        if which == side:
            side_rows.append(rows)
    if side is None:
        return
    turned = turn_rows(jnp.concatenate(side_rows, axis=1))
    for t in range(block // 128):
        for q in range(4):
            lane = t % 16 * 8 + q
            col_scr[q, t * 128 : (t + 1) * 128, :] = jnp.broadcast_to(
                turned[t // 16][:, lane : lane + 1], (128, 128)
            )


def fill_rho(row_scr, col_scr, out_ref, out_col, side_row, count, cols_at, col_off, tile):
    step = min(count, 256)
    cols = [
        jnp.broadcast_to(row_scr[cols_at + q : cols_at + q + 1, pl.ds(col_off, tile)], (8, tile))
        for q in range(4)
    ]

    @pl.loop(0, count // step)
    def _(t):
        for k in range(0, step, 8):
            at = pl.multiple_of(t * step, step) + k
            high, low, alpha, zeta = (col_scr[q, pl.ds(side_row + at, 8), :] for q in range(4))
            for c in range(0, tile, 128):
                col = [value[:, c : c + 128] for value in cols]
                spread = high * col[1] - low * col[0]
                pair = alpha + col[2]
                bottom = spread * spread + pair * (zeta + col[3])
                out_ref[pl.ds(at, 8), out_col + c : out_col + c + 128] = pair / bottom


def rho_near_kernel(freq_ref, rate_ref, diag_ref, mate_ref, col_scr, row_scr):
    block = diag_ref.shape[0]
    half = block // 2
    tile = block // 4
    own, mate, parity = place()[0], place()[1], place()[3]
    place_modes(freq_ref, rate_ref, row_scr, col_scr, (own, mate), 0, block)
    for j in range(4):
        fill_rho(row_scr, col_scr, diag_ref, j * tile, 0, (j + 1) * tile, 0, j * tile, tile)
    for i in range(2):
        for j in range(2):
            off = pl.multiple_of((i ^ parity) * half + j * tile, tile)
            fill_rho(row_scr, col_scr, mate_ref.at[i], j * tile, i * half, half, 8, off, tile)


def rho_own_kernel(freq_ref, rate_ref, side_ref, out_ref, row_scr):
    block = out_ref.shape[0]
    tile = block // 4
    place_modes(freq_ref, rate_ref, row_scr, None, (place()[2],), None, block)
    for j in range(4):
        fill_rho(row_scr, side_ref, out_ref, j * tile, 0, block, 0, j * tile, tile)


def rho_mate_kernel(freq_ref, rate_ref, out_ref, col_scr, row_scr):
    block = out_ref.shape[0]
    tile = block // 4
    place_modes(freq_ref, rate_ref, row_scr, col_scr, (place()[1], place()[2]), 0, block)
    for j in range(4):
        fill_rho(row_scr, col_scr, out_ref, j * tile, 0, block, 8, j * tile, tile)


def forces_kernel(at, dims, rim_ref, first_ref, second_ref, local_ref, *refs):
    all_ref, part_ref, rim_scr = refs[-3:]
    comps, chunk = all_ref.shape[0], part_ref.shape[1]
    width = first_ref.shape[0] // dims
    part = comps // 2
    lanes = slice(at, at + chunk)
    for copy in range(2):
        for d in range(dims):
            base = (copy * dims + d) * 2 * width
            rim_scr[base : base + width, :] = first_ref[d * width : (d + 1) * width, lanes]
            rim_scr[base + width : base + 2 * width, :] = second_ref[d * width : (d + 1) * width, lanes]
    for c in range(0, chunk, 256):
        total = jnp.dot(rim_ref[...], rim_scr[:, c : c + 256], preferred_element_type=F32)
        all_ref[:, at + c : at + c + 256] = (local_ref[:, at + c : at + c + 256] + total).astype(BF16)
    part_ref[...] = all_ref[pl.ds(pl.multiple_of(place()[5] * part, part), part), lanes]
    if at:
        all_ref[:, :at] = refs[0][...]


def join_kernel(*refs):
    out_ref = refs[-1]
    size = refs[0].shape[0]
    for q, ref in enumerate(refs[:-1]):
        out_ref[q * size : (q + 1) * size, :] = ref[...]


def amps_kernel(stats_ref, extra_ref, spectral_ref, freq_ref, rate_ref, *out_refs):
    dims, block = spectral_ref.shape[0], stats_ref.shape[1]
    for q, out_ref in enumerate(out_refs):
        lanes = pl.ds(pl.multiple_of(place()[q] * block, block), block)
        rows = slice(q * (dims + 1), (q + 1) * (dims + 1))
        total = stats_ref[rows, :] + extra_ref[rows, :]
        scale = 2.0 * jnp.sqrt(freq_ref[:, lanes] / rate_ref[:, lanes])
        amps = total[:dims] / total[dims : dims + 1] * spectral_ref[:, lanes] * scale
        out_ref[...] = jnp.concatenate([amps, jnp.zeros((8 - dims, block), F32)], axis=0)


def fold(value):
    total = value[:, :128]
    for c in range(128, value.shape[1], 128):
        total = total + value[:, c : c + 128]
    return total


def to_row(acc, turned, per_elem):
    elems = acc.shape[0] // per_elem
    for k in range(per_elem):
        turned[pl.ds(k, elems, stride=per_elem), :] = acc[k * elems : (k + 1) * elems, :]
    pieces = jnp.concatenate([piece.astype(BF16) for piece in split(turned[...])], axis=1)
    return lax.dot_general(
        jnp.ones((8, pieces.shape[1]), BF16), pieces, (((1,), (1,)), ((), ())), preferred_element_type=F32
    )[0:1]


def split(value):
    top = value.astype(BF16).astype(F32)
    rest = value - top
    middle = rest.astype(BF16).astype(F32)
    return top, middle, rest - middle


def side_terms(out_scr, at, amps, dims):
    top, middle, last = split(amps[:dims])
    rows = jnp.concatenate([top, top, middle, middle, top, last], axis=0)
    rows = jnp.concatenate([rows, jnp.zeros((32 - rows.shape[0], rows.shape[1]), F32)], axis=0)
    for c in range(0, amps.shape[1], 512):
        stack = [rows[:, c + q : c + q + 128] for q in range(0, 512, 128)]
        turned = jnp.concatenate(stack, axis=0).T
        for q in range(4):
            out_scr[at + c + q * 128 : at + c + (q + 1) * 128, :] = turned[:, q * 32 : (q + 1) * 32].astype(BF16)


def col_terms(amps, dims, factor):
    top, middle, last = split(amps[:dims] * factor)
    rows = jnp.concatenate([top, middle, top, middle, last, top], axis=0)
    rows = jnp.concatenate([rows, jnp.zeros((32 - rows.shape[0], rows.shape[1]), F32)], axis=0)
    return rows.astype(BF16)


def weigh(rho, side, cols):
    return (rho * jnp.dot(side, cols, preferred_element_type=F32)).astype(BF16)


def near_kernel(dims, chunks, *refs):
    own_amps_ref, mate_amps_ref, diag_ref, cross_ref = refs[:4]
    own_refs, mate_refs = refs[4 : 4 + chunks], refs[4 + chunks : 4 + 2 * chunks]
    acc, side_scr, w_scr = refs[4 + 2 * chunks :]
    _, chunk = own_refs[0].shape
    block = diag_ref.shape[0]
    tile = block // 4
    half = block // 2
    parity = place()[3]

    def part(parts, at, size):
        return parts[at // chunk][:, at % chunk : at % chunk + size]

    def product(w, at, depth):
        total = None
        for c in range(at, at + depth, min(chunk, depth)):
            size = min(chunk, at + depth - c)
            got = jnp.dot(part(own_refs, c, size), w[c - at : c - at + size, :], preferred_element_type=F32)
            total = got if total is None else total + got
        return total

    side_terms(side_scr, 0, own_amps_ref[...], dims)
    once, twice = (col_terms(own_amps_ref[...], dims, factor) for factor in (1.0, 2.0))
    straight = parity == 0
    turn = 0
    for j in range(4):
        spot = slice(j * tile, (j + 1) * tile)
        for i in range(j + 1):
            rows = slice(i * tile, (i + 1) * tile)
            cols = twice if i < j else once
            w_scr[turn, rows, :] = weigh(diag_ref[rows, spot], side_scr[rows, :], cols[:, spot])
        got = product(w_scr.at[turn], 0, (j + 1) * tile)
        got = fold(got * part(own_refs, j * tile, tile).astype(F32))
        acc[...] = got if j == 0 else acc[...] + got
        turn = 1 - turn
    for i in range(2):
        for j in range(half // tile):
            here, there = i * half + j * tile, (1 - i) * half + j * tile
            cols = jnp.where(
                straight, mate_amps_ref[:, here : here + tile], mate_amps_ref[:, there : there + tile]
            )
            w_scr[turn, :half, :] = weigh(
                cross_ref[i, :, j * tile : (j + 1) * tile],
                side_scr[i * half : (i + 1) * half, :], col_terms(cols, dims, 2.0),
            )
            got = product(w_scr.at[turn], i * half, half)
            other = jnp.where(
                straight, part(mate_refs, here, tile).astype(F32), part(mate_refs, there, tile).astype(F32)
            )
            acc[...] += fold(got * other)
            turn = 1 - turn


def weights_kernel(dims, own_amps_ref, mate_amps_ref, far_amps_ref, own_ref, mate_ref, out_ref, side_scr):
    block = own_ref.shape[1]
    tile = block // 4
    cols = col_terms(far_amps_ref[...], dims, 2.0)
    for q, (amps_ref, rho_ref) in enumerate(((own_amps_ref, own_ref), (mate_amps_ref, mate_ref))):
        side_terms(side_scr, q * block, amps_ref[...], dims)
        for at in range(0, block, tile):
            base = q * block + at
            for c in range(0, block, tile):
                spot = slice(c, c + tile)
                out_ref[base : base + tile, spot] = weigh(
                    rho_ref[at : at + tile, spot], side_scr[base : base + tile, :], cols[:, spot]
                )


def far_kernel(at, per_elem, chunks, near_ref, w_ref, far_ref, *refs):
    sides, (out_ref, *scratch) = refs[: 2 * chunks], refs[2 * chunks :]
    _, chunk = sides[0].shape
    part, size = far_ref.shape
    tile = min(256, size)
    rows = pl.ds(pl.multiple_of(place()[4] * part, part), part)
    total = near_ref[rows, :]
    for c in range(0, size, tile):
        spot = slice(at + c, at + c + tile)
        got = None
        for q, side_ref in enumerate(sides):
            w = w_ref[q * chunk : (q + 1) * chunk, spot]
            piece = jnp.dot(side_ref[rows, :], w, preferred_element_type=F32)
            got = piece if got is None else got + piece
        total = total + fold(got * far_ref[:, c : c + tile].astype(F32))
    acc = scratch[0] if scratch else out_ref
    acc[...] = near_ref[...]
    acc[rows, :] = total
    if scratch:
        out_ref[...] = to_row(acc, scratch[1], per_elem)


CHUNKS = 2


def four_groups(*args):
    return combined(*args)


def combined(
    shapes, masses, spectral, frequencies, damping, recovery, connectivity, node_count, shared
):
    dims, nodes, block = shapes.shape
    elems, slots = connectivity.shape
    per_elem = recovery.shape[1]
    comps = elems * per_elem
    part = comps // 2
    width = shared.shape[1]
    parts = lax.axis_size("dom")
    sds = jax.ShapeDtypeStruct
    halves = [[], []]
    for i in range(parts - 1):
        halves[i % 2] += [(i, i + 1), (i + 1, i)]
    freq = frequencies.reshape(1, -1)
    rate = damping.reshape(1, -1)

    picked = call(pick_kernel, sds((2 * width, nodes), BF16), (shared,), 2.0)
    rows = sds((dims * width, block), BF16)
    outgoing = call(pair_rows_kernel, rows, (picked, shapes), 0.4)
    other, held = call(
        next_rows_kernel, [rows, sds(shapes.shape, BF16)], (picked, shapes), 0.7, hbm=(1,),
        scratch=[pltpu.SemaphoreType.DMA],
    )
    rims = (lax.ppermute(outgoing, "dom", halves[0]), lax.ppermute(other, "dom", halves[1]))
    stats = call(
        stats_kernel, sds((dims + 1, block), F32), (masses.reshape(1, nodes), held), 0.8,
        scratch=[pltpu.VMEM((nodes, 128), F32)],
    )
    rho_diag, rho_mate, sides = call(
        rho_near_kernel,
        (sds((block, block), F32), sds((2, block // 2, block // 2), F32), sds((4, block, 128), F32)),
        (freq, rate), 3.0,
        scratch=[pltpu.VMEM((16, block), F32)], after=(stats,),
    )
    far_own = call(
        rho_own_kernel, sds((block, block), F32), (freq, rate, sides), 1.9,
        scratch=[pltpu.VMEM((8, block), F32)],
    )
    taken = slots * elems
    local, rim = call(
        local_kernel, (sds((comps, block), F32), sds((comps, 4 * dims * width), BF16)),
        (connectivity.T, node_count.reshape(1, elems), recovery.transpose(1, 3, 2, 0), held),
        1.8, after=(far_own,),
        scratch=[
            pltpu.VMEM((taken, nodes + 2 * width), BF16), pltpu.VMEM((comps, dims * taken), BF16),
            pltpu.VMEM((dims * taken, block), BF16),
        ],
    )
    far_mate = call(
        rho_mate_kernel, sds((block, block), F32), (freq, rate), 2.5,
        scratch=[pltpu.VMEM((4, block, 128), F32), pltpu.VMEM((16, block), F32)],
    )
    given = [stats] + [lax.ppermute(stats, "mode", [(i, i ^ q) for i in range(4)]) for q in (1, 2)]
    stats = call(join_kernel, sds((3 * (dims + 1), block), F32), given, 0.5)
    order = [1 << q for q in range(1, parts.bit_length() - 1)] + [1]
    if parts & (parts - 1) or parts == 1:
        stats = lax.psum(stats, "dom")
        order = []
    extra = jnp.zeros_like(stats)
    for q, reach in enumerate(order):
        if q:
            stats = call(
                add_kernel, sds(stats.shape, F32), (stats, extra), 0.5, after=(rim,) if q == 1 else ()
            )
        extra = lax.ppermute(stats, "dom", [(i, i ^ reach) for i in range(parts)])
    amps, mate_amps, far_amps = call(
        amps_kernel, [sds((8, block), F32)] * 3, (stats, extra, spectral, freq, rate), 0.8,
    )

    chunk = block // CHUNKS
    far, forces = [], ()
    for c in range(CHUNKS):
        *forces, sent = call(
            functools.partial(forces_kernel, c * chunk, dims),
            [sds((comps, (c + 1) * chunk), BF16), sds((part, chunk), BF16)],
            (rim, *rims, local, *forces), 0.6,
            scratch=[pltpu.VMEM((4 * dims * width, chunk), BF16)],
        )
        far.append(lax.ppermute(sent, "mode", [(i, i ^ 2) for i in range(4)]))
    forces = forces[0]
    mate = lax.ppermute(forces, "mode", [(i, i ^ 1) for i in range(4)])
    near = call(
        functools.partial(near_kernel, dims, 1), sds((comps, 128), F32),
        (amps, mate_amps, rho_diag, rho_mate, forces, mate),
        3.4,
        scratch=[pltpu.VMEM((block, 32), BF16), pltpu.VMEM((2, block, block // 4), BF16)],
    )
    weights = call(
        functools.partial(weights_kernel, dims), sds((2 * block, block), BF16),
        (amps, mate_amps, far_amps, far_own, far_mate), 1.4,
        scratch=[pltpu.VMEM((2 * block, 32), BF16)],
    )
    value = near
    for c in range(CHUNKS):
        last = c == CHUNKS - 1
        value = call(
            functools.partial(far_kernel, c * chunk, per_elem, 1),
            sds((1, comps) if last else (comps, 128), F32),
            (value, weights, far[c], forces, mate), 1.0,
            scratch=[pltpu.VMEM((comps, 128), F32)] * 2 if last else (),
        )
    value = value.reshape(comps)
    for reach in (1, 2):
        value = value + lax.ppermute(value, "mode", [(i, i ^ reach) for i in range(4)])
    return value


def extended_2(block, sides, width):
    for axis, dim in sides:
        count = lax.axis_size(axis)
        forward = [(i, i + 1) for i in range(count - 1)]
        backward = [(target, source) for source, target in forward]
        low = lax.ppermute(
            lax.slice_in_dim(block, block.shape[dim] - width, None, axis=dim), axis, forward
        )
        high = lax.ppermute(lax.slice_in_dim(block, 0, width, axis=dim), axis, backward)
        block = jnp.concatenate([low, block, high], axis=dim)
    return block


def shifted(value, axis, steps):
    count = lax.axis_size(axis)
    pairs = [(source, (source + steps) % count) for source in range(count)]
    return lax.ppermute(value, axis, pairs)


def correlation_block(freq_rows, freq_cols, rate_rows, rate_cols):
    ratio = freq_cols[None, :] / freq_rows[:, None]
    ratio_sq = ratio * ratio
    rate_row = rate_rows[:, None]
    rate_col = rate_cols[None, :]
    top_part = (
        8.0
        * jnp.sqrt(rate_row * rate_col)
        * (rate_row + ratio * rate_col)
        * ratio
        * jnp.sqrt(ratio)
    )
    spread = 1.0 - ratio_sq
    bottom_part = (
        spread * spread
        + 4.0 * rate_row * rate_col * ratio * (1.0 + ratio_sq)
        + 4.0 * (rate_row * rate_row + rate_col * rate_col) * ratio_sq
    )
    return top_part / bottom_part


def block_terms(own_forces, own_start, far_forces, far_start, amplitudes, frequencies, damping):
    row_count = own_forces.shape[1]
    col_count = far_forces.shape[1]
    freq_rows = lax.dynamic_slice_in_dim(frequencies, own_start, row_count)
    freq_cols = lax.dynamic_slice_in_dim(frequencies, far_start, col_count)
    rate_rows = lax.dynamic_slice_in_dim(damping, own_start, row_count)
    rate_cols = lax.dynamic_slice_in_dim(damping, far_start, col_count)
    correlation = correlation_block(freq_rows, freq_cols, rate_rows, rate_cols)
    amp_rows = lax.dynamic_slice_in_dim(amplitudes, own_start, row_count, 1)
    amp_cols = lax.dynamic_slice_in_dim(amplitudes, far_start, col_count, 1)
    weights = (amp_rows.T[:, :, None] * correlation[:, None, :] * amp_cols[None, :, :]).astype(
        jnp.bfloat16
    )
    weights = weights.reshape(row_count, 3 * col_count)
    projected = jnp.dot(own_forces, weights, preferred_element_type=jnp.float32)
    projected = projected.reshape(own_forces.shape[0], 3, col_count)
    far_wide = far_forces.astype(jnp.float32)
    return jnp.sum(projected * far_wide[:, None, :], axis=(1, 2))


def any_groups(
    shapes, masses, spectral, frequencies, damping, recovery, connectivity, node_count, shared
):
    rim_width = shared.shape[1]
    block_width = shapes.shape[2]
    elem_count = connectivity.shape[0]
    slot_count = connectivity.shape[1]
    mode_index = lax.axis_index("mode")
    own_start = mode_index * block_width
    shape_wide = shapes.astype(jnp.float32)
    weighted = masses[None, :, None] * shape_wide
    lever_arm = jnp.sum(weighted, axis=1)
    general = jnp.sum(weighted * shape_wide, axis=(0, 1))
    lever_sum, general_sum = lax.psum((lever_arm, general), "dom")
    own_spectral = lax.dynamic_slice_in_dim(spectral, own_start, block_width, 1)
    local_amps = lever_sum / general_sum[None, :] * own_spectral
    amplitudes = lax.all_gather(local_amps, "mode", axis=1, tiled=True)
    outgoing = jnp.concatenate(
        [jnp.take(shapes, shared[0], axis=1), jnp.take(shapes, shared[1], axis=1)], axis=1
    )
    extended = extended_2(outgoing, (("dom", 1),), rim_width)
    node_table = jnp.concatenate(
        [shapes, extended[:, :rim_width], extended[:, 3 * rim_width :]], axis=1
    )
    gathered = jnp.take(node_table, connectivity.reshape(-1), axis=1).reshape(
        3, elem_count, slot_count, block_width
    )
    slot_live = (jnp.arange(slot_count)[None, :] < node_count[:, None]).astype(jnp.bfloat16)
    masked = recovery * slot_live[:, None, :, None]
    forces = jnp.einsum("ekna,aenm->ekm", masked, gathered, preferred_element_type=jnp.float32)
    forces = forces.astype(jnp.bfloat16).reshape(elem_count * recovery.shape[1], block_width)
    groups = lax.axis_size("mode")
    half_count = groups // 2
    partial_value = block_terms(
        forces, own_start, forces, own_start, amplitudes, frequencies, damping
    )

    def advance(turn_index, carried):
        incoming, summed = carried
        incoming = shifted(incoming, "mode", 1)
        source = (mode_index - turn_index) % groups * block_width
        factor = jnp.where(turn_index == half_count, jnp.float32(1.0), jnp.float32(2.0))
        summed = summed + factor * block_terms(
            forces, own_start, incoming, source, amplitudes, frequencies, damping
        )
        return (incoming, summed)

    carried = lax.fori_loop(1, half_count + 1, advance, (forces, partial_value))
    partial_value = carried[1]
    return lax.psum(partial_value, "mode")


def solution(mesh):
    in_specs = (
        P(None, "dom", "mode"),
        P("dom"),
        P(),
        P(),
        P(),
        P("dom", None, None, None),
        P("dom", None),
        P("dom"),
        P(None, "dom"),
    )
    out_specs = P("dom")
    special = mesh.shape["mode"] == 4
    step = four_groups if special else any_groups
    step = jax.shard_map(
        step, mesh=mesh, in_specs=in_specs, out_specs=out_specs, check_vma=False
    )
    return step
```

```python
import functools
import jax
import jax.numpy as jnp
from jax import lax
from jax.experimental import pallas as pl
from jax.experimental.pallas import tpu as pltpu
from jax.sharding import PartitionSpec as P


F32 = jnp.float32
BF16 = jnp.bfloat16
VMEM = pl.BlockSpec(memory_space=pltpu.VMEM)
HBM = pl.BlockSpec(memory_space=pltpu.HBM)
ANY = pl.BlockSpec(memory_space=pl.ANY)
SMEM = pl.BlockSpec(memory_space=pltpu.SMEM)


def call(kernel, out_shape, args, cost, smem=(), hbm=(), scratch=(), vmem=14 << 20, after=()):
    count = len(args)
    specs = [SMEM if i in smem else HBM if i in hbm else VMEM for i in range(count)]
    specs += [ANY] * len(after)
    many = isinstance(out_shape, (tuple, list))

    def body(*refs):
        kernel(*refs[:count], *refs[count + len(after) :])

    return pl.pallas_call(
        body,
        out_shape=out_shape,
        in_specs=specs,
        out_specs=[VMEM] * len(out_shape) if many else VMEM,
        scratch_shapes=list(scratch),
        cost_estimate=pl.CostEstimate(flops=int(1.1e9 * cost), bytes_accessed=0, transcendentals=0),
        compiler_params=pltpu.CompilerParams(vmem_limit_bytes=vmem),
    )(*args, *after)


def place():
    group = lax.axis_index("mode")
    return (group, group ^ 1, group ^ 2, group & 1, group >> 1, 1 - (group >> 1))


def add_kernel(left_ref, right_ref, out_ref):
    out_ref[...] = left_ref[...] + right_ref[...]


def pick_kernel(shared_ref, pick_ref):
    nodes = pick_ref.shape[1]
    odd = lax.axis_index("dom") & 1
    wanted = jnp.concatenate([shared_ref[pl.ds(1 - odd, 1), :], shared_ref[pl.ds(odd, 1), :]], axis=1)
    node = lax.broadcasted_iota(jnp.int32, (nodes, wanted.shape[1]), 0)
    pick_ref[...] = jnp.where(node == wanted, 1.0, 0.0).astype(F32).T.astype(BF16)


def pair_rows_kernel(pick_ref, shapes_ref, out_ref):
    dims = shapes_ref.shape[0]
    width = out_ref.shape[0] // dims
    for d in range(dims):
        got = jnp.dot(pick_ref[:width, :], shapes_ref[d], preferred_element_type=F32)
        out_ref[d * width : (d + 1) * width, :] = got.astype(BF16)


def next_rows_kernel(pick_ref, shapes_ref, out_ref, held_ref, sem):
    dims = held_ref.shape[0]
    width = out_ref.shape[0] // dims
    load = pltpu.make_async_copy(shapes_ref, held_ref, sem)
    load.start()
    load.wait()
    for d in range(dims):
        got = jnp.dot(pick_ref[width:, :], held_ref[d], preferred_element_type=F32)
        out_ref[d * width : (d + 1) * width, :] = got.astype(BF16)


def stats_kernel(mass_ref, shapes_ref, out_ref, mass_scr):
    dims, nodes, block = shapes_ref.shape
    column = jnp.broadcast_to(mass_ref[...], (8, nodes)).T
    mass_scr[...] = jnp.broadcast_to(column[:, 0:1], (nodes, 128))
    for at in range(0, block, 128):
        lanes = slice(at, at + 128)
        general = jnp.zeros((8, 128), F32)
        for d in range(dims):
            lever = jnp.zeros((8, 128), F32)
            for r in range(0, nodes, 16):
                wide = shapes_ref[d, r : r + 16, lanes].astype(F32)
                weighted = wide * mass_scr[r : r + 16, :]
                square = weighted * wide
                lever += weighted[:8] + weighted[8:]
                general += square[:8] + square[8:]
            out_ref[d : d + 1, lanes] = jnp.sum(lever, axis=0, keepdims=True)
        out_ref[dims : dims + 1, lanes] = jnp.sum(general, axis=0, keepdims=True)


def local_kernel(codes_ref, count_ref, recovery_ref, shapes_ref, local_ref, rim_ref, pick_ref, force_ref, got_scr):
    slots, elems = codes_ref.shape
    per_elem, dims = recovery_ref.shape[0], recovery_ref.shape[1]
    nodes, block = shapes_ref.shape[1], shapes_ref.shape[2]
    taken = slots * elems
    span = pick_ref.shape[1]
    node = lax.broadcasted_iota(jnp.int32, (span, elems), 0)
    width = (span - nodes) // 2
    even = 1 - (lax.axis_index("dom") & 1)
    swapped = jnp.where(node < nodes + width, node + width, node - width)
    node = jnp.where((node >= nodes) & (even == 1), swapped, node)
    for s in range(0, slots, 2):
        picks = []
        for q in range(s, min(s + 2, slots)):
            code = jnp.where(q < count_ref[...], codes_ref[q : q + 1, :], -1)
            picks.append(jnp.where(node == code, 1.0, 0.0).astype(F32))
        pick_ref[s * elems : s * elems + len(picks) * elems, :] = (
            jnp.concatenate(picks, axis=1).T.astype(BF16)
        )
    row = lax.broadcasted_iota(jnp.int32, (elems, 2 * elems), 0)
    column = lax.broadcasted_iota(jnp.int32, (elems, 2 * elems), 1)
    same = (column == row) | (column == row + elems)
    for k in range(per_elem):
        for d in range(dims):
            value = recovery_ref[k, d].astype(F32)
            for s in range(0, slots, 2):
                pair = jnp.concatenate([value[s : s + 1], value[s + 1 : s + 2]], axis=1)
                at = (d * slots + s) * elems
                force_ref[k * elems : (k + 1) * elems, at : at + 2 * elems] = jnp.where(
                    same, pair, 0.0
                ).astype(BF16)
    rim = span - nodes
    for d in range(dims):
        rows = slice(d * taken, (d + 1) * taken)
        value = jnp.dot(force_ref[:, rows], pick_ref[:, nodes:], preferred_element_type=F32)
        high = value.astype(BF16)
        rim_ref[:, d * rim : (d + 1) * rim] = high
        rim_ref[:, (dims + d) * rim : (dims + d + 1) * rim] = (value - high.astype(F32)).astype(BF16)
        got = jnp.dot(pick_ref[:, :nodes], shapes_ref[d], preferred_element_type=F32)
        got_scr[rows, :] = got.astype(BF16)
    for c in range(0, block, 256):
        local_ref[:, c : c + 256] = jnp.dot(
            force_ref[...], got_scr[:, c : c + 256], preferred_element_type=F32
        )


def mode_rows(freq, rate):
    alpha = rate * freq
    inverse = 1.0 / jnp.sqrt(alpha)
    return (freq * freq * inverse, inverse, 2.0 * alpha, 2.0 * (freq / rate))


def turn_rows(rows):
    pieces = [rows[:, c : c + 128] for c in range(0, rows.shape[1], 128)]
    while len(pieces) * 8 % 128:
        pieces.append(jnp.zeros((8, 128), F32))
    return [jnp.concatenate(pieces[c : c + 16], axis=0).T for c in range(0, len(pieces), 16)]


def place_modes(freq_ref, rate_ref, row_scr, col_scr, groups, side, block):
    side_rows = []
    for which, group in enumerate(groups):
        lanes = pl.ds(pl.multiple_of(group * block, block), block)
        rows = jnp.concatenate(list(mode_rows(freq_ref[:, lanes], rate_ref[:, lanes])) * 2, axis=0)
        row_scr[which * 8 : which * 8 + 8, :] = rows
        if which == side:
            side_rows.append(rows)
    if side is None:
        return
    turned = turn_rows(jnp.concatenate(side_rows, axis=1))
    for t in range(block // 128):
        for q in range(4):
            lane = t % 16 * 8 + q
            col_scr[q, t * 128 : (t + 1) * 128, :] = jnp.broadcast_to(
                turned[t // 16][:, lane : lane + 1], (128, 128)
            )


def fill_rho(row_scr, col_scr, out_ref, out_col, side_row, count, cols_at, col_off, tile):
    step = min(count, 256)
    cols = [
        jnp.broadcast_to(row_scr[cols_at + q : cols_at + q + 1, pl.ds(col_off, tile)], (8, tile))
        for q in range(4)
    ]

    @pl.loop(0, count // step)
    def _(t):
        for k in range(0, step, 8):
            at = pl.multiple_of(t * step, step) + k
            high, low, alpha, zeta = (col_scr[q, pl.ds(side_row + at, 8), :] for q in range(4))
            for c in range(0, tile, 128):
                col = [value[:, c : c + 128] for value in cols]
                spread = high * col[1] - low * col[0]
                pair = alpha + col[2]
                bottom = spread * spread + pair * (zeta + col[3])
                out_ref[pl.ds(at, 8), out_col + c : out_col + c + 128] = pair / bottom


def rho_near_kernel(freq_ref, rate_ref, diag_ref, mate_ref, col_scr, row_scr):
    block = diag_ref.shape[0]
    half = block // 2
    tile = block // 4
    own, mate, parity = place()[0], place()[1], place()[3]
    place_modes(freq_ref, rate_ref, row_scr, col_scr, (own, mate), 0, block)
    for j in range(4):
        fill_rho(row_scr, col_scr, diag_ref, j * tile, 0, (j + 1) * tile, 0, j * tile, tile)
    for i in range(2):
        for j in range(2):
            off = pl.multiple_of((i ^ parity) * half + j * tile, tile)
            fill_rho(row_scr, col_scr, mate_ref.at[i], j * tile, i * half, half, 8, off, tile)


def rho_own_kernel(freq_ref, rate_ref, side_ref, out_ref, row_scr):
    block = out_ref.shape[0]
    tile = block // 4
    place_modes(freq_ref, rate_ref, row_scr, None, (place()[2],), None, block)
    for j in range(4):
        fill_rho(row_scr, side_ref, out_ref, j * tile, 0, block, 0, j * tile, tile)


def rho_mate_kernel(freq_ref, rate_ref, out_ref, col_scr, row_scr):
    block = out_ref.shape[0]
    tile = block // 4
    place_modes(freq_ref, rate_ref, row_scr, col_scr, (place()[1], place()[2]), 0, block)
    for j in range(4):
        fill_rho(row_scr, col_scr, out_ref, j * tile, 0, block, 8, j * tile, tile)


def forces_kernel(at, dims, rim_ref, first_ref, second_ref, local_ref, *refs):
    all_ref, part_ref, rim_scr = refs[-3:]
    comps, chunk = all_ref.shape[0], part_ref.shape[1]
    width = first_ref.shape[0] // dims
    part = comps // 2
    lanes = slice(at, at + chunk)
    for copy in range(2):
        for d in range(dims):
            base = (copy * dims + d) * 2 * width
            rim_scr[base : base + width, :] = first_ref[d * width : (d + 1) * width, lanes]
            rim_scr[base + width : base + 2 * width, :] = second_ref[d * width : (d + 1) * width, lanes]
    for c in range(0, chunk, 256):
        total = jnp.dot(rim_ref[...], rim_scr[:, c : c + 256], preferred_element_type=F32)
        all_ref[:, at + c : at + c + 256] = (local_ref[:, at + c : at + c + 256] + total).astype(BF16)
    part_ref[...] = all_ref[pl.ds(pl.multiple_of(place()[5] * part, part), part), lanes]
    if at:
        all_ref[:, :at] = refs[0][...]


def join_kernel(*refs):
    out_ref = refs[-1]
    size = refs[0].shape[0]
    for q, ref in enumerate(refs[:-1]):
        out_ref[q * size : (q + 1) * size, :] = ref[...]


def amps_kernel(stats_ref, extra_ref, spectral_ref, freq_ref, rate_ref, *out_refs):
    dims, block = spectral_ref.shape[0], stats_ref.shape[1]
    for q, out_ref in enumerate(out_refs):
        lanes = pl.ds(pl.multiple_of(place()[q] * block, block), block)
        rows = slice(q * (dims + 1), (q + 1) * (dims + 1))
        total = stats_ref[rows, :] + extra_ref[rows, :]
        scale = 2.0 * jnp.sqrt(freq_ref[:, lanes] / rate_ref[:, lanes])
        amps = total[:dims] / total[dims : dims + 1] * spectral_ref[:, lanes] * scale
        out_ref[...] = jnp.concatenate([amps, jnp.zeros((8 - dims, block), F32)], axis=0)


def fold(value):
    total = value[:, :128]
    for c in range(128, value.shape[1], 128):
        total = total + value[:, c : c + 128]
    return total


def to_row(acc, turned, per_elem):
    elems = acc.shape[0] // per_elem
    for k in range(per_elem):
        turned[pl.ds(k, elems, stride=per_elem), :] = acc[k * elems : (k + 1) * elems, :]
    pieces = jnp.concatenate([piece.astype(BF16) for piece in split(turned[...])], axis=1)
    return lax.dot_general(
        jnp.ones((8, pieces.shape[1]), BF16), pieces, (((1,), (1,)), ((), ())), preferred_element_type=F32
    )[0:1]


def split(value):
    top = value.astype(BF16).astype(F32)
    rest = value - top
    middle = rest.astype(BF16).astype(F32)
    return top, middle, rest - middle


def side_terms(out_scr, at, amps, dims):
    top, middle, last = split(amps[:dims])
    rows = jnp.concatenate([top, top, middle, middle, top, last], axis=0)
    rows = jnp.concatenate([rows, jnp.zeros((32 - rows.shape[0], rows.shape[1]), F32)], axis=0)
    for c in range(0, amps.shape[1], 512):
        stack = [rows[:, c + q : c + q + 128] for q in range(0, 512, 128)]
        turned = jnp.concatenate(stack, axis=0).T
        for q in range(4):
            out_scr[at + c + q * 128 : at + c + (q + 1) * 128, :] = turned[:, q * 32 : (q + 1) * 32].astype(BF16)


def col_terms(amps, dims, factor):
    top, middle, last = split(amps[:dims] * factor)
    rows = jnp.concatenate([top, middle, top, middle, last, top], axis=0)
    rows = jnp.concatenate([rows, jnp.zeros((32 - rows.shape[0], rows.shape[1]), F32)], axis=0)
    return rows.astype(BF16)


def weigh(rho, side, cols):
    return (rho * jnp.dot(side, cols, preferred_element_type=F32)).astype(BF16)


def near_kernel(dims, chunks, *refs):
    own_amps_ref, mate_amps_ref, diag_ref, cross_ref = refs[:4]
    own_refs, mate_refs = refs[4 : 4 + chunks], refs[4 + chunks : 4 + 2 * chunks]
    acc, side_scr, w_scr = refs[4 + 2 * chunks :]
    _, chunk = own_refs[0].shape
    block = diag_ref.shape[0]
    tile = block // 4
    half = block // 2
    parity = place()[3]

    def part(parts, at, size):
        return parts[at // chunk][:, at % chunk : at % chunk + size]

    def product(w, at, depth):
        total = None
        for c in range(at, at + depth, min(chunk, depth)):
            size = min(chunk, at + depth - c)
            got = jnp.dot(part(own_refs, c, size), w[c - at : c - at + size, :], preferred_element_type=F32)
            total = got if total is None else total + got
        return total

    side_terms(side_scr, 0, own_amps_ref[...], dims)
    once, twice = (col_terms(own_amps_ref[...], dims, factor) for factor in (1.0, 2.0))
    straight = parity == 0
    turn = 0
    for j in range(4):
        spot = slice(j * tile, (j + 1) * tile)
        for i in range(j + 1):
            rows = slice(i * tile, (i + 1) * tile)
            cols = twice if i < j else once
            w_scr[turn, rows, :] = weigh(diag_ref[rows, spot], side_scr[rows, :], cols[:, spot])
        got = product(w_scr.at[turn], 0, (j + 1) * tile)
        got = fold(got * part(own_refs, j * tile, tile).astype(F32))
        acc[...] = got if j == 0 else acc[...] + got
        turn = 1 - turn
    for i in range(2):
        for j in range(half // tile):
            here, there = i * half + j * tile, (1 - i) * half + j * tile
            cols = jnp.where(
                straight, mate_amps_ref[:, here : here + tile], mate_amps_ref[:, there : there + tile]
            )
            w_scr[turn, :half, :] = weigh(
                cross_ref[i, :, j * tile : (j + 1) * tile],
                side_scr[i * half : (i + 1) * half, :], col_terms(cols, dims, 2.0),
            )
            got = product(w_scr.at[turn], i * half, half)
            other = jnp.where(
                straight, part(mate_refs, here, tile).astype(F32), part(mate_refs, there, tile).astype(F32)
            )
            acc[...] += fold(got * other)
            turn = 1 - turn


def weights_kernel(dims, own_amps_ref, mate_amps_ref, far_amps_ref, own_ref, mate_ref, out_ref, side_scr):
    block = own_ref.shape[1]
    tile = block // 4
    cols = col_terms(far_amps_ref[...], dims, 2.0)
    for q, (amps_ref, rho_ref) in enumerate(((own_amps_ref, own_ref), (mate_amps_ref, mate_ref))):
        side_terms(side_scr, q * block, amps_ref[...], dims)
        for at in range(0, block, tile):
            base = q * block + at
            for c in range(0, block, tile):
                spot = slice(c, c + tile)
                out_ref[base : base + tile, spot] = weigh(
                    rho_ref[at : at + tile, spot], side_scr[base : base + tile, :], cols[:, spot]
                )


def far_kernel(at, per_elem, chunks, near_ref, w_ref, far_ref, *refs):
    sides, (out_ref, *scratch) = refs[: 2 * chunks], refs[2 * chunks :]
    _, chunk = sides[0].shape
    part, size = far_ref.shape
    tile = min(256, size)
    rows = pl.ds(pl.multiple_of(place()[4] * part, part), part)
    total = near_ref[rows, :]
    for c in range(0, size, tile):
        spot = slice(at + c, at + c + tile)
        got = None
        for q, side_ref in enumerate(sides):
            w = w_ref[q * chunk : (q + 1) * chunk, spot]
            piece = jnp.dot(side_ref[rows, :], w, preferred_element_type=F32)
            got = piece if got is None else got + piece
        total = total + fold(got * far_ref[:, c : c + tile].astype(F32))
    acc = scratch[0] if scratch else out_ref
    acc[...] = near_ref[...]
    acc[rows, :] = total
    if scratch:
        out_ref[...] = to_row(acc, scratch[1], per_elem)


CHUNKS = 2


def four_groups(*args):
    return combined(*args)


def combined(
    shapes, masses, spectral, frequencies, damping, recovery, connectivity, node_count, shared
):
    dims, nodes, block = shapes.shape
    elems, slots = connectivity.shape
    per_elem = recovery.shape[1]
    comps = elems * per_elem
    part = comps // 2
    width = shared.shape[1]
    parts = lax.axis_size("dom")
    sds = jax.ShapeDtypeStruct
    halves = [[], []]
    for i in range(parts - 1):
        halves[i % 2] += [(i, i + 1), (i + 1, i)]
    freq = frequencies.reshape(1, -1)
    rate = damping.reshape(1, -1)

    picked = call(pick_kernel, sds((2 * width, nodes), BF16), (shared,), 2.0)
    rows = sds((dims * width, block), BF16)
    outgoing = call(pair_rows_kernel, rows, (picked, shapes), 0.4)
    other, held = call(
        next_rows_kernel, [rows, sds(shapes.shape, BF16)], (picked, shapes), 0.7, hbm=(1,),
        scratch=[pltpu.SemaphoreType.DMA],
    )
    rims = (lax.ppermute(outgoing, "dom", halves[0]), lax.ppermute(other, "dom", halves[1]))
    stats = call(
        stats_kernel, sds((dims + 1, block), F32), (masses.reshape(1, nodes), held), 0.8,
        scratch=[pltpu.VMEM((nodes, 128), F32)],
    )
    rho_diag, rho_mate, sides = call(
        rho_near_kernel,
        (sds((block, block), F32), sds((2, block // 2, block // 2), F32), sds((4, block, 128), F32)),
        (freq, rate), 3.0,
        scratch=[pltpu.VMEM((16, block), F32)], after=(stats,),
    )
    far_own = call(
        rho_own_kernel, sds((block, block), F32), (freq, rate, sides), 1.9,
        scratch=[pltpu.VMEM((8, block), F32)],
    )
    taken = slots * elems
    local, rim = call(
        local_kernel, (sds((comps, block), F32), sds((comps, 4 * dims * width), BF16)),
        (connectivity.T, node_count.reshape(1, elems), recovery.transpose(1, 3, 2, 0), held),
        1.8, after=(far_own,),
        scratch=[
            pltpu.VMEM((taken, nodes + 2 * width), BF16), pltpu.VMEM((comps, dims * taken), BF16),
            pltpu.VMEM((dims * taken, block), BF16),
        ],
    )
    far_mate = call(
        rho_mate_kernel, sds((block, block), F32), (freq, rate), 2.5,
        scratch=[pltpu.VMEM((4, block, 128), F32), pltpu.VMEM((16, block), F32)],
    )
    given = [stats] + [lax.ppermute(stats, "mode", [(i, i ^ q) for i in range(4)]) for q in (1, 2)]
    stats = call(join_kernel, sds((3 * (dims + 1), block), F32), given, 0.5)
    order = [1 << q for q in reversed(range(1, parts.bit_length() - 1))] + [1]
    if parts & (parts - 1) or parts == 1:
        stats = lax.psum(stats, "dom")
        order = []
    extra = jnp.zeros_like(stats)
    for q, reach in enumerate(order):
        if q:
            stats = call(
                add_kernel, sds(stats.shape, F32), (stats, extra), 0.5, after=(rim,) if q == 1 else ()
            )
        extra = lax.ppermute(stats, "dom", [(i, i ^ reach) for i in range(parts)])
    amps, mate_amps, far_amps = call(
        amps_kernel, [sds((8, block), F32)] * 3, (stats, extra, spectral, freq, rate), 0.8,
    )

    chunk = block // CHUNKS
    far, forces = [], ()
    for c in range(CHUNKS):
        *forces, sent = call(
            functools.partial(forces_kernel, c * chunk, dims),
            [sds((comps, (c + 1) * chunk), BF16), sds((part, chunk), BF16)],
            (rim, *rims, local, *forces), 0.6,
            scratch=[pltpu.VMEM((4 * dims * width, chunk), BF16)],
        )
        far.append(lax.ppermute(sent, "mode", [(i, i ^ 2) for i in range(4)]))
    forces = forces[0]
    mate = lax.ppermute(forces, "mode", [(i, i ^ 1) for i in range(4)])
    near = call(
        functools.partial(near_kernel, dims, 1), sds((comps, 128), F32),
        (amps, mate_amps, rho_diag, rho_mate, forces, mate),
        3.4,
        scratch=[pltpu.VMEM((block, 32), BF16), pltpu.VMEM((2, block, block // 4), BF16)],
    )
    weights = call(
        functools.partial(weights_kernel, dims), sds((2 * block, block), BF16),
        (amps, mate_amps, far_amps, far_own, far_mate), 1.4,
        scratch=[pltpu.VMEM((2 * block, 32), BF16)],
    )
    value = near
    for c in range(CHUNKS):
        last = c == CHUNKS - 1
        value = call(
            functools.partial(far_kernel, c * chunk, per_elem, 1),
            sds((1, comps) if last else (comps, 128), F32),
            (value, weights, far[c], forces, mate), 1.0,
            scratch=[pltpu.VMEM((comps, 128), F32)] * 2 if last else (),
        )
    value = value.reshape(comps)
    far, diagonal, mate = (
        lax.ppermute(value, "mode", [(i, i ^ reach) for i in range(4)]) for reach in (2, 3, 1)
    )
    return (value + mate) + (far + diagonal)


def extended_2(block, sides, width):
    for axis, dim in sides:
        count = lax.axis_size(axis)
        forward = [(i, i + 1) for i in range(count - 1)]
        backward = [(target, source) for source, target in forward]
        low = lax.ppermute(
            lax.slice_in_dim(block, block.shape[dim] - width, None, axis=dim), axis, forward
        )
        high = lax.ppermute(lax.slice_in_dim(block, 0, width, axis=dim), axis, backward)
        block = jnp.concatenate([low, block, high], axis=dim)
    return block


def shifted(value, axis, steps):
    count = lax.axis_size(axis)
    pairs = [(source, (source + steps) % count) for source in range(count)]
    return lax.ppermute(value, axis, pairs)


def correlation_block(freq_rows, freq_cols, rate_rows, rate_cols):
    ratio = freq_cols[None, :] / freq_rows[:, None]
    ratio_sq = ratio * ratio
    rate_row = rate_rows[:, None]
    rate_col = rate_cols[None, :]
    top_part = (
        8.0
        * jnp.sqrt(rate_row * rate_col)
        * (rate_row + ratio * rate_col)
        * ratio
        * jnp.sqrt(ratio)
    )
    spread = 1.0 - ratio_sq
    bottom_part = (
        spread * spread
        + 4.0 * rate_row * rate_col * ratio * (1.0 + ratio_sq)
        + 4.0 * (rate_row * rate_row + rate_col * rate_col) * ratio_sq
    )
    return top_part / bottom_part


def block_terms(own_forces, own_start, far_forces, far_start, amplitudes, frequencies, damping):
    row_count = own_forces.shape[1]
    col_count = far_forces.shape[1]
    freq_rows = lax.dynamic_slice_in_dim(frequencies, own_start, row_count)
    freq_cols = lax.dynamic_slice_in_dim(frequencies, far_start, col_count)
    rate_rows = lax.dynamic_slice_in_dim(damping, own_start, row_count)
    rate_cols = lax.dynamic_slice_in_dim(damping, far_start, col_count)
    correlation = correlation_block(freq_rows, freq_cols, rate_rows, rate_cols)
    amp_rows = lax.dynamic_slice_in_dim(amplitudes, own_start, row_count, 1)
    amp_cols = lax.dynamic_slice_in_dim(amplitudes, far_start, col_count, 1)
    weights = (amp_rows.T[:, :, None] * correlation[:, None, :] * amp_cols[None, :, :]).astype(
        jnp.bfloat16
    )
    weights = weights.reshape(row_count, 3 * col_count)
    projected = jnp.dot(own_forces, weights, preferred_element_type=jnp.float32)
    projected = projected.reshape(own_forces.shape[0], 3, col_count)
    far_wide = far_forces.astype(jnp.float32)
    return jnp.sum(projected * far_wide[:, None, :], axis=(1, 2))


def any_groups(
    shapes, masses, spectral, frequencies, damping, recovery, connectivity, node_count, shared
):
    rim_width = shared.shape[1]
    block_width = shapes.shape[2]
    elem_count = connectivity.shape[0]
    slot_count = connectivity.shape[1]
    mode_index = lax.axis_index("mode")
    own_start = mode_index * block_width
    shape_wide = shapes.astype(jnp.float32)
    weighted = masses[None, :, None] * shape_wide
    lever_arm = jnp.sum(weighted, axis=1)
    general = jnp.sum(weighted * shape_wide, axis=(0, 1))
    lever_sum, general_sum = lax.psum((lever_arm, general), "dom")
    own_spectral = lax.dynamic_slice_in_dim(spectral, own_start, block_width, 1)
    local_amps = lever_sum / general_sum[None, :] * own_spectral
    amplitudes = lax.all_gather(local_amps, "mode", axis=1, tiled=True)
    outgoing = jnp.concatenate(
        [jnp.take(shapes, shared[0], axis=1), jnp.take(shapes, shared[1], axis=1)], axis=1
    )
    extended = extended_2(outgoing, (("dom", 1),), rim_width)
    node_table = jnp.concatenate(
        [shapes, extended[:, :rim_width], extended[:, 3 * rim_width :]], axis=1
    )
    gathered = jnp.take(node_table, connectivity.reshape(-1), axis=1).reshape(
        3, elem_count, slot_count, block_width
    )
    slot_live = (jnp.arange(slot_count)[None, :] < node_count[:, None]).astype(jnp.bfloat16)
    masked = recovery * slot_live[:, None, :, None]
    forces = jnp.einsum("ekna,aenm->ekm", masked, gathered, preferred_element_type=jnp.float32)
    forces = forces.astype(jnp.bfloat16).reshape(elem_count * recovery.shape[1], block_width)
    groups = lax.axis_size("mode")
    half_count = groups // 2
    partial_value = block_terms(
        forces, own_start, forces, own_start, amplitudes, frequencies, damping
    )

    def advance(turn_index, carried):
        incoming, summed = carried
        incoming = shifted(incoming, "mode", 1)
        source = (mode_index - turn_index) % groups * block_width
        factor = jnp.where(turn_index == half_count, jnp.float32(1.0), jnp.float32(2.0))
        summed = summed + factor * block_terms(
            forces, own_start, incoming, source, amplitudes, frequencies, damping
        )
        return (incoming, summed)

    carried = lax.fori_loop(1, half_count + 1, advance, (forces, partial_value))
    partial_value = carried[1]
    return lax.psum(partial_value, "mode")


def solution(mesh):
    in_specs = (
        P(None, "dom", "mode"),
        P("dom"),
        P(),
        P(),
        P(),
        P("dom", None, None, None),
        P("dom", None),
        P("dom"),
        P(None, "dom"),
    )
    out_specs = P("dom")
    special = mesh.shape["mode"] == 4
    step = four_groups if special else any_groups
    step = jax.shard_map(
        step, mesh=mesh, in_specs=in_specs, out_specs=out_specs, check_vma=False
    )
    return step
```
